128 devices in a mesh: grp: 4 (over x), seq: 2 (over core), shard: 16 (over z, y).
Axes of the slice: x: 4, y: 4, z: 4, core: 2. Of those that a mesh axis runs over, the one named last changes fastest.
Arguments:
- states: bfloat16 [4, 4096, 1280], P('grp', ('seq', 'shard')), may hold values from -6 to 6
- w_query: bfloat16 [1280, 1280], P('shard'), may hold values from -0.15625 to 0.15625
- w_key: bfloat16 [1280, 1280], P('shard'), may hold values from -0.15625 to 0.15625
- w_value: bfloat16 [1280, 1280], P('shard'), may hold values from -0.15625 to 0.15625
- w_out: bfloat16 [1280, 1280], P('shard'), may hold values from -0.15625 to 0.15625
- w_up: bfloat16 [1280, 5120], P('shard'), may hold values from -0.15625 to 0.15625
- w_gate: bfloat16 [1280, 5120], P('shard'), may hold values from -0.15625 to 0.15625
- w_down: bfloat16 [5120, 1280], P('shard'), may hold values from -0.078125 to 0.078125
- scale_qk: bfloat16 [1280], P('shard'), may hold values from 0.796875 to 1.59375
- alpha_attn: bfloat16 [1280], P('shard'), may hold values from 0.14941406 to 0.59765625
- alpha_mlp: bfloat16 [1280], P('shard'), may hold values from 0.14941406 to 0.59765625
- scale_up: bfloat16 [5120], P('shard'), may hold values from 0.5 to 2
- scale_gate: bfloat16 [5120], P('shard'), may hold values from 0.5 to 2
- lengths: int32 [4], P('grp'), may hold values from 1024 to 4096, as said below
- cotangent: bfloat16 [4, 4096, 1280], P('grp', ('seq', 'shard')), may hold values from -6 to 6
Outputs:
- result: bfloat16 [4, 4096, 1280], P('grp', ('seq', 'shard'))
- grad_input: float32 [4, 4096, 1280], P('grp', ('seq', 'shard'))
- grad_query: float32 [1280, 1280], P('shard')
- grad_key: float32 [1280, 1280], P('shard')
- grad_value: float32 [1280, 1280], P('shard')
- grad_outproj: float32 [1280, 1280], P('shard')
- grad_up: float32 [1280, 5120], P('shard')
- grad_gate: float32 [1280, 5120], P('shard')
- grad_down: float32 [5120, 1280], P('shard')
- grad_scale_qk: float32 [1280], P('shard')
- grad_alpha_attn: float32 [1280], P('shard')
- grad_alpha_mlp: float32 [1280], P('shard')
- grad_scale_up: float32 [5120], P('shard')
- grad_scale_gate: float32 [5120], P('shard')
The draws below stay inside these ranges and needn't reach their ends.
Inputs may be any that keep to these rules, and one draw needn't show every extreme that they name: `lengths`: each slot holds one sequence from its first position on; positions from its length on are padding. Some slot is full in every draw.
All inputs are finite; a program needn't handle non-finite values.
Results may differ from the reference program's by a relative error of at most 0.028.
Values may be sent and summed in bfloat16 or wider, within the bound.
A program may use at most 320 MiB of HBM per device.

```python
import math
import jax
import jax.numpy as jnp
from jax import lax

D = 1280
HEADS = 20
HDIM = 64
FF = 5120
SEQ_LEN = 4096
SLOTS = 4


def draw_lengths(key, part):
    lowest = SEQ_LEN // 4
    picks = jax.random.randint(jax.random.fold_in(key, 11), (SLOTS,), lowest, SEQ_LEN + 1)
    chosen = jax.random.randint(jax.random.fold_in(key, 12), (), 0, SLOTS)
    return jnp.where(jnp.arange(SLOTS) == chosen, SEQ_LEN, picks).astype(jnp.int32)


def block_levels(key, dims, shards, low, top_value):
    gain = 1.0
    for position, shards_of in shards:
        steps = jax.random.uniform(jax.random.fold_in(jax.random.fold_in(key, 6), position), (shards_of,), jnp.float32, low / len(shards), top_value / len(shards))
        gain = gain * jnp.repeat(jnp.exp(steps), dims[position] // shards_of).reshape((-1,) + (1,) * (len(dims) - 1 - position))
    return gain


def normal_values(rng, shape, scale, bound, cuts=(), kind=jnp.bfloat16):
    entries = jax.random.normal(rng, shape, jnp.float32) * scale
    if len(cuts) > 0:
        entries = block_levels(rng, shape, cuts, -0.22, 0.18) * entries
    return jnp.clip(entries, min=-bound, max=bound).astype(kind)


def setup_inputs(seed: int = 0) -> dict:
    splits = jax.random.split(jax.random.key(seed), 16)
    return {
        "states": normal_values(splits[0], (SLOTS, SEQ_LEN, D), 1.0, 6.0, ((0, 4), (1, 32))),
        "w_query": normal_values(splits[1], (D, D), D ** -0.5, 0.15625, ((0, 16),)),
        "w_key": normal_values(splits[2], (D, D), D ** -0.5, 0.15625, ((0, 16),)),
        "w_value": normal_values(splits[3], (D, D), D ** -0.5, 0.15625, ((0, 16),)),
        "w_out": normal_values(splits[4], (D, D), D ** -0.5, 0.15625, ((0, 16),)),
        "w_up": normal_values(splits[5], (D, FF), D ** -0.5, 0.15625, ((0, 16),)),
        "w_gate": normal_values(splits[6], (D, FF), D ** -0.5, 0.15625, ((0, 16),)),
        "w_down": normal_values(splits[7], (FF, D), FF ** -0.5, 0.078125, ((0, 16),)),
        "scale_qk": jnp.clip(jnp.exp(math.log(1.59375) - 0.6931472 * jax.random.uniform(splits[8], (D,), jnp.float32) ** block_levels(splits[8], (D,), ((0, 16),), -0.2, 0.2)), 0.796875, 1.59375).astype(jnp.bfloat16),
        "alpha_attn": jnp.clip(0.14941406 + 0.4482422 * jax.random.uniform(splits[9], (D,), jnp.float32) ** block_levels(splits[9], (D,), ((0, 16),), -0.2, 0.2), 0.14941406, 0.59765625).astype(jnp.bfloat16),
        "alpha_mlp": jnp.clip(0.14941406 + 0.4482422 * jax.random.uniform(splits[10], (D,), jnp.float32) ** block_levels(splits[10], (D,), ((0, 16),), -0.2, 0.2), 0.14941406, 0.59765625).astype(jnp.bfloat16),
        "scale_up": jnp.clip(jnp.exp(math.log(2.0) - 1.3862944 * jax.random.uniform(splits[11], (FF,), jnp.float32) ** block_levels(splits[11], (FF,), ((0, 16),), -0.2, 0.2)), 0.5, 2.0).astype(jnp.bfloat16),
        "scale_gate": jnp.clip(jnp.exp(math.log(2.0) - 1.3862944 * jax.random.uniform(splits[12], (FF,), jnp.float32) ** block_levels(splits[12], (FF,), ((0, 16),), -0.2, 0.2)), 0.5, 2.0).astype(jnp.bfloat16),
        "lengths": draw_lengths(jax.random.fold_in(splits[15], 71), 0),
        "cotangent": normal_values(splits[14], (SLOTS, SEQ_LEN, D), 1.0, 6.0, ((0, 4), (1, 32))),
    }


@jax.custom_vjp
def low(v):
    return lax.optimization_barrier(v.astype(jnp.bfloat16)).astype(jnp.float32)

@jax.custom_vjp
def low_back(v):
    return v

def low_keep(v):
    return (low(v), None)

def low_pass(kept, grad):
    return (grad,)

def back_keep(v):
    return (v, None)

def back_low(kept, grad):
    return (low(grad),)
low.defvjp(low_keep, low_pass)
low_back.defvjp(back_keep, back_low)

def unit_rms(values):
    return values * lax.rsqrt(lax.optimization_barrier(jnp.mean(values * values, axis=-1, keepdims=True)) + 1e-06)

def rotate(values, positions):
    rows = values.shape[0]
    width = values.shape[1] // HEADS
    half = width // 2
    freqs = jnp.exp(jnp.arange(half, dtype=jnp.float32) * (-2.0 * math.log(10000.0) / width))
    angles = positions.astype(jnp.float32)[:, None] * freqs[None, :]
    cosine = jnp.cos(angles)[:, None, :]
    sine = jnp.sin(angles)[:, None, :]
    shaped = values.reshape(rows, HEADS, width)
    former = shaped[..., :half]
    latter = shaped[..., half:]
    turned = jnp.concatenate([former * cosine - latter * sine, latter * cosine + former * sine], axis=-1)
    return turned.reshape(rows, HEADS * width)

def head_norm(values, positions, scale):
    rows = values.shape[0]
    turned = rotate(values, positions)
    return unit_rms(turned.reshape(rows, HEADS, -1)).reshape(values.shape) * scale

def product(left, right):
    return jnp.dot(left, right, precision=lax.Precision.HIGHEST)

def layer(states, w_query, w_key, w_value, w_out, w_up, w_gate, w_down, scale_qk, alpha_attn, alpha_mlp, scale_up, scale_gate, length):
    rows = states.shape[0]
    positions = jnp.arange(rows, dtype=jnp.int32)
    valid_rows = (positions < length).astype(jnp.float32)[:, None]
    q_raw = low_back(product(states, w_query))
    k_raw = low_back(product(states, w_key))
    values = low_back(low(product(states, w_value)))
    queries = low_back(low(head_norm(q_raw, positions, scale_qk)))
    keys = low_back(low(head_norm(k_raw, positions, scale_qk)))
    query_heads = queries.reshape(rows, HEADS, HDIM)
    key_heads = keys.reshape(rows, HEADS, HDIM)
    value_heads = values.reshape(rows, HEADS, HDIM)
    block = 512 if rows % 512 == 0 else rows
    count = rows // block

    def attend(index):
        first_row = (index * block).astype(jnp.int32)
        query_block = lax.dynamic_slice_in_dim(query_heads, first_row, block, 0)
        query_pos = first_row + jnp.arange(block, dtype=jnp.int32)
        scores = jnp.einsum('qhd,khd->qhk', query_block, key_heads, precision=lax.Precision.HIGHEST) * HDIM ** (-0.5)
        scores = low_back(scores)
        allowed = (positions[None, :] <= query_pos[:, None]) & (positions[None, :] < length)
        scores = jnp.where(allowed[:, None, :], scores, -1e+30)
        weights = low(jax.nn.softmax(scores, axis=-1))
        output = jnp.einsum('qhk,khd->qhd', weights, value_heads, precision=lax.Precision.HIGHEST)
        return low_back(low(output))
    attended = lax.map(jax.checkpoint(attend), jnp.arange(count, dtype=jnp.int32)).reshape(rows, D)
    mixed = low_back(product(attended, w_out))
    first = unit_rms(states + alpha_attn * (unit_rms(mixed) - states))
    first_low = low(first)
    up_part = low_back(product(first_low, w_up))
    gate_part = low_back(product(first_low, w_gate))
    hidden = low(up_part * scale_up * jax.nn.silu(gate_part * scale_gate))
    down_part = low_back(product(hidden, w_down))
    return unit_rms(first + alpha_mlp * (unit_rms(down_part) - first)) * valid_rows

def reference(states, w_query, w_key, w_value, w_out, w_up, w_gate, w_down, scale_qk, alpha_attn, alpha_mlp, scale_up, scale_gate, lengths, cotangent):
    params = tuple((item.astype(jnp.float32) for item in (w_query, w_key, w_value, w_out, w_up, w_gate, w_down, scale_qk, alpha_attn, alpha_mlp, scale_up, scale_gate)))

    def slot_step(totals, inputs):
        slot_states, slot_cot, length = inputs

        def forward(slot_in, *weights):
            return layer(slot_in, *weights, length)
        output, pullback = jax.vjp(forward, slot_states.astype(jnp.float32), *params)
        grads = pullback(slot_cot.astype(jnp.float32))
        totals = tuple((left + right for left, right in zip(totals, grads[1:])))
        return (totals, (output.astype(jnp.bfloat16), grads[0]))
    zeros = tuple((jnp.zeros_like(item) for item in params))
    totals, (outputs, grad_input) = lax.scan(slot_step, zeros, (states, cotangent, lengths))
    return (outputs, grad_input, totals[0], totals[1], totals[2], totals[3], totals[4], totals[5], totals[6], totals[7], totals[8], totals[9], totals[10], totals[11])
```

```python
import functools
import math

import jax
import jax.numpy as jnp
import numpy as np
from jax import lax
from jax.experimental import pallas as pl
from jax.experimental.pallas import tpu as pltpu
from jax.sharding import PartitionSpec as P


D, HEADS, HDIM, FF = 1280, 20, 64, 5120
ROWS, BLOCKS, HG = 128, 4, 5
GROUP = HG * HDIM
EPS = 1e-6
BF, F32 = jnp.bfloat16, jnp.float32
MESH = pl.DeviceIdType.MESH
VMEM_LIMIT = 60 << 20


def here():
    s = lax.axis_index("shard")
    return lax.axis_index("grp"), lax.axis_index("seq"), s // 4, s % 4


def dev(x, c, z, y):
    return (x, c, z * 4 + y)


def worker(z):
    return ((z + 1) // 2) % 2


def owner_z(w, i):
    return i * (3 - 2 * w) + w


def step(v, d):
    return (v + d) % 4


def rcopy(src, dst, ss, rs, to):
    return pltpu.make_async_remote_copy(
        src_ref=src, dst_ref=dst, send_sem=ss, recv_sem=rs, device_id=to, device_id_type=MESH
    )


def lcopy(src, dst, sem):
    return pltpu.make_async_copy(src, dst, sem)


def landed(dst, sem):
    pltpu.make_async_copy(dst, dst, sem).wait()


def greet(peers):
    bar = pltpu.get_barrier_semaphore()
    for p in peers:
        pl.semaphore_signal(bar, inc=1, device_id=p, device_id_type=MESH)
    pl.semaphore_wait(bar, len(peers))


def z_peers(x, c, z, y):
    far = [dev(x, cc, step(z, d), y) for d in (1, 2, 3) for cc in (0, 1)]
    return [dev(x, 1 - c, z, y)] + far


def z_gather_start(src, dst, ss, rs, x, c, z, y):
    w = worker(z)
    slot = c * 2 + z // 2
    for d in (2, 1, 3):
        rcopy(src, dst.at[slot], ss.at[d], rs.at[slot], dev(x, w, step(z, d), y)).start()

    @pl.when(c == w)
    def _():
        lcopy(src, dst.at[slot], rs.at[slot]).start()

    @pl.when(c != w)
    def _():
        rcopy(src, dst.at[slot], ss.at[0], rs.at[slot], dev(x, w, z, y)).start()


def z_gather_wait(src, dst, ss, rs, c, z):
    for j in range(BLOCKS):
        landed(dst.at[j], rs.at[j])
    for d in (1, 2, 3):
        landed(src, ss.at[d])

    @pl.when(c != worker(z))
    def _():
        landed(src, ss.at[0])


def z_scatter_start(part, dst, ss, rs, x, c, z, y):
    for j in range(BLOCKS):
        oc, oz = j // 2, owner_z(c, j % 2)
        mine = jnp.logical_and(c == oc, z == oz)

        @pl.when(mine)
        def _(j=j):
            lcopy(part.at[j], dst.at[z], rs.at[z]).start()

        @pl.when(jnp.logical_not(mine))
        def _(j=j, oc=oc, oz=oz):
            rcopy(part.at[j], dst.at[z], ss.at[j], rs.at[z], dev(x, oc, oz, y)).start()


def z_scatter_wait(part, dst, ss, rs, c, z):
    for k in range(4):
        landed(dst.at[k], rs.at[k])
    for j in range(BLOCKS):
        mine = jnp.logical_and(c == j // 2, z == owner_z(c, j % 2))

        @pl.when(jnp.logical_not(mine))
        def _(j=j):
            landed(part.at[j], ss.at[j])


def remote_call(kernel, outs, ins_spaces, scratch, cid, name):
    any_spec = pl.BlockSpec(memory_space=pl.ANY)
    vmem = pl.BlockSpec(memory_space=pltpu.VMEM)
    return pl.pallas_call(
        kernel,
        out_shape=[jax.ShapeDtypeStruct(s, d) for s, d, _ in outs],
        in_specs=[any_spec if s == "a" else vmem for s in ins_spaces],
        out_specs=[any_spec if s == "a" else vmem for _, _, s in outs],
        scratch_shapes=scratch,
        compiler_params=pltpu.CompilerParams(
            collective_id=cid, has_side_effects=True, vmem_limit_bytes=VMEM_LIMIT
        ),
        name=name,
    )


def local_call(kernel, outs, n_in, scratch, name, smem=0):
    vmem = pl.BlockSpec(memory_space=pltpu.VMEM)
    sm = pl.BlockSpec(memory_space=pltpu.SMEM)
    return pl.pallas_call(
        kernel,
        out_shape=[jax.ShapeDtypeStruct(s, d) for s, d in outs],
        in_specs=[sm] * smem + [vmem] * n_in,
        out_specs=[vmem for _ in outs],
        scratch_shapes=scratch,
        compiler_params=pltpu.CompilerParams(vmem_limit_bytes=VMEM_LIMIT),
        name=name,
    )


def dma(*shape):
    return pltpu.SemaphoreType.DMA(shape)


def open_kernel(st, wq, vec, wo, xg, wqkv, vecs, wog, xs, xr, s1, r1, s2, r2, s3, r3, sv, rv, so, ro, lo):
    x, c, z, y = here()
    sib = dev(x, 1 - c, z, y)
    half = pl.ds(pl.multiple_of(c * 640, 128), 640)
    other = pl.ds(pl.multiple_of((1 - c) * 640, 128), 640)
    greet(z_peers(x, c, z, y) + [dev(x, c, z, step(y, d)) for d in (1, 2, 3)])
    for d in (2, 1, 3):
        z2 = step(z, d)
        rcopy(wq.at[c, z2], wqkv.at[c, z, y], s1.at[d], r1.at[z], dev(x, c, z2, y)).start()
        rcopy(vec, vecs.at[z, y], sv.at[0, d], rv.at[0, z], dev(x, c, z2, y)).start()
    own = lcopy(wq.at[c, z], wqkv.at[c, z, y], lo.at[0])
    own.start()
    own_v = lcopy(vec, vecs.at[z, y], lo.at[1])
    own_v.start()
    own_o = lcopy(wo.at[:, half], wog.at[y, :, half], lo.at[2])
    own_o.start()
    for d in (2, 1, 3):
        rcopy(wo.at[:, half], wog.at[y, :, half], so.at[0, d], ro.at[0, y], dev(x, c, z, step(y, d))).start()
    rcopy(wo.at[:, half], wog.at[y, :, half], so.at[0, 0], ro.at[1, y], sib).start()
    z_gather_start(st, xg, xs, xr, x, c, z, y)
    for d in (1, 2, 3):
        z2 = step(z, d)
        landed(wqkv.at[c, z2, y], r1.at[z2])
        landed(vecs.at[z2, y], rv.at[0, z2])
    own.wait()
    own_v.wait()
    for d in (2, 1, 3):
        to = dev(x, c, z, step(y, d))
        rcopy(wqkv.at[c, :, y], wqkv.at[c, :, y], s2.at[d], r2.at[y], to).start()
        rcopy(vecs.at[:, y], vecs.at[:, y], sv.at[1, d], rv.at[1, y], to).start()
    rcopy(wqkv.at[c, :, y], wqkv.at[c, :, y], s3.at[0], r3.at[y], sib).start()
    for d in (1, 3, 2):
        y2 = step(y, d)
        landed(wog.at[y2, :, half], ro.at[0, y2])
        rcopy(wog.at[y2, :, half], wog.at[y2, :, half], so.at[1, d], ro.at[1, y2], sib).start()
        landed(wqkv.at[c, :, y2], r2.at[y2])
        rcopy(wqkv.at[c, :, y2], wqkv.at[c, :, y2], s3.at[d], r3.at[y2], sib).start()
    z_gather_wait(st, xg, xs, xr, c, z)
    own_o.wait()
    for k in range(4):
        landed(wqkv.at[1 - c, :, k], r3.at[k])
        landed(wog.at[k, :, other], ro.at[1, k])
        landed(wqkv.at[c, :, k], s3.at[k])
    landed(wo.at[:, half], so.at[0, 0])
    for d in (1, 2, 3):
        landed(vecs.at[:, step(y, d)], rv.at[1, step(y, d)])
        landed(wq.at[c, z], s1.at[d])
        landed(vec, sv.at[0, d])
        landed(vecs.at[:, y], sv.at[1, d])
        landed(wqkv.at[c, :, y], s2.at[d])
        landed(wo.at[:, half], so.at[0, d])
        landed(wog.at[y, :, half], so.at[1, d])


def open_gather(st, wq, vec, wo):
    return remote_call(
        open_kernel,
        [
            ((BLOCKS, ROWS, D), BF, "a"),
            ((2, 4, 4, 80, 512), BF, "a"),
            ((4, 4, 8, 896), F32, "a"),
            ((4, 80, D), BF, "a"),
        ],
        "aaaa",
        [dma(4), dma(4), dma(4), dma(4), dma(4), dma(4), dma(4), dma(4), dma(2, 4), dma(2, 4), dma(2, 4), dma(2, 4), dma(3)],
        0,
        "open_gather",
    )(st, wq, vec, wo)


def ff_kernel(wu, wg, wd, wff, wdn, s1, r1, s2, r2, s3, r3, lo):
    x, c, z, y = here()
    sib = dev(x, 1 - c, z, y)
    half = pl.ds(pl.multiple_of(c * 640, 128), 640)
    other = pl.ds(pl.multiple_of((1 - c) * 640, 128), 640)
    greet(
        [sib]
        + [dev(x, c, step(z, d), y) for d in (1, 2, 3)]
        + [dev(x, c, z, step(y, d)) for d in (1, 2, 3)]
    )

    def columns(ref, k):
        return ref.at[:, pl.ds(pl.multiple_of(k * D, 128), D)]

    for which, ref in ((0, wu), (1, wg)):

        @pl.when(c == which)
        def _(ref=ref):
            for d in (2, 1, 3):
                z2 = step(z, d)
                rcopy(columns(ref, z2), wff.at[c, z, y], s1.at[d], r1.at[z], dev(x, c, z2, y)).start()
            lcopy(columns(ref, z), wff.at[c, z, y], lo.at[0]).start()

    lcopy(wd.at[:, half], wdn.at[y, :, half], lo.at[1]).start()
    for d in (2, 1, 3):
        rcopy(wd.at[:, half], wdn.at[y, :, half], s2.at[0, d], r2.at[0, y], dev(x, c, z, step(y, d))).start()
    rcopy(wd.at[:, half], wdn.at[y, :, half], s3.at[0, 0], r3.at[0, y], sib).start()
    for d in (1, 2, 3):
        landed(wff.at[c, step(z, d), y], r1.at[step(z, d)])
    landed(wff.at[c, z, y], lo.at[0])
    for d in (2, 1, 3):
        rcopy(wff.at[c, :, y], wff.at[c, :, y], s2.at[1, d], r2.at[1, y], dev(x, c, z, step(y, d))).start()
    rcopy(wff.at[c, :, y], wff.at[c, :, y], s3.at[1, 0], r3.at[1, y], sib).start()
    for d in (1, 3, 2):
        y2 = step(y, d)
        landed(wdn.at[y2, :, half], r2.at[0, y2])
        rcopy(wdn.at[y2, :, half], wdn.at[y2, :, half], s3.at[0, d], r3.at[0, y2], sib).start()
    for d in (1, 3, 2):
        y2 = step(y, d)
        landed(wff.at[c, :, y2], r2.at[1, y2])
        rcopy(wff.at[c, :, y2], wff.at[c, :, y2], s3.at[1, d], r3.at[1, y2], sib).start()
    landed(wdn.at[y, :, half], lo.at[1])
    for k in range(4):
        landed(wdn.at[k, :, other], r3.at[0, k])
        landed(wff.at[1 - c, :, k], r3.at[1, k])
        landed(wdn.at[k, :, half], s3.at[0, k])
        landed(wff.at[c, :, k], s3.at[1, k])
    for d in (1, 2, 3):
        landed(wff.at[c, z, y], s1.at[d])
        landed(wdn.at[y, :, half], s2.at[0, d])
        landed(wff.at[c, :, y], s2.at[1, d])


def ff_gather(wu, wg, wd):
    return remote_call(
        ff_kernel,
        [((2, 4, 4, 80, D), BF, "a"), ((4, 320, D), BF, "a")],
        "aaa",
        [dma(4), dma(4), dma(2, 4), dma(2, 4), dma(2, 4), dma(2, 4), dma(2)],
        1,
        "ff_gather",
    )(wu, wg, wd)


def rope_tables():
    freqs = np.exp(np.arange(32) * (-2.0 * math.log(10000.0) / 64))
    freqs = np.concatenate([freqs, freqs])
    sign = np.concatenate([-np.ones(32), np.ones(32)])
    inner = np.arange(ROWS)[:, None] * freqs
    outer = (np.arange(32) * ROWS)[:, None] * freqs
    return (
        np.stack([np.cos(inner), np.sin(inner) * sign]).astype(np.float32),
        np.stack([np.cos(outer), np.sin(outer) * sign]).astype(np.float32),
    )


def block_index(c, y, j):
    return (j // 2) * 16 + owner_z(c, j % 2) * 4 + y


def turn_of(inner, outer, b):
    oc = outer[0, pl.ds(b, 1), :]
    os = outer[1, pl.ds(b, 1), :]
    return oc * inner[0] - os * inner[1], os * inner[0] + oc * inner[1]


def swap(v):
    return jnp.concatenate([v[:, 32:], v[:, :32]], axis=1)


def qkv_kernel(xg, w, scale, inner, outer, q_out, kv_out, t_out, y0, y1):
    _, c, _, y = here()
    xs = xg[...]
    y0[...] = jnp.dot(xs, w[0], preferred_element_type=F32)
    y1[...] = jnp.dot(xs, w[1], preferred_element_type=F32)

    def per_block(j, carry):
        rows = pl.ds(pl.multiple_of(j * ROWS, ROWS), ROWS)
        cosine, sine = turn_of(inner, outer, block_index(c, y, j))
        a0, a1 = y0[rows, :], y1[rows, :]
        for h in range(HG):
            cols = slice(h * HDIM, (h + 1) * HDIM)
            sc = scale[0:1, cols]
            turned = []
            for raw in (a0[:, cols], a1[:, cols]):
                t = raw * cosine + swap(raw) * sine
                turned.append(t)
            qn, kn = [
                t * lax.rsqrt(jnp.mean(t * t, axis=-1, keepdims=True) + EPS) * sc for t in turned
            ]
            q = qn.astype(BF).astype(F32) * 0.125
            if h < 3:
                v = a0[:, GROUP + h * HDIM : GROUP + (h + 1) * HDIM]
            else:
                v = a1[:, GROUP + (h - 3) * HDIM : GROUP + (h - 2) * HDIM]
            t_out[h, rows, :] = jnp.concatenate(turned, axis=1)
            q_out[h, rows, :] = jnp.concatenate([q, jnp.zeros_like(q)], axis=1).astype(BF)
            kv_out[h, rows, :] = jnp.concatenate([kn, v], axis=1).astype(BF)
        return carry

    lax.fori_loop(0, BLOCKS, per_block, 0)


def make_qkv(xg, w, scale, inner, outer):
    n = BLOCKS * ROWS
    return local_call(
        qkv_kernel,
        [((HG, n, 128), BF), ((HG, n, 128), BF), ((HG, n, 128), F32)],
        5,
        [pltpu.VMEM((n, 512), F32), pltpu.VMEM((n, 512), F32)],
        "make_qkv",
    )(xg, w, scale, inner, outer)


def kv_kernel(kv, out, sy, ry, ss, rs, lo):
    x, c, z, y = here()
    sib = dev(x, 1 - c, z, y)
    greet([sib] + [dev(x, c, z, step(y, d)) for d in (1, 2, 3)])

    def place(w, j, yy):
        return out.at[:, j // 2, owner_z(w, j % 2), yy]

    for j in range(BLOCKS):
        for d in (2, 1, 3):
            rcopy(kv.at[:, j], place(c, j, y), sy.at[d, j], ry.at[y, j], dev(x, c, z, step(y, d))).start()
        rcopy(kv.at[:, j], place(c, j, y), ss.at[0, j], rs.at[y, j], sib).start()
        lcopy(kv.at[:, j], place(c, j, y), lo.at[j]).start()
    for j in range(BLOCKS):
        for d in (1, 3, 2):
            y2 = step(y, d)
            landed(place(c, j, y2), ry.at[y2, j])
            rcopy(place(c, j, y2), place(c, j, y2), ss.at[d, j], rs.at[y2, j], sib).start()
    for j in range(BLOCKS):
        landed(kv.at[:, j], lo.at[j])
        for k in range(4):
            landed(place(1 - c, j, k), rs.at[k, j])
            landed(kv.at[:, j], ss.at[k, j])
        for d in (1, 2, 3):
            landed(kv.at[:, j], sy.at[d, j])


def kv_gather(kv):
    return remote_call(
        kv_kernel,
        [((HG, 2, 4, 4, ROWS, 128), BF, "a")],
        "a",
        [dma(4, 4), dma(4, 4), dma(4, 4), dma(4, 4), dma(4)],
        2,
        "kv_gather",
    )(kv)[0]


TILE = 512


def tiles_of(c, j):
    return (j // 2) * 4 + owner_z(c, j % 2) + 1


def causal(y):
    key = lax.broadcasted_iota(jnp.int32, (TILE, ROWS), 0)
    query = lax.broadcasted_iota(jnp.int32, (TILE, ROWS), 1)
    return key <= query + y * ROWS


def nt(a, b):
    return lax.dot_general(a, b, (((1,), (1,)), ((), ())), preferred_element_type=F32)


def tn(a, b):
    return lax.dot_general(a, b, (((0,), (0,)), ((), ())), preferred_element_type=F32)


def key_valid(length, t):
    pos = t * TILE + lax.broadcasted_iota(jnp.int32, (1, TILE), 1)
    return (pos < length).astype(F32)


def attend_kernel(length, q, kv, wo, part, att, lse, kvt, low):
    _, c, _, y = here()
    tri = causal(y)

    def per_head(h, carry):
        def flip(t, carry):
            keys = pl.ds(pl.multiple_of(t * TILE, TILE), TILE)
            valid = key_valid(length[0], t)
            turned = kv[h, keys, :].astype(F32).T * valid
            row = lax.broadcasted_iota(jnp.int32, (128, TILE), 0)
            kvt[t] = jnp.where(row < HDIM, valid, turned).astype(BF)
            return carry

        lax.fori_loop(0, 8, flip, 0)

        def per_block(j, carry):
            rows = pl.ds(pl.multiple_of(j * ROWS, ROWS), ROWS)
            qj = q[h, rows, :]
            last = tiles_of(c, j) - 1

            def scores(t):
                keys = pl.ds(pl.multiple_of(t * TILE, TILE), TILE)
                return nt(kv[h, keys, :], qj)

            def full(t, acc):
                p = jnp.exp(scores(t)).astype(BF)
                return acc + jnp.dot(kvt[t], p, preferred_element_type=F32)

            acc = lax.fori_loop(0, last, full, jnp.zeros((128, ROWS), F32))
            p = jnp.where(tri, jnp.exp(scores(last)), 0.0).astype(BF)
            acc = acc + jnp.dot(kvt[last], p, preferred_element_type=F32)
            total = acc[0:1]
            lse[h, pl.ds(j, 1), :] = jnp.log(total)
            out = (acc[HDIM:] / total).T
            att[h, rows, :] = out
            return carry

        lax.fori_loop(0, BLOCKS, per_block, 0)
        return carry

    lax.fori_loop(0, HG, per_head, 0)
    for h in range(HG):
        low[:, h * HDIM : (h + 1) * HDIM] = att[h].astype(BF)
    part[...] = jnp.dot(low[...], wo[...], preferred_element_type=F32).astype(BF)


def attend(length, q, kv, wo):
    n = BLOCKS * ROWS
    return local_call(
        attend_kernel,
        [((n, D), BF), ((HG, n, HDIM), F32), ((HG, BLOCKS, 128), F32)],
        3,
        [pltpu.VMEM((8, 128, TILE), BF), pltpu.VMEM((n, GROUP), BF)],
        "attend",
        smem=1,
    )(length, q, kv, wo)


def attend_back_kernel(length, q, kv, wo, dmix, att, lse, dq, dkv, gout, qdo, delta, kt, acc, low):
    _, c, _, y = here()
    tri = causal(y)
    d_att = nt(dmix[...], wo[...]).astype(BF)
    for h in range(HG):
        low[:, h * HDIM : (h + 1) * HDIM] = att[h].astype(BF)
        dh = d_att[:, h * HDIM : (h + 1) * HDIM].astype(F32)
        wide = jnp.concatenate([jnp.zeros_like(dh), dh], axis=1).astype(BF)
        prod = dh * att[h]
        for j in range(BLOCKS):
            rows = slice(j * ROWS, (j + 1) * ROWS)
            qdo[h, j, :ROWS] = q[h, rows, :]
            qdo[h, j, ROWS:] = wide[rows]
            delta[h, j : j + 1, :] = jnp.sum(prod[rows].T, axis=0, keepdims=True)
    gout[...] = tn(low[...], dmix[...]).astype(BF)

    def per_head(h, carry):
        def flip(t, carry):
            keys = pl.ds(pl.multiple_of(t * TILE, TILE), TILE)
            kt[t] = (kv[h, keys, :].astype(F32).T * key_valid(length[0], t)).astype(BF)
            acc[t] = jnp.zeros((TILE, 128), F32)
            return carry

        lax.fori_loop(0, 8, flip, 0)

        def per_block(j, carry):
            rows = pl.ds(pl.multiple_of(j * ROWS, ROWS), ROWS)
            both = qdo[h, j]
            l_row = lse[h, pl.ds(j, 1), :]
            d_row = delta[h, pl.ds(j, 1), :]
            last = tiles_of(c, j) - 1

            def tile(t, dqt, mask):
                keys = pl.ds(pl.multiple_of(t * TILE, TILE), TILE)
                sd = nt(kv[h, keys, :], both)
                p = jnp.exp(sd[:, :ROWS] - l_row)
                if mask:
                    p = jnp.where(tri, p, 0.0)
                ds = (p * (sd[:, ROWS:] - d_row)).astype(BF)
                pair = jnp.concatenate([ds, p.astype(BF)], axis=1)
                acc[t] += jnp.dot(pair, both, preferred_element_type=F32)
                return dqt + jnp.dot(kt[t], ds, preferred_element_type=F32)

            dqt = lax.fori_loop(0, last, lambda t, s: tile(t, s, False), jnp.zeros((128, ROWS), F32))
            dqt = tile(last, dqt, True)
            dq[h, rows, :] = dqt[:HDIM].T * 0.125
            return carry

        lax.fori_loop(0, BLOCKS, per_block, 0)

        def store(t, carry):
            keys = pl.ds(pl.multiple_of(t * TILE, TILE), TILE)
            dkv[h, keys, :] = acc[t].astype(BF)
            return carry

        lax.fori_loop(0, 8, store, 0)
        return carry

    lax.fori_loop(0, HG, per_head, 0)


def attend_back(length, q, kv, wo, dmix, att, lse):
    n = BLOCKS * ROWS
    return local_call(
        attend_back_kernel,
        [((HG, n, HDIM), F32), ((HG, 4096, 128), BF), ((GROUP, D), BF)],
        6,
        [
            pltpu.VMEM((HG, BLOCKS, 2 * ROWS, 128), BF),
            pltpu.VMEM((HG, BLOCKS, 128), F32),
            pltpu.VMEM((8, 128, TILE), BF),
            pltpu.VMEM((8, TILE, 128), F32),
            pltpu.VMEM((n, GROUP), BF),
        ],
        "attend_back",
        smem=1,
    )(length, q, kv, wo, dmix, att, lse)


def inv_rms(v):
    return lax.rsqrt(jnp.mean(v * v, axis=-1, keepdims=True) + EPS)


def back_rms(dy, yy, inv):
    return (dy - yy * jnp.mean(dy * yy, axis=-1, keepdims=True)) * inv


def total_of(buf):
    return (buf[0].astype(F32) + buf[1].astype(F32)) + (buf[2].astype(F32) + buf[3].astype(F32))


def mix_of(res, part, rate):
    inv_p = inv_rms(part)
    unit = part * inv_p
    diff = unit - res
    u = res + rate * diff
    inv_u = inv_rms(u)
    return u * inv_u, unit, inv_p, inv_u, diff


def mix_back(dy, res, part, rate):
    yy, unit, inv_p, inv_u, diff = mix_of(res, part, rate)
    du = back_rms(dy, yy, inv_u)
    return du * (1.0 - rate), back_rms(du * rate, unit, inv_p), jnp.sum(du * diff, axis=0, keepdims=True)


def meet(kernel, outs, ins_spaces, extra, cid, name):
    scratch = [
        pltpu.VMEM((4, ROWS, D), BF),
        pltpu.VMEM((ROWS, D), BF),
        dma(4),
        dma(4),
        dma(4),
        dma(4),
    ]
    return remote_call(kernel, outs, ins_spaces, scratch + extra, cid, name)


def first_kernel(part, st, rate, gathered, mixed, first, buf, low, s1, r1, s2, r2):
    x, c, z, y = here()
    greet(z_peers(x, c, z, y))
    z_scatter_start(part, buf, s1, r1, x, c, z, y)
    z_scatter_wait(part, buf, s1, r1, c, z)
    total = total_of(buf)
    mixed[...] = total
    out = mix_of(st[...].astype(F32), total, rate[0:1])[0]
    first[...] = out
    low[...] = out.astype(BF)
    z_gather_start(low, gathered, s2, r2, x, c, z, y)
    z_gather_wait(low, gathered, s2, r2, c, z)


def meet_first(part, st, rate):
    return meet(
        first_kernel,
        [((BLOCKS, ROWS, D), BF, "a"), ((ROWS, D), F32, "v"), ((ROWS, D), F32, "v")],
        "avv",
        [],
        3,
        "meet_first",
    )(part, st, rate)


def result_kernel(part, first, cot, rate, valid, gathered, result, d_first, grad, buf, low, s1, r1, s2, r2):
    x, c, z, y = here()
    greet(z_peers(x, c, z, y))
    z_scatter_start(part, buf, s1, r1, x, c, z, y)
    z_scatter_wait(part, buf, s1, r1, c, z)
    total = total_of(buf)
    live = valid[:, 0:1]
    base = first[...]
    am = rate[0:1]
    dy = cot[...].astype(F32) * live
    d_base, d_part, g = mix_back(dy, base, total, am)
    low[...] = d_part.astype(BF)
    z_gather_start(low, gathered, s2, r2, x, c, z, y)
    result[...] = (mix_of(base, total, am)[0] * live).astype(BF)
    d_first[...] = d_base
    grad[...] = jnp.broadcast_to(g, (8, D))
    z_gather_wait(low, gathered, s2, r2, c, z)


def meet_result(part, first, cot, rate, valid):
    return meet(
        result_kernel,
        [
            ((BLOCKS, ROWS, D), BF, "a"),
            ((ROWS, D), BF, "v"),
            ((ROWS, D), F32, "v"),
            ((8, D), F32, "v"),
        ],
        "avvvv",
        [],
        4,
        "meet_result",
    )(part, first, cot, rate, valid)


def back_kernel(part, d_base, st, mixed, rate, gathered, d_st, grad, buf, low, s1, r1, s2, r2):
    x, c, z, y = here()
    greet(z_peers(x, c, z, y))
    z_scatter_start(part, buf, s1, r1, x, c, z, y)
    z_scatter_wait(part, buf, s1, r1, c, z)
    dy = d_base[...] + total_of(buf)
    d_res, d_part, g = mix_back(dy, st[...].astype(F32), mixed[...], rate[0:1])
    low[...] = d_part.astype(BF)
    z_gather_start(low, gathered, s2, r2, x, c, z, y)
    d_st[...] = d_res
    grad[...] = jnp.broadcast_to(g, (8, D))
    z_gather_wait(low, gathered, s2, r2, c, z)


def meet_back(part, d_base, st, mixed, rate):
    return meet(
        back_kernel,
        [((BLOCKS, ROWS, D), BF, "a"), ((ROWS, D), F32, "v"), ((8, D), F32, "v")],
        "avvvv",
        [],
        5,
        "meet_back",
    )(part, d_base, st, mixed, rate)


def dkv_kernel(dkv, out, other, mine, got, ss, rs, sy, ry, lo):
    x, c, z, y = here()
    sib = dev(x, 1 - c, z, y)
    greet([sib] + [dev(x, c, z, step(y, d)) for d in (1, 2, 3)])
    for j in range(BLOCKS):
        oz, oc = owner_z(c, j % 2), owner_z(1 - c, j % 2)
        rcopy(dkv.at[:, j // 2, oc], other.at[:, j], ss.at[j], rs.at[j], sib).start()
        lcopy(dkv.at[:, j // 2, oz], mine.at[:, j], lo.at[j]).start()
    for j in range(BLOCKS):
        landed(mine.at[:, j], lo.at[j])
        landed(other.at[:, j], rs.at[j])
        for h in range(HG):
            mine[h, j] = (mine[h, j].astype(F32) + other[h, j].astype(F32)).astype(BF)
        for d in (2, 1, 3):
            y2 = step(y, d)
            rcopy(mine.at[:, j, y2], got.at[y, :, j], sy.at[d, j], ry.at[y, j], dev(x, c, z, y2)).start()
    for j in range(BLOCKS):
        for d in (1, 2, 3):
            landed(got.at[step(y, d), :, j], ry.at[step(y, d), j])
        for h in range(HG):
            acc = mine[h, j, y].astype(F32)
            for d in (1, 2, 3):
                acc = acc + got[step(y, d), h, j].astype(F32)
            out[h, j] = acc.astype(BF)
    for j in range(BLOCKS):
        landed(mine.at[:, j], ss.at[j])
        for d in (1, 2, 3):
            landed(mine.at[:, j, y], sy.at[d, j])


def dkv_reduce(dkv):
    return remote_call(
        dkv_kernel,
        [((HG, BLOCKS, ROWS, 128), BF, "v")],
        "a",
        [
            pltpu.VMEM((HG, BLOCKS, 4, ROWS, 128), BF),
            pltpu.VMEM((HG, BLOCKS, 4, ROWS, 128), BF),
            pltpu.VMEM((4, HG, BLOCKS, ROWS, 128), BF),
            dma(4),
            dma(4),
            dma(4, 4),
            dma(4, 4),
            dma(4),
        ],
        6,
        "dkv_reduce",
    )(dkv)[0]


def qkv_back_kernel(length, dq, dkv, t, scale, inner, outer, xg, w, part, gw, gs, d0, d1):
    _, c, _, y = here()
    gs[...] = jnp.zeros_like(gs)
    d1[:, 448:] = jnp.zeros((BLOCKS * ROWS, 64), BF)

    def per_block(j, carry):
        rows = pl.ds(pl.multiple_of(j * ROWS, ROWS), ROWS)
        b = block_index(c, y, j)
        cosine, sine = turn_of(inner, outer, b)
        live = (b * ROWS + lax.broadcasted_iota(jnp.int32, (ROWS, 1), 0) < length[0]).astype(F32)
        for h in range(HG):
            cols = slice(h * HDIM, (h + 1) * HDIM)
            sc = scale[0:1, cols]
            both = t[h, rows, :]
            kv = dkv[h, rows, :].astype(F32) * live
            for k, dy in ((0, dq[h, rows, :]), (1, kv[:, :HDIM])):
                dy = dy.astype(BF).astype(F32)
                tt = both[:, k * HDIM : (k + 1) * HDIM]
                inv = inv_rms(tt)
                unit = tt * inv
                gs[0:1, cols] += jnp.sum(dy * unit, axis=0, keepdims=True)
                dt = back_rms(dy * sc, unit, inv)
                draw = (dt * cosine + swap(dt * sine)).astype(BF)
                if k == 0:
                    d0[rows, cols] = draw
                else:
                    d1[rows, cols] = draw
            dv = kv[:, HDIM:].astype(BF)
            if h < 3:
                d0[rows, GROUP + h * HDIM : GROUP + (h + 1) * HDIM] = dv
            else:
                d1[rows, GROUP + (h - 3) * HDIM : GROUP + (h - 2) * HDIM] = dv
        return carry

    lax.fori_loop(0, BLOCKS, per_block, 0)
    part[...] = (nt(d0[...], w[0]) + nt(d1[...], w[1])).astype(BF)
    gw[0] = tn(xg[...], d0[...]).astype(BF)
    gw[1] = tn(xg[...], d1[...]).astype(BF)


def qkv_back(length, dq, dkv, t, scale, inner, outer, xg, w):
    n = BLOCKS * ROWS
    return local_call(
        qkv_back_kernel,
        [((n, D), BF), ((2, D, 512), BF), ((8, GROUP), F32)],
        8,
        [pltpu.VMEM((n, 512), BF), pltpu.VMEM((n, 512), BF)],
        "qkv_back",
        smem=1,
    )(length, dq, dkv, t, scale, inner, outer, xg, w)


def close_kernel(
    part, d_st, ga, gq, gd, go, vec,
    g_in, o_up, o_gate, o_qkv, o_down, o_out, o_vec,
    pbuf, ps, pr,
    ha, hq, hd, ra, rq, rd, fa, fq, fd, za, zq, zd, ob, oy, ox, o2, vs, vb,
    sc, rc, lo, sy, ry, sx, rx, s2, r2, sg, rg, sz, rz, sf, rf, so, ro, sv, rv,
):
    x, c, z, y = here()
    sib = dev(x, 1 - c, z, y)
    to_y = [None] + [dev(x, c, z, step(y, d)) for d in (1, 2, 3)]
    to_x = [None] + [dev(step(x, d), c, z, y) for d in (1, 2, 3)]
    greet(z_peers(x, c, z, y) + to_y[1:] + to_x[1:])
    z_scatter_start(part, pbuf, ps, pr, x, c, z, y)
    items = ((ga, ha, ra), (gq, hq, rq), (gd, hd, rd))
    for i, (g, h, _) in enumerate(items):
        rcopy(g.at[1 - c], h.at[1], sc.at[i], rc.at[i], sib).start()
        lcopy(g.at[c], h.at[0], lo.at[i]).start()
    rcopy(vec, vb.at[0], sv.at[0, 0], rv.at[0, 0], sib).start()
    rcopy(go, ob, so.at[0, 0], ro.at[0, 0], sib).start()
    lcopy(go, oy, lo.at[3]).start()

    def add_into(dst, terms, n):
        def body(k, carry):
            acc = terms[0](k).astype(F32)
            for f in terms[1:]:
                acc = acc + f(k).astype(F32)
            dst(k, acc)
            return carry

        lax.fori_loop(0, n, body, 0)

    for i, (g, h, _) in enumerate(items):
        landed(h.at[0], lo.at[i])
        landed(h.at[1], rc.at[i])

        def put(k, v, h=h):
            h[0, k // 4, k % 4] = v.astype(BF)

        add_into(put, [lambda k, h=h: h[0, k // 4, k % 4], lambda k, h=h: h[1, k // 4, k % 4]], 16)
        if i == 0:
            for d in (2, 1, 3):
                y2 = step(y, d)
                rcopy(ha.at[0, :, y2], ra.at[y], sy.at[0, d], ry.at[0, y], to_y[d]).start()
        elif i == 1:
            for d in (2, 1, 3):
                x2 = step(x, d)
                rcopy(hq.at[0, x2], rq.at[x], sx.at[0, d], rx.at[0, x], to_x[d]).start()
        else:
            for d in (2, 1, 3):
                x2 = step(x, d)
                rcopy(hd.at[0, :, x2], rd.at[x], sx.at[1, d], rx.at[1, x], to_x[d]).start()
    landed(oy, lo.at[3])
    landed(ob, ro.at[0, 0])
    vs[...] = vec[...]
    landed(vb.at[0], rv.at[0, 0])
    landed(vec, sv.at[0, 0])
    vs[...] = vs[...] + vb[0]
    for k in range(4):
        oy[k] = (oy[k].astype(F32) + ob[k].astype(F32)).astype(BF)
    for d in (2, 1, 3):
        y2 = step(y, d)
        rcopy(oy.at[y2], ox.at[y], sy.at[1, d], ry.at[1, y], to_y[d]).start()
        rcopy(vs, vb.at[d], sv.at[1, d], rv.at[1, d], to_y[d]).start()
    for d in (1, 2, 3):
        landed(ra.at[step(y, d)], ry.at[0, step(y, d)])

    def put_a(k, v):
        fa[0, k] = v.astype(BF)

    add_into(put_a, [lambda k: ha[0, k, y]] + [lambda k, d=d: ra[step(y, d), k] for d in (1, 2, 3)], 4)
    for d in (2, 1, 3):
        x2 = step(x, d)
        rcopy(fa.at[0, x2], fa.at[1, x], s2.at[0, d], r2.at[0, x], to_x[d]).start()
    for d in (1, 2, 3):
        landed(rq.at[step(x, d)], rx.at[0, step(x, d)])
        landed(rd.at[step(x, d)], rx.at[1, step(x, d)])

    def put_q(k, v):
        fq[0, k] = v.astype(BF)

    def put_d(k, v):
        fd[0, k] = v.astype(BF)

    add_into(put_q, [lambda k: hq[0, x, k]] + [lambda k, d=d: rq[step(x, d), k] for d in (1, 2, 3)], 4)
    add_into(put_d, [lambda k: hd[0, k, x]] + [lambda k, d=d: rd[step(x, d), k] for d in (1, 2, 3)], 4)
    for d in (2, 1, 3):
        y2 = step(y, d)
        rcopy(fq.at[0, y2], fq.at[1, y], s2.at[1, d], r2.at[1, y], to_y[d]).start()
        rcopy(fd.at[0, y2], fd.at[1, y], s2.at[2, d], r2.at[2, y], to_y[d]).start()
    acc = oy[y].astype(F32)
    tot = vs[...]
    for d in (1, 2, 3):
        landed(ox.at[step(y, d)], ry.at[1, step(y, d)])
        landed(vb.at[d], rv.at[1, d])
        landed(vs, sv.at[1, d])
        acc = acc + ox[step(y, d)].astype(F32)
        tot = tot + vb[d]
    ox[y] = acc.astype(BF)
    vs[...] = tot
    for d in (2, 1, 3):
        rcopy(ox.at[y], o2.at[d], so.at[1, d], ro.at[1, d], to_x[d]).start()
        rcopy(vs, vb.at[3 + d], sv.at[2, d], rv.at[2, d], to_x[d]).start()
    for d in (1, 2, 3):
        landed(fa.at[1, step(x, d)], r2.at[0, step(x, d)])
    sum_a = fa[0, x].astype(F32)
    for d in (1, 2, 3):
        sum_a = sum_a + fa[1, step(x, d)].astype(F32)
    za[0, x] = sum_a.astype(BF)
    for d in (2, 1, 3):
        rcopy(za.at[0, x], za.at[0, x], sg.at[0, d], rg.at[0, x], to_x[d]).start()
    for d in (1, 2, 3):
        landed(fq.at[1, step(y, d)], r2.at[1, step(y, d)])
        landed(fd.at[1, step(y, d)], r2.at[2, step(y, d)])
    sum_q = fq[0, y].astype(F32)
    sum_d = fd[0, y].astype(F32)
    for d in (1, 2, 3):
        sum_q = sum_q + fq[1, step(y, d)].astype(F32)
        sum_d = sum_d + fd[1, step(y, d)].astype(F32)
    zq[0, x] = sum_q.astype(BF)
    zd[c, x] = sum_d.astype(BF)
    for d in (2, 1, 3):
        rcopy(zq.at[0, x], zq.at[0, x], sg.at[1, d], rg.at[1, x], to_x[d]).start()
        rcopy(zd.at[c, x], zd.at[c, x], sg.at[2, d], rg.at[2, x], to_x[d]).start()
    acc = ox[y].astype(F32)
    tot = vs[...]
    for d in (1, 2, 3):
        landed(o2.at[d], ro.at[1, d])
        landed(vb.at[3 + d], rv.at[2, d])
        landed(vs, sv.at[2, d])
        acc = acc + o2[d].astype(F32)
        tot = tot + vb[3 + d]
    o_out[...] = acc
    vs[...] = tot
    for d in (2, 1, 3):
        rcopy(vs, vb.at[6 + d], sv.at[3, d], rv.at[3, d], dev(x, c, step(z, d), y)).start()
    for d in (1, 2, 3):
        landed(za.at[0, step(x, d)], rg.at[0, step(x, d)])
        landed(zq.at[0, step(x, d)], rg.at[1, step(x, d)])
    for d in (2, 1, 3):
        z2 = step(z, d)
        to = dev(x, c, z2, y)
        rcopy(za.at[0, z2], za.at[1 + c, z], sz.at[0, d], rz.at[0, z], to).start()
        rcopy(zq.at[0, z2], zq.at[1 + c, z], sz.at[1, d], rz.at[1, z], to).start()
    za[1 + c, z] = za[0, z]
    zq[1 + c, z] = zq[0, z]
    z_scatter_wait(part, pbuf, ps, pr, c, z)
    g_in[...] = d_st[...] + total_of(pbuf)
    for d in (1, 2, 3):
        landed(zd.at[c, step(x, d)], rg.at[2, step(x, d)])
    rcopy(zd.at[c], zd.at[c], sf.at[2], rf.at[2], sib).start()
    for d in (1, 2, 3):
        landed(za.at[1 + c, step(z, d)], rz.at[0, step(z, d)])
        landed(zq.at[1 + c, step(z, d)], rz.at[1, step(z, d)])
    rcopy(za.at[1 + c], za.at[1 + c], sf.at[0], rf.at[0], sib).start()
    rcopy(zq.at[1 + c], zq.at[1 + c], sf.at[1], rf.at[1], sib).start()
    tot = vs[...]
    for d in (1, 2, 3):
        landed(vb.at[6 + d], rv.at[3, d])
        landed(vs, sv.at[3, d])
        tot = tot + vb[6 + d]
    o_vec[0:2] = tot[0:2]
    o_vec[2:] = vs[2:]
    landed(za.at[2 - c], rf.at[0])
    landed(zq.at[2 - c], rf.at[1])
    landed(zd.at[1 - c], rf.at[2])
    for k in range(4):
        cols = slice(k * D, (k + 1) * D)
        o_up[:, cols] = za[1, k].astype(F32)
        o_gate[:, cols] = za[2, k].astype(F32)
        o_qkv[0, k] = zq[1, k].astype(F32)
        o_qkv[1, k] = zq[2, k].astype(F32)
        for half in range(2):
            o_down[k * 80 : (k + 1) * 80, half * 640 : (half + 1) * 640] = zd[half, k].astype(F32)
    for i, (g, h, r) in enumerate(items):
        landed(h.at[0], sc.at[i])
    landed(go, so.at[0, 0])
    landed(za.at[1], sf.at[0])
    landed(zq.at[1], sf.at[1])
    landed(zd.at[0], sf.at[2])
    for d in (1, 2, 3):
        landed(ra.at[0], sy.at[0, d])
        landed(ox.at[0], sy.at[1, d])
        landed(rq.at[0], sx.at[0, d])
        landed(rd.at[0], sx.at[1, d])
        landed(fa.at[0, 0], s2.at[0, d])
        landed(fq.at[0, 0], s2.at[1, d])
        landed(fd.at[0, 0], s2.at[2, d])
        landed(za.at[0, 0], sg.at[0, d])
        landed(zq.at[0, 0], sg.at[1, d])
        landed(zd.at[0, 0], sg.at[2, d])
        landed(za.at[0, 0], sz.at[0, d])
        landed(zq.at[0, 0], sz.at[1, d])
        landed(ox.at[0], so.at[1, d])


def close(part, d_st, ga, gq, gd, go, vec):
    V = pltpu.VMEM
    return remote_call(
        close_kernel,
        [
            ((ROWS, D), F32, "v"),
            ((80, FF), F32, "v"),
            ((80, FF), F32, "v"),
            ((2, 4, 80, 512), F32, "v"),
            ((320, D), F32, "v"),
            ((80, D), F32, "v"),
            ((8, D), F32, "v"),
        ],
        "avaaaav",
        [
            V((4, ROWS, D), BF), dma(4), dma(4),
            V((2, 4, 4, 80, D), BF), V((2, 4, 4, 80, 512), BF), V((2, 4, 4, 80, 640), BF),
            V((4, 4, 80, D), BF), V((4, 4, 80, 512), BF), V((4, 4, 80, 640), BF),
            V((2, 4, 80, D), BF), V((2, 4, 80, 512), BF), V((2, 4, 80, 640), BF),
            V((3, 4, 80, D), BF), V((3, 4, 80, 512), BF), V((2, 4, 80, 640), BF),
            V((4, 80, D), BF), V((4, 80, D), BF), V((4, 80, D), BF), V((4, 80, D), BF), V((8, D), F32), V((10, 8, D), F32),
            dma(3), dma(3), dma(4),
            dma(2, 4), dma(2, 4), dma(2, 4), dma(2, 4), dma(3, 4), dma(3, 4), dma(3, 4), dma(3, 4),
            dma(2, 4), dma(2, 4), dma(3), dma(3), dma(2, 4), dma(2, 4), dma(4, 4), dma(4, 4),
        ],
        7,
        "close",
    )(part, d_st, ga, gq, gd, go, vec)


def shards(
    states, w_query, w_key, w_value, w_out, w_up, w_gate, w_down,
    scale_qk, alpha_attn, alpha_mlp, scale_up, scale_gate, lengths, cotangent,
):
    x, c, z, y = here()
    st = states[0]
    position = (c * 16 + z * 4 + y) * ROWS + jnp.arange(ROWS, dtype=jnp.int32)
    valid = jnp.broadcast_to((position < lengths[0]).astype(F32)[:, None], (ROWS, 128))

    def heads(w):
        return w.reshape(80, 4, HG, HDIM)

    q4, k4, v4 = heads(w_query), heads(w_key), heads(w_value)
    half0 = jnp.concatenate([q4, v4[:, :, :3]], axis=2)
    half1 = jnp.concatenate([k4, v4[:, :, 3:], jnp.zeros_like(v4[:, :, :1])], axis=2)
    wq = jnp.stack([half0, half1]).reshape(2, 80, 4, 512).transpose(0, 2, 1, 3)
    vec = jnp.concatenate([scale_qk, alpha_attn, alpha_mlp, scale_up, scale_gate, jnp.zeros((16,), BF)])
    vec = jnp.broadcast_to(vec.astype(F32)[None], (8, 896))
    xg, wqkv, vecs, wo = open_gather(st, wq, vec, w_out)
    rows = vecs[:, :, 0].reshape(16, 896)
    mine = lax.dynamic_slice_in_dim(rows, z * 4, 4, 0)

    def wide(v):
        return jnp.broadcast_to(v.reshape(1, -1), (8, v.size))

    scale_g = wide(mine[:, :80])
    rate_a = wide(rows[:, 80:160])
    rate_m = wide(rows[:, 160:240])
    su = mine[:, 240:560].reshape(1, D)
    sg = mine[:, 560:880].reshape(1, D)

    wff, wdn = ff_gather(w_up, w_gate, w_down)
    wff = wff.reshape(2, D, D)
    wdn = wdn.reshape(D, D)
    inner, outer = (jnp.asarray(t) for t in rope_tables())
    n = BLOCKS * ROWS
    xg2 = xg.reshape(n, D)
    wqkv2 = wqkv.reshape(2, D, 512)
    q, kv, turned = make_qkv(xg2, wqkv2, scale_g, inner, outer)
    kv_all = kv_gather(kv.reshape(HG, BLOCKS, ROWS, 128)).reshape(HG, 4096, 128)
    wo2 = wo.reshape(GROUP, D)
    part, att, lse = attend(lengths, q, kv_all, wo2)
    first_g, mixed, first = meet_first(part.reshape(BLOCKS, ROWS, D), st, rate_a)

    first_g = first_g.reshape(n, D)
    up = jnp.dot(first_g, wff[0], preferred_element_type=F32)
    gate = jnp.dot(first_g, wff[1], preferred_element_type=F32)
    t = gate * sg
    sig = jax.nn.sigmoid(t)
    silu = t * sig
    hidden = (up * su * silu).astype(BF)
    part = jnp.dot(hidden, wdn, preferred_element_type=F32).astype(BF)
    dd, result, d_first, g_am = meet_result(part.reshape(BLOCKS, ROWS, D), first, cotangent[0], rate_m, valid)

    dd = dd.reshape(n, D)
    dh = lax.dot_general(dd, wdn, (((1,), (1,)), ((), ())), preferred_element_type=F32)
    dsilu = sig * (1.0 + t * (1.0 - sig))
    d_up = (dh * su * silu).astype(BF)
    d_gate = (dh * up * su * sg * dsilu).astype(BF)
    g_su = jnp.sum(dh * up * silu, axis=0)
    g_sg = jnp.sum(dh * up * su * gate * dsilu, axis=0)
    part = (
        lax.dot_general(d_up, wff[0], (((1,), (1,)), ((), ())), preferred_element_type=F32)
        + lax.dot_general(d_gate, wff[1], (((1,), (1,)), ((), ())), preferred_element_type=F32)
    ).astype(BF)
    dm, d_st, g_aa = meet_back(part.reshape(BLOCKS, ROWS, D), d_first, st, mixed, rate_a)

    def outer_sum(a, b):
        return lax.dot_general(a, b, (((0,), (0,)), ((), ())), preferred_element_type=F32).astype(BF)

    ga = jnp.stack([outer_sum(first_g, d_up), outer_sum(first_g, d_gate)]).reshape(2, 4, 4, 80, D)
    gd = jnp.stack([outer_sum(hidden, dd[:, :640]), outer_sum(hidden, dd[:, 640:])]).reshape(2, 4, 4, 80, 640)

    dq, dkv, go = attend_back(lengths, q, kv_all, wo2, dm.reshape(n, D), att, lse)
    dkv = dkv_reduce(dkv.reshape(HG, 2, 4, 4, ROWS, 128)).reshape(HG, n, 128)
    part, gq, g_sq = qkv_back(lengths, dq, dkv, turned, scale_g, inner, outer, xg2, wqkv2)
    vec = jnp.concatenate(
        [
            g_aa[0:1],
            g_am[0:1],
            g_su[None],
            g_sg[None],
            jnp.pad(g_sq[0:1], ((0, 0), (0, D - GROUP))),
            jnp.zeros((3, D), F32),
        ]
    )
    g_in, o_up, o_gate, o_qkv, o_down, o_out, o_vec = close(
        part.reshape(BLOCKS, ROWS, D),
        d_st,
        ga,
        gq.reshape(2, 4, 4, 80, 512),
        gd,
        go.reshape(4, 80, D),
        vec,
    )
    half0, half1 = (o_qkv[i].reshape(4, 80, 8, HDIM).transpose(1, 0, 2, 3) for i in (0, 1))
    gr_q = half0[:, :, :5].reshape(80, D)
    gr_k = half1[:, :, :5].reshape(80, D)
    gr_v = jnp.concatenate([half0[:, :, 5:], half1[:, :, 5:7]], axis=2).reshape(80, D)
    shard = z * 4 + y
    cut = lax.dynamic_slice_in_dim
    return (
        result[None],
        g_in[None],
        gr_q,
        gr_k,
        gr_v,
        o_out,
        o_up,
        o_gate,
        o_down,
        cut(o_vec[4], y * 80, 80, 0),
        cut(o_vec[0], shard * 80, 80, 0),
        cut(o_vec[1], shard * 80, 80, 0),
        cut(o_vec[2], y * 320, 320, 0),
        cut(o_vec[3], y * 320, 320, 0),
    )


def solution(mesh):
    row = P("grp", ("seq", "shard"), None)
    mat = P("shard", None)
    one = P("shard")
    return jax.shard_map(
        shards,
        mesh=mesh,
        in_specs=(row,) + (mat,) * 7 + (one,) * 5 + (P("grp"), row),
        out_specs=(row, row) + (mat,) * 7 + (one,) * 5,
        check_vma=False,
    )
```

```python
import functools
import math

import jax
import jax.numpy as jnp
import numpy as np
from jax import lax
from jax.experimental import pallas as pl
from jax.experimental.pallas import tpu as pltpu
from jax.sharding import PartitionSpec as P


D, HEADS, HDIM, FF = 1280, 20, 64, 5120
ROWS, BLOCKS, HG = 128, 4, 5
GROUP = HG * HDIM
EPS = 1e-6
BF, F32 = jnp.bfloat16, jnp.float32
MESH = pl.DeviceIdType.MESH
VMEM_LIMIT = 60 << 20


def here():
    s = lax.axis_index("shard")
    return lax.axis_index("grp"), lax.axis_index("seq"), s // 4, s % 4


def dev(x, c, z, y):
    return (x, c, z * 4 + y)


def worker(z):
    return ((z + 1) // 2) % 2


def owner_z(w, i):
    return i * (3 - 2 * w) + w


def step(v, d):
    return (v + d) % 4


def rcopy(src, dst, ss, rs, to):
    return pltpu.make_async_remote_copy(
        src_ref=src, dst_ref=dst, send_sem=ss, recv_sem=rs, device_id=to, device_id_type=MESH
    )


def lcopy(src, dst, sem):
    return pltpu.make_async_copy(src, dst, sem)


def landed(dst, sem):
    pltpu.make_async_copy(dst, dst, sem).wait()


def greet(peers):
    bar = pltpu.get_barrier_semaphore()
    for p in peers:
        pl.semaphore_signal(bar, inc=1, device_id=p, device_id_type=MESH)
    pl.semaphore_wait(bar, len(peers))


def z_peers(x, c, z, y):
    far = [dev(x, cc, step(z, d), y) for d in (1, 2, 3) for cc in (0, 1)]
    return [dev(x, 1 - c, z, y)] + far


def z_gather_start(src, dst, ss, rs, x, c, z, y):
    w = worker(z)
    slot = (z // 2, c)
    for d in (1, 3, 2):
        rcopy(src, dst.at[slot], ss.at[d], rs.at[slot], dev(x, w, step(z, d), y)).start()

    @pl.when(c == w)
    def _():
        lcopy(src, dst.at[slot], rs.at[slot]).start()

    @pl.when(c != w)
    def _():
        rcopy(src, dst.at[slot], ss.at[0], rs.at[slot], dev(x, w, z, y)).start()


def z_gather_take(dst, rs, p):
    for k in range(2):
        landed(dst.at[p, k], rs.at[p, k])


def z_gather_sent(src, ss, c, z):
    for d in (1, 2, 3):
        landed(src, ss.at[d])

    @pl.when(c != worker(z))
    def _():
        landed(src, ss.at[0])


def z_gather_wait(src, dst, ss, rs, c, z):
    for p in range(2):
        z_gather_take(dst, rs, p)
    z_gather_sent(src, ss, c, z)


def z_scatter_pair(part, dst, ss, rs, p, x, c, z, y):
    oz = owner_z(c, p)
    for oc in range(2):
        mine = jnp.logical_and(c == oc, z == oz)

        @pl.when(mine)
        def _(oc=oc):
            lcopy(part.at[p, oc], dst.at[z], rs.at[z]).start()

        @pl.when(jnp.logical_not(mine))
        def _(oc=oc):
            rcopy(part.at[p, oc], dst.at[z], ss.at[p, oc], rs.at[z], dev(x, oc, oz, y)).start()


def z_scatter_start(part, dst, ss, rs, x, c, z, y):
    for p in range(2):
        z_scatter_pair(part, dst, ss, rs, p, x, c, z, y)


def z_scatter_take(dst, rs):
    for k in range(4):
        landed(dst.at[k], rs.at[k])


def z_scatter_sent(part, ss, c, z):
    for p in range(2):
        for oc in range(2):
            mine = jnp.logical_and(c == oc, z == owner_z(c, p))

            @pl.when(jnp.logical_not(mine))
            def _(p=p, oc=oc):
                landed(part.at[p, oc], ss.at[p, oc])


def remote_call(kernel, outs, ins_spaces, scratch, cid, name):
    spec = {
        "a": pl.BlockSpec(memory_space=pl.ANY),
        "v": pl.BlockSpec(memory_space=pltpu.VMEM),
        "s": pl.BlockSpec(memory_space=pltpu.SMEM),
    }
    return pl.pallas_call(
        kernel,
        out_shape=[jax.ShapeDtypeStruct(s, d) for s, d, _ in outs],
        in_specs=[spec[s] for s in ins_spaces],
        out_specs=[spec[s] for _, _, s in outs],
        scratch_shapes=scratch,
        compiler_params=pltpu.CompilerParams(
            collective_id=cid, has_side_effects=True, vmem_limit_bytes=VMEM_LIMIT
        ),
        name=name,
    )


def local_call(kernel, outs, n_in, scratch, name, smem=0):
    vmem = pl.BlockSpec(memory_space=pltpu.VMEM)
    sm = pl.BlockSpec(memory_space=pltpu.SMEM)
    return pl.pallas_call(
        kernel,
        out_shape=[jax.ShapeDtypeStruct(s, d) for s, d in outs],
        in_specs=[sm] * smem + [vmem] * n_in,
        out_specs=[vmem for _ in outs],
        scratch_shapes=scratch,
        compiler_params=pltpu.CompilerParams(vmem_limit_bytes=VMEM_LIMIT),
        name=name,
    )


def dma(*shape):
    return pltpu.SemaphoreType.DMA(shape)


def open_kernel(st, wq, vec, wo, xg, wqkv, vecs, wog, xs, xr, s1, r1, s2, r2, s3, r3, sv, rv, so, ro, lo):
    x, c, z, y = here()
    sib = dev(x, 1 - c, z, y)
    half = pl.ds(pl.multiple_of(c * 640, 128), 640)
    other = pl.ds(pl.multiple_of((1 - c) * 640, 128), 640)
    greet(z_peers(x, c, z, y) + [dev(x, c, z, step(y, d)) for d in (1, 2, 3)])
    for d in (2, 1, 3):
        z2 = step(z, d)
        rcopy(wq.at[c, z2], wqkv.at[c, z, y], s1.at[d], r1.at[z], dev(x, c, z2, y)).start()
        rcopy(vec, vecs.at[z, y], sv.at[0, d], rv.at[0, z], dev(x, c, z2, y)).start()
    own = lcopy(wq.at[c, z], wqkv.at[c, z, y], lo.at[0])
    own.start()
    own_v = lcopy(vec, vecs.at[z, y], lo.at[1])
    own_v.start()
    own_o = lcopy(wo.at[:, half], wog.at[y, :, half], lo.at[2])
    own_o.start()
    for d in (2, 1, 3):
        rcopy(wo.at[:, half], wog.at[y, :, half], so.at[0, d], ro.at[0, y], dev(x, c, z, step(y, d))).start()
    rcopy(wo.at[:, half], wog.at[y, :, half], so.at[0, 0], ro.at[1, y], sib).start()
    z_gather_start(st, xg, xs, xr, x, c, z, y)
    for d in (1, 2, 3):
        z2 = step(z, d)
        landed(wqkv.at[c, z2, y], r1.at[z2])
        landed(vecs.at[z2, y], rv.at[0, z2])
    own.wait()
    own_v.wait()
    for d in (2, 1, 3):
        to = dev(x, c, z, step(y, d))
        rcopy(wqkv.at[c, :, y], wqkv.at[c, :, y], s2.at[d], r2.at[y], to).start()
        rcopy(vecs.at[:, y], vecs.at[:, y], sv.at[1, d], rv.at[1, y], to).start()
    rcopy(wqkv.at[c, :, y], wqkv.at[c, :, y], s3.at[0], r3.at[y], sib).start()
    for d in (1, 3, 2):
        y2 = step(y, d)
        landed(wog.at[y2, :, half], ro.at[0, y2])
        rcopy(wog.at[y2, :, half], wog.at[y2, :, half], so.at[1, d], ro.at[1, y2], sib).start()
        landed(wqkv.at[c, :, y2], r2.at[y2])
        rcopy(wqkv.at[c, :, y2], wqkv.at[c, :, y2], s3.at[d], r3.at[y2], sib).start()
    z_gather_wait(st, xg, xs, xr, c, z)
    own_o.wait()
    for k in range(4):
        landed(wqkv.at[1 - c, :, k], r3.at[k])
        landed(wog.at[k, :, other], ro.at[1, k])
        landed(wqkv.at[c, :, k], s3.at[k])
    landed(wo.at[:, half], so.at[0, 0])
    for d in (1, 2, 3):
        landed(vecs.at[:, step(y, d)], rv.at[1, step(y, d)])
        landed(wq.at[c, z], s1.at[d])
        landed(vec, sv.at[0, d])
        landed(vecs.at[:, y], sv.at[1, d])
        landed(wqkv.at[c, :, y], s2.at[d])
        landed(wo.at[:, half], so.at[0, d])
        landed(wog.at[y, :, half], so.at[1, d])


def open_gather(st, wq, vec, wo):
    return remote_call(
        open_kernel,
        [
            ((2, 2, ROWS, D), BF, "a"),
            ((2, 4, 4, 80, 512), BF, "a"),
            ((4, 4, 8, 896), F32, "a"),
            ((4, 80, D), BF, "a"),
        ],
        "aaaa",
        [dma(4), dma(2, 2), dma(4), dma(4), dma(4), dma(4), dma(4), dma(4), dma(2, 4), dma(2, 4), dma(2, 4), dma(2, 4), dma(3)],
        0,
        "open_gather",
    )(st, wq, vec, wo)


def rope_tables():
    freqs = np.exp(np.arange(32) * (-2.0 * math.log(10000.0) / 64))
    freqs = np.concatenate([freqs, freqs])
    sign = np.concatenate([-np.ones(32), np.ones(32)])
    inner = np.arange(ROWS)[:, None] * freqs
    outer = (np.arange(32) * ROWS)[:, None] * freqs
    return (
        np.stack([np.cos(inner), np.sin(inner) * sign]).astype(np.float32),
        np.stack([np.cos(outer), np.sin(outer) * sign]).astype(np.float32),
    )


def block_index(c, y, j):
    return (j % 2) * 16 + owner_z(c, j // 2) * 4 + y


def turn_of(inner, outer, b):
    oc = outer[0, pl.ds(b, 1), :]
    os = outer[1, pl.ds(b, 1), :]
    return oc * inner[0] - os * inner[1], os * inner[0] + oc * inner[1]


def swap(v):
    return jnp.concatenate([v[:, 32:], v[:, :32]], axis=1)


def qkv_kernel(xg, w, scale, inner, outer, q_out, kv_out, t_out, y0, y1):
    _, c, _, y = here()
    xs = xg[...]
    y0[...] = jnp.dot(xs, w[0], preferred_element_type=F32)
    y1[...] = jnp.dot(xs, w[1], preferred_element_type=F32)

    def per_block(j, carry):
        rows = pl.ds(pl.multiple_of(j * ROWS, ROWS), ROWS)
        cosine, sine = turn_of(inner, outer, block_index(c, y, j))
        a0, a1 = y0[rows, :], y1[rows, :]
        for h in range(HG):
            cols = slice(h * HDIM, (h + 1) * HDIM)
            sc = scale[0:1, cols]
            turned = []
            for raw in (a0[:, cols], a1[:, cols]):
                t = raw * cosine + swap(raw) * sine
                turned.append(t)
            qn, kn = [
                t * lax.rsqrt(jnp.mean(t * t, axis=-1, keepdims=True) + EPS) * sc for t in turned
            ]
            q = qn.astype(BF).astype(F32) * 0.125
            if h < 3:
                v = a0[:, GROUP + h * HDIM : GROUP + (h + 1) * HDIM]
            else:
                v = a1[:, GROUP + (h - 3) * HDIM : GROUP + (h - 2) * HDIM]
            t_out[h, rows, :] = jnp.concatenate(turned, axis=1)
            q_out[h, rows, :] = jnp.concatenate([q, jnp.zeros_like(q)], axis=1).astype(BF)
            kv_out[h, rows, :] = jnp.concatenate([kn, v], axis=1).astype(BF)
        return carry

    lax.fori_loop(0, BLOCKS, per_block, 0)


def make_qkv(xg, w, scale, inner, outer):
    n = BLOCKS * ROWS
    return local_call(
        qkv_kernel,
        [((HG, n, 128), BF), ((HG, n, 128), BF), ((HG, n, 128), F32)],
        5,
        [pltpu.VMEM((n, 512), F32), pltpu.VMEM((n, 512), F32)],
        "make_qkv",
    )(xg, w, scale, inner, outer)


TILE = 512


def tiles_of(c, j):
    return (j % 2) * 4 + owner_z(c, j // 2) + 1


def causal(y):
    key = lax.broadcasted_iota(jnp.int32, (TILE, ROWS), 0)
    query = lax.broadcasted_iota(jnp.int32, (TILE, ROWS), 1)
    return key <= query + y * ROWS


def nt(a, b):
    return lax.dot_general(a, b, (((1,), (1,)), ((), ())), preferred_element_type=F32)


def tn(a, b):
    return lax.dot_general(a, b, (((0,), (0,)), ((), ())), preferred_element_type=F32)


def key_valid(length, t):
    pos = t * TILE + lax.broadcasted_iota(jnp.int32, (1, TILE), 1)
    return (pos < length).astype(F32)


def key_tile(ref, h, t):
    zz = t % 4
    return ref[h, worker(zz), zz // 2, t // 4].reshape(TILE, 128)


def columns(ref, k, half):
    return ref.at[:, pl.ds(pl.multiple_of(k * D + half * 640, 128), 640)]


def attend_kernel(
    length, q, kv, wo, w_up, w_gate,
    part, att, lse, kvb, wu, gz,
    kvt, low, sy, ry, ss, rs, lo, s1, r1, s2, r2, s3, r3, lw,
):
    x, c, z, y = here()
    sib = dev(x, 1 - c, z, y)
    half = pl.ds(pl.multiple_of(c * 640, 128), 640)
    other = pl.ds(pl.multiple_of((1 - c) * 640, 128), 640)
    greet(
        [sib]
        + [dev(x, c, step(z, d), y) for d in (1, 2, 3)]
        + [dev(x, c, z, step(y, d)) for d in (1, 2, 3)]
    )

    def send(h, carry):
        for d in (1, 3, 2):
            rcopy(kv.at[h], kvb.at[h, c, :, :, y], sy.at[h, d], ry.at[h, y], dev(x, c, z, step(y, d))).start()
        rcopy(kv.at[h], kvb.at[h, c, :, :, y], ss.at[h, 0], rs.at[h, y], sib).start()
        lcopy(kv.at[h], kvb.at[h, c, :, :, y], lo.at[h]).start()
        return carry

    lax.fori_loop(0, HG, send, 0)
    for d in (1, 3, 2):
        z2 = step(z, d)
        to = dev(x, c, z2, y)
        rcopy(columns(w_up, z2, c), wu.at[z, y, :, half], s1.at[0, d], r1.at[0, z], to).start()
        rcopy(columns(w_gate, z2, c), gz.at[z], s1.at[1, d], r1.at[1, z], to).start()
    lcopy(columns(w_up, z, c), wu.at[z, y, :, half], lw.at[0]).start()
    lcopy(columns(w_gate, z, c), gz.at[z], lw.at[1]).start()

    def forward(h):
        for d in (1, 3, 2):
            y2 = step(y, d)
            landed(kvb.at[h, c, :, :, y2], ry.at[h, y2])
            rcopy(kvb.at[h, c, :, :, y2], kvb.at[h, c, :, :, y2], ss.at[h, d], rs.at[h, y2], sib).start()

    def spread_up():
        for d in (1, 2, 3):
            landed(wu.at[step(z, d), y, :, half], r1.at[0, step(z, d)])
            landed(gz.at[step(z, d)], r1.at[1, step(z, d)])
        landed(wu.at[z, y, :, half], lw.at[0])
        landed(gz.at[z], lw.at[1])
        for d in (1, 3, 2):
            rcopy(wu.at[:, y, :, half], wu.at[:, y, :, half], s2.at[d], r2.at[y], dev(x, c, z, step(y, d))).start()
        rcopy(wu.at[:, y, :, half], wu.at[:, y, :, half], s3.at[0], r3.at[y], sib).start()

    tri = causal(y)
    forward(0)

    def per_head(h, carry):
        landed(kvb.at[h, c, :, :, y], lo.at[h])
        for k in range(4):
            landed(kvb.at[h, 1 - c, :, :, k], rs.at[h, k])

        def flip(t, carry):
            valid = key_valid(length[0], t)
            turned = key_tile(kvb, h, t).astype(F32).T * valid
            row = lax.broadcasted_iota(jnp.int32, (128, TILE), 0)
            kvt[t] = jnp.where(row < HDIM, valid, turned).astype(BF)
            return carry

        lax.fori_loop(0, 8, flip, 0)

        def per_block(j, carry):
            @pl.when(jnp.logical_and(j == 2, h < HG - 1))
            def _():
                forward(h + 1)

            @pl.when(jnp.logical_and(j == 2, h == 2))
            def _():
                spread_up()

            rows = pl.ds(pl.multiple_of(j * ROWS, ROWS), ROWS)
            qj = q[h, rows, :]
            last = tiles_of(c, j) - 1

            def full(t, acc):
                p = jnp.exp(nt(key_tile(kvb, h, t), qj)).astype(BF)
                return acc + jnp.dot(kvt[t], p, preferred_element_type=F32)

            acc = lax.fori_loop(0, last, full, jnp.zeros((128, ROWS), F32))
            p = jnp.where(tri, jnp.exp(nt(key_tile(kvb, h, last), qj)), 0.0).astype(BF)
            acc = acc + jnp.dot(kvt[last], p, preferred_element_type=F32)
            total = acc[0:1]
            lse[h, pl.ds(j, 1), :] = jnp.log(total)
            att[h, rows, :] = (acc[HDIM:] / total).T
            return carry

        lax.fori_loop(0, BLOCKS, per_block, 0)
        return carry

    lax.fori_loop(0, HG, per_head, 0)
    for h in range(HG):
        low[:, h * HDIM : (h + 1) * HDIM] = att[h].astype(BF)
    part[...] = jnp.dot(low[...], wo[...], preferred_element_type=F32).astype(BF)
    for d in (1, 3, 2):
        y2 = step(y, d)
        landed(wu.at[:, y2, :, half], r2.at[y2])
        rcopy(wu.at[:, y2, :, half], wu.at[:, y2, :, half], s3.at[d], r3.at[y2], sib).start()

    def sent(h, carry):
        for k in range(4):
            landed(kv.at[h], ss.at[h, k])
        for d in (1, 2, 3):
            landed(kv.at[h], sy.at[h, d])
        return carry

    lax.fori_loop(0, HG, sent, 0)
    for k in range(4):
        landed(wu.at[:, k, :, other], r3.at[k])
        landed(wu.at[:, k, :, half], s3.at[k])
    for d in (1, 2, 3):
        landed(gz.at[z], s1.at[0, d])
        landed(gz.at[z], s1.at[1, d])
        landed(wu.at[:, y, :, half], s2.at[d])


def attend(length, q, kv, wo, w_up, w_gate):
    n = BLOCKS * ROWS
    return remote_call(
        attend_kernel,
        [
            ((n, D), BF, "v"),
            ((HG, n, HDIM), F32, "v"),
            ((HG, BLOCKS, 128), F32, "v"),
            ((HG, 2, 2, 2, 4, ROWS, 128), BF, "v"),
            ((4, 4, 80, D), BF, "a"),
            ((4, 80, 640), BF, "a"),
        ],
        "svvvaa",
        [
            pltpu.VMEM((8, 128, TILE), BF), pltpu.VMEM((n, GROUP), BF),
            dma(HG, 4), dma(HG, 4), dma(HG, 4), dma(HG, 4), dma(HG),
            dma(2, 4), dma(2, 4), dma(4), dma(4), dma(4), dma(4), dma(2),
        ],
        1,
        "attend",
    )(length, q, kv, wo, w_up, w_gate)


def attend_back_kernel(
    length, q, kv, wo, dmix, att, lse, ha, hd,
    dq, dkv, gout, za, zd,
    qdo, delta, kt, acc, low, give, mine, got, got_y, oa, od, ra, rd, fa, fd,
    sg, rg, sy, ry, s1, r1, s2, r2, s3, r3, lo,
):
    x, c, z, y = here()
    sib = dev(x, 1 - c, z, y)
    to_y = [None] + [dev(x, c, z, step(y, d)) for d in (1, 2, 3)]
    to_x = [None] + [dev(step(x, d), c, z, y) for d in (1, 2, 3)]
    greet([sib] + to_y[1:] + to_x[1:])
    for d in (1, 3, 2):
        rcopy(ha.at[step(x, d)], ra.at[x], s1.at[0, d], r1.at[0, x], to_x[d]).start()
        rcopy(hd.at[step(y, d)], rd.at[y], s1.at[1, d], r1.at[1, y], to_y[d]).start()
    lcopy(ha.at[x], oa, lo.at[0]).start()
    lcopy(hd.at[y], od, lo.at[1]).start()

    def first_sums():
        landed(oa, lo.at[0])
        landed(od, lo.at[1])
        for d in (1, 2, 3):
            landed(ra.at[step(x, d)], r1.at[0, step(x, d)])
            landed(rd.at[step(y, d)], r1.at[1, step(y, d)])

        def body(k, carry):
            va = oa[k].astype(F32)
            vd = od[k].astype(F32)
            for d in (1, 2, 3):
                va = va + ra[step(x, d), k].astype(F32)
                vd = vd + rd[step(y, d), k].astype(F32)
            oa[k] = va.astype(BF)
            od[k] = vd.astype(BF)
            return carry

        lax.fori_loop(0, 4, body, 0)
        for d in (1, 3, 2):
            rcopy(oa.at[step(y, d)], fa.at[y], s2.at[0, d], r2.at[0, y], to_y[d]).start()
            rcopy(od.at[step(x, d)], fd.at[x], s2.at[1, d], r2.at[1, x], to_x[d]).start()

    def second_sums():
        for d in (1, 2, 3):
            landed(fa.at[step(y, d)], r2.at[0, step(y, d)])
            landed(fd.at[step(x, d)], r2.at[1, step(x, d)])
        va = oa[y].astype(F32)
        vd = od[x].astype(F32)
        for d in (1, 2, 3):
            va = va + fa[step(y, d)].astype(F32)
            vd = vd + fd[step(x, d)].astype(F32)
        fa[y] = va.astype(BF)
        fd[x] = vd.astype(BF)
        for d in (1, 3, 2):
            rcopy(fa.at[y], za.at[x], s3.at[0, d], r3.at[0, x], to_x[d]).start()
            rcopy(fd.at[x], zd.at[x], s3.at[1, d], r3.at[1, x], to_x[d]).start()
        lcopy(fa.at[y], za.at[x], lo.at[2]).start()
        lcopy(fd.at[x], zd.at[x], lo.at[3]).start()

    def settle(h):
        landed(got.at[h], rg.at[h])
        for i in range(2):
            for k in range(2):
                mine[h, i, k] = (mine[h, i, k].astype(F32) + got[h, i, k].astype(F32)).astype(BF)
        for d in (1, 3, 2):
            rcopy(mine.at[h, :, :, step(y, d)], got_y.at[h, y], sy.at[h, d], ry.at[h, y], to_y[d]).start()

    tri = causal(y)
    d_att = nt(dmix[...], wo[...]).astype(BF)
    for h in range(HG):
        low[:, h * HDIM : (h + 1) * HDIM] = att[h].astype(BF)
        dh = d_att[:, h * HDIM : (h + 1) * HDIM].astype(F32)
        wide = jnp.concatenate([jnp.zeros_like(dh), dh], axis=1).astype(BF)
        prod = dh * att[h]
        for j in range(BLOCKS):
            rows = slice(j * ROWS, (j + 1) * ROWS)
            qdo[h, j, :ROWS] = q[h, rows, :]
            qdo[h, j, ROWS:] = wide[rows]
            delta[h, j : j + 1, :] = jnp.sum(prod[rows].T, axis=0, keepdims=True)
    gout[...] = tn(low[...], dmix[...]).astype(BF)

    def per_head(h, carry):
        def flip(t, carry):
            kt[t] = (key_tile(kv, h, t).astype(F32).T * key_valid(length[0], t)).astype(BF)
            acc[t] = jnp.zeros((TILE, 128), F32)
            return carry

        lax.fori_loop(0, 8, flip, 0)

        def per_block(j, carry):
            @pl.when(jnp.logical_and(j == 2, h > 0))
            def _():
                settle(h - 1)

            @pl.when(jnp.logical_and(j == 0, h == 3))
            def _():
                first_sums()

            @pl.when(jnp.logical_and(j == 0, h == 4))
            def _():
                second_sums()

            rows = pl.ds(pl.multiple_of(j * ROWS, ROWS), ROWS)
            both = qdo[h, j]
            l_row = lse[h, pl.ds(j, 1), :]
            d_row = delta[h, pl.ds(j, 1), :]
            last = tiles_of(c, j) - 1

            def tile(t, dqt, mask):
                sd = nt(key_tile(kv, h, t), both)
                p = jnp.exp(sd[:, :ROWS] - l_row)
                if mask:
                    p = jnp.where(tri, p, 0.0)
                ds = (p * (sd[:, ROWS:] - d_row)).astype(BF)
                pair = jnp.concatenate([ds, p.astype(BF)], axis=1)
                acc[t] += jnp.dot(pair, both, preferred_element_type=F32)
                return dqt + jnp.dot(kt[t], ds, preferred_element_type=F32)

            dqt = lax.fori_loop(0, last, lambda t, s: tile(t, s, False), jnp.zeros((128, ROWS), F32))
            dqt = tile(last, dqt, True)
            dq[h, rows, :] = dqt[:HDIM].T * 0.125
            return carry

        lax.fori_loop(0, BLOCKS, per_block, 0)

        def store(i, carry):
            zi, k = i // 2, i % 2
            give[h, zi, k] = acc[k * 4 + owner_z(1 - c, zi)].astype(BF).reshape(4, ROWS, 128)
            mine[h, zi, k] = acc[k * 4 + owner_z(c, zi)].astype(BF).reshape(4, ROWS, 128)
            return carry

        lax.fori_loop(0, 4, store, 0)
        rcopy(give.at[h], got.at[h], sg.at[h], rg.at[h], sib).start()
        return carry

    lax.fori_loop(0, HG, per_head, 0)
    settle(HG - 1)

    def final(h, carry):
        for d in (1, 2, 3):
            landed(got_y.at[h, step(y, d)], ry.at[h, step(y, d)])
        for i in range(2):
            for k in range(2):
                v = mine[h, i, k, y].astype(F32)
                for d in (1, 2, 3):
                    v = v + got_y[h, step(y, d), i, k].astype(F32)
                dkv[h, i, k] = v.astype(BF)
        landed(give.at[h], sg.at[h])
        for d in (1, 2, 3):
            landed(got_y.at[h, y], sy.at[h, d])
        return carry

    lax.fori_loop(0, HG, final, 0)
    for d in (1, 2, 3):
        landed(za.at[step(x, d)], r3.at[0, step(x, d)])
        landed(zd.at[step(x, d)], r3.at[1, step(x, d)])
    landed(za.at[x], lo.at[2])
    landed(zd.at[x], lo.at[3])
    for d in (1, 2, 3):
        landed(ra.at[x], s1.at[0, d])
        landed(rd.at[y], s1.at[1, d])
        landed(fa.at[0], s2.at[0, d])
        landed(fd.at[0], s2.at[1, d])
        landed(fa.at[0], s3.at[0, d])
        landed(fd.at[0], s3.at[1, d])


def attend_back(length, q, kv, wo, dmix, att, lse, ha, hd):
    n = BLOCKS * ROWS
    V = pltpu.VMEM
    return remote_call(
        attend_back_kernel,
        [
            ((HG, n, HDIM), F32, "v"),
            ((HG, 2, 2, ROWS, 128), BF, "v"),
            ((GROUP, D), BF, "v"),
            ((4, 80, D), BF, "a"),
            ((4, 80, 640), BF, "a"),
        ],
        "svvvvvvaa",
        [
            V((HG, BLOCKS, 2 * ROWS, 128), BF),
            V((HG, BLOCKS, 128), F32),
            V((8, 128, TILE), BF),
            V((8, TILE, 128), F32),
            V((n, GROUP), BF),
            V((HG, 2, 2, 4, ROWS, 128), BF),
            V((HG, 2, 2, 4, ROWS, 128), BF),
            V((HG, 2, 2, 4, ROWS, 128), BF),
            V((HG, 4, 2, 2, ROWS, 128), BF),
            V((4, 80, D), BF), V((4, 80, 640), BF),
            V((4, 4, 80, D), BF), V((4, 4, 80, 640), BF),
            V((4, 80, D), BF), V((4, 80, 640), BF),
            dma(HG), dma(HG), dma(HG, 4), dma(HG, 4),
            dma(2, 4), dma(2, 4), dma(2, 4), dma(2, 4), dma(2, 4), dma(2, 4), dma(4),
        ],
        3,
        "attend_back",
    )(length, q, kv, wo, dmix, att, lse, ha, hd)


def inv_rms(v):
    return lax.rsqrt(jnp.mean(v * v, axis=-1, keepdims=True) + EPS)


def back_rms(dy, yy, inv):
    return (dy - yy * jnp.mean(dy * yy, axis=-1, keepdims=True)) * inv


def total_of(buf):
    return (buf[0].astype(F32) + buf[1].astype(F32)) + (buf[2].astype(F32) + buf[3].astype(F32))


def mix_of(res, part, rate):
    inv_p = inv_rms(part)
    unit = part * inv_p
    diff = unit - res
    u = res + rate * diff
    inv_u = inv_rms(u)
    return u * inv_u, unit, inv_p, inv_u, diff


def mix_back(dy, res, part, rate):
    yy, unit, inv_p, inv_u, diff = mix_of(res, part, rate)
    du = back_rms(dy, yy, inv_u)
    return du * (1.0 - rate), back_rms(du * rate, unit, inv_p), jnp.sum(du * diff, axis=0, keepdims=True)


def mid_kernel(
    part0, st, cot, rate_a, rate_m, su, sg, valid, wu_in, gz, w_down,
    result, d_st, dm, ha, hd, vec,
    buf, low, xg, dd, wu, wg, wd, up, gate, hid, dug, part, xt, ht, mixed, first, dfirst, ga, gd, ra, rd,
    ps, pr, gs, gr, s2, r2, s3, r3, sx, rx, lo,
):
    x, c, z, y = here()
    sib = dev(x, 1 - c, z, y)
    half = pl.ds(pl.multiple_of(c * 640, 128), 640)
    other = pl.ds(pl.multiple_of((1 - c) * 640, 128), 640)
    near = z // 2
    greet(z_peers(x, c, z, y) + [dev(x, c, z, step(y, d)) for d in (1, 2, 3)])
    z_scatter_start(part0, buf.at[0], ps.at[0], pr.at[0], x, c, z, y)

    def down_rows(k):
        return pl.ds(pl.multiple_of(k * 320, 16), 320)

    for d in (1, 3, 2):
        rcopy(gz, wg.at[:, y, :, half], s2.at[0, d], r2.at[0, y], dev(x, c, z, step(y, d))).start()
    rcopy(gz, wg.at[:, y, :, half], s3.at[0, 0], r3.at[0, y], sib).start()
    for d in (1, 3, 2):
        to = dev(x, c, z, step(y, d))
        rcopy(w_down.at[:, half], wd.at[down_rows(y), half], s2.at[1, d], r2.at[1, y], to).start()
    rcopy(w_down.at[:, half], wd.at[down_rows(y), half], s3.at[1, 0], r3.at[1, y], sib).start()
    lcopy(wu_in, wu, lo.at[0]).start()
    lcopy(gz, wg.at[:, y, :, half], lo.at[1]).start()
    lcopy(w_down.at[:, half], wd.at[down_rows(y), half], lo.at[2]).start()
    vec[...] = jnp.zeros_like(vec)

    z_scatter_take(buf.at[0], pr.at[0])
    total = total_of(buf.at[0])
    mixed[...] = total
    out = mix_of(st[...].astype(F32), total, rate_a[0:1])[0]
    first[...] = out
    low[0] = out.astype(BF)
    z_gather_start(low.at[0], xg, gs.at[0], gr.at[0], x, c, z, y)

    for d in (1, 3, 2):
        y2 = step(y, d)
        landed(wg.at[:, y2, :, half], r2.at[0, y2])
        rcopy(wg.at[:, y2, :, half], wg.at[:, y2, :, half], s3.at[0, d], r3.at[0, y2], sib).start()
    landed(wu, lo.at[0])
    landed(wg.at[:, y, :, half], lo.at[1])
    for k in range(4):
        landed(wg.at[:, k, :, other], r3.at[0, k])

    def rows_of(ref, p):
        return ref[p].reshape(2 * ROWS, D)

    def forward_cols(p):
        z_gather_take(xg, gr.at[0], p)

        def body(t, carry):
            cs = pl.ds(pl.multiple_of(t * 256, 256), 256)
            xs = rows_of(xg, p)
            u = jnp.dot(xs, wu[:, :, :, cs].reshape(D, 256), preferred_element_type=F32)
            g = jnp.dot(xs, wg[:, :, :, cs].reshape(D, 256), preferred_element_type=F32)
            tt = g * sg[0:1, cs]
            up[p, :, cs] = u
            gate[p, :, cs] = g
            hid[p, :, cs] = (u * su[0:1, cs] * (tt * jax.nn.sigmoid(tt))).astype(BF)
            return carry

        lax.fori_loop(0, 5, body, 0)

    def forward_down(p):
        def body(t, carry):
            cs = pl.ds(pl.multiple_of(t * 256, 256), 256)
            v = jnp.dot(hid[p], wd[:, cs], preferred_element_type=F32)
            part[0, p, :, :, cs] = v.astype(BF).reshape(2, ROWS, 256)
            return carry

        lax.fori_loop(0, 5, body, 0)
        z_scatter_pair(part.at[0], buf.at[1], ps.at[1], pr.at[1], p, x, c, z, y)

    forward_cols(near)
    for d in (1, 3, 2):
        y2 = step(y, d)
        landed(wd.at[down_rows(y2), half], r2.at[1, y2])
        rcopy(wd.at[down_rows(y2), half], wd.at[down_rows(y2), half], s3.at[1, d], r3.at[1, y2], sib).start()
    landed(wd.at[down_rows(y), half], lo.at[2])
    for k in range(4):
        landed(wd.at[down_rows(k), other], r3.at[1, k])
    forward_down(near)
    forward_cols(1 - near)
    forward_down(1 - near)

    def turn(dst, load):
        def body(t, carry):
            cs = pl.ds(pl.multiple_of(t * 256, 256), 256)
            for p in range(2):
                dst[cs, p * 256 : (p + 1) * 256] = load(p, cs).T
            return carry

        lax.fori_loop(0, 5, body, 0)

    turn(xt, lambda p, cs: xg[p, :, :, cs].reshape(256, 256))
    turn(ht, lambda p, cs: hid[p, :, cs])

    z_scatter_take(buf.at[1], pr.at[1])
    total = total_of(buf.at[1])
    live = valid[:, 0:1]
    base = first[...]
    d_base, d_part, g_am = mix_back(cot[...].astype(F32) * live, base, total, rate_m[0:1])
    low[1] = d_part.astype(BF)
    z_gather_start(low.at[1], dd, gs.at[1], gr.at[1], x, c, z, y)
    dfirst[...] = d_base
    vec[1:2] = g_am
    result[...] = (mix_of(base, total, rate_m[0:1])[0] * live).astype(BF)

    def backward_cols(p):
        z_gather_take(dd, gr.at[1], p)

        def body(t, carry):
            cs = pl.ds(pl.multiple_of(t * 256, 256), 256)
            dh = nt(rows_of(dd, p), wd[cs, :])
            u, g = up[p, :, cs], gate[p, :, cs]
            sc, sgc = su[0:1, cs], sg[0:1, cs]
            tt = g * sgc
            sig = jax.nn.sigmoid(tt)
            silu = tt * sig
            dsilu = sig * (1.0 + tt * (1.0 - sig))
            dhs = dh * sc
            dhu = dh * u
            both = dhu * dsilu * sc
            dug[0, p, :, cs] = (dhs * silu).astype(BF)
            dug[1, p, :, cs] = (both * sgc).astype(BF)
            vec[2:3, cs] += jnp.sum(dhu * silu, axis=0, keepdims=True)
            vec[3:4, cs] += jnp.sum(both * g, axis=0, keepdims=True)
            return carry

        lax.fori_loop(0, 5, body, 0)
        for t in range(2):
            v = nt(dug[0, p], wu[2 * t : 2 * t + 2].reshape(640, D)) + nt(
                dug[1, p], wg[2 * t : 2 * t + 2].reshape(640, D)
            )
            part[1, p, :, :, t * 640 : (t + 1) * 640] = v.astype(BF).reshape(2, ROWS, 640)
        z_scatter_pair(part.at[1], buf.at[2], ps.at[2], pr.at[2], p, x, c, z, y)

    backward_cols(near)
    backward_cols(1 - near)

    def gradients(w):
        cols = pl.ds(pl.multiple_of(w * 640, 128), 640)

        def body(k, carry):
            rows = pl.ds(pl.multiple_of(k * 320, 64), 320)
            for t in range(2):
                cs = slice(t * 640, (t + 1) * 640)
                v = jnp.dot(xt[rows, :], dug[w, :, :, cs].reshape(512, 640), preferred_element_type=F32)
                ga[w, k, :, :, cs] = v.astype(BF).reshape(4, 80, 640)
            v = jnp.dot(ht[rows, :], dd[:, :, :, cols].reshape(512, 640), preferred_element_type=F32)
            gd[w, k] = v.astype(BF).reshape(4, 80, 640)
            return carry

        lax.fori_loop(0, 4, body, 0)

    gradients(1 - c)
    rcopy(ga.at[1 - c], ra, sx.at[0], rx.at[0], sib).start()
    rcopy(gd.at[1 - c], rd, sx.at[1], rx.at[1], sib).start()

    z_scatter_take(buf.at[2], pr.at[2])
    dy = dfirst[...] + total_of(buf.at[2])
    d_res, d_part, g_aa = mix_back(dy, st[...].astype(F32), mixed[...], rate_a[0:1])
    low[2] = d_part.astype(BF)
    z_gather_start(low.at[2], dm, gs.at[2], gr.at[2], x, c, z, y)
    d_st[...] = d_res
    vec[0:1] = g_aa
    gradients(c)
    landed(ra, rx.at[0])
    landed(rd, rx.at[1])

    def add(k, carry):
        i, j = k // 4, k % 4
        ha[i, j] = (ga[c, i, j].astype(F32) + ra[i, j].astype(F32)).astype(BF)
        hd[i, j] = (gd[c, i, j].astype(F32) + rd[i, j].astype(F32)).astype(BF)
        return carry

    lax.fori_loop(0, 16, add, 0)
    for p in range(2):
        z_gather_take(dm, gr.at[2], p)
    for k in range(3):
        z_gather_sent(low.at[k], gs.at[k], c, z)
    z_scatter_sent(part0, ps.at[0], c, z)
    z_scatter_sent(part.at[0], ps.at[1], c, z)
    z_scatter_sent(part.at[1], ps.at[2], c, z)
    for k in range(4):
        landed(gz, s3.at[0, k])
        landed(w_down.at[:, half], s3.at[1, k])
    for d in (1, 2, 3):
        landed(gz, s2.at[0, d])
        landed(w_down.at[:, half], s2.at[1, d])
    landed(ra, sx.at[0])
    landed(rd, sx.at[1])


def middle(part0, st, cot, rate_a, rate_m, su, sg, valid, wu, gz, w_down):
    V = pltpu.VMEM
    return remote_call(
        mid_kernel,
        [
            ((ROWS, D), BF, "v"),
            ((ROWS, D), F32, "v"),
            ((2, 2, ROWS, D), BF, "a"),
            ((4, 4, 80, D), BF, "v"),
            ((4, 4, 80, 640), BF, "v"),
            ((8, D), F32, "v"),
        ],
        "avvvvvvvaaa",
        [
            V((3, 4, ROWS, D), BF), V((3, ROWS, D), BF), V((2, 2, ROWS, D), BF), V((2, 2, ROWS, D), BF),
            V((4, 4, 80, D), BF), V((4, 4, 80, D), BF), V((D, D), BF),
            V((2, 256, D), F32), V((2, 256, D), F32), V((2, 256, D), BF), V((2, 2, 256, D), BF),
            V((2, 2, 2, ROWS, D), BF), V((D, 512), BF), V((D, 512), BF),
            V((ROWS, D), F32), V((ROWS, D), F32), V((ROWS, D), F32),
            V((2, 4, 4, 80, D), BF), V((2, 4, 4, 80, 640), BF), V((4, 4, 80, D), BF), V((4, 4, 80, 640), BF),
            dma(3, 2, 2), dma(3, 4), dma(3, 4), dma(3, 2, 2),
            dma(2, 4), dma(2, 4), dma(2, 4), dma(2, 4), dma(2), dma(2), dma(3),
        ],
        2,
        "middle",
    )(part0, st, cot, rate_a, rate_m, su, sg, valid, wu, gz, w_down)


def qkv_back_kernel(length, dq, dkv, t, scale, inner, outer, xg, w, part, gw, gs, d0, d1):
    _, c, _, y = here()
    gs[...] = jnp.zeros_like(gs)
    d1[:, 448:] = jnp.zeros((BLOCKS * ROWS, 64), BF)

    def per_block(j, carry):
        rows = pl.ds(pl.multiple_of(j * ROWS, ROWS), ROWS)
        b = block_index(c, y, j)
        cosine, sine = turn_of(inner, outer, b)
        live = (b * ROWS + lax.broadcasted_iota(jnp.int32, (ROWS, 1), 0) < length[0]).astype(F32)
        for h in range(HG):
            cols = slice(h * HDIM, (h + 1) * HDIM)
            sc = scale[0:1, cols]
            both = t[h, rows, :]
            kv = dkv[h, rows, :].astype(F32) * live
            for k, dy in ((0, dq[h, rows, :]), (1, kv[:, :HDIM])):
                dy = dy.astype(BF).astype(F32)
                tt = both[:, k * HDIM : (k + 1) * HDIM]
                inv = inv_rms(tt)
                unit = tt * inv
                gs[0:1, cols] += jnp.sum(dy * unit, axis=0, keepdims=True)
                dt = back_rms(dy * sc, unit, inv)
                draw = (dt * cosine + swap(dt * sine)).astype(BF)
                if k == 0:
                    d0[rows, cols] = draw
                else:
                    d1[rows, cols] = draw
            dv = kv[:, HDIM:].astype(BF)
            if h < 3:
                d0[rows, GROUP + h * HDIM : GROUP + (h + 1) * HDIM] = dv
            else:
                d1[rows, GROUP + (h - 3) * HDIM : GROUP + (h - 2) * HDIM] = dv
        return carry

    lax.fori_loop(0, BLOCKS, per_block, 0)
    part[...] = (nt(d0[...], w[0]) + nt(d1[...], w[1])).astype(BF)
    gw[0] = tn(xg[...], d0[...]).astype(BF)
    gw[1] = tn(xg[...], d1[...]).astype(BF)


def qkv_back(length, dq, dkv, t, scale, inner, outer, xg, w):
    n = BLOCKS * ROWS
    return local_call(
        qkv_back_kernel,
        [((n, D), BF), ((2, D, 512), BF), ((8, GROUP), F32)],
        8,
        [pltpu.VMEM((n, 512), BF), pltpu.VMEM((n, 512), BF)],
        "qkv_back",
        smem=1,
    )(length, dq, dkv, t, scale, inner, outer, xg, w)


def close_kernel(
    part, d_st, za_in, zd_in, gq, go, vec,
    g_in, o_q, o_k, o_v, o_out, o_up, o_gate, o_down, o_vec,
    pbuf, za, zd, hq, rq, fq, zq, ob, oy, ox, o2, vs, vb,
    ps, pr, sc, rc, lo, s1, r1, s2, r2, s3, r3, sz, rz, sf, rf, so, ro, sv, rv,
):
    x, c, z, y = here()
    sib = dev(x, 1 - c, z, y)
    to_y = [None] + [dev(x, c, z, step(y, d)) for d in (1, 2, 3)]
    to_x = [None] + [dev(step(x, d), c, z, y) for d in (1, 2, 3)]
    to_z = [None] + [dev(x, c, step(z, d), y) for d in (1, 2, 3)]
    greet(z_peers(x, c, z, y) + to_y[1:] + to_x[1:])
    rcopy(gq.at[1 - c], hq.at[1], sc.at[0], rc.at[0], sib).start()
    rcopy(vec, vb.at[0], sv.at[0, 0], rv.at[0, 0], sib).start()
    rcopy(go, ob, sc.at[1], rc.at[1], sib).start()
    z_scatter_start(part, pbuf, ps, pr, x, c, z, y)
    lcopy(gq.at[c], hq.at[0], lo.at[0]).start()
    lcopy(go, oy, lo.at[1]).start()
    for d in (1, 3, 2):
        rcopy(za_in.at[step(z, d)], za.at[c, z], sz.at[1, d], rz.at[1, z], to_z[d]).start()
    lcopy(za_in.at[z], za.at[c, z], lo.at[2]).start()
    lcopy(zd_in, zd.at[c], lo.at[3]).start()
    rcopy(zd_in, zd.at[c], sf.at[2], rf.at[2], sib).start()

    landed(hq.at[0], lo.at[0])
    landed(hq.at[1], rc.at[0])

    def add(k, carry):
        i, j = k // 4, k % 4
        hq[0, i, j] = (hq[0, i, j].astype(F32) + hq[1, i, j].astype(F32)).astype(BF)
        return carry

    lax.fori_loop(0, 16, add, 0)
    for d in (1, 3, 2):
        rcopy(hq.at[0, step(x, d)], rq.at[x], s1.at[0, d], r1.at[0, x], to_x[d]).start()
    landed(oy, lo.at[1])
    landed(ob, rc.at[1])
    landed(vb.at[0], rv.at[0, 0])
    vs[...] = vec[...] + vb[0]
    for k in range(4):
        oy[k] = (oy[k].astype(F32) + ob[k].astype(F32)).astype(BF)
    for d in (1, 3, 2):
        rcopy(oy.at[step(y, d)], ox.at[y], s1.at[1, d], r1.at[1, y], to_y[d]).start()
        rcopy(vs, vb.at[d], sv.at[1, d], rv.at[1, d], to_y[d]).start()
    acc = oy[y].astype(F32)
    tot = vs[...]
    for d in (1, 2, 3):
        landed(ox.at[step(y, d)], r1.at[1, step(y, d)])
        landed(vb.at[d], rv.at[1, d])
        landed(vs, sv.at[1, d])
        acc = acc + ox[step(y, d)].astype(F32)
        tot = tot + vb[d]
    ox[y] = acc.astype(BF)
    vs[...] = tot
    for d in (1, 3, 2):
        rcopy(ox.at[y], o2.at[d], so.at[d], ro.at[d], to_x[d]).start()
        rcopy(vs, vb.at[3 + d], sv.at[2, d], rv.at[2, d], to_x[d]).start()
    for d in (1, 2, 3):
        landed(rq.at[step(x, d)], r1.at[0, step(x, d)])
    for k in range(4):
        v = hq[0, x, k].astype(F32)
        for d in (1, 2, 3):
            v = v + rq[step(x, d), k].astype(F32)
        fq[0, k] = v.astype(BF)
    for d in (1, 3, 2):
        rcopy(fq.at[0, step(y, d)], fq.at[1, y], s2.at[d], r2.at[y], to_y[d]).start()
    acc = ox[y].astype(F32)
    tot = vs[...]
    for d in (1, 2, 3):
        landed(o2.at[d], ro.at[d])
        landed(vb.at[3 + d], rv.at[2, d])
        landed(vs, sv.at[2, d])
        acc = acc + o2[d].astype(F32)
        tot = tot + vb[3 + d]
    o_out[...] = acc
    vs[...] = tot
    for d in (1, 3, 2):
        rcopy(vs, vb.at[6 + d], sv.at[3, d], rv.at[3, d], to_z[d]).start()
    landed(za.at[c, z], lo.at[2])
    for d in (1, 2, 3):
        landed(za.at[c, step(z, d)], rz.at[1, step(z, d)])
    rcopy(za.at[c], za.at[c], sf.at[1], rf.at[1], sib).start()
    for d in (1, 2, 3):
        landed(fq.at[1, step(y, d)], r2.at[step(y, d)])
    v = fq[0, y].astype(F32)
    for d in (1, 2, 3):
        v = v + fq[1, step(y, d)].astype(F32)
    zq[0, x] = v.astype(BF)
    for d in (1, 3, 2):
        rcopy(zq.at[0, x], zq.at[0, x], s3.at[d], r3.at[x], to_x[d]).start()
    z_scatter_take(pbuf, pr)
    g_in[...] = d_st[...] + total_of(pbuf)
    for d in (1, 2, 3):
        landed(zq.at[0, step(x, d)], r3.at[step(x, d)])
    for d in (1, 3, 2):
        rcopy(zq.at[0, step(z, d)], zq.at[1 + c, z], sz.at[0, d], rz.at[0, z], to_z[d]).start()
    zq[1 + c, z] = zq[0, z]
    landed(zd.at[c], lo.at[3])
    landed(zd.at[1 - c], rf.at[2])
    landed(za.at[1 - c], rf.at[1])
    for k in range(4):
        cols = slice(k * D, (k + 1) * D)
        o_up[:, cols] = za[0, k].astype(F32)
        o_gate[:, cols] = za[1, k].astype(F32)
        for h in range(2):
            o_down[k * 80 : (k + 1) * 80, h * 640 : (h + 1) * 640] = zd[h, k].astype(F32)
    for d in (1, 2, 3):
        landed(zq.at[1 + c, step(z, d)], rz.at[0, step(z, d)])
    rcopy(zq.at[1 + c], zq.at[1 + c], sf.at[0], rf.at[0], sib).start()
    tot = vs[...]
    for d in (1, 2, 3):
        landed(vb.at[6 + d], rv.at[3, d])
        landed(vs, sv.at[3, d])
        tot = tot + vb[6 + d]
    o_vec[0:2] = tot[0:2]
    o_vec[2:] = vs[2:]
    landed(zq.at[2 - c], rf.at[0])
    for k in range(4):
        a, b = zq[1, k].astype(F32), zq[2, k].astype(F32)
        at = k * GROUP
        o_q[:, at : at + GROUP] = a[:, :GROUP]
        o_k[:, at : at + GROUP] = b[:, :GROUP]
        o_v[:, at : at + GROUP] = jnp.concatenate([a[:, GROUP:], b[:, GROUP:448]], axis=1)
    z_scatter_sent(part, ps, c, z)
    landed(hq.at[1], sc.at[0])
    landed(go, sc.at[1])
    landed(vec, sv.at[0, 0])
    landed(zq.at[1], sf.at[0])
    landed(za.at[0], sf.at[1])
    landed(zd.at[0], sf.at[2])
    for d in (1, 2, 3):
        landed(rq.at[0], s1.at[0, d])
        landed(ox.at[0], s1.at[1, d])
        landed(fq.at[0, 0], s2.at[d])
        landed(zq.at[0, 0], s3.at[d])
        landed(zq.at[0, 0], sz.at[0, d])
        landed(za.at[0, 0], sz.at[1, d])
        landed(ox.at[0], so.at[d])


def close(part, d_st, za, zd, gq, go, vec):
    V = pltpu.VMEM
    return remote_call(
        close_kernel,
        [
            ((ROWS, D), F32, "v"),
            ((80, D), F32, "v"),
            ((80, D), F32, "v"),
            ((80, D), F32, "v"),
            ((80, D), F32, "v"),
            ((80, FF), F32, "v"),
            ((80, FF), F32, "v"),
            ((320, D), F32, "v"),
            ((8, D), F32, "v"),
        ],
        "avaaaav",
        [
            V((4, ROWS, D), BF), V((2, 4, 80, D), BF), V((2, 4, 80, 640), BF),
            V((2, 4, 4, 80, 512), BF), V((4, 4, 80, 512), BF), V((2, 4, 80, 512), BF), V((3, 4, 80, 512), BF),
            V((4, 80, D), BF), V((4, 80, D), BF), V((4, 80, D), BF), V((4, 80, D), BF), V((8, D), F32), V((10, 8, D), F32),
            dma(2, 2), dma(4), dma(2), dma(2), dma(4),
            dma(2, 4), dma(2, 4), dma(4), dma(4), dma(4), dma(4), dma(2, 4), dma(2, 4), dma(3), dma(3),
            dma(4), dma(4), dma(4, 4), dma(4, 4),
        ],
        4,
        "close",
    )(part, d_st, za, zd, gq, go, vec)


def shards(
    states, w_query, w_key, w_value, w_out, w_up, w_gate, w_down,
    scale_qk, alpha_attn, alpha_mlp, scale_up, scale_gate, lengths, cotangent,
):
    x, c, z, y = here()
    st = states[0]
    position = (c * 16 + z * 4 + y) * ROWS + jnp.arange(ROWS, dtype=jnp.int32)
    valid = jnp.broadcast_to((position < lengths[0]).astype(F32)[:, None], (ROWS, 128))

    def heads(w):
        return w.reshape(80, 4, HG, HDIM)

    q4, k4, v4 = heads(w_query), heads(w_key), heads(w_value)
    half0 = jnp.concatenate([q4, v4[:, :, :3]], axis=2)
    half1 = jnp.concatenate([k4, v4[:, :, 3:], jnp.zeros_like(v4[:, :, :1])], axis=2)
    wq = jnp.stack([half0, half1]).reshape(2, 80, 4, 512).transpose(0, 2, 1, 3)
    vec = jnp.concatenate([scale_qk, alpha_attn, alpha_mlp, scale_up, scale_gate, jnp.zeros((16,), BF)])
    vec = jnp.broadcast_to(vec.astype(F32)[None], (8, 896))
    xg, wqkv, vecs, wo = open_gather(st, wq, vec, w_out)
    rows = vecs[:, :, 0].reshape(16, 896)
    mine = lax.dynamic_slice_in_dim(rows, z * 4, 4, 0)

    def wide(v):
        return jnp.broadcast_to(v.reshape(1, -1), (8, v.size))

    scale_g = wide(mine[:, :80])
    rate_a = wide(rows[:, 80:160])
    rate_m = wide(rows[:, 160:240])
    su = wide(mine[:, 240:560])
    sg = wide(mine[:, 560:880])

    inner, outer = (jnp.asarray(t) for t in rope_tables())
    n = BLOCKS * ROWS
    xg2 = xg.reshape(n, D)
    wqkv2 = wqkv.reshape(2, D, 512)
    wo2 = wo.reshape(GROUP, D)
    q, kv, turned = make_qkv(xg2, wqkv2, scale_g, inner, outer)
    part, att, lse, kv_all, wu, gz = attend(lengths, q, kv.reshape(HG, 2, 2, ROWS, 128), wo2, w_up, w_gate)
    result, d_st, dm, ha, hd, vec = middle(
        part.reshape(2, 2, ROWS, D), st, cotangent[0], rate_a, rate_m, su, sg, valid, wu, gz, w_down
    )
    dq, dkv, go, za, zd = attend_back(lengths, q, kv_all, wo2, dm.reshape(n, D), att, lse, ha, hd)
    part, gq, g_sq = qkv_back(lengths, dq, dkv.reshape(HG, n, 128), turned, scale_g, inner, outer, xg2, wqkv2)
    vec = jnp.concatenate([vec[:4], jnp.pad(g_sq[0:1], ((0, 0), (0, D - GROUP))), vec[5:]])
    g_in, o_q, o_k, o_v, o_out, o_up, o_gate, o_down, o_vec = close(
        part.reshape(2, 2, ROWS, D), d_st, za, zd, gq.reshape(2, 4, 4, 80, 512), go.reshape(4, 80, D), vec
    )
    shard = z * 4 + y
    cut = lax.dynamic_slice_in_dim
    return (
        result[None],
        g_in[None],
        o_q,
        o_k,
        o_v,
        o_out,
        o_up,
        o_gate,
        o_down,
        cut(o_vec[4], y * 80, 80, 0),
        cut(o_vec[0], shard * 80, 80, 0),
        cut(o_vec[1], shard * 80, 80, 0),
        cut(o_vec[2], y * 320, 320, 0),
        cut(o_vec[3], y * 320, 320, 0),
    )


def solution(mesh):
    row = P("grp", ("seq", "shard"), None)
    mat = P("shard", None)
    one = P("shard")
    return jax.shard_map(
        shards,
        mesh=mesh,
        in_specs=(row,) + (mat,) * 7 + (one,) * 5 + (P("grp"), row),
        out_specs=(row, row) + (mat,) * 7 + (one,) * 5,
        check_vma=False,
    )
```

```python
import functools
import math

import jax
import jax.numpy as jnp
import numpy as np
from jax import lax
from jax.experimental import pallas as pl
from jax.experimental.pallas import tpu as pltpu
from jax.sharding import PartitionSpec as P


D, HEADS, HDIM, FF = 1280, 20, 64, 5120
ROWS, BLOCKS, HG = 128, 4, 5
GROUP = HG * HDIM
EPS = 1e-6
BF, F32 = jnp.bfloat16, jnp.float32
MESH = pl.DeviceIdType.MESH
VMEM_LIMIT = 60 << 20


def here():
    s = lax.axis_index("shard")
    return lax.axis_index("grp"), lax.axis_index("seq"), s // 4, s % 4


def dev(x, c, z, y):
    return (x, c, z * 4 + y)


def worker(z):
    return ((z + 1) // 2) % 2


def owner_z(w, i):
    return i * (3 - 2 * w) + w


def step(v, d):
    return (v + d) % 4


def rcopy(src, dst, ss, rs, to):
    return pltpu.make_async_remote_copy(
        src_ref=src, dst_ref=dst, send_sem=ss, recv_sem=rs, device_id=to, device_id_type=MESH
    )


def lcopy(src, dst, sem):
    return pltpu.make_async_copy(src, dst, sem)


def landed(dst, sem):
    pltpu.make_async_copy(dst, dst, sem).wait()


def greet(peers):
    bar = pltpu.get_barrier_semaphore()
    for p in peers:
        pl.semaphore_signal(bar, inc=1, device_id=p, device_id_type=MESH)
    pl.semaphore_wait(bar, len(peers))


def z_peers(x, c, z, y):
    far = [dev(x, cc, step(z, d), y) for d in (1, 2, 3) for cc in (0, 1)]
    return [dev(x, 1 - c, z, y)] + far


def z_gather_start(src, dst, ss, rs, x, c, z, y):
    w = worker(z)
    slot = (z // 2, c)
    for d in (1, 3, 2):
        rcopy(src, dst.at[slot], ss.at[d], rs.at[slot], dev(x, w, step(z, d), y)).start()

    @pl.when(c == w)
    def _():
        lcopy(src, dst.at[slot], rs.at[slot]).start()

    @pl.when(c != w)
    def _():
        rcopy(src, dst.at[slot], ss.at[0], rs.at[slot], dev(x, w, z, y)).start()


def z_gather_take(dst, rs, p):
    for k in range(2):
        landed(dst.at[p, k], rs.at[p, k])


def z_gather_sent(src, ss, c, z):
    for d in (1, 2, 3):
        landed(src, ss.at[d])

    @pl.when(c != worker(z))
    def _():
        landed(src, ss.at[0])


def z_gather_wait(src, dst, ss, rs, c, z):
    for p in range(2):
        z_gather_take(dst, rs, p)
    z_gather_sent(src, ss, c, z)


def z_scatter_pair(part, dst, ss, rs, p, x, c, z, y):
    oz = owner_z(c, p)
    for oc in range(2):
        mine = jnp.logical_and(c == oc, z == oz)

        @pl.when(mine)
        def _(oc=oc):
            lcopy(part.at[p, oc], dst.at[z], rs.at[z]).start()

        @pl.when(jnp.logical_not(mine))
        def _(oc=oc):
            rcopy(part.at[p, oc], dst.at[z], ss.at[p, oc], rs.at[z], dev(x, oc, oz, y)).start()


def z_scatter_start(part, dst, ss, rs, x, c, z, y):
    for p in range(2):
        z_scatter_pair(part, dst, ss, rs, p, x, c, z, y)


def z_scatter_take(dst, rs):
    for k in range(4):
        landed(dst.at[k], rs.at[k])


def z_scatter_sent(part, ss, c, z):
    for p in range(2):
        for oc in range(2):
            mine = jnp.logical_and(c == oc, z == owner_z(c, p))

            @pl.when(jnp.logical_not(mine))
            def _(p=p, oc=oc):
                landed(part.at[p, oc], ss.at[p, oc])


def remote_call(kernel, outs, ins_spaces, scratch, cid, name):
    spec = {
        "a": pl.BlockSpec(memory_space=pl.ANY),
        "v": pl.BlockSpec(memory_space=pltpu.VMEM),
        "s": pl.BlockSpec(memory_space=pltpu.SMEM),
    }
    return pl.pallas_call(
        kernel,
        out_shape=[jax.ShapeDtypeStruct(s, d) for s, d, _ in outs],
        in_specs=[spec[s] for s in ins_spaces],
        out_specs=[spec[s] for _, _, s in outs],
        scratch_shapes=scratch,
        compiler_params=pltpu.CompilerParams(
            collective_id=cid, has_side_effects=True, vmem_limit_bytes=VMEM_LIMIT
        ),
        name=name,
    )


def local_call(kernel, outs, n_in, scratch, name, smem=0):
    vmem = pl.BlockSpec(memory_space=pltpu.VMEM)
    sm = pl.BlockSpec(memory_space=pltpu.SMEM)
    return pl.pallas_call(
        kernel,
        out_shape=[jax.ShapeDtypeStruct(s, d) for s, d in outs],
        in_specs=[sm] * smem + [vmem] * n_in,
        out_specs=[vmem for _ in outs],
        scratch_shapes=scratch,
        compiler_params=pltpu.CompilerParams(vmem_limit_bytes=VMEM_LIMIT),
        name=name,
    )


def dma(*shape):
    return pltpu.SemaphoreType.DMA(shape)


def rope_tables():
    freqs = np.exp(np.arange(32) * (-2.0 * math.log(10000.0) / 64))
    freqs = np.tile(freqs, 4)
    sign = np.tile(np.concatenate([-np.ones(32), np.ones(32)]), 2)
    inner = np.arange(ROWS)[:, None] * freqs
    outer = (np.arange(32) * ROWS)[:, None] * freqs
    return (
        np.stack([np.cos(inner), np.sin(inner) * sign]).astype(np.float32),
        np.stack([np.cos(outer), np.sin(outer) * sign]).astype(np.float32),
    )


def block_index(c, y, j):
    return (j % 2) * 16 + owner_z(c, j // 2) * 4 + y


def turn_of(inner, outer, b):
    oc = outer[0, pl.ds(b, 1), :]
    os = outer[1, pl.ds(b, 1), :]
    return oc * inner[0] - os * inner[1], os * inner[0] + oc * inner[1]


def lanes():
    return lax.broadcasted_iota(jnp.int32, (ROWS, 128), 1)


def swap(v, lane):
    return jnp.where(lane % 64 < 32, pltpu.roll(v, 96, 1), pltpu.roll(v, 32, 1))


def half_means(v, lane):
    low = jnp.sum(jnp.where(lane < 64, v, 0.0), axis=-1, keepdims=True)
    high = jnp.sum(jnp.where(lane < 64, 0.0, v), axis=-1, keepdims=True)
    return jnp.where(lane < 64, low, high) * (1.0 / 64)


TILE = 512
STEP = 6


def tiles_of(c, j):
    return (j % 2) * 4 + owner_z(c, j // 2) + 1


def nt(a, b):
    return lax.dot_general(a, b, (((1,), (1,)), ((), ())), preferred_element_type=F32)


def tn(a, b):
    return lax.dot_general(a, b, (((0,), (0,)), ((), ())), preferred_element_type=F32)


def key_tile(ref, h, t):
    zz = t % 4
    return ref[h, worker(zz), zz // 2, t // 4].reshape(TILE, 128)


def work_items(c, y, length):
    n = [tiles_of(c, j) for j in range(BLOCKS)]
    starts = [n[0], n[0] + n[1], n[0] + n[1] + n[2]]
    query = lax.broadcasted_iota(jnp.int32, (1, ROWS), 1)

    def item(i):
        hits = [(i >= s).astype(jnp.int32) for s in starts]
        j = hits[0] + hits[1] + hits[2]
        t = i - hits[0] * n[0] - hits[1] * n[1] - hits[2] * n[2]
        last = query + y * ROWS + (tiles_of(c, j) - 1 - t) * TILE
        return j, t, jnp.minimum(last, length - 1 - t * TILE)

    return item


def columns(ref, k, half):
    return ref.at[:, pl.ds(pl.multiple_of(k * D + half * 640, 128), 640)]


def front_kernel(
    length, st, wq, vec, w_out, w_up, w_gate, w_down, inner, outer,
    part, att, lse, kv_o, q_o, t_o, xg_o, wqkv_o, wo_o, scale_o, rate_a, rate_m, su, sg, wu, wd, gy,
    xg, wqkv, vecs, wo, y0, y1, kv, kvb, q, tt, low, acc, tot, gz,
    xs, xr, w1s, w1r, w2s, w2r, w3s, w3r, vs, vr, os, orr, lo,
    f1s, f1r, f2s, f2r, f3s, f3r, f4s, f4r, fl, sy, ry, sf, rf, ss, rs, kl, ol,
):
    x, c, z, y = here()
    sib = dev(x, 1 - c, z, y)
    half = pl.ds(pl.multiple_of(c * 640, 128), 640)
    other = pl.ds(pl.multiple_of((1 - c) * 640, 128), 640)
    to_z = [None] + [dev(x, c, step(z, d), y) for d in (1, 2, 3)]
    to_y = [None] + [dev(x, c, z, step(y, d)) for d in (1, 2, 3)]
    to_x = [None] + [dev(step(x, d), c, z, y) for d in (1, 2, 3)]
    near_first = (1, 3, 2)
    greet(z_peers(x, c, z, y) + to_y[1:] + to_x[1:])

    for d in near_first:
        rcopy(wq.at[c, step(z, d)], wqkv.at[c, z, y], w1s.at[d], w1r.at[z], to_z[d]).start()
        rcopy(vec, vecs.at[z, y], vs.at[0, d], vr.at[0, z], to_z[d]).start()
    lcopy(wq.at[c, z], wqkv.at[c, z, y], lo.at[0]).start()
    lcopy(vec, vecs.at[z, y], lo.at[1]).start()
    z_gather_start(st, xg, xs, xr, x, c, z, y)
    for d in near_first:
        rcopy(w_out.at[:, half], wo.at[y, :, half], os.at[0, d], orr.at[0, y], to_y[d]).start()
    rcopy(w_out.at[:, half], wo.at[y, :, half], os.at[0, 0], orr.at[1, y], sib).start()
    lcopy(w_out.at[:, half], wo.at[y, :, half], lo.at[2]).start()
    down = w_down.at[pl.ds(pl.multiple_of(x * 80, 16), 80), half]
    for d in near_first:
        rcopy(down, wd.at[y, x, :, half], f2s.at[2, d], f2r.at[2, y], to_y[d]).start()
    lcopy(down, wd.at[y, x, :, half], fl.at[2]).start()

    @pl.when(z == x)
    def _():
        for d in near_first:
            z2 = step(z, d)
            rcopy(columns(w_up, z2, c), wu.at[x, y, :, half], f1s.at[0, d], f1r.at[0], to_z[d]).start()
            rcopy(columns(w_gate, z2, c), gz, f1s.at[1, d], f1r.at[1], to_z[d]).start()
        lcopy(columns(w_up, z, c), wu.at[x, y, :, half], f1r.at[0]).start()
        lcopy(columns(w_gate, z, c), gz, f1r.at[1]).start()

    for d in (1, 2, 3):
        landed(wqkv.at[c, step(z, d), y], w1r.at[step(z, d)])
        landed(vecs.at[step(z, d), y], vr.at[0, step(z, d)])
    landed(wqkv.at[c, z, y], lo.at[0])
    landed(vecs.at[z, y], lo.at[1])
    for d in near_first:
        rcopy(wqkv.at[c, :, y], wqkv.at[c, :, y], w2s.at[d], w2r.at[y], to_y[d]).start()
        rcopy(vecs.at[:, y], vecs.at[:, y], vs.at[1, d], vr.at[1, y], to_y[d]).start()
    rcopy(wqkv.at[c, :, y], wqkv.at[c, :, y], w3s.at[0], w3r.at[y], sib).start()
    landed(wd.at[y, x, :, half], fl.at[2])
    for d in (1, 2, 3):
        landed(wd.at[step(y, d), x, :, half], f2r.at[2, step(y, d)])
    for d in near_first:
        rcopy(wd.at[:, x, :, half], wd.at[:, x, :, half], f3s.at[1, d], f3r.at[1, x], to_x[d]).start()
    rcopy(wd.at[:, x, :, half], wd.at[:, x, :, half], f4s.at[1, 0], f4r.at[1, x], sib).start()
    landed(wu.at[x, y, :, half], f1r.at[0])
    landed(gz, f1r.at[1])
    for d in near_first:
        rcopy(wu.at[x, y, :, half], wu.at[x, y, :, half], f2s.at[0, d], f2r.at[0, y], to_y[d]).start()
        rcopy(gz, gy.at[y], f2s.at[1, d], f2r.at[1, y], to_y[d]).start()
    lcopy(gz, gy.at[y], fl.at[1]).start()
    for d in near_first:
        y2 = step(y, d)
        landed(wqkv.at[c, :, y2], w2r.at[y2])
        rcopy(wqkv.at[c, :, y2], wqkv.at[c, :, y2], w3s.at[d], w3r.at[y2], sib).start()
        landed(wo.at[y2, :, half], orr.at[0, y2])
        rcopy(wo.at[y2, :, half], wo.at[y2, :, half], os.at[1, d], orr.at[1, y2], sib).start()
        landed(vecs.at[:, y2], vr.at[1, y2])
    for zz in range(4):
        for yy in range(4):
            at = (zz * 4 + yy) * 80
            rate_a[:, at : at + 80] = vecs[zz, yy, :, 80:160]
            rate_m[:, at : at + 80] = vecs[zz, yy, :, 160:240]
    for yy in range(4):
        su[:, yy * 320 : (yy + 1) * 320] = vecs[z, yy, :, 240:560]
        sg[:, yy * 320 : (yy + 1) * 320] = vecs[z, yy, :, 560:880]
    scale = jnp.concatenate([vecs[z, yy, :, :80] for yy in range(4)], axis=1)
    for h in range(HG):
        sh = scale[:, h * HDIM : (h + 1) * HDIM]
        scale_o[:, h * 128 : (h + 1) * 128] = jnp.concatenate([sh, sh], axis=1)

    for d in (1, 2, 3):
        landed(wu.at[x, step(y, d), :, half], f2r.at[0, step(y, d)])
    for d in near_first:
        rcopy(wu.at[x, :, :, half], wu.at[x, :, :, half], f3s.at[0, d], f3r.at[0, x], to_x[d]).start()
    rcopy(wu.at[x, :, :, half], wu.at[x, :, :, half], f4s.at[0, 0], f4r.at[0, x], sib).start()

    for p in range(2):
        z_gather_take(xg, xr, p)
    for k in range(4):
        landed(wqkv.at[1 - c, :, k], w3r.at[k])
    lcopy(xg, xg_o, ol.at[0]).start()
    lcopy(wqkv, wqkv_o, ol.at[1]).start()

    def project(p, carry):
        rows = xg[p].reshape(2 * ROWS, D)
        y0[p] = jnp.dot(rows, wqkv[0].reshape(D, 512), preferred_element_type=F32)
        y1[p] = jnp.dot(rows, wqkv[1].reshape(D, 512), preferred_element_type=F32)
        return carry

    lax.fori_loop(0, 2, project, 0)
    lane = lanes()

    def send(h):
        rcopy(kv.at[h], kvb.at[h, c, :, :, y], sy.at[h, 0], ry.at[h, 0], to_y[1]).start()
        rcopy(kv.at[h], kvb.at[h, c, :, :, y], sy.at[h, 1], ry.at[h, 1], to_y[3]).start()
        rcopy(kv.at[h], kvb.at[h, c, :, :, y], ss.at[h, 0], rs.at[h, 0], sib).start()
        lcopy(kv.at[h], kvb.at[h, c, :, :, y], kl.at[h]).start()

    for h in range(HG):

        def per_block(j, carry, h=h):
            p, r = j // 2, pl.ds(pl.multiple_of((j % 2) * ROWS, ROWS), ROWS)
            cosine, sine = turn_of(inner, outer, block_index(c, y, j))
            raw = y0[p, r, h * 128 : (h + 1) * 128] if h < 4 else y1[p, r, 0:128]
            t = raw * cosine + swap(raw, lane) * sine
            unit = t * lax.rsqrt(half_means(t * t, lane) + EPS)
            both = unit * scale_o[0:1, h * 128 : (h + 1) * 128]
            pair = y1[p, r, 128 + (h // 2) * 128 : 256 + (h // 2) * 128]
            v = pair if h % 2 else pltpu.roll(pair, 64, 1)
            kv[h, p, j % 2] = jnp.where(lane < 64, pltpu.roll(both, 64, 1), v).astype(BF)
            rows = pl.ds(pl.multiple_of(j * ROWS, ROWS), ROWS)
            tt[h, rows, :] = t
            q[h, rows, :] = (jnp.where(lane < 64, both, 0.0).astype(BF).astype(F32) * 0.125).astype(BF)
            return carry

        lax.fori_loop(0, BLOCKS, per_block, 0)
        send(h)
    lcopy(q, q_o, ol.at[2]).start()
    lcopy(tt, t_o, ol.at[3]).start()

    def near(h):
        for k, src, to in ((0, step(y, 3), to_y[1]), (1, step(y, 1), to_y[3])):
            landed(kvb.at[h, c, :, :, src], ry.at[h, k])
            rcopy(kvb.at[h, c, k, :, src], kvb.at[h, c, k, :, src], sf.at[h, k], rf.at[h, k], to).start()
            rcopy(kvb.at[h, c, :, :, src], kvb.at[h, c, :, :, src], ss.at[h, 1 + k], rs.at[h, 1 + k], sib).start()

    def far(h):
        src = step(y, 2)
        for k in range(2):
            landed(kvb.at[h, c, k, :, src], rf.at[h, k])
            rcopy(kvb.at[h, c, k, :, src], kvb.at[h, c, k, :, src], ss.at[h, 3 + k], rs.at[h, 3 + k], sib).start()

    def ready(h):
        landed(kvb.at[h, c, :, :, y], kl.at[h])
        landed(kvb.at[h, 1 - c, :, :, y], rs.at[h, 0])
        landed(kvb.at[h, 1 - c, :, :, step(y, 3)], rs.at[h, 1])
        landed(kvb.at[h, 1 - c, :, :, step(y, 1)], rs.at[h, 2])
        for k in range(2):
            landed(kvb.at[h, 1 - c, k, :, step(y, 2)], rs.at[h, 3 + k])
        lcopy(kvb.at[h], kv_o.at[h], kl.at[h]).start()

    item = work_items(c, y, length[0])

    def compute(h):
        acc[...] = jnp.zeros_like(acc)
        tot[...] = jnp.zeros_like(tot)

        def body(g, carry):
            key = lax.broadcasted_iota(jnp.int32, (TILE, ROWS), 0)
            its = [item(g * STEP + u) for u in range(STEP)]
            ks = [key_tile(kvb, h, t) for _, t, _ in its]
            ss_ = [
                nt(k, q[h, pl.ds(pl.multiple_of(j * ROWS, ROWS), ROWS), :]) for k, (j, _, _) in zip(ks, its)
            ]
            ps = [jnp.where(key <= bound, jnp.exp(s), 0.0) for s, (_, _, bound) in zip(ss_, its)]
            for k, p, (j, _, _) in zip(ks, ps, its):
                tot[j] += jnp.sum(p.reshape(TILE // 8, 8, ROWS), axis=0)
                acc[j] += tn(k, p.astype(BF))
            return carry

        lax.fori_loop(0, 18 // STEP, body, 0)
        for j in range(BLOCKS):
            total = jnp.sum(tot[j], axis=0, keepdims=True)
            lse[h, j : j + 1, :] = jnp.log(total)
            att[h, j * ROWS : (j + 1) * ROWS, :] = (acc[j, HDIM:] / total).T

    near(0)

    def per_head(i, carry):
        @pl.when(i + 1 < HG)
        def _():
            near(i + 1)

        @pl.when(i < HG)
        def _():
            far(i)

        @pl.when(i > 0)
        def _():
            ready(i - 1)
            compute(i - 1)

        return carry

    lax.fori_loop(0, HG + 1, per_head, 0)
    for h in range(HG):
        low[:, h * HDIM : (h + 1) * HDIM] = att[h].astype(BF)
    landed(wo.at[y, :, half], lo.at[2])
    for k in range(4):
        landed(wo.at[k, :, other], orr.at[1, k])
    lcopy(wo, wo_o, ol.at[4]).start()
    for p in range(2):
        v = jnp.dot(low[p * 256 : (p + 1) * 256, :], wo[...].reshape(GROUP, D), preferred_element_type=F32)
        part[p] = v.astype(BF).reshape(2, ROWS, D)

    for d in near_first:
        x2 = step(x, d)
        landed(wd.at[:, x2, :, half], f3r.at[1, x2])
        rcopy(wd.at[:, x2, :, half], wd.at[:, x2, :, half], f4s.at[1, d], f4r.at[1, x2], sib).start()
    for d in near_first:
        x2 = step(x, d)
        landed(wu.at[x2, :, :, half], f3r.at[0, x2])
        rcopy(wu.at[x2, :, :, half], wu.at[x2, :, :, half], f4s.at[0, d], f4r.at[0, x2], sib).start()
    landed(gz, fl.at[1])
    for d in (1, 2, 3):
        landed(gy.at[step(y, d)], f2r.at[1, step(y, d)])

    def sent(h, carry):
        for k in range(2):
            landed(kv.at[h], sy.at[h, k])
            landed(kv.at[h, 0], sf.at[h, k])
            landed(kv.at[h, 0], ss.at[h, 3 + k])
        for k in range(3):
            landed(kv.at[h], ss.at[h, k])
        landed(kvb.at[h], kl.at[h])
        return carry

    lax.fori_loop(0, HG, sent, 0)
    z_gather_sent(st, xs, c, z)
    for k in range(4):
        landed(wd.at[:, k, :, other], f4r.at[1, k])
        landed(wu.at[k, :, :, other], f4r.at[0, k])
        landed(wd.at[:, k, :, half], f4s.at[1, k])
        landed(wu.at[k, :, :, half], f4s.at[0, k])
        landed(wqkv.at[c, :, k], w3s.at[k])
    landed(wo.at[0, :, half], os.at[0, 0])
    for d in (1, 2, 3):
        landed(wqkv.at[c, z, y], w1s.at[d])
        landed(vec, vs.at[0, d])
        landed(vecs.at[:, y], vs.at[1, d])
        landed(wqkv.at[c, :, y], w2s.at[d])
        landed(wo.at[0, :, half], os.at[0, d])
        landed(wo.at[0, :, half], os.at[1, d])
        landed(gz, f2s.at[0, d])
        landed(gz, f2s.at[1, d])
        landed(gz, f2s.at[2, d])
        landed(wu.at[x, :, :, half], f3s.at[0, d])
        landed(wd.at[:, x, :, half], f3s.at[1, d])

    @pl.when(z == x)
    def _():
        for d in (1, 2, 3):
            landed(gz, f1s.at[0, d])
            landed(gz, f1s.at[1, d])

    landed(xg, ol.at[0])
    landed(wqkv, ol.at[1])
    landed(q, ol.at[2])
    landed(tt, ol.at[3])
    landed(wo, ol.at[4])


def front(length, st, wq, vec, w_out, w_up, w_gate, w_down, inner, outer):
    n = BLOCKS * ROWS
    V = pltpu.VMEM
    return remote_call(
        front_kernel,
        [
            ((2, 2, ROWS, D), BF, "v"),
            ((HG, n, HDIM), F32, "v"),
            ((HG, BLOCKS, 128), F32, "v"),
            ((HG, 2, 2, 2, 4, ROWS, 128), BF, "a"),
            ((HG, n, 128), BF, "a"),
            ((HG, n, 128), F32, "a"),
            ((2, 2, ROWS, D), BF, "a"),
            ((2, 4, 4, 80, 512), BF, "a"),
            ((4, 80, D), BF, "a"),
            ((8, HG * 128), F32, "v"),
            ((8, D), F32, "v"),
            ((8, D), F32, "v"),
            ((8, D), F32, "v"),
            ((8, D), F32, "v"),
            ((4, 4, 80, D), BF, "a"),
            ((4, 4, 80, D), BF, "a"),
            ((4, 80, 640), BF, "a"),
        ],
        "saavaaaavv",
        [
            V((2, 2, ROWS, D), BF), V((2, 4, 4, 80, 512), BF), V((4, 4, 8, 896), F32), V((4, 80, D), BF),
            V((2, 256, 512), F32), V((2, 256, 512), F32),
            V((HG, 2, 2, ROWS, 128), BF), V((HG, 2, 2, 2, 4, ROWS, 128), BF), V((HG, n, 128), BF), V((HG, n, 128), F32),
            V((n, GROUP), BF), V((BLOCKS, 128, ROWS), F32), V((BLOCKS, 8, ROWS), F32), V((80, 640), BF),
            dma(4), dma(2, 2), dma(4), dma(4), dma(4), dma(4), dma(4), dma(4), dma(2, 4), dma(2, 4), dma(2, 4), dma(2, 4), dma(3),
            dma(2, 4), dma(2), dma(3, 4), dma(3, 4), dma(2, 4), dma(2, 4), dma(2, 4), dma(2, 4), dma(3),
            dma(HG, 2), dma(HG, 2), dma(HG, 2), dma(HG, 2), dma(HG, 5), dma(HG, 5), dma(HG), dma(5),
        ],
        0,
        "front",
    )(length, st, wq, vec, w_out, w_up, w_gate, w_down, inner, outer)


def attend_back_kernel(
    length, q, kv, wo, dmix, att, lse, ha, hd,
    dq, dkv, gout, za, zd,
    qdo, delta, dqt, acc, low, give, mine, got, got_y, oa, od, ra, rd, fa, fd,
    sg, rg, sy, ry, s1, r1, s2, r2, s3, r3, lo,
):
    x, c, z, y = here()
    sib = dev(x, 1 - c, z, y)
    to_y = [None] + [dev(x, c, z, step(y, d)) for d in (1, 2, 3)]
    to_x = [None] + [dev(step(x, d), c, z, y) for d in (1, 2, 3)]
    greet([sib] + to_y[1:] + to_x[1:])
    for d in (1, 3, 2):
        rcopy(ha.at[step(x, d)], ra.at[x], s1.at[0, d], r1.at[0, x], to_x[d]).start()
        rcopy(hd.at[step(y, d)], rd.at[y], s1.at[1, d], r1.at[1, y], to_y[d]).start()
    lcopy(ha.at[x], oa, lo.at[0]).start()
    lcopy(hd.at[y], od, lo.at[1]).start()

    def first_sums():
        landed(oa, lo.at[0])
        landed(od, lo.at[1])
        for d in (1, 2, 3):
            landed(ra.at[step(x, d)], r1.at[0, step(x, d)])
            landed(rd.at[step(y, d)], r1.at[1, step(y, d)])

        def body(k, carry):
            va = oa[k].astype(F32)
            vd = od[k].astype(F32)
            for d in (1, 2, 3):
                va = va + ra[step(x, d), k].astype(F32)
                vd = vd + rd[step(y, d), k].astype(F32)
            oa[k] = va.astype(BF)
            od[k] = vd.astype(BF)
            return carry

        lax.fori_loop(0, 4, body, 0)
        for d in (1, 3, 2):
            rcopy(oa.at[step(y, d)], fa.at[y], s2.at[0, d], r2.at[0, y], to_y[d]).start()
            rcopy(od.at[step(x, d)], fd.at[x], s2.at[1, d], r2.at[1, x], to_x[d]).start()

    def second_sums():
        for d in (1, 2, 3):
            landed(fa.at[step(y, d)], r2.at[0, step(y, d)])
            landed(fd.at[step(x, d)], r2.at[1, step(x, d)])
        va = oa[y].astype(F32)
        vd = od[x].astype(F32)
        for d in (1, 2, 3):
            va = va + fa[step(y, d)].astype(F32)
            vd = vd + fd[step(x, d)].astype(F32)
        fa[y] = va.astype(BF)
        fd[x] = vd.astype(BF)
        for d in (1, 3, 2):
            rcopy(fa.at[y], za.at[x], s3.at[0, d], r3.at[0, x], to_x[d]).start()
            rcopy(fd.at[x], zd.at[x], s3.at[1, d], r3.at[1, x], to_x[d]).start()
        lcopy(fa.at[y], za.at[x], lo.at[2]).start()
        lcopy(fd.at[x], zd.at[x], lo.at[3]).start()

    def settle(h):
        landed(got.at[h], rg.at[h])
        for i in range(2):
            for k in range(2):
                mine[h, i, k] = (mine[h, i, k].astype(F32) + got[h, i, k].astype(F32)).astype(BF)
        for d in (1, 3, 2):
            rcopy(mine.at[h, :, :, step(y, d)], got_y.at[h, y], sy.at[h, d], ry.at[h, y], to_y[d]).start()

    d_att = nt(dmix[...], wo[...]).astype(BF)
    for h in range(HG):
        low[:, h * HDIM : (h + 1) * HDIM] = att[h].astype(BF)
        dh = d_att[:, h * HDIM : (h + 1) * HDIM].astype(F32)
        wide = jnp.concatenate([jnp.zeros_like(dh), dh], axis=1).astype(BF)
        prod = dh * att[h]
        for j in range(BLOCKS):
            rows = slice(j * ROWS, (j + 1) * ROWS)
            qdo[h, j, :ROWS] = q[h, rows, :]
            qdo[h, j, ROWS:] = wide[rows]
            delta[h, j : j + 1, :] = jnp.sum(prod[rows].T, axis=0, keepdims=True)
    gout[...] = tn(low[...], dmix[...]).astype(BF)
    item = work_items(c, y, length[0])

    def per_head(h, carry):
        acc[...] = jnp.zeros_like(acc)
        dqt[...] = jnp.zeros_like(dqt)

        @pl.when(h == 3)
        def _():
            first_sums()

        @pl.when(h == 4)
        def _():
            second_sums()

        def body(g, carry):
            @pl.when(jnp.logical_and(g == 1, h > 0))
            def _():
                settle(h - 1)

            key = lax.broadcasted_iota(jnp.int32, (TILE, ROWS), 0)
            its = [item(g * STEP + u) for u in range(STEP)]
            ks = [key_tile(kv, h, t) for _, t, _ in its]
            bs = [qdo[h, j] for j, _, _ in its]
            sds = [nt(k, b) for k, b in zip(ks, bs)]
            dss, ps = [], []
            for sd, (j, _, bound) in zip(sds, its):
                p = jnp.where(key <= bound, jnp.exp(sd[:, :ROWS] - lse[h, pl.ds(j, 1), :]), 0.0)
                dss.append((p * (sd[:, ROWS:] - delta[h, pl.ds(j, 1), :])).astype(BF))
                ps.append(p.astype(BF))
            for ds, p, b, (_, t, _) in zip(dss, ps, bs, its):
                acc[t] += jnp.dot(jnp.concatenate([ds, p], axis=1), b, preferred_element_type=F32)
            for k, ds, (j, _, _) in zip(ks, dss, its):
                dqt[j] += tn(k, ds)
            return carry

        lax.fori_loop(0, 18 // STEP, body, 0)
        for j in range(BLOCKS):
            dq[h, j * ROWS : (j + 1) * ROWS, :] = dqt[j].T * 0.125

        def store(i, carry):
            zi, k = i // 2, i % 2
            give[h, zi, k] = acc[k * 4 + owner_z(1 - c, zi)].astype(BF).reshape(4, ROWS, 128)
            mine[h, zi, k] = acc[k * 4 + owner_z(c, zi)].astype(BF).reshape(4, ROWS, 128)
            return carry

        lax.fori_loop(0, 4, store, 0)
        rcopy(give.at[h], got.at[h], sg.at[h], rg.at[h], sib).start()
        return carry

    lax.fori_loop(0, HG, per_head, 0)
    settle(HG - 1)

    def final(h, carry):
        for d in (1, 2, 3):
            landed(got_y.at[h, step(y, d)], ry.at[h, step(y, d)])
        for i in range(2):
            for k in range(2):
                v = mine[h, i, k, y].astype(F32)
                for d in (1, 2, 3):
                    v = v + got_y[h, step(y, d), i, k].astype(F32)
                dkv[h, i, k] = v.astype(BF)
        landed(give.at[h], sg.at[h])
        for d in (1, 2, 3):
            landed(got_y.at[h, y], sy.at[h, d])
        return carry

    lax.fori_loop(0, HG, final, 0)
    for d in (1, 2, 3):
        landed(za.at[step(x, d)], r3.at[0, step(x, d)])
        landed(zd.at[step(x, d)], r3.at[1, step(x, d)])
    landed(za.at[x], lo.at[2])
    landed(zd.at[x], lo.at[3])
    for d in (1, 2, 3):
        landed(ra.at[x], s1.at[0, d])
        landed(rd.at[y], s1.at[1, d])
        landed(fa.at[0], s2.at[0, d])
        landed(fd.at[0], s2.at[1, d])
        landed(fa.at[0], s3.at[0, d])
        landed(fd.at[0], s3.at[1, d])


def attend_back(length, q, kv, wo, dmix, att, lse, ha, hd):
    n = BLOCKS * ROWS
    V = pltpu.VMEM
    return remote_call(
        attend_back_kernel,
        [
            ((HG, n, 128), F32, "v"),
            ((HG, 2, 2, ROWS, 128), BF, "v"),
            ((GROUP, D), BF, "v"),
            ((4, 80, D), BF, "a"),
            ((4, 80, 640), BF, "a"),
        ],
        "svvvvvvaa",
        [
            V((HG, BLOCKS, 2 * ROWS, 128), BF),
            V((HG, BLOCKS, 128), F32),
            V((BLOCKS, 128, ROWS), F32),
            V((8, TILE, 128), F32),
            V((n, GROUP), BF),
            V((HG, 2, 2, 4, ROWS, 128), BF),
            V((HG, 2, 2, 4, ROWS, 128), BF),
            V((HG, 2, 2, 4, ROWS, 128), BF),
            V((HG, 4, 2, 2, ROWS, 128), BF),
            V((4, 80, D), BF), V((4, 80, 640), BF),
            V((4, 4, 80, D), BF), V((4, 4, 80, 640), BF),
            V((4, 80, D), BF), V((4, 80, 640), BF),
            dma(HG), dma(HG), dma(HG, 4), dma(HG, 4),
            dma(2, 4), dma(2, 4), dma(2, 4), dma(2, 4), dma(2, 4), dma(2, 4), dma(4),
        ],
        3,
        "attend_back",
    )(length, q, kv, wo, dmix, att, lse, ha, hd)


def inv_rms(v):
    return lax.rsqrt(jnp.mean(v * v, axis=-1, keepdims=True) + EPS)


def back_rms(dy, yy, inv):
    return (dy - yy * jnp.mean(dy * yy, axis=-1, keepdims=True)) * inv


def total_of(buf):
    return (buf[0].astype(F32) + buf[1].astype(F32)) + (buf[2].astype(F32) + buf[3].astype(F32))


def mix_of(res, part, rate):
    inv_p = inv_rms(part)
    unit = part * inv_p
    diff = unit - res
    u = res + rate * diff
    inv_u = inv_rms(u)
    return u * inv_u, unit, inv_p, inv_u, diff


def mix_back(dy, res, part, rate):
    yy, unit, inv_p, inv_u, diff = mix_of(res, part, rate)
    du = back_rms(dy, yy, inv_u)
    return du * (1.0 - rate), back_rms(du * rate, unit, inv_p), jnp.sum(du * diff, axis=0, keepdims=True)


def mid_kernel(
    length, part0, st, cot, rate_a, rate_m, su, sg, wu_in, wd_in, gy,
    result, d_st, dm, ha, hd, vec,
    buf, low, xg, dd, wu, wg, wd, up, gate, hid, dug, part, xt, ht, mixed, first, dfirst, ga, gd, ra, rd,
    ps, pr, gs, gr, s2, r2, s3, r3, sx, rx, lo,
):
    x, c, z, y = here()
    sib = dev(x, 1 - c, z, y)
    half = pl.ds(pl.multiple_of(c * 640, 128), 640)
    other = pl.ds(pl.multiple_of((1 - c) * 640, 128), 640)
    near = z // 2
    greet(z_peers(x, c, z, y) + [dev(step(x, d), c, z, y) for d in (1, 2, 3)])
    z_scatter_start(part0, buf.at[0], ps.at[0], pr.at[0], x, c, z, y)
    for d in (1, 3, 2):
        rcopy(gy, wg.at[x, :, :, half], s2.at[d], r2.at[x], dev(step(x, d), c, z, y)).start()
    rcopy(gy, wg.at[x, :, :, half], s3.at[0], r3.at[x], sib).start()
    lcopy(gy, wg.at[x, :, :, half], lo.at[1]).start()
    lcopy(wu_in, wu, lo.at[0]).start()
    lcopy(wd_in, wd, lo.at[2]).start()
    vec[...] = jnp.zeros_like(vec)

    z_scatter_take(buf.at[0], pr.at[0])
    total = total_of(buf.at[0])
    mixed[...] = total
    out = mix_of(st[...].astype(F32), total, rate_a[0:1])[0]
    first[...] = out
    low[0] = out.astype(BF)
    z_gather_start(low.at[0], xg, gs.at[0], gr.at[0], x, c, z, y)

    for d in (1, 3, 2):
        x2 = step(x, d)
        landed(wg.at[x2, :, :, half], r2.at[x2])
        rcopy(wg.at[x2, :, :, half], wg.at[x2, :, :, half], s3.at[d], r3.at[x2], sib).start()
    landed(wu, lo.at[0])
    landed(wg.at[x, :, :, half], lo.at[1])
    landed(wd, lo.at[2])
    for k in range(4):
        landed(wg.at[k, :, :, other], r3.at[k])

    def rows_of(ref, p):
        return ref[p].reshape(2 * ROWS, D)

    def forward_cols(p):
        z_gather_take(xg, gr.at[0], p)

        def body(t, carry):
            cs = pl.ds(pl.multiple_of(t * 256, 256), 256)
            xs = rows_of(xg, p)
            u = jnp.dot(xs, wu[:, cs], preferred_element_type=F32)
            g = jnp.dot(xs, wg[:, :, :, cs].reshape(D, 256), preferred_element_type=F32)
            tt = g * sg[0:1, cs]
            up[p, :, cs] = u
            gate[p, :, cs] = g
            hid[p, :, cs] = (u * su[0:1, cs] * (tt * jax.nn.sigmoid(tt))).astype(BF)
            return carry

        lax.fori_loop(0, 5, body, 0)

    def forward_down(p):
        def body(t, carry):
            cs = pl.ds(pl.multiple_of(t * 256, 256), 256)
            v = jnp.dot(hid[p], wd[:, cs], preferred_element_type=F32)
            part[0, p, :, :, cs] = v.astype(BF).reshape(2, ROWS, 256)
            return carry

        lax.fori_loop(0, 5, body, 0)
        z_scatter_pair(part.at[0], buf.at[1], ps.at[1], pr.at[1], p, x, c, z, y)

    forward_cols(near)
    forward_down(near)
    forward_cols(1 - near)
    forward_down(1 - near)

    def turn(dst, load):
        def body(t, carry):
            cs = pl.ds(pl.multiple_of(t * 256, 256), 256)
            for p in range(2):
                dst[cs, p * 256 : (p + 1) * 256] = load(p, cs).T
            return carry

        lax.fori_loop(0, 5, body, 0)

    turn(xt, lambda p, cs: xg[p, :, :, cs].reshape(256, 256))
    turn(ht, lambda p, cs: hid[p, :, cs])

    z_scatter_take(buf.at[1], pr.at[1])
    total = total_of(buf.at[1])
    position = (c * 16 + z * 4 + y) * ROWS + lax.broadcasted_iota(jnp.int32, (ROWS, 1), 0)
    live = (position < length[0]).astype(F32)
    base = first[...]
    d_base, d_part, g_am = mix_back(cot[...].astype(F32) * live, base, total, rate_m[0:1])
    low[1] = d_part.astype(BF)
    z_gather_start(low.at[1], dd, gs.at[1], gr.at[1], x, c, z, y)
    dfirst[...] = d_base
    vec[1:2] = g_am
    result[...] = (mix_of(base, total, rate_m[0:1])[0] * live).astype(BF)

    def backward_cols(p):
        z_gather_take(dd, gr.at[1], p)

        def body(t, carry):
            cs = pl.ds(pl.multiple_of(t * 256, 256), 256)
            dh = nt(rows_of(dd, p), wd[cs, :])
            u, g = up[p, :, cs], gate[p, :, cs]
            sc, sgc = su[0:1, cs], sg[0:1, cs]
            tt = g * sgc
            sig = jax.nn.sigmoid(tt)
            silu = tt * sig
            dsilu = sig * (1.0 + tt * (1.0 - sig))
            dhs = dh * sc
            dhu = dh * u
            both = dhu * dsilu * sc
            dug[0, p, :, cs] = (dhs * silu).astype(BF)
            dug[1, p, :, cs] = (both * sgc).astype(BF)
            vec[2:3, cs] += jnp.sum(dhu * silu, axis=0, keepdims=True)
            vec[3:4, cs] += jnp.sum(both * g, axis=0, keepdims=True)
            return carry

        lax.fori_loop(0, 5, body, 0)
        for t in range(2):
            v = nt(dug[0, p], wu[t * 640 : (t + 1) * 640, :]) + nt(
                dug[1, p], wg[2 * t : 2 * t + 2].reshape(640, D)
            )
            part[1, p, :, :, t * 640 : (t + 1) * 640] = v.astype(BF).reshape(2, ROWS, 640)
        z_scatter_pair(part.at[1], buf.at[2], ps.at[2], pr.at[2], p, x, c, z, y)

    backward_cols(near)
    backward_cols(1 - near)

    def gradients(w):
        cols = pl.ds(pl.multiple_of(w * 640, 128), 640)

        def body(k, carry):
            rows = pl.ds(pl.multiple_of(k * 320, 64), 320)
            for t in range(2):
                cs = slice(t * 640, (t + 1) * 640)
                v = jnp.dot(xt[rows, :], dug[w, :, :, cs].reshape(512, 640), preferred_element_type=F32)
                ga[w, k, :, :, cs] = v.astype(BF).reshape(4, 80, 640)
            v = jnp.dot(ht[rows, :], dd[:, :, :, cols].reshape(512, 640), preferred_element_type=F32)
            gd[w, k] = v.astype(BF).reshape(4, 80, 640)
            return carry

        lax.fori_loop(0, 4, body, 0)

    gradients(1 - c)
    rcopy(ga.at[1 - c], ra, sx.at[0], rx.at[0], sib).start()
    rcopy(gd.at[1 - c], rd, sx.at[1], rx.at[1], sib).start()

    z_scatter_take(buf.at[2], pr.at[2])
    dy = dfirst[...] + total_of(buf.at[2])
    d_res, d_part, g_aa = mix_back(dy, st[...].astype(F32), mixed[...], rate_a[0:1])
    low[2] = d_part.astype(BF)
    z_gather_start(low.at[2], dm, gs.at[2], gr.at[2], x, c, z, y)
    d_st[...] = d_res
    vec[0:1] = g_aa
    gradients(c)
    landed(ra, rx.at[0])
    landed(rd, rx.at[1])

    def add(k, carry):
        i, j = k // 4, k % 4
        ha[i, j] = (ga[c, i, j].astype(F32) + ra[i, j].astype(F32)).astype(BF)
        hd[i, j] = (gd[c, i, j].astype(F32) + rd[i, j].astype(F32)).astype(BF)
        return carry

    lax.fori_loop(0, 16, add, 0)
    for p in range(2):
        z_gather_take(dm, gr.at[2], p)
    for k in range(3):
        z_gather_sent(low.at[k], gs.at[k], c, z)
    z_scatter_sent(part0, ps.at[0], c, z)
    z_scatter_sent(part.at[0], ps.at[1], c, z)
    z_scatter_sent(part.at[1], ps.at[2], c, z)
    for k in range(4):
        landed(gy, s3.at[k])
    for d in (1, 2, 3):
        landed(gy, s2.at[d])
    landed(ra, sx.at[0])
    landed(rd, sx.at[1])


def middle(length, part0, st, cot, rate_a, rate_m, su, sg, wu, wd, gy):
    V = pltpu.VMEM
    return remote_call(
        mid_kernel,
        [
            ((ROWS, D), BF, "v"),
            ((ROWS, D), F32, "v"),
            ((2, 2, ROWS, D), BF, "a"),
            ((4, 4, 80, D), BF, "v"),
            ((4, 4, 80, 640), BF, "v"),
            ((8, D), F32, "v"),
        ],
        "savvvvvvaaa",
        [
            V((3, 4, ROWS, D), BF), V((3, ROWS, D), BF), V((2, 2, ROWS, D), BF), V((2, 2, ROWS, D), BF),
            V((D, D), BF), V((4, 4, 80, D), BF), V((D, D), BF),
            V((2, 256, D), F32), V((2, 256, D), F32), V((2, 256, D), BF), V((2, 2, 256, D), BF),
            V((2, 2, 2, ROWS, D), BF), V((D, 512), BF), V((D, 512), BF),
            V((ROWS, D), F32), V((ROWS, D), F32), V((ROWS, D), F32),
            V((2, 4, 4, 80, D), BF), V((2, 4, 4, 80, 640), BF), V((4, 4, 80, D), BF), V((4, 4, 80, 640), BF),
            dma(3, 2, 2), dma(3, 4), dma(3, 4), dma(3, 2, 2),
            dma(4), dma(4), dma(4), dma(4), dma(2), dma(2), dma(3),
        ],
        2,
        "middle",
    )(length, part0, st, cot, rate_a, rate_m, su, sg, wu, wd, gy)


def qkv_back_kernel(dq, dkv, t, scale, inner, outer, xg, w, part, gw, gs, d0, d1, sums):
    _, c, _, y = here()
    sums[...] = jnp.zeros_like(sums)
    gs[...] = jnp.zeros_like(gs)
    lane = lanes()

    def per_block(j, carry):
        rows = pl.ds(pl.multiple_of(j * ROWS, ROWS), ROWS)
        cosine, sine = turn_of(inner, outer, block_index(c, y, j))
        pair = None
        for h in range(HG):
            cols = slice(h * 128, (h + 1) * 128)
            tt = t[h, rows, :]
            grads = dkv[h, rows, :].astype(F32)
            turned = pltpu.roll(grads, 64, 1)
            dy = jnp.where(lane < 64, dq[h, rows, :].astype(BF).astype(F32), turned)
            inv = lax.rsqrt(half_means(tt * tt, lane) + EPS)
            unit = tt * inv
            sums[:, cols] += jnp.sum((dy * unit).reshape(ROWS // 8, 8, 128), axis=0)
            dyh = dy * scale[0:1, cols]
            dt = (dyh - unit * half_means(dyh * unit, lane)) * inv
            draw = (dt * cosine + swap(dt * sine, lane)).astype(BF)
            if h < 4:
                d0[rows, cols] = draw
            else:
                d1[rows, 0:128] = draw
            if h % 2 == 0:
                pair = turned
            if h % 2 == 1 or h == 4:
                at = 128 + (h // 2) * 128
                d1[rows, at : at + 128] = jnp.where(lane < 64, pair, grads if h % 2 else 0.0).astype(BF)
        return carry

    lax.fori_loop(0, BLOCKS, per_block, 0)
    for h in range(HG):
        v = jnp.sum(sums[:, h * 128 : (h + 1) * 128], axis=0, keepdims=True)
        gs[0:1, h * HDIM : (h + 1) * HDIM] = v[:, :HDIM] + v[:, HDIM:]
    part[...] = (nt(d0[...], w[0]) + nt(d1[...], w[1])).astype(BF)
    gw[0] = tn(xg[...], d0[...]).astype(BF)
    gw[1] = tn(xg[...], d1[...]).astype(BF)


def qkv_back(dq, dkv, t, scale, inner, outer, xg, w):
    n = BLOCKS * ROWS
    return local_call(
        qkv_back_kernel,
        [((n, D), BF), ((2, D, 512), BF), ((8, D), F32)],
        8,
        [pltpu.VMEM((n, 512), BF), pltpu.VMEM((n, 512), BF), pltpu.VMEM((8, HG * 128), F32)],
        "qkv_back",
    )(dq, dkv, t, scale, inner, outer, xg, w)


def close_kernel(
    part, za_in, zd_in, gq, go, vec,
    pbuf, za, zd, zq, o_out, o_vec,
    hq, rq, fq, ob, oy, ox, o2, vs, vb,
    ps, pr, sc, rc, lo, s1, r1, s2, r2, s3, r3, sz, rz, sf, rf, so, ro, sv, rv,
):
    x, c, z, y = here()
    sib = dev(x, 1 - c, z, y)
    to_y = [None] + [dev(x, c, z, step(y, d)) for d in (1, 2, 3)]
    to_x = [None] + [dev(step(x, d), c, z, y) for d in (1, 2, 3)]
    to_z = [None] + [dev(x, c, step(z, d), y) for d in (1, 2, 3)]
    greet(z_peers(x, c, z, y) + to_y[1:] + to_x[1:])
    rcopy(gq.at[1 - c], hq.at[1], sc.at[0], rc.at[0], sib).start()
    rcopy(vec, vb.at[0], sv.at[0, 0], rv.at[0, 0], sib).start()
    rcopy(go, ob, sc.at[1], rc.at[1], sib).start()
    z_scatter_start(part, pbuf, ps, pr, x, c, z, y)
    lcopy(gq.at[c], hq.at[0], lo.at[0]).start()
    lcopy(go, oy, lo.at[1]).start()
    for d in (1, 3, 2):
        rcopy(za_in.at[step(z, d)], za.at[c, z], sz.at[1, d], rz.at[1, z], to_z[d]).start()
    lcopy(za_in.at[z], za.at[c, z], lo.at[2]).start()
    lcopy(zd_in, zd.at[c], lo.at[3]).start()
    rcopy(zd_in, zd.at[c], sf.at[2], rf.at[2], sib).start()

    landed(hq.at[0], lo.at[0])
    landed(hq.at[1], rc.at[0])

    def add(k, carry):
        i, j = k // 4, k % 4
        hq[0, i, j] = (hq[0, i, j].astype(F32) + hq[1, i, j].astype(F32)).astype(BF)
        return carry

    lax.fori_loop(0, 16, add, 0)
    for d in (1, 3, 2):
        rcopy(hq.at[0, step(x, d)], rq.at[x], s1.at[0, d], r1.at[0, x], to_x[d]).start()
    landed(oy, lo.at[1])
    landed(ob, rc.at[1])
    landed(vb.at[0], rv.at[0, 0])
    vs[...] = vec[...] + vb[0]
    for k in range(4):
        oy[k] = (oy[k].astype(F32) + ob[k].astype(F32)).astype(BF)
    for d in (1, 3, 2):
        rcopy(oy.at[step(y, d)], ox.at[y], s1.at[1, d], r1.at[1, y], to_y[d]).start()
        rcopy(vs, vb.at[d], sv.at[1, d], rv.at[1, d], to_y[d]).start()
    acc = oy[y].astype(F32)
    tot = vs[...]
    for d in (1, 2, 3):
        landed(ox.at[step(y, d)], r1.at[1, step(y, d)])
        landed(vb.at[d], rv.at[1, d])
        landed(vs, sv.at[1, d])
        acc = acc + ox[step(y, d)].astype(F32)
        tot = tot + vb[d]
    ox[y] = acc.astype(BF)
    vs[...] = tot
    for d in (1, 3, 2):
        rcopy(ox.at[y], o2.at[d], so.at[d], ro.at[d], to_x[d]).start()
        rcopy(vs, vb.at[3 + d], sv.at[2, d], rv.at[2, d], to_x[d]).start()
    for d in (1, 2, 3):
        landed(rq.at[step(x, d)], r1.at[0, step(x, d)])
    for k in range(4):
        v = hq[0, x, k].astype(F32)
        for d in (1, 2, 3):
            v = v + rq[step(x, d), k].astype(F32)
        fq[0, k] = v.astype(BF)
    for d in (1, 3, 2):
        rcopy(fq.at[0, step(y, d)], fq.at[1, y], s2.at[d], r2.at[y], to_y[d]).start()
    acc = ox[y].astype(F32)
    tot = vs[...]
    for d in (1, 2, 3):
        landed(o2.at[d], ro.at[d])
        landed(vb.at[3 + d], rv.at[2, d])
        landed(vs, sv.at[2, d])
        acc = acc + o2[d].astype(F32)
        tot = tot + vb[3 + d]
    o_out[...] = acc
    vs[...] = tot
    for d in (1, 3, 2):
        rcopy(vs, vb.at[6 + d], sv.at[3, d], rv.at[3, d], to_z[d]).start()
    landed(za.at[c, z], lo.at[2])
    for d in (1, 2, 3):
        landed(za.at[c, step(z, d)], rz.at[1, step(z, d)])
    rcopy(za.at[c], za.at[c], sf.at[1], rf.at[1], sib).start()
    for d in (1, 2, 3):
        landed(fq.at[1, step(y, d)], r2.at[step(y, d)])
    v = fq[0, y].astype(F32)
    for d in (1, 2, 3):
        v = v + fq[1, step(y, d)].astype(F32)
    zq[0, x] = v.astype(BF)
    for d in (1, 3, 2):
        rcopy(zq.at[0, x], zq.at[0, x], s3.at[d], r3.at[x], to_x[d]).start()
    z_scatter_take(pbuf, pr)
    for d in (1, 2, 3):
        landed(zq.at[0, step(x, d)], r3.at[step(x, d)])
    for d in (1, 3, 2):
        rcopy(zq.at[0, step(z, d)], zq.at[1 + c, z], sz.at[0, d], rz.at[0, z], to_z[d]).start()
    zq[1 + c, z] = zq[0, z]
    landed(zd.at[c], lo.at[3])
    landed(zd.at[1 - c], rf.at[2])
    landed(za.at[1 - c], rf.at[1])
    for d in (1, 2, 3):
        landed(zq.at[1 + c, step(z, d)], rz.at[0, step(z, d)])
    rcopy(zq.at[1 + c], zq.at[1 + c], sf.at[0], rf.at[0], sib).start()
    tot = vs[...]
    for d in (1, 2, 3):
        landed(vb.at[6 + d], rv.at[3, d])
        landed(vs, sv.at[3, d])
        tot = tot + vb[6 + d]
    o_vec[0:2] = tot[0:2]
    o_vec[2:] = vs[2:]
    landed(zq.at[2 - c], rf.at[0])
    z_scatter_sent(part, ps, c, z)
    landed(hq.at[1], sc.at[0])
    landed(go, sc.at[1])
    landed(vec, sv.at[0, 0])
    landed(zq.at[1], sf.at[0])
    landed(za.at[0], sf.at[1])
    landed(zd.at[0], sf.at[2])
    for d in (1, 2, 3):
        landed(rq.at[0], s1.at[0, d])
        landed(ox.at[0], s1.at[1, d])
        landed(fq.at[0, 0], s2.at[d])
        landed(zq.at[0, 0], s3.at[d])
        landed(zq.at[0, 0], sz.at[0, d])
        landed(za.at[0, 0], sz.at[1, d])
        landed(ox.at[0], so.at[d])


def close(part, za, zd, gq, go, vec):
    V = pltpu.VMEM
    return remote_call(
        close_kernel,
        [
            ((4, ROWS, D), BF, "v"),
            ((2, 4, 80, D), BF, "v"),
            ((2, 4, 80, 640), BF, "v"),
            ((3, 4, 80, 512), BF, "v"),
            ((80, D), F32, "v"),
            ((8, D), F32, "v"),
        ],
        "aaaaav",
        [
            V((2, 4, 4, 80, 512), BF), V((4, 4, 80, 512), BF), V((2, 4, 80, 512), BF),
            V((4, 80, D), BF), V((4, 80, D), BF), V((4, 80, D), BF), V((4, 80, D), BF), V((8, D), F32), V((10, 8, D), F32),
            dma(2, 2), dma(4), dma(2), dma(2), dma(4),
            dma(2, 4), dma(2, 4), dma(4), dma(4), dma(4), dma(4), dma(2, 4), dma(2, 4), dma(3), dma(3),
            dma(4), dma(4), dma(4, 4), dma(4, 4),
        ],
        4,
        "close",
    )(part, za, zd, gq, go, vec)


def finish_kernel(res, d_st, pbuf, za, zd, zq, out, vec, result, g_in, o_q, o_k, o_v, o_out, o_up, o_gate, o_down, o_vec):
    _, _, z, y = here()
    result[...] = res[...]
    g_in[...] = d_st[...] + total_of(pbuf)
    o_out[...] = out[...]
    for k in range(4):
        cols = slice(k * D, (k + 1) * D)
        o_up[:, cols] = za[0, k].astype(F32)
        o_gate[:, cols] = za[1, k].astype(F32)
        for h in range(2):
            o_down[k * 80 : (k + 1) * 80, h * 640 : (h + 1) * 640] = zd[h, k].astype(F32)
        a, b = zq[1, k].astype(F32), zq[2, k].astype(F32)
        at = k * GROUP
        pairs = [a[:, h * 128 : (h + 1) * 128] for h in range(4)] + [b[:, :128]]
        o_q[:, at : at + GROUP] = jnp.concatenate([v[:, :HDIM] for v in pairs], axis=1)
        o_k[:, at : at + GROUP] = jnp.concatenate([v[:, HDIM:] for v in pairs], axis=1)
        o_v[:, at : at + GROUP] = b[:, 128:448]
    v = vec[...]
    o_vec[0:2] = pltpu.roll(v, (16 - (z * 4 + y)) % 16 * 80, 1)[0:2]
    o_vec[2:4] = pltpu.roll(v, (4 - y) % 4 * 320, 1)[2:4]
    o_vec[4:] = pltpu.roll(v, (16 - y) % 16 * 80, 1)[4:]


def finish(res, d_st, pbuf, za, zd, zq, out, vec):
    return local_call(
        finish_kernel,
        [
            ((ROWS, D), BF),
            ((ROWS, D), F32),
            ((80, D), F32),
            ((80, D), F32),
            ((80, D), F32),
            ((80, D), F32),
            ((80, FF), F32),
            ((80, FF), F32),
            ((320, D), F32),
            ((8, D), F32),
        ],
        8,
        [],
        "finish",
    )(res, d_st, pbuf, za, zd, zq, out, vec)


def shards(
    states, w_query, w_key, w_value, w_out, w_up, w_gate, w_down,
    scale_qk, alpha_attn, alpha_mlp, scale_up, scale_gate, lengths, cotangent,
):
    x, c, z, y = here()
    st = states[0]

    def heads(w):
        return w.reshape(80, 4, HG, HDIM)

    q4, k4, v4 = heads(w_query), heads(w_key), heads(w_value)
    qk = jnp.stack([q4, k4], axis=3).reshape(80, 4, HG * 128)
    half1 = jnp.concatenate([qk[:, :, 512:], v4.reshape(80, 4, GROUP), jnp.zeros((80, 4, HDIM), BF)], axis=2)
    wq = jnp.stack([qk[:, :, :512], half1]).transpose(0, 2, 1, 3)
    vec = jnp.concatenate([scale_qk, alpha_attn, alpha_mlp, scale_up, scale_gate, jnp.zeros((16,), BF)])
    vec = jnp.broadcast_to(vec.astype(F32)[None], (8, 896))
    inner, outer = (jnp.asarray(t) for t in rope_tables())
    n = BLOCKS * ROWS
    part, att, lse, kv, q, turned, xg, wqkv, wo, scale, rate_a, rate_m, su, sg, wu, wd, gy = front(
        lengths, st, wq, vec, w_out, w_up, w_gate, w_down, inner, outer
    )
    result, d_st, dm, ha, hd, vec = middle(
        lengths, part, st, cotangent[0], rate_a, rate_m, su, sg, wu.reshape(D, D), wd.reshape(D, D), gy
    )
    dq, dkv, go, za, zd = attend_back(
        lengths, q, kv, wo.reshape(GROUP, D), dm.reshape(n, D), att, lse, ha, hd
    )
    part, gq, g_sq = qkv_back(
        dq, dkv.reshape(HG, n, 128), turned, scale, inner, outer, xg.reshape(n, D), wqkv.reshape(2, D, 512)
    )
    vec = jnp.concatenate([vec[:4], g_sq[0:1], vec[5:]])
    pbuf, za, zd, zq, out, vec = close(
        part.reshape(2, 2, ROWS, D), za, zd, gq.reshape(2, 4, 4, 80, 512), go.reshape(4, 80, D), vec
    )
    result, g_in, o_q, o_k, o_v, o_out, o_up, o_gate, o_down, o_vec = finish(
        result, d_st, pbuf, za, zd, zq, out, vec
    )
    return (
        result[None],
        g_in[None],
        o_q,
        o_k,
        o_v,
        o_out,
        o_up,
        o_gate,
        o_down,
        o_vec[4, :80],
        o_vec[0, :80],
        o_vec[1, :80],
        o_vec[2, :320],
        o_vec[3, :320],
    )


def solution(mesh):
    row = P("grp", ("seq", "shard"), None)
    mat = P("shard", None)
    one = P("shard")
    return jax.shard_map(
        shards,
        mesh=mesh,
        in_specs=(row,) + (mat,) * 7 + (one,) * 5 + (P("grp"), row),
        out_specs=(row, row) + (mat,) * 7 + (one,) * 5,
        check_vma=False,
    )
```

```python
import functools
import math

import jax
import jax.numpy as jnp
import numpy as np
from jax import lax
from jax.experimental import pallas as pl
from jax.experimental.pallas import tpu as pltpu
from jax.sharding import PartitionSpec as P


D, HEADS, HDIM, FF = 1280, 20, 64, 5120
ROWS, BLOCKS, HG = 128, 4, 5
GROUP = HG * HDIM
EPS = 1e-6
BF, F32 = jnp.bfloat16, jnp.float32
MESH = pl.DeviceIdType.MESH
VMEM_LIMIT = 60 << 20


def here():
    s = lax.axis_index("shard")
    return lax.axis_index("grp"), lax.axis_index("seq"), s // 4, s % 4


def dev(x, c, z, y):
    return (x, c, z * 4 + y)


def worker(z):
    return ((z + 1) // 2) % 2


def owner_z(w, i):
    return i * (3 - 2 * w) + w


def step(v, d):
    return (v + d) % 4


def rcopy(src, dst, ss, rs, to):
    return pltpu.make_async_remote_copy(
        src_ref=src, dst_ref=dst, send_sem=ss, recv_sem=rs, device_id=to, device_id_type=MESH
    )


def lcopy(src, dst, sem):
    return pltpu.make_async_copy(src, dst, sem)


def landed(dst, sem):
    pltpu.make_async_copy(dst, dst, sem).wait()


def greet(peers):
    bar = pltpu.get_barrier_semaphore()
    for p in peers:
        pl.semaphore_signal(bar, inc=1, device_id=p, device_id_type=MESH)
    pl.semaphore_wait(bar, len(peers))


def z_peers(x, c, z, y):
    far = [dev(x, cc, step(z, d), y) for d in (1, 2, 3) for cc in (0, 1)]
    return [dev(x, 1 - c, z, y)] + far


def z_gather_start(src, dst, ss, rs, x, c, z, y):
    w = worker(z)
    slot = (z // 2, c)
    for d in (1, 3, 2):
        rcopy(src, dst.at[slot], ss.at[d], rs.at[slot], dev(x, w, step(z, d), y)).start()

    @pl.when(c == w)
    def _():
        lcopy(src, dst.at[slot], rs.at[slot]).start()

    @pl.when(c != w)
    def _():
        rcopy(src, dst.at[slot], ss.at[0], rs.at[slot], dev(x, w, z, y)).start()


def z_gather_take(dst, rs, p):
    for k in range(2):
        landed(dst.at[p, k], rs.at[p, k])


def z_gather_sent(src, ss, c, z):
    for d in (1, 2, 3):
        landed(src, ss.at[d])

    @pl.when(c != worker(z))
    def _():
        landed(src, ss.at[0])


def z_gather_wait(src, dst, ss, rs, c, z):
    for p in range(2):
        z_gather_take(dst, rs, p)
    z_gather_sent(src, ss, c, z)


def z_scatter_pair(part, dst, ss, rs, p, x, c, z, y):
    oz = owner_z(c, p)
    for oc in range(2):
        mine = jnp.logical_and(c == oc, z == oz)

        @pl.when(mine)
        def _(oc=oc):
            lcopy(part.at[p, oc], dst.at[z], rs.at[z]).start()

        @pl.when(jnp.logical_not(mine))
        def _(oc=oc):
            rcopy(part.at[p, oc], dst.at[z], ss.at[p, oc], rs.at[z], dev(x, oc, oz, y)).start()


def z_scatter_start(part, dst, ss, rs, x, c, z, y):
    for p in range(2):
        z_scatter_pair(part, dst, ss, rs, p, x, c, z, y)


def z_scatter_take(dst, rs):
    for k in range(4):
        landed(dst.at[k], rs.at[k])


def z_scatter_sent(part, ss, c, z):
    for p in range(2):
        for oc in range(2):
            mine = jnp.logical_and(c == oc, z == owner_z(c, p))

            @pl.when(jnp.logical_not(mine))
            def _(p=p, oc=oc):
                landed(part.at[p, oc], ss.at[p, oc])


def remote_call(kernel, outs, ins_spaces, scratch, cid, name):
    spec = {
        "a": pl.BlockSpec(memory_space=pl.ANY),
        "v": pl.BlockSpec(memory_space=pltpu.VMEM),
        "s": pl.BlockSpec(memory_space=pltpu.SMEM),
    }
    return pl.pallas_call(
        kernel,
        out_shape=[jax.ShapeDtypeStruct(s, d) for s, d, _ in outs],
        in_specs=[spec[s] for s in ins_spaces],
        out_specs=[spec[s] for _, _, s in outs],
        scratch_shapes=scratch,
        compiler_params=pltpu.CompilerParams(
            collective_id=cid, has_side_effects=True, vmem_limit_bytes=VMEM_LIMIT
        ),
        name=name,
    )


def local_call(kernel, outs, n_in, scratch, name, smem=0):
    vmem = pl.BlockSpec(memory_space=pltpu.VMEM)
    sm = pl.BlockSpec(memory_space=pltpu.SMEM)
    return pl.pallas_call(
        kernel,
        out_shape=[jax.ShapeDtypeStruct(s, d) for s, d in outs],
        in_specs=[sm] * smem + [vmem] * n_in,
        out_specs=[vmem for _ in outs],
        scratch_shapes=scratch,
        compiler_params=pltpu.CompilerParams(vmem_limit_bytes=VMEM_LIMIT),
        name=name,
    )


def dma(*shape):
    return pltpu.SemaphoreType.DMA(shape)


def rope_tables():
    freqs = np.exp(np.arange(32) * (-2.0 * math.log(10000.0) / 64))
    freqs = np.tile(freqs, 4)
    sign = np.tile(np.concatenate([-np.ones(32), np.ones(32)]), 2)
    inner = np.arange(ROWS)[:, None] * freqs
    outer = (np.arange(32) * ROWS)[:, None] * freqs
    return (
        np.stack([np.cos(inner), np.sin(inner) * sign]).astype(np.float32),
        np.stack([np.cos(outer), np.sin(outer) * sign]).astype(np.float32),
    )


def block_index(c, y, j):
    return (j % 2) * 16 + owner_z(c, j // 2) * 4 + y


def turn_of(inner, outer, b):
    oc = outer[0, pl.ds(b, 1), :]
    os = outer[1, pl.ds(b, 1), :]
    return oc * inner[0] - os * inner[1], os * inner[0] + oc * inner[1]


def lanes():
    return lax.broadcasted_iota(jnp.int32, (ROWS, 128), 1)


def swap(v, lane):
    return jnp.where(lane % 64 < 32, pltpu.roll(v, 96, 1), pltpu.roll(v, 32, 1))


def half_means(v, lane):
    low = jnp.sum(jnp.where(lane < 64, v, 0.0), axis=-1, keepdims=True)
    high = jnp.sum(jnp.where(lane < 64, 0.0, v), axis=-1, keepdims=True)
    return jnp.where(lane < 64, low, high) * (1.0 / 64)


TILE = 512
STEP = 6


def tiles_of(c, j):
    return (j % 2) * 4 + owner_z(c, j // 2) + 1


def nt(a, b):
    return lax.dot_general(a, b, (((1,), (1,)), ((), ())), preferred_element_type=F32)


def tn(a, b):
    return lax.dot_general(a, b, (((0,), (0,)), ((), ())), preferred_element_type=F32)


def key_tile(ref, h, t):
    zz = t % 4
    return ref[h, worker(zz), zz // 2, t // 4].reshape(TILE, 128)


def work_items(c, y, length):
    n = [tiles_of(c, j) for j in range(BLOCKS)]
    starts = [n[0], n[0] + n[1], n[0] + n[1] + n[2]]
    query = lax.broadcasted_iota(jnp.int32, (1, ROWS), 1)

    def item(i):
        hits = [(i >= s).astype(jnp.int32) for s in starts]
        j = hits[0] + hits[1] + hits[2]
        t = i - hits[0] * n[0] - hits[1] * n[1] - hits[2] * n[2]
        last = query + y * ROWS + (tiles_of(c, j) - 1 - t) * TILE
        return j, t, jnp.minimum(last, length - 1 - t * TILE)

    return item


def columns(ref, k, half):
    return ref.at[:, pl.ds(pl.multiple_of(k * D + half * 640, 128), 640)]


def front_kernel(
    length, st, wq, vec, w_out, w_up, w_gate, w_down, inner, outer,
    part, att, lse, kv_o, q_o, t_o, xg_o, wqkv_o, wo_o, scale_o, rate_a, rate_m, su, sg, uq, wd, gz,
    xg, wqkv, vecs, wo, y0, y1, kv, kvb, q, tt, low, acc, tot, uz,
    xs, xr, w1s, w1r, w2s, w2r, w3s, w3r, vs, vr, os, orr, lo,
    f1s, f1r, f2s, f2r, f3s, f3r, f4s, f4r, fl, sy, ry, sf, rf, ss, rs, kl, ol,
):
    x, c, z, y = here()
    sib = dev(x, 1 - c, z, y)
    half = pl.ds(pl.multiple_of(c * 640, 128), 640)
    other = pl.ds(pl.multiple_of((1 - c) * 640, 128), 640)
    to_z = [None] + [dev(x, c, step(z, d), y) for d in (1, 2, 3)]
    to_y = [None] + [dev(x, c, z, step(y, d)) for d in (1, 2, 3)]
    to_x = [None] + [dev(step(x, d), c, z, y) for d in (1, 2, 3)]
    near_first = (1, 3, 2)
    greet(z_peers(x, c, z, y) + to_y[1:] + to_x[1:])

    for d in near_first:
        rcopy(wq.at[c, step(z, d)], wqkv.at[c, z, y], w1s.at[d], w1r.at[z], to_z[d]).start()
        rcopy(vec, vecs.at[z, y], vs.at[0, d], vr.at[0, z], to_z[d]).start()
    lcopy(wq.at[c, z], wqkv.at[c, z, y], lo.at[0]).start()
    lcopy(vec, vecs.at[z, y], lo.at[1]).start()
    for d in near_first:
        rcopy(w_out.at[:, half], wo.at[y, :, half], os.at[0, d], orr.at[0, y], to_y[d]).start()
    rcopy(w_out.at[:, half], wo.at[y, :, half], os.at[0, 0], orr.at[1, y], sib).start()
    lcopy(w_out.at[:, half], wo.at[y, :, half], lo.at[2]).start()

    for d in (1, 2, 3):
        landed(wqkv.at[c, step(z, d), y], w1r.at[step(z, d)])
        landed(vecs.at[step(z, d), y], vr.at[0, step(z, d)])
    landed(wqkv.at[c, z, y], lo.at[0])
    landed(vecs.at[z, y], lo.at[1])
    mine = wqkv.at[c, :, y]
    rcopy(mine, mine, w2s.at[0], w2r.at[0], to_y[1]).start()
    rcopy(mine, mine, w2s.at[1], w2r.at[1], to_y[3]).start()
    rcopy(mine, mine, w3s.at[0], w3r.at[0], sib).start()
    for d in near_first:
        rcopy(vecs.at[:, y], vecs.at[:, y], vs.at[1, d], vr.at[1, y], to_y[d]).start()
    z_gather_start(st, xg, xs, xr, x, c, z, y)
    for k, src, to in ((0, step(y, 3), to_y[1]), (1, step(y, 1), to_y[3])):
        block, piece = wqkv.at[c, :, src], wqkv.at[c, 2 * k : 2 * k + 2, src]
        landed(block, w2r.at[k])
        rcopy(piece, piece, w2s.at[2 + k], w2r.at[2 + k], to).start()
        rcopy(block, block, w3s.at[1 + k], w3r.at[1 + k], sib).start()
    for k in range(2):
        piece = wqkv.at[c, 2 * k : 2 * k + 2, step(y, 2)]
        landed(piece, w2r.at[2 + k])
        rcopy(piece, piece, w3s.at[3 + k], w3r.at[3 + k], sib).start()
    down = w_down.at[pl.ds(pl.multiple_of(x * 80, 16), 80), half]
    for d in near_first:
        rcopy(down, wd.at[y, x, :, half], f2s.at[1, d], f2r.at[1, y], to_y[d]).start()
    lcopy(down, wd.at[y, x, :, half], fl.at[2]).start()
    for d in (1, 2, 3):
        landed(vecs.at[:, step(y, d)], vr.at[1, step(y, d)])
    for zz in range(4):
        for yy in range(4):
            at = (zz * 4 + yy) * 80
            rate_a[:, at : at + 80] = vecs[zz, yy, :, 80:160]
            rate_m[:, at : at + 80] = vecs[zz, yy, :, 160:240]
    for yy in range(4):
        su[:, yy * 320 : (yy + 1) * 320] = vecs[z, yy, :, 240:560]
        sg[:, yy * 320 : (yy + 1) * 320] = vecs[z, yy, :, 560:880]
    scale = jnp.concatenate([vecs[z, yy, :, :80] for yy in range(4)], axis=1)
    for h in range(HG):
        sh = scale[:, h * HDIM : (h + 1) * HDIM]
        scale_o[:, h * 128 : (h + 1) * 128] = jnp.concatenate([sh, sh], axis=1)

    for p in range(2):
        z_gather_take(xg, xr, p)
    for d in near_first:
        rcopy(columns(w_gate, step(z, d), c), gz.at[z], f1s.at[1, d], f1r.at[1 + z], to_z[d]).start()
    lcopy(columns(w_gate, z, c), gz.at[z], fl.at[0]).start()

    @pl.when(z == x)
    def _():
        for d in near_first:
            rcopy(columns(w_up, step(z, d), c), uz, f1s.at[0, d], f1r.at[0], to_z[d]).start()
        lcopy(columns(w_up, z, c), uz, f1r.at[0]).start()

    for k, src in ((0, y), (1, step(y, 3)), (2, step(y, 1))):
        landed(wqkv.at[1 - c, :, src], w3r.at[k])
    for k in range(2):
        landed(wqkv.at[1 - c, 2 * k : 2 * k + 2, step(y, 2)], w3r.at[3 + k])
    lcopy(xg, xg_o, ol.at[0]).start()
    lcopy(wqkv, wqkv_o, ol.at[1]).start()

    def project(p, carry):
        rows = xg[p].reshape(2 * ROWS, D)
        y0[p] = jnp.dot(rows, wqkv[0].reshape(D, 512), preferred_element_type=F32)
        y1[p] = jnp.dot(rows, wqkv[1].reshape(D, 512), preferred_element_type=F32)
        return carry

    lax.fori_loop(0, 2, project, 0)
    lane = lanes()

    def send(h):
        rcopy(kv.at[h], kvb.at[h, c, :, :, y], sy.at[h, 0], ry.at[h, 0], to_y[1]).start()
        rcopy(kv.at[h], kvb.at[h, c, :, :, y], sy.at[h, 1], ry.at[h, 1], to_y[3]).start()
        rcopy(kv.at[h], kvb.at[h, c, :, :, y], ss.at[h, 0], rs.at[h, 0], sib).start()
        lcopy(kv.at[h], kvb.at[h, c, :, :, y], kl.at[h]).start()

    for h in range(HG):

        def per_block(j, carry, h=h):
            p, r = j // 2, pl.ds(pl.multiple_of((j % 2) * ROWS, ROWS), ROWS)
            cosine, sine = turn_of(inner, outer, block_index(c, y, j))
            raw = y0[p, r, h * 128 : (h + 1) * 128] if h < 4 else y1[p, r, 0:128]
            t = raw * cosine + swap(raw, lane) * sine
            unit = t * lax.rsqrt(half_means(t * t, lane) + EPS)
            both = unit * scale_o[0:1, h * 128 : (h + 1) * 128]
            pair = y1[p, r, 128 + (h // 2) * 128 : 256 + (h // 2) * 128]
            v = pair if h % 2 else pltpu.roll(pair, 64, 1)
            kv[h, p, j % 2] = jnp.where(lane < 64, pltpu.roll(both, 64, 1), v).astype(BF)
            rows = pl.ds(pl.multiple_of(j * ROWS, ROWS), ROWS)
            tt[h, rows, :] = t
            q[h, rows, :] = (jnp.where(lane < 64, both, 0.0).astype(BF).astype(F32) * 0.125).astype(BF)
            return carry

        lax.fori_loop(0, BLOCKS, per_block, 0)
        send(h)
    landed(wd.at[y, x, :, half], fl.at[2])
    for d in (1, 2, 3):
        landed(wd.at[step(y, d), x, :, half], f2r.at[1, step(y, d)])
    for d in near_first:
        rcopy(wd.at[:, x, :, half], wd.at[:, x, :, half], f3s.at[d], f3r.at[x], to_x[d]).start()
    rcopy(wd.at[:, x, :, half], wd.at[:, x, :, half], f4s.at[0], f4r.at[x], sib).start()
    lcopy(q, q_o, ol.at[2]).start()
    lcopy(tt, t_o, ol.at[3]).start()

    def near(h):
        for k, src, to in ((0, step(y, 3), to_y[1]), (1, step(y, 1), to_y[3])):
            landed(kvb.at[h, c, :, :, src], ry.at[h, k])
            rcopy(kvb.at[h, c, k, :, src], kvb.at[h, c, k, :, src], sf.at[h, k], rf.at[h, k], to).start()
            rcopy(kvb.at[h, c, :, :, src], kvb.at[h, c, :, :, src], ss.at[h, 1 + k], rs.at[h, 1 + k], sib).start()

    def far(h):
        src = step(y, 2)
        for k in range(2):
            landed(kvb.at[h, c, k, :, src], rf.at[h, k])
            rcopy(kvb.at[h, c, k, :, src], kvb.at[h, c, k, :, src], ss.at[h, 3 + k], rs.at[h, 3 + k], sib).start()

    def ready(h):
        landed(kvb.at[h, c, :, :, y], kl.at[h])
        landed(kvb.at[h, 1 - c, :, :, y], rs.at[h, 0])
        landed(kvb.at[h, 1 - c, :, :, step(y, 3)], rs.at[h, 1])
        landed(kvb.at[h, 1 - c, :, :, step(y, 1)], rs.at[h, 2])
        for k in range(2):
            landed(kvb.at[h, 1 - c, k, :, step(y, 2)], rs.at[h, 3 + k])
        lcopy(kvb.at[h], kv_o.at[h], kl.at[h]).start()

    item = work_items(c, y, length[0])

    def compute(h):
        acc[...] = jnp.zeros_like(acc)
        tot[...] = jnp.zeros_like(tot)

        def body(g, carry):
            key = lax.broadcasted_iota(jnp.int32, (TILE, ROWS), 0)
            its = [item(g * STEP + u) for u in range(STEP)]
            ks = [key_tile(kvb, h, t) for _, t, _ in its]
            ss_ = [
                nt(k, q[h, pl.ds(pl.multiple_of(j * ROWS, ROWS), ROWS), :]) for k, (j, _, _) in zip(ks, its)
            ]
            ps = [jnp.where(key <= bound, jnp.exp(s), 0.0) for s, (_, _, bound) in zip(ss_, its)]
            for k, p, (j, _, _) in zip(ks, ps, its):
                tot[j] += jnp.sum(p.reshape(TILE // 8, 8, ROWS), axis=0)
                acc[j] += tn(k, p.astype(BF))
            return carry

        lax.fori_loop(0, 18 // STEP, body, 0)
        for j in range(BLOCKS):
            total = jnp.sum(tot[j], axis=0, keepdims=True)
            lse[h, j : j + 1, :] = jnp.log(total)
            att[h, j * ROWS : (j + 1) * ROWS, :] = (acc[j, HDIM:] / total).T

    def spread_up():
        landed(uz, f1r.at[0])
        for d in near_first:
            rcopy(uz, uq.at[y], f2s.at[0, d], f2r.at[0, y], to_y[d]).start()
        lcopy(uz, uq.at[y], fl.at[1]).start()

    near(0)

    def per_head(i, carry):
        @pl.when(i + 1 < HG)
        def _():
            near(i + 1)

        @pl.when(i == HG)
        def _():
            spread_up()

        @pl.when(i > 0)
        def _():
            ready(i - 1)
            compute(i - 1)

        @pl.when(i < HG)
        def _():
            far(i)

        return carry

    lax.fori_loop(0, HG + 1, per_head, 0)
    for h in range(HG):
        low[:, h * HDIM : (h + 1) * HDIM] = att[h].astype(BF)
    for d in near_first:
        y2 = step(y, d)
        landed(wo.at[y2, :, half], orr.at[0, y2])
        rcopy(wo.at[y2, :, half], wo.at[y2, :, half], os.at[1, d], orr.at[1, y2], sib).start()
    landed(wo.at[y, :, half], lo.at[2])
    for k in range(4):
        landed(wo.at[k, :, other], orr.at[1, k])
    lcopy(wo, wo_o, ol.at[4]).start()
    for p in range(2):
        v = jnp.dot(low[p * 256 : (p + 1) * 256, :], wo[...].reshape(GROUP, D), preferred_element_type=F32)
        part[p] = v.astype(BF).reshape(2, ROWS, D)

    for d in near_first:
        x2 = step(x, d)
        landed(wd.at[:, x2, :, half], f3r.at[x2])
        rcopy(wd.at[:, x2, :, half], wd.at[:, x2, :, half], f4s.at[d], f4r.at[x2], sib).start()
    landed(uz, fl.at[1])
    landed(uz, fl.at[0])
    for d in (1, 2, 3):
        landed(uq.at[step(y, d)], f2r.at[0, step(y, d)])
        landed(gz.at[step(z, d)], f1r.at[1 + step(z, d)])

    def sent(h, carry):
        for k in range(2):
            landed(kv.at[h], sy.at[h, k])
            landed(kv.at[h, 0], sf.at[h, k])
            landed(kv.at[h, 0], ss.at[h, 3 + k])
        for k in range(3):
            landed(kv.at[h], ss.at[h, k])
        landed(kvb.at[h], kl.at[h])
        return carry

    lax.fori_loop(0, HG, sent, 0)
    z_gather_sent(st, xs, c, z)
    for k in range(4):
        landed(wd.at[:, k, :, other], f4r.at[k])
        landed(wd.at[:, k, :, half], f4s.at[k])
    landed(wo.at[0, :, half], os.at[0, 0])
    for k in range(2):
        landed(mine, w2s.at[k])
        landed(wqkv.at[c, 0:2, y], w2s.at[2 + k])
        landed(wqkv.at[c, 0:2, y], w3s.at[3 + k])
    for k in range(3):
        landed(mine, w3s.at[k])
    for d in (1, 2, 3):
        landed(wqkv.at[c, z, y], w1s.at[d])
        landed(vec, vs.at[0, d])
        landed(vecs.at[:, y], vs.at[1, d])
        landed(wo.at[0, :, half], os.at[0, d])
        landed(wo.at[0, :, half], os.at[1, d])
        landed(uz, f1s.at[1, d])
        landed(uz, f2s.at[0, d])
        landed(uz, f2s.at[1, d])
        landed(wd.at[:, x, :, half], f3s.at[d])

    @pl.when(z == x)
    def _():
        for d in (1, 2, 3):
            landed(uz, f1s.at[0, d])

    landed(xg, ol.at[0])
    landed(wqkv, ol.at[1])
    landed(q, ol.at[2])
    landed(tt, ol.at[3])
    landed(wo, ol.at[4])


def front(length, st, wq, vec, w_out, w_up, w_gate, w_down, inner, outer):
    n = BLOCKS * ROWS
    V = pltpu.VMEM
    return remote_call(
        front_kernel,
        [
            ((2, 2, ROWS, D), BF, "v"),
            ((HG, n, HDIM), F32, "v"),
            ((HG, BLOCKS, 128), F32, "v"),
            ((HG, 2, 2, 2, 4, ROWS, 128), BF, "a"),
            ((HG, n, 128), BF, "a"),
            ((HG, n, 128), F32, "a"),
            ((2, 2, ROWS, D), BF, "a"),
            ((2, 4, 4, 80, 512), BF, "a"),
            ((4, 80, D), BF, "a"),
            ((8, HG * 128), F32, "v"),
            ((8, D), F32, "v"),
            ((8, D), F32, "v"),
            ((8, D), F32, "v"),
            ((8, D), F32, "v"),
            ((4, 80, 640), BF, "a"),
            ((4, 4, 80, D), BF, "a"),
            ((4, 80, 640), BF, "a"),
        ],
        "saavaaaavv",
        [
            V((2, 2, ROWS, D), BF), V((2, 4, 4, 80, 512), BF), V((4, 4, 8, 896), F32), V((4, 80, D), BF),
            V((2, 256, 512), F32), V((2, 256, 512), F32),
            V((HG, 2, 2, ROWS, 128), BF), V((HG, 2, 2, 2, 4, ROWS, 128), BF), V((HG, n, 128), BF), V((HG, n, 128), F32),
            V((n, GROUP), BF), V((BLOCKS, 128, ROWS), F32), V((BLOCKS, 8, ROWS), F32), V((80, 640), BF),
            dma(4), dma(2, 2), dma(4), dma(4), dma(4), dma(4), dma(5), dma(5), dma(2, 4), dma(2, 4), dma(2, 4), dma(2, 4), dma(3),
            dma(2, 4), dma(5), dma(2, 4), dma(2, 4), dma(4), dma(4), dma(4), dma(4), dma(3),
            dma(HG, 2), dma(HG, 2), dma(HG, 2), dma(HG, 2), dma(HG, 5), dma(HG, 5), dma(HG), dma(5),
        ],
        0,
        "front",
    )(length, st, wq, vec, w_out, w_up, w_gate, w_down, inner, outer)


def inv_rms(v):
    return lax.rsqrt(jnp.mean(v * v, axis=-1, keepdims=True) + EPS)


def back_rms(dy, yy, inv):
    return (dy - yy * jnp.mean(dy * yy, axis=-1, keepdims=True)) * inv


def total_of(buf):
    return (buf[0].astype(F32) + buf[1].astype(F32)) + (buf[2].astype(F32) + buf[3].astype(F32))


def mix_of(res, part, rate):
    inv_p = inv_rms(part)
    unit = part * inv_p
    diff = unit - res
    u = res + rate * diff
    inv_u = inv_rms(u)
    return u * inv_u, unit, inv_p, inv_u, diff


def mix_back(dy, res, part, rate):
    yy, unit, inv_p, inv_u, diff = mix_of(res, part, rate)
    du = back_rms(dy, yy, inv_u)
    return du * (1.0 - rate), back_rms(du * rate, unit, inv_p), jnp.sum(du * diff, axis=0, keepdims=True)


HALF = ROWS // 2


def mid_kernel(
    length, part0, st, cot, rate_a, rate_m, su, sg, uq, wd_in, gz,
    result, d_st, dm, ha, hd, vec,
    buf, low, xg, dd, wu, wg, wd, up, gate, hid, dug, part, xt, ht, mixed, first, dfirst, ga, gd, ra, rd, rdy,
    ps, pr, gs, gr, s2, r2, s3, r3, sx, rx, sy, ry, lo,
):
    x, c, z, y = here()
    sib = dev(x, 1 - c, z, y)
    half = pl.ds(pl.multiple_of(c * 640, 128), 640)
    other = pl.ds(pl.multiple_of((1 - c) * 640, 128), 640)
    to_x = [None] + [dev(step(x, d), c, z, y) for d in (1, 2, 3)]
    to_y = [None] + [dev(x, c, z, step(y, d)) for d in (1, 2, 3)]

    def cut(k):
        return pl.ds(k * HALF, HALF)

    def scatter(n, src, k):
        for p in range(2):
            oz = owner_z(c, p)
            for oc in range(2):
                mine = jnp.logical_and(c == oc, z == oz)
                piece, to = src.at[p, oc, cut(k)], buf.at[n, z, cut(k)]

                @pl.when(mine)
                def _(piece=piece, to=to):
                    lcopy(piece, to, pr.at[n, k, z]).start()

                @pl.when(jnp.logical_not(mine))
                def _(piece=piece, to=to, p=p, oc=oc, oz=oz):
                    rcopy(piece, to, ps.at[n, k, p, oc], pr.at[n, k, z], dev(x, oc, oz, y)).start()

    def scatter_take(n, k):
        for i in range(4):
            landed(buf.at[n, i, cut(k)], pr.at[n, k, i])
        return total_of(buf.at[n, :, cut(k)])

    def scatter_sent(n, src):
        for k in range(2):
            for p in range(2):
                for oc in range(2):
                    mine = jnp.logical_and(c == oc, z == owner_z(c, p))

                    @pl.when(jnp.logical_not(mine))
                    def _(k=k, p=p, oc=oc):
                        landed(src.at[p, oc, cut(k)], ps.at[n, k, p, oc])

    def gather(n, dst, k):
        w = worker(z)
        piece, to, sem = low.at[n, cut(k)], dst.at[z // 2, c, cut(k)], gr.at[n, k, z // 2, c]
        for d in (1, 3, 2):
            rcopy(piece, to, gs.at[n, k, d], sem, dev(x, w, step(z, d), y)).start()

        @pl.when(c == w)
        def _():
            lcopy(piece, to, sem).start()

        @pl.when(c != w)
        def _():
            rcopy(piece, to, gs.at[n, k, 0], sem, dev(x, w, z, y)).start()

    def gather_take(n, dst, k):
        for p in range(2):
            for i in range(2):
                landed(dst.at[p, i, cut(k)], gr.at[n, k, p, i])

    def gather_sent(n):
        for k in range(2):
            for d in (1, 2, 3):
                landed(low.at[n, cut(k)], gs.at[n, k, d])

            @pl.when(c != worker(z))
            def _(k=k):
                landed(low.at[n, cut(k)], gs.at[n, k, 0])

    greet(z_peers(x, c, z, y) + to_x[1:] + to_y[1:])
    for k in range(2):
        scatter(0, part0, k)
    for d in (1, 3, 2):
        rcopy(uq, wu.at[x, :, :, half], s2.at[0, d], r2.at[0, x], to_x[d]).start()
        rcopy(gz, wg.at[:, y, :, half], s2.at[1, d], r2.at[1, y], to_y[d]).start()
    rcopy(uq, wu.at[x, :, :, half], s3.at[0, 0], r3.at[0, x], sib).start()
    rcopy(gz, wg.at[:, y, :, half], s3.at[1, 0], r3.at[1, y], sib).start()
    lcopy(uq, wu.at[x, :, :, half], lo.at[0]).start()
    lcopy(gz, wg.at[:, y, :, half], lo.at[1]).start()
    lcopy(wd_in, wd, lo.at[2]).start()
    vec[...] = jnp.zeros_like(vec)

    for k in range(2):
        total = scatter_take(0, k)
        out = mix_of(st[cut(k)].astype(F32), total, rate_a[0:1])[0]
        low[0, cut(k)] = out.astype(BF)
        gather(0, xg, k)
        mixed[cut(k)] = total
        first[cut(k)] = out

    for d in (1, 3, 2):
        x2, y2 = step(x, d), step(y, d)
        landed(wu.at[x2, :, :, half], r2.at[0, x2])
        rcopy(wu.at[x2, :, :, half], wu.at[x2, :, :, half], s3.at[0, d], r3.at[0, x2], sib).start()
        landed(wg.at[:, y2, :, half], r2.at[1, y2])
        rcopy(wg.at[:, y2, :, half], wg.at[:, y2, :, half], s3.at[1, d], r3.at[1, y2], sib).start()
    landed(wu.at[x, :, :, half], lo.at[0])
    landed(wg.at[:, y, :, half], lo.at[1])
    landed(wd, lo.at[2])
    for k in range(4):
        landed(wu.at[k, :, :, other], r3.at[0, k])
        landed(wg.at[:, k, :, other], r3.at[1, k])

    def rows_of(ref, k):
        return ref[:, :, cut(k)].reshape(4 * HALF, D)

    def forward(k):
        gather_take(0, xg, k)

        def cols(t, carry):
            cs = pl.ds(pl.multiple_of(t * 256, 256), 256)
            xs = rows_of(xg, k)
            u = jnp.dot(xs, wu[:, :, :, cs].reshape(D, 256), preferred_element_type=F32)
            g = jnp.dot(xs, wg[:, :, :, cs].reshape(D, 256), preferred_element_type=F32)
            tt = g * sg[0:1, cs]
            up[k, :, cs] = u
            gate[k, :, cs] = g
            hid[k, :, cs] = (u * su[0:1, cs] * (tt * jax.nn.sigmoid(tt))).astype(BF)
            return carry

        lax.fori_loop(0, 5, cols, 0)

        def down(t, carry):
            cs = pl.ds(pl.multiple_of(t * 256, 256), 256)
            v = jnp.dot(hid[k], wd[:, cs], preferred_element_type=F32)
            part[0, :, :, cut(k), cs] = v.astype(BF).reshape(2, 2, HALF, 256)
            return carry

        lax.fori_loop(0, 5, down, 0)
        scatter(1, part.at[0], k)

    for k in range(2):
        forward(k)

    def turn(dst, load):
        def body(t, carry):
            cs = pl.ds(pl.multiple_of(t * 256, 256), 256)
            for k in range(2):
                dst[cs, k * 256 : (k + 1) * 256] = load(k, cs).T
            return carry

        lax.fori_loop(0, 5, body, 0)

    turn(ht, lambda k, cs: hid[k, :, cs])
    am = rate_m[0:1]
    at = (c * 16 + z * 4 + y) * ROWS
    for k in range(2):
        total = scatter_take(1, k)
        position = at + k * HALF + lax.broadcasted_iota(jnp.int32, (HALF, 1), 0)
        live = (position < length[0]).astype(F32)
        base = first[cut(k)]
        d_base, d_part, g_am = mix_back(cot[cut(k)].astype(F32) * live, base, total, am)
        low[1, cut(k)] = d_part.astype(BF)
        gather(1, dd, k)
        dfirst[cut(k)] = d_base
        vec[1:2] += g_am
        result[cut(k)] = (mix_of(base, total, am)[0] * live).astype(BF)
    turn(xt, lambda k, cs: xg[:, :, cut(k), cs].reshape(256, 256))

    def backward(k):
        gather_take(1, dd, k)

        def cols(t, carry):
            cs = pl.ds(pl.multiple_of(t * 256, 256), 256)
            dh = nt(rows_of(dd, k), wd[cs, :])
            u, g = up[k, :, cs], gate[k, :, cs]
            sc, sgc = su[0:1, cs], sg[0:1, cs]
            tt = g * sgc
            sig = jax.nn.sigmoid(tt)
            silu = tt * sig
            dsilu = sig * (1.0 + tt * (1.0 - sig))
            dhs = dh * sc
            dhu = dh * u
            both = dhu * dsilu * sc
            dug[0, k, :, cs] = (dhs * silu).astype(BF)
            dug[1, k, :, cs] = (both * sgc).astype(BF)
            vec[2:3, cs] += jnp.sum(dhu * silu, axis=0, keepdims=True)
            vec[3:4, cs] += jnp.sum(both * g, axis=0, keepdims=True)
            return carry

        lax.fori_loop(0, 5, cols, 0)
        for t in range(2):
            v = nt(dug[0, k], wu[2 * t : 2 * t + 2].reshape(640, D)) + nt(
                dug[1, k], wg[2 * t : 2 * t + 2].reshape(640, D)
            )
            part[1, :, :, cut(k), t * 640 : (t + 1) * 640] = v.astype(BF).reshape(2, 2, HALF, 640)
        scatter(2, part.at[1], k)

    for k in range(2):
        backward(k)

    def meet(k):
        dy = dfirst[cut(k)] + scatter_take(2, k)
        d_res, d_part, g_aa = mix_back(dy, st[cut(k)].astype(F32), mixed[cut(k)], rate_a[0:1])
        low[2, cut(k)] = d_part.astype(BF)
        gather(2, dm, k)
        d_st[cut(k)] = d_res
        vec[0:1] += g_aa

    def grad_down(i, carry):
        w = jnp.where(i == 0, 1 - c, c)
        cols = pl.ds(pl.multiple_of(w * 640, 128), 640)
        for k in range(4):
            rhs = jnp.concatenate([dd[:, :, cut(j), cols].reshape(256, 640) for j in range(2)], axis=0)
            v = jnp.dot(ht[k * 320 : (k + 1) * 320, :], rhs, preferred_element_type=F32)
            gd[w, k] = v.astype(BF).reshape(4, 80, 640)

        @pl.when(i == 0)
        def _():
            rcopy(gd.at[1 - c], rd, sx.at[1], rx.at[1], sib).start()

        return carry

    def grad_up(w):
        def body(k, carry):
            rows = pl.ds(pl.multiple_of(k * 320, 64), 320)
            for t in range(2):
                cs = slice(t * 640, (t + 1) * 640)
                v = jnp.dot(xt[rows, :], dug[w, :, :, cs].reshape(512, 640), preferred_element_type=F32)
                ga[w, k, :, :, cs] = v.astype(BF).reshape(4, 80, 640)
            return carry

        lax.fori_loop(0, 4, body, 0)

    lax.fori_loop(0, 2, grad_down, 0)
    meet(0)
    landed(rd, rx.at[1])

    def add_d(k, carry):
        i, j = k // 4, k % 4
        rd[i, j] = (gd[c, i, j].astype(F32) + rd[i, j].astype(F32)).astype(BF)
        return carry

    lax.fori_loop(0, 16, add_d, 0)
    for d in (1, 3, 2):
        rcopy(rd.at[step(y, d)], rdy.at[y], sy.at[d], ry.at[y], to_y[d]).start()
    grad_up(1 - c)
    rcopy(ga.at[1 - c], ra, sx.at[0], rx.at[0], sib).start()
    meet(1)
    grad_up(c)
    landed(ra, rx.at[0])

    def add_a(k, carry):
        i, j = k // 4, k % 4
        ha[i, j] = (ga[c, i, j].astype(F32) + ra[i, j].astype(F32)).astype(BF)
        return carry

    lax.fori_loop(0, 16, add_a, 0)
    for d in (1, 2, 3):
        landed(rdy.at[step(y, d)], ry.at[step(y, d)])

    def sum_d(k, carry):
        v = rd[y, k].astype(F32)
        for d in (1, 2, 3):
            v = v + rdy[step(y, d), k].astype(F32)
        hd[k] = v.astype(BF)
        return carry

    lax.fori_loop(0, 4, sum_d, 0)
    for k in range(2):
        gather_take(2, dm, k)
    for n in range(3):
        gather_sent(n)
    for n, src in ((0, part0), (1, part.at[0]), (2, part.at[1])):
        scatter_sent(n, src)
    for i in range(2):
        for k in range(4):
            landed(gz, s3.at[i, k])
        for d in (1, 2, 3):
            landed(gz, s2.at[i, d])
    landed(ra, sx.at[0])
    landed(rd, sx.at[1])
    for d in (1, 2, 3):
        landed(rdy.at[y], sy.at[d])


def middle(length, part0, st, cot, rate_a, rate_m, su, sg, uq, wd, gz):
    V = pltpu.VMEM
    return remote_call(
        mid_kernel,
        [
            ((ROWS, D), BF, "v"),
            ((ROWS, D), F32, "v"),
            ((2, 2, ROWS, D), BF, "a"),
            ((4, 4, 80, D), BF, "v"),
            ((4, 80, 640), BF, "v"),
            ((8, D), F32, "v"),
        ],
        "savvvvvvaaa",
        [
            V((3, 4, ROWS, D), BF), V((3, ROWS, D), BF), V((2, 2, ROWS, D), BF), V((2, 2, ROWS, D), BF),
            V((4, 4, 80, D), BF), V((4, 4, 80, D), BF), V((D, D), BF),
            V((2, 256, D), F32), V((2, 256, D), F32), V((2, 256, D), BF), V((2, 2, 256, D), BF),
            V((2, 2, 2, ROWS, D), BF), V((D, 512), BF), V((D, 512), BF),
            V((ROWS, D), F32), V((ROWS, D), F32), V((ROWS, D), F32),
            V((2, 4, 4, 80, D), BF), V((2, 4, 4, 80, 640), BF), V((4, 4, 80, D), BF), V((4, 4, 80, 640), BF),
            V((4, 4, 80, 640), BF),
            dma(3, 2, 2, 2), dma(3, 2, 4), dma(3, 2, 4), dma(3, 2, 2, 2),
            dma(2, 4), dma(2, 4), dma(2, 4), dma(2, 4), dma(2), dma(2), dma(4), dma(4), dma(3),
        ],
        2,
        "middle",
    )(length, part0, st, cot, rate_a, rate_m, su, sg, uq, wd, gz)


CUT = 768


def back_kernel(
    length, q, kv_in, wo, dmix, att, lse, ha, hd, tt_in, xg_in, wq_in, scale, inner, outer, vec,
    pbuf, za, zd, zq, o_out, o_vec,
    kv, tt, xg, wq,
    qdo, delta, dqt, acc, low, give, mine, got, got_y, dq, dd, sums, part, gq, go,
    oax, oay, rax, ray, fax, fay, fd, hq, rqx, rqy, fqx, fqy, ob, ox, o2, vs, vb, ws, wb,
    lo, sg, rg, sy, ry, s1, r1, s2, r2, s3, r3, sz, rz, sc, rc, q1, p1, q2, p2, q3, p3, so, ro, sv, rv, sw, rw, ps, pr, sf, rf,
):
    x, c, z, y = here()
    sib = dev(x, 1 - c, z, y)
    to_y = [None] + [dev(x, c, z, step(y, d)) for d in (1, 2, 3)]
    to_x = [None] + [dev(step(x, d), c, z, y) for d in (1, 2, 3)]
    to_z = [None] + [dev(x, c, step(z, d), y) for d in (1, 2, 3)]
    near_first = (1, 3, 2)
    lcopy(kv_in, kv, lo.at[0]).start()
    lcopy(ha.at[x, :, :, 0:CUT], oax, lo.at[1]).start()
    lcopy(ha.at[:, y, :, CUT:D], oay, lo.at[2]).start()
    lcopy(tt_in, tt, lo.at[3]).start()
    lcopy(xg_in, xg, lo.at[4]).start()
    lcopy(wq_in, wq, lo.at[5]).start()
    greet(z_peers(x, c, z, y) + to_y[1:] + to_x[1:])
    for d in near_first:
        rcopy(hd.at[step(x, d)], fd.at[x], s2.at[1, d], r2.at[1, x], to_x[d]).start()
    for d in near_first:
        rcopy(ha.at[step(x, d), :, :, 0:CUT], rax.at[x], s1.at[0, d], r1.at[0, x], to_x[d]).start()
        rcopy(ha.at[:, step(y, d), :, CUT:D], ray.at[y], s1.at[1, d], r1.at[1, y], to_y[d]).start()

    def settle(h):
        landed(got.at[h], rg.at[h])
        for i in range(2):
            for k in range(2):
                mine[h, i, k] = (mine[h, i, k].astype(F32) + got[h, i, k].astype(F32)).astype(BF)
        for d in near_first:
            rcopy(mine.at[h, :, :, step(y, d)], got_y.at[h, y], sy.at[h, d], ry.at[h, y], to_y[d]).start()

    d_att = nt(dmix[...], wo[...]).astype(BF)
    for h in range(HG):
        low[:, h * HDIM : (h + 1) * HDIM] = att[h].astype(BF)
        dh = d_att[:, h * HDIM : (h + 1) * HDIM].astype(F32)
        wide = jnp.concatenate([jnp.zeros_like(dh), dh], axis=1).astype(BF)
        prod = dh * att[h]
        for j in range(BLOCKS):
            rows = slice(j * ROWS, (j + 1) * ROWS)
            qdo[h, j, :ROWS] = q[h, rows, :]
            qdo[h, j, ROWS:] = wide[rows]
            delta[h, j : j + 1, :] = jnp.sum(prod[rows].T, axis=0, keepdims=True)
    for k in range(2):
        g = tn(low[...], dmix[:, k * 640 : (k + 1) * 640])
        go[k] = g.astype(BF).reshape(4, 80, 640)
    rcopy(go.at[1 - c], ob, sc.at[1], rc.at[1], sib).start()
    rcopy(vec, vb.at[0], sv.at[0, 0], rv.at[0, 0], sib).start()

    def small_cores():
        landed(ob, rc.at[1])
        landed(vb.at[0], rv.at[0, 0])
        vs[...] = vec[...] + vb[0]
        for k in range(4):
            ob[k] = (go[c, k].astype(F32) + ob[k].astype(F32)).astype(BF)
        for d in near_first:
            rcopy(ob.at[step(y, d)], ox.at[y], so.at[0, d], ro.at[0, y], to_y[d]).start()
            rcopy(vs, vb.at[d], sv.at[1, d], rv.at[1, d], to_y[d]).start()

    def small_y():
        v, tot = ob[y].astype(F32), vs[...]
        for d in (1, 2, 3):
            landed(ox.at[step(y, d)], ro.at[0, step(y, d)])
            landed(vb.at[d], rv.at[1, d])
            landed(vs, sv.at[1, d])
            v = v + ox[step(y, d)].astype(F32)
            tot = tot + vb[d]
        ox[y] = v.astype(BF)
        vs[...] = tot
        for d in near_first:
            rcopy(ox.at[y], o2.at[d], so.at[1, d], ro.at[1, d], to_x[d]).start()
            rcopy(vs, vb.at[3 + d], sv.at[2, d], rv.at[2, d], to_x[d]).start()

    def small_x():
        v, tot = ox[y].astype(F32), vs[...]
        for d in (1, 2, 3):
            landed(o2.at[d], ro.at[1, d])
            landed(vb.at[3 + d], rv.at[2, d])
            landed(vs, sv.at[2, d])
            v = v + o2[d].astype(F32)
            tot = tot + vb[3 + d]
        o_out[c] = v.astype(BF)
        vs[...] = tot
        rcopy(o_out.at[c], o_out.at[c], sf.at[3], rf.at[3], sib).start()
        for d in near_first:
            rcopy(vs, vb.at[6 + d], sv.at[3, d], rv.at[3, d], to_z[d]).start()

    def small_z():
        tot = vs[...]
        for d in (1, 2, 3):
            landed(vb.at[6 + d], rv.at[3, d])
            landed(vs, sv.at[3, d])
            tot = tot + vb[6 + d]
        o_vec[0:2] = tot[0:2]
        o_vec[2:] = vs[2:]

    def down_x():
        v = hd[x].astype(F32)
        for d in (1, 2, 3):
            landed(fd.at[step(x, d)], r2.at[1, step(x, d)])
            v = v + fd[step(x, d)].astype(F32)
        zd[c, x] = v.astype(BF)
        for d in near_first:
            rcopy(zd.at[c, x], zd.at[c, x], s3.at[1, d], r3.at[1, x], to_x[d]).start()

    def down_done():
        for d in (1, 2, 3):
            landed(zd.at[c, step(x, d)], r3.at[1, step(x, d)])
        rcopy(zd.at[c], zd.at[c], sf.at[1], rf.at[1], sib).start()

    def up_first():
        landed(oax, lo.at[1])
        landed(oay, lo.at[2])
        for d in (1, 2, 3):
            landed(rax.at[step(x, d)], r1.at[0, step(x, d)])
            landed(ray.at[step(y, d)], r1.at[1, step(y, d)])

        def body(k, carry):
            v, w = oax[k].astype(F32), oay[k].astype(F32)
            for d in (1, 2, 3):
                v = v + rax[step(x, d), k].astype(F32)
                w = w + ray[step(y, d), k].astype(F32)
            oax[k] = v.astype(BF)
            oay[k] = w.astype(BF)
            return carry

        lax.fori_loop(0, 4, body, 0)
        for d in near_first:
            rcopy(oax.at[step(y, d)], fax.at[y], s2.at[0, d], r2.at[0, y], to_y[d]).start()
            rcopy(oay.at[step(x, d)], fay.at[x], s2.at[2, d], r2.at[2, x], to_x[d]).start()

    landed(kv, lo.at[0])
    item = work_items(c, y, length[0])

    def per_head(h, carry):
        acc[...] = jnp.zeros_like(acc)
        dqt[...] = jnp.zeros_like(dqt)
        for k, f in ((1, small_cores), (2, small_y), (2, down_x), (3, small_x), (4, small_z), (4, down_done)):
            pl.when(h == k)(f)

        def body(g, carry):
            @pl.when(jnp.logical_and(g == 1, h > 0))
            def _():
                settle(h - 1)

            pl.when(jnp.logical_and(g == 2, h == HG - 1))(up_first)
            key = lax.broadcasted_iota(jnp.int32, (TILE, ROWS), 0)
            its = [item(g * STEP + u) for u in range(STEP)]
            ks = [key_tile(kv, h, t) for _, t, _ in its]
            bs = [qdo[h, j] for j, _, _ in its]
            sds = [nt(k, b) for k, b in zip(ks, bs)]
            dss, pp = [], []
            for sd, (j, _, bound) in zip(sds, its):
                p = jnp.where(key <= bound, jnp.exp(sd[:, :ROWS] - lse[h, pl.ds(j, 1), :]), 0.0)
                dss.append((p * (sd[:, ROWS:] - delta[h, pl.ds(j, 1), :])).astype(BF))
                pp.append(p.astype(BF))
            for ds, p, b, (_, t, _) in zip(dss, pp, bs, its):
                acc[t] += jnp.dot(jnp.concatenate([ds, p], axis=1), b, preferred_element_type=F32)
            for k, ds, (j, _, _) in zip(ks, dss, its):
                dqt[j] += tn(k, ds)
            return carry

        lax.fori_loop(0, 18 // STEP, body, 0)

        def store(i, carry):
            zi, k = i // 2, i % 2
            give[h, zi, k] = acc[k * 4 + owner_z(1 - c, zi)].astype(BF).reshape(4, ROWS, 128)
            mine[h, zi, k] = acc[k * 4 + owner_z(c, zi)].astype(BF).reshape(4, ROWS, 128)
            return carry

        lax.fori_loop(0, 4, store, 0)
        rcopy(give.at[h], got.at[h], sg.at[h], rg.at[h], sib).start()
        for j in range(BLOCKS):
            dq[h, j * ROWS : (j + 1) * ROWS, :] = dqt[j].T * 0.125
        return carry

    lax.fori_loop(0, HG, per_head, 0)
    settle(HG - 1)
    ws[...] = jnp.zeros_like(ws)
    landed(tt, lo.at[3])
    landed(xg, lo.at[4])
    landed(wq, lo.at[5])
    sums[...] = jnp.zeros_like(sums)
    lane = lanes()

    def through(h, carry):
        for d in (1, 2, 3):
            landed(got_y.at[h, step(y, d)], ry.at[h, step(y, d)])
        cols = pl.ds(pl.multiple_of(h * 128, 128), 128)
        pair = pl.ds(pl.multiple_of(640 + (h // 2) * 128, 128), 128)
        odd = h % 2 == 1

        def per_block(j, carry):
            i, k = j // 2, j % 2
            rows = pl.ds(pl.multiple_of(j * ROWS, ROWS), ROWS)
            cosine, sine = turn_of(inner, outer, block_index(c, y, j))
            grads = mine[h, i, k, y].astype(F32)
            for d in (1, 2, 3):
                grads = grads + got_y[h, step(y, d), i, k].astype(F32)
            grads = grads.astype(BF).astype(F32)
            turned = pltpu.roll(grads, 64, 1)
            t = tt[h, rows, :]
            dy = jnp.where(lane < 64, dq[h, rows, :].astype(BF).astype(F32), turned)
            inv = lax.rsqrt(half_means(t * t, lane) + EPS)
            unit = t * inv
            sums[:, cols] += jnp.sum((dy * unit).reshape(ROWS // 8, 8, 128), axis=0)
            dyh = dy * scale[0:1, cols]
            dt = (dyh - unit * half_means(dyh * unit, lane)) * inv
            dd[rows, cols] = (dt * cosine + swap(dt * sine, lane)).astype(BF)
            before = jnp.where(odd, dd[rows, pair].astype(F32), turned)
            dd[rows, pair] = jnp.where(lane < 64, before, jnp.where(odd, grads, 0.0)).astype(BF)
            return carry

        lax.fori_loop(0, BLOCKS, per_block, 0)
        return carry

    lax.fori_loop(0, HG - 1, through, 0)
    for d in (1, 2, 3):
        landed(fax.at[step(y, d)], r2.at[0, step(y, d)])
        landed(fay.at[step(x, d)], r2.at[2, step(x, d)])
    v, w = oax[y].astype(F32), oay[x].astype(F32)
    for d in (1, 2, 3):
        v = v + fax[step(y, d)].astype(F32)
        w = w + fay[step(x, d)].astype(F32)
    za[2, x, :, 0:CUT] = v.astype(BF)
    za[2, x, :, CUT:D] = w.astype(BF)
    for d in near_first:
        rcopy(za.at[2, x], za.at[2, x], s3.at[0, d], r3.at[0, x], to_x[d]).start()
    through(HG - 1, 0)

    def weights(i, carry):
        h = jnp.where(i == 0, 1 - c, c)
        cols = pl.ds(pl.multiple_of(h * 512, 128), 512)
        gq[h] = tn(xg[...].reshape(512, D), dd[:, cols]).astype(BF).reshape(4, 4, 80, 512)

        @pl.when(i == 0)
        def _():
            rcopy(gq.at[1 - c], hq, sc.at[0], rc.at[0], sib).start()

        return carry

    def inputs(p, carry):
        rows = pl.ds(pl.multiple_of(p * 256, 256), 256)
        v = nt(dd[rows, 0:512], wq[0].reshape(D, 512)) + nt(dd[rows, 512:1024], wq[1].reshape(D, 512))
        part[p] = v.astype(BF).reshape(2, ROWS, D)
        z_scatter_pair(part, pbuf, ps, pr, p, x, c, z, y)
        return carry

    lax.fori_loop(0, 2, weights, 0)
    for h in range(HG):
        v = jnp.sum(sums[:, h * 128 : (h + 1) * 128], axis=0, keepdims=True)
        ws[:, h * HDIM : (h + 1) * HDIM] = jnp.broadcast_to(v[:, :HDIM] + v[:, HDIM:], (8, HDIM))
    rcopy(ws, wb.at[0], sw.at[0, 0], rw.at[0, 0], sib).start()

    landed(hq, rc.at[0])

    def add_q(k, carry):
        i, j = k // 4, k % 4
        v = (gq[c, i, j].astype(F32) + hq[i, j].astype(F32)).astype(BF)
        fqx[i, j] = v[:, :256]
        fqy[j, i] = v[:, 256:]
        return carry

    lax.fori_loop(0, 16, add_q, 0)
    for d in near_first:
        rcopy(fqx.at[step(x, d)], rqx.at[x], q1.at[0, d], p1.at[0, x], to_x[d]).start()
        rcopy(fqy.at[step(y, d)], rqy.at[y], q1.at[1, d], p1.at[1, y], to_y[d]).start()
    landed(wb.at[0], rw.at[0, 0])
    landed(ws, sw.at[0, 0])
    ws[...] = ws[...] + wb[0]
    for d in near_first:
        rcopy(ws, wb.at[d], sw.at[1, d], rw.at[1, d], to_y[d]).start()
    for d in (1, 2, 3):
        landed(za.at[2, step(x, d)], r3.at[0, step(x, d)])
    for d in near_first:
        rcopy(za.at[2, step(z, d)], za.at[c, z], sz.at[0, d], rz.at[0, z], to_z[d]).start()
    za[c, z] = za[2, z]
    lax.fori_loop(0, 2, inputs, 0)
    for d in (1, 2, 3):
        landed(rqx.at[step(x, d)], p1.at[0, step(x, d)])
        landed(rqy.at[step(y, d)], p1.at[1, step(y, d)])

    def add_q1(k, carry):
        a, b = fqx[x, k].astype(F32), fqy[y, k].astype(F32)
        for d in (1, 2, 3):
            a = a + rqx[step(x, d), k].astype(F32)
            b = b + rqy[step(y, d), k].astype(F32)
        rqx[x, k] = a.astype(BF)
        rqy[y, k] = b.astype(BF)
        return carry

    lax.fori_loop(0, 4, add_q1, 0)
    for d in near_first:
        rcopy(rqx.at[x, step(y, d)], fqx.at[4, y], q2.at[0, d], p2.at[0, y], to_y[d]).start()
        rcopy(rqy.at[y, step(x, d)], fqy.at[4, x], q2.at[1, d], p2.at[1, x], to_x[d]).start()
    tot = ws[...]
    for d in (1, 2, 3):
        landed(wb.at[d], rw.at[1, d])
        landed(ws, sw.at[1, d])
        tot = tot + wb[d]
    ws[...] = tot
    for d in near_first:
        rcopy(ws, wb.at[3 + d], sw.at[2, d], rw.at[2, d], to_x[d]).start()
    for d in (1, 2, 3):
        landed(fqx.at[4, step(y, d)], p2.at[0, step(y, d)])
        landed(fqy.at[4, step(x, d)], p2.at[1, step(x, d)])
    a, b = rqx[x, y].astype(F32), rqy[y, x].astype(F32)
    for d in (1, 2, 3):
        a = a + fqx[4, step(y, d)].astype(F32)
        b = b + fqy[4, step(x, d)].astype(F32)
    zq[0, x] = jnp.concatenate([a, b], axis=1).astype(BF)
    for d in near_first:
        rcopy(zq.at[0, x], zq.at[0, x], q3.at[d], p3.at[x], to_x[d]).start()
    tot = ws[...]
    for d in (1, 2, 3):
        landed(wb.at[3 + d], rw.at[2, d])
        landed(ws, sw.at[2, d])
        tot = tot + wb[3 + d]
    o_vec[4:5, 0:384] = tot[0:1]
    for d in (1, 2, 3):
        landed(zq.at[0, step(x, d)], p3.at[step(x, d)])
    for d in near_first:
        rcopy(zq.at[0, step(z, d)], zq.at[1 + c, z], sz.at[1, d], rz.at[1, z], to_z[d]).start()
    zq[1 + c, z] = zq[0, z]
    for d in (1, 2, 3):
        landed(za.at[c, step(z, d)], rz.at[0, step(z, d)])
    rcopy(za.at[c], za.at[c], sf.at[0], rf.at[0], sib).start()
    for d in (1, 2, 3):
        landed(zq.at[1 + c, step(z, d)], rz.at[1, step(z, d)])
    rcopy(zq.at[1 + c], zq.at[1 + c], sf.at[2], rf.at[2], sib).start()
    z_scatter_take(pbuf, pr)
    landed(za.at[1 - c], rf.at[0])
    landed(zd.at[1 - c], rf.at[1])
    landed(zq.at[2 - c], rf.at[2])
    landed(o_out.at[1 - c], rf.at[3])
    def sent(h, carry):
        landed(give.at[h], sg.at[h])
        for d in (1, 2, 3):
            landed(got_y.at[h, y], sy.at[h, d])
        return carry

    lax.fori_loop(0, HG, sent, 0)
    z_scatter_sent(part, ps, c, z)
    landed(hq, sc.at[0])
    landed(ob, sc.at[1])
    landed(vec, sv.at[0, 0])
    landed(o_out.at[0], sf.at[3])
    landed(za.at[0], sf.at[0])
    landed(zd.at[0], sf.at[1])
    landed(zq.at[1], sf.at[2])
    for d in (1, 2, 3):
        landed(rax.at[x], s1.at[0, d])
        landed(ray.at[y], s1.at[1, d])
        landed(fax.at[0], s2.at[0, d])
        landed(fd.at[0], s2.at[1, d])
        landed(fay.at[0], s2.at[2, d])
        landed(za.at[0, 0], s3.at[0, d])
        landed(fd.at[0], s3.at[1, d])
        landed(za.at[0, 0], sz.at[0, d])
        landed(zq.at[0, 0], sz.at[1, d])
        landed(rqx.at[0], q1.at[0, d])
        landed(rqy.at[0], q1.at[1, d])
        landed(fqx.at[0, 0], q2.at[0, d])
        landed(fqy.at[0, 0], q2.at[1, d])
        landed(zq.at[0, 0], q3.at[d])
        landed(ox.at[0], so.at[0, d])
        landed(ox.at[0], so.at[1, d])


def back(length, q, kv, wo, dmix, att, lse, ha, hd, tt, xg, wq, scale, inner, outer, vec):
    n = BLOCKS * ROWS
    V = pltpu.VMEM
    return remote_call(
        back_kernel,
        [
            ((4, ROWS, D), BF, "v"),
            ((3, 4, 80, D), BF, "v"),
            ((2, 4, 80, 640), BF, "v"),
            ((3, 4, 80, 512), BF, "v"),
            ((2, 80, 640), BF, "v"),
            ((8, D), F32, "v"),
        ],
        "svavvvvavaaavvvv",
        [
            V((HG, 2, 2, 2, 4, ROWS, 128), BF), V((HG, n, 128), F32), V((2, 2, ROWS, D), BF), V((2, 4, 4, 80, 512), BF),
            V((HG, BLOCKS, 2 * ROWS, 128), BF), V((HG, BLOCKS, 128), F32), V((BLOCKS, 128, ROWS), F32), V((8, TILE, 128), F32),
            V((n, GROUP), BF),
            V((HG, 2, 2, 4, ROWS, 128), BF), V((HG, 2, 2, 4, ROWS, 128), BF), V((HG, 2, 2, 4, ROWS, 128), BF),
            V((HG, 4, 2, 2, ROWS, 128), BF), V((HG, n, 128), F32), V((n, 1024), BF), V((8, HG * 128), F32),
            V((2, 2, ROWS, D), BF), V((2, 4, 4, 80, 512), BF), V((2, 4, 80, 640), BF),
            V((4, 80, CUT), BF), V((4, 80, D - CUT), BF), V((4, 4, 80, CUT), BF), V((4, 4, 80, D - CUT), BF),
            V((4, 80, CUT), BF), V((4, 80, D - CUT), BF), V((4, 80, 640), BF),
            V((4, 4, 80, 512), BF), V((4, 4, 80, 256), BF), V((4, 4, 80, 256), BF), V((5, 4, 80, 256), BF), V((5, 4, 80, 256), BF),
            V((4, 80, 640), BF), V((4, 80, 640), BF), V((4, 80, 640), BF), V((8, D), F32), V((10, 8, D), F32), V((8, 384), F32), V((7, 8, 384), F32),
            dma(6), dma(HG), dma(HG), dma(HG, 4), dma(HG, 4),
            dma(2, 4), dma(2, 4), dma(3, 4), dma(3, 4), dma(2, 4), dma(2, 4), dma(2, 4), dma(2, 4), dma(2), dma(2),
            dma(2, 4), dma(2, 4), dma(2, 4), dma(2, 4), dma(4), dma(4), dma(2, 4), dma(2, 4), dma(4, 4), dma(4, 4), dma(3, 4), dma(3, 4),
            dma(2, 2), dma(4), dma(4), dma(4),
        ],
        3,
        "back",
    )(length, q, kv, wo, dmix, att, lse, ha, hd, tt, xg, wq, scale, inner, outer, vec)


def finish_kernel(res, d_st, pbuf, za, zd, zq, out, vec, result, g_in, o_q, o_k, o_v, o_out, o_up, o_gate, o_down, o_vec):
    _, _, z, y = here()
    result[...] = res[...]
    g_in[...] = d_st[...] + total_of(pbuf)
    o_out[:, :640] = out[0].astype(F32)
    o_out[:, 640:] = out[1].astype(F32)
    for k in range(4):
        cols = slice(k * D, (k + 1) * D)
        o_up[:, cols] = za[0, k].astype(F32)
        o_gate[:, cols] = za[1, k].astype(F32)
        for h in range(2):
            o_down[k * 80 : (k + 1) * 80, h * 640 : (h + 1) * 640] = zd[h, k].astype(F32)
        a, b = zq[1, k].astype(F32), zq[2, k].astype(F32)
        at = k * GROUP
        pairs = [a[:, h * 128 : (h + 1) * 128] for h in range(4)] + [b[:, :128]]
        o_q[:, at : at + GROUP] = jnp.concatenate([v[:, :HDIM] for v in pairs], axis=1)
        o_k[:, at : at + GROUP] = jnp.concatenate([v[:, HDIM:] for v in pairs], axis=1)
        o_v[:, at : at + GROUP] = b[:, 128:448]
    v = vec[...]
    o_vec[0:2] = pltpu.roll(v, (16 - (z * 4 + y)) % 16 * 80, 1)[0:2]
    o_vec[2:4] = pltpu.roll(v, (4 - y) % 4 * 320, 1)[2:4]
    o_vec[4:] = pltpu.roll(v, (16 - y) % 16 * 80, 1)[4:]


def finish(res, d_st, pbuf, za, zd, zq, out, vec):
    return local_call(
        finish_kernel,
        [
            ((ROWS, D), BF),
            ((ROWS, D), F32),
            ((80, D), F32),
            ((80, D), F32),
            ((80, D), F32),
            ((80, D), F32),
            ((80, FF), F32),
            ((80, FF), F32),
            ((320, D), F32),
            ((8, D), F32),
        ],
        8,
        [],
        "finish",
    )(res, d_st, pbuf, za, zd, zq, out, vec)


def shards(
    states, w_query, w_key, w_value, w_out, w_up, w_gate, w_down,
    scale_qk, alpha_attn, alpha_mlp, scale_up, scale_gate, lengths, cotangent,
):
    x, c, z, y = here()
    st = states[0]

    def heads(w):
        return w.reshape(80, 4, HG, HDIM)

    q4, k4, v4 = heads(w_query), heads(w_key), heads(w_value)
    qk = jnp.stack([q4, k4], axis=3).reshape(80, 4, HG * 128)
    half1 = jnp.concatenate([qk[:, :, 512:], v4.reshape(80, 4, GROUP), jnp.zeros((80, 4, HDIM), BF)], axis=2)
    wq = jnp.stack([qk[:, :, :512], half1]).transpose(0, 2, 1, 3)
    vec = jnp.concatenate([scale_qk, alpha_attn, alpha_mlp, scale_up, scale_gate, jnp.zeros((16,), BF)])
    vec = jnp.broadcast_to(vec.astype(F32)[None], (8, 896))
    inner, outer = (jnp.asarray(t) for t in rope_tables())
    n = BLOCKS * ROWS
    part, att, lse, kv, q, turned, xg, wqkv, wo, scale, rate_a, rate_m, su, sg, uq, wd, gz = front(
        lengths, st, wq, vec, w_out, w_up, w_gate, w_down, inner, outer
    )
    result, d_st, dm, ha, hd, vec = middle(
        lengths, part, st, cotangent[0], rate_a, rate_m, su, sg, uq, wd.reshape(D, D), gz
    )
    pbuf, za, zd, zq, out, vec = back(
        lengths, q, kv, wo.reshape(GROUP, D), dm.reshape(n, D), att, lse, ha, hd, turned, xg, wqkv, scale, inner, outer, vec
    )
    result, g_in, o_q, o_k, o_v, o_out, o_up, o_gate, o_down, o_vec = finish(
        result, d_st, pbuf, za, zd, zq, out, vec
    )
    return (
        result[None],
        g_in[None],
        o_q,
        o_k,
        o_v,
        o_out,
        o_up,
        o_gate,
        o_down,
        o_vec[4, :80],
        o_vec[0, :80],
        o_vec[1, :80],
        o_vec[2, :320],
        o_vec[3, :320],
    )


def solution(mesh):
    row = P("grp", ("seq", "shard"), None)
    mat = P("shard", None)
    one = P("shard")
    return jax.shard_map(
        shards,
        mesh=mesh,
        in_specs=(row,) + (mat,) * 7 + (one,) * 5 + (P("grp"), row),
        out_specs=(row, row) + (mat,) * 7 + (one,) * 5,
        check_vma=False,
    )
```

```python
import functools
import math

import jax
import jax.numpy as jnp
import numpy as np
from jax import lax
from jax.experimental import pallas as pl
from jax.experimental.pallas import tpu as pltpu
from jax.sharding import PartitionSpec as P


D, HEADS, HDIM, FF = 1280, 20, 64, 5120
ROWS, BLOCKS, HG = 128, 4, 5
GROUP = HG * HDIM
EPS = 1e-6
BF, F32 = jnp.bfloat16, jnp.float32
MESH = pl.DeviceIdType.MESH
VMEM_LIMIT = 60 << 20


def here():
    s = lax.axis_index("shard")
    return lax.axis_index("grp"), lax.axis_index("seq"), s // 4, s % 4


def dev(x, c, z, y):
    return (x, c, z * 4 + y)


def worker(z):
    return ((z + 1) // 2) % 2


def owner_z(w, i):
    return i * (3 - 2 * w) + w


def step(v, d):
    return (v + d) % 4


def rcopy(src, dst, ss, rs, to):
    return pltpu.make_async_remote_copy(
        src_ref=src, dst_ref=dst, send_sem=ss, recv_sem=rs, device_id=to, device_id_type=MESH
    )


def lcopy(src, dst, sem):
    return pltpu.make_async_copy(src, dst, sem)


def landed(dst, sem):
    pltpu.make_async_copy(dst, dst, sem).wait()


def greet(peers):
    bar = pltpu.get_barrier_semaphore()
    for p in peers:
        pl.semaphore_signal(bar, inc=1, device_id=p, device_id_type=MESH)
    pl.semaphore_wait(bar, len(peers))


def z_peers(x, c, z, y):
    far = [dev(x, cc, step(z, d), y) for d in (1, 2, 3) for cc in (0, 1)]
    return [dev(x, 1 - c, z, y)] + far


def z_gather_start(src, dst, ss, rs, x, c, z, y):
    w = worker(z)
    slot = (z // 2, c)
    for d in (1, 3, 2):
        rcopy(src, dst.at[slot], ss.at[d], rs.at[slot], dev(x, w, step(z, d), y)).start()

    @pl.when(c == w)
    def _():
        lcopy(src, dst.at[slot], rs.at[slot]).start()

    @pl.when(c != w)
    def _():
        rcopy(src, dst.at[slot], ss.at[0], rs.at[slot], dev(x, w, z, y)).start()


def z_gather_take(dst, rs, p):
    for k in range(2):
        landed(dst.at[p, k], rs.at[p, k])


def z_gather_sent(src, ss, c, z):
    for d in (1, 2, 3):
        landed(src, ss.at[d])

    @pl.when(c != worker(z))
    def _():
        landed(src, ss.at[0])


def z_gather_wait(src, dst, ss, rs, c, z):
    for p in range(2):
        z_gather_take(dst, rs, p)
    z_gather_sent(src, ss, c, z)


def z_scatter_pair(part, dst, ss, rs, p, x, c, z, y):
    oz = owner_z(c, p)
    for oc in range(2):
        mine = jnp.logical_and(c == oc, z == oz)

        @pl.when(mine)
        def _(oc=oc):
            lcopy(part.at[p, oc], dst.at[z], rs.at[z]).start()

        @pl.when(jnp.logical_not(mine))
        def _(oc=oc):
            rcopy(part.at[p, oc], dst.at[z], ss.at[p, oc], rs.at[z], dev(x, oc, oz, y)).start()


def z_scatter_start(part, dst, ss, rs, x, c, z, y):
    for p in range(2):
        z_scatter_pair(part, dst, ss, rs, p, x, c, z, y)


def z_scatter_take(dst, rs):
    for k in range(4):
        landed(dst.at[k], rs.at[k])


def z_scatter_sent(part, ss, c, z):
    for p in range(2):
        for oc in range(2):
            mine = jnp.logical_and(c == oc, z == owner_z(c, p))

            @pl.when(jnp.logical_not(mine))
            def _(p=p, oc=oc):
                landed(part.at[p, oc], ss.at[p, oc])


def remote_call(kernel, outs, ins_spaces, scratch, cid, name):
    spec = {
        "a": pl.BlockSpec(memory_space=pl.ANY),
        "v": pl.BlockSpec(memory_space=pltpu.VMEM),
        "s": pl.BlockSpec(memory_space=pltpu.SMEM),
    }
    return pl.pallas_call(
        kernel,
        out_shape=[jax.ShapeDtypeStruct(s, d) for s, d, _ in outs],
        in_specs=[spec[s] for s in ins_spaces],
        out_specs=[spec[s] for _, _, s in outs],
        scratch_shapes=scratch,
        compiler_params=pltpu.CompilerParams(
            collective_id=cid, has_side_effects=True, vmem_limit_bytes=VMEM_LIMIT
        ),
        name=name,
    )


def local_call(kernel, outs, n_in, scratch, name, smem=0):
    vmem = pl.BlockSpec(memory_space=pltpu.VMEM)
    sm = pl.BlockSpec(memory_space=pltpu.SMEM)
    return pl.pallas_call(
        kernel,
        out_shape=[jax.ShapeDtypeStruct(s, d) for s, d in outs],
        in_specs=[sm] * smem + [vmem] * n_in,
        out_specs=[vmem for _ in outs],
        scratch_shapes=scratch,
        compiler_params=pltpu.CompilerParams(vmem_limit_bytes=VMEM_LIMIT),
        name=name,
    )


def dma(*shape):
    return pltpu.SemaphoreType.DMA(shape)


def rope_tables():
    freqs = np.exp(np.arange(32) * (-2.0 * math.log(10000.0) / 64))
    freqs = np.tile(freqs, 4)
    sign = np.tile(np.concatenate([-np.ones(32), np.ones(32)]), 2)
    inner = np.arange(ROWS)[:, None] * freqs
    outer = (np.arange(32) * ROWS)[:, None] * freqs
    return (
        np.stack([np.cos(inner), np.sin(inner) * sign]).astype(np.float32),
        np.stack([np.cos(outer), np.sin(outer) * sign]).astype(np.float32),
    )


def block_index(c, y, j):
    return (j % 2) * 16 + owner_z(c, j // 2) * 4 + y


def turn_of(inner, outer, b):
    oc = outer[0, pl.ds(b, 1), :]
    os = outer[1, pl.ds(b, 1), :]
    return oc * inner[0] - os * inner[1], os * inner[0] + oc * inner[1]


def lanes():
    return lax.broadcasted_iota(jnp.int32, (ROWS, 128), 1)


def swap(v, lane):
    return jnp.where(lane % 64 < 32, pltpu.roll(v, 96, 1), pltpu.roll(v, 32, 1))


def half_means(v, lane):
    low = jnp.sum(jnp.where(lane < 64, v, 0.0), axis=-1, keepdims=True)
    high = jnp.sum(jnp.where(lane < 64, 0.0, v), axis=-1, keepdims=True)
    return jnp.where(lane < 64, low, high) * (1.0 / 64)


TILE = 512
STEP = 6


def tiles_of(c, j):
    return (j % 2) * 4 + owner_z(c, j // 2) + 1


def nt(a, b):
    return lax.dot_general(a, b, (((1,), (1,)), ((), ())), preferred_element_type=F32)


def tn(a, b):
    return lax.dot_general(a, b, (((0,), (0,)), ((), ())), preferred_element_type=F32)


def key_tile(ref, h, t):
    zz = t % 4
    return ref[h, worker(zz), zz // 2, t // 4].reshape(TILE, 128)


def work_items(c, y, length):
    n = [tiles_of(c, j) for j in range(BLOCKS)]
    starts = [n[0], n[0] + n[1], n[0] + n[1] + n[2]]
    query = lax.broadcasted_iota(jnp.int32, (1, ROWS), 1)

    def item(i):
        hits = [(i >= s).astype(jnp.int32) for s in starts]
        j = hits[0] + hits[1] + hits[2]
        t = i - hits[0] * n[0] - hits[1] * n[1] - hits[2] * n[2]
        last = query + y * ROWS + (tiles_of(c, j) - 1 - t) * TILE
        return j, t, jnp.minimum(last, length - 1 - t * TILE)

    return item


def columns(ref, k, half):
    return ref.at[:, pl.ds(pl.multiple_of(k * D + half * 640, 128), 640)]


def front_kernel(
    length, st, w_query, w_key, w_value, v_qk, v_attn, v_mlp, v_up, v_gate, w_out, w_up, w_gate, w_down, inner, outer,
    part, att, lse, kv_o, q_o, t_o, xg_o, wqkv_o, wo_o, scale_o, rate_a, rate_m, su, sg, uq, wd, gz,
    xg, wqkv, vecs, wo, y0, y1, kv, kvb, q, tt, low, acc, tot, uz, wq, vec,
    xs, xr, w1s, w1r, w2s, w2r, w3s, w3r, vs, vr, os, orr, lo,
    f1s, f1r, f2s, f2r, f3s, f3r, f4s, f4r, fl, sy, ry, sf, rf, ss, rs, kl, ol,
):
    x, c, z, y = here()
    sib = dev(x, 1 - c, z, y)
    half = pl.ds(pl.multiple_of(c * 640, 128), 640)
    other = pl.ds(pl.multiple_of((1 - c) * 640, 128), 640)
    to_z = [None] + [dev(x, c, step(z, d), y) for d in (1, 2, 3)]
    to_y = [None] + [dev(x, c, z, step(y, d)) for d in (1, 2, 3)]
    to_x = [None] + [dev(step(x, d), c, z, y) for d in (1, 2, 3)]
    near_first = (1, 3, 2)

    def head(ref, k):
        return ref[:, k * HDIM : (k + 1) * HDIM]

    @pl.when(c == 0)
    def _():
        for zz in range(4):
            for h in range(4):
                k = zz * HG + h
                wq[zz, :, h * 128 : (h + 1) * 128] = jnp.concatenate([head(w_query, k), head(w_key, k)], axis=1)

    @pl.when(c == 1)
    def _():
        for zz in range(4):
            k = zz * HG
            wq[zz, :, 0:128] = jnp.concatenate([head(w_query, k + 4), head(w_key, k + 4)], axis=1)
            for h in range(2):
                wq[zz, :, 128 + h * 128 : 256 + h * 128] = w_value[:, (k + 2 * h) * HDIM : (k + 2 * h + 2) * HDIM]
            last = head(w_value, k + 4)
            wq[zz, :, 384:512] = jnp.concatenate([last, jnp.zeros_like(last)], axis=1)

    vec[...] = jnp.zeros_like(vec)
    for ref, at, n in ((v_qk, 0, 80), (v_attn, 80, 80), (v_mlp, 160, 80), (v_up, 240, 320), (v_gate, 560, 320)):
        vec[:, at : at + n] = jnp.broadcast_to(ref[...].astype(F32), (8, n))
    greet(z_peers(x, c, z, y) + to_y[1:] + to_x[1:])

    for d in near_first:
        rcopy(wq.at[step(z, d)], wqkv.at[c, z, y], w1s.at[d], w1r.at[z], to_z[d]).start()
        rcopy(vec, vecs.at[z, y], vs.at[0, d], vr.at[0, z], to_z[d]).start()
    lcopy(wq.at[z], wqkv.at[c, z, y], lo.at[0]).start()
    lcopy(vec, vecs.at[z, y], lo.at[1]).start()
    for d in near_first:
        rcopy(w_out.at[:, half], wo.at[y, :, half], os.at[0, d], orr.at[0, y], to_y[d]).start()
    rcopy(w_out.at[:, half], wo.at[y, :, half], os.at[0, 0], orr.at[1, y], sib).start()
    lcopy(w_out.at[:, half], wo.at[y, :, half], lo.at[2]).start()

    for d in (1, 2, 3):
        landed(wqkv.at[c, step(z, d), y], w1r.at[step(z, d)])
        landed(vecs.at[step(z, d), y], vr.at[0, step(z, d)])
    landed(wqkv.at[c, z, y], lo.at[0])
    landed(vecs.at[z, y], lo.at[1])
    mine = wqkv.at[c, :, y]
    rcopy(mine, mine, w2s.at[0], w2r.at[0], to_y[1]).start()
    rcopy(mine, mine, w2s.at[1], w2r.at[1], to_y[3]).start()
    rcopy(mine, mine, w3s.at[0], w3r.at[0], sib).start()
    for d in near_first:
        rcopy(vecs.at[:, y], vecs.at[:, y], vs.at[1, d], vr.at[1, y], to_y[d]).start()
    z_gather_start(st, xg, xs, xr, x, c, z, y)
    for k, src, to in ((0, step(y, 3), to_y[1]), (1, step(y, 1), to_y[3])):
        block, piece = wqkv.at[c, :, src], wqkv.at[c, 2 * k : 2 * k + 2, src]
        landed(block, w2r.at[k])
        rcopy(piece, piece, w2s.at[2 + k], w2r.at[2 + k], to).start()
        rcopy(block, block, w3s.at[1 + k], w3r.at[1 + k], sib).start()
    for k in range(2):
        piece = wqkv.at[c, 2 * k : 2 * k + 2, step(y, 2)]
        landed(piece, w2r.at[2 + k])
        rcopy(piece, piece, w3s.at[3 + k], w3r.at[3 + k], sib).start()
    down = w_down.at[pl.ds(pl.multiple_of(x * 80, 16), 80), half]
    for d in near_first:
        rcopy(down, wd.at[y, x, :, half], f2s.at[1, d], f2r.at[1, y], to_y[d]).start()
    lcopy(down, wd.at[y, x, :, half], fl.at[2]).start()
    for d in (1, 2, 3):
        landed(vecs.at[:, step(y, d)], vr.at[1, step(y, d)])
    for zz in range(4):
        for yy in range(4):
            at = (zz * 4 + yy) * 80
            rate_a[:, at : at + 80] = vecs[zz, yy, :, 80:160]
            rate_m[:, at : at + 80] = vecs[zz, yy, :, 160:240]
    for yy in range(4):
        su[:, yy * 320 : (yy + 1) * 320] = vecs[z, yy, :, 240:560]
        sg[:, yy * 320 : (yy + 1) * 320] = vecs[z, yy, :, 560:880]
    scale = jnp.concatenate([vecs[z, yy, :, :80] for yy in range(4)], axis=1)
    for h in range(HG):
        sh = scale[:, h * HDIM : (h + 1) * HDIM]
        scale_o[:, h * 128 : (h + 1) * 128] = jnp.concatenate([sh, sh], axis=1)

    for p in range(2):
        z_gather_take(xg, xr, p)
    for d in near_first:
        rcopy(columns(w_gate, step(z, d), c), gz.at[z], f1s.at[1, d], f1r.at[1 + z], to_z[d]).start()
    lcopy(columns(w_gate, z, c), gz.at[z], fl.at[0]).start()

    @pl.when(z == x)
    def _():
        for d in near_first:
            rcopy(columns(w_up, step(z, d), c), uz, f1s.at[0, d], f1r.at[0], to_z[d]).start()
        lcopy(columns(w_up, z, c), uz, f1r.at[0]).start()

    for k, src in ((0, y), (1, step(y, 3)), (2, step(y, 1))):
        landed(wqkv.at[1 - c, :, src], w3r.at[k])
    for k in range(2):
        landed(wqkv.at[1 - c, 2 * k : 2 * k + 2, step(y, 2)], w3r.at[3 + k])
    lcopy(xg, xg_o, ol.at[0]).start()
    lcopy(wqkv, wqkv_o, ol.at[1]).start()

    def project(p, carry):
        rows = xg[p].reshape(2 * ROWS, D)
        y0[p] = jnp.dot(rows, wqkv[0].reshape(D, 512), preferred_element_type=F32)
        y1[p] = jnp.dot(rows, wqkv[1].reshape(D, 512), preferred_element_type=F32)
        return carry

    lax.fori_loop(0, 2, project, 0)
    lane = lanes()

    def send(h):
        rcopy(kv.at[h], kvb.at[h, c, :, :, y], sy.at[h, 0], ry.at[h, 0], to_y[1]).start()
        rcopy(kv.at[h], kvb.at[h, c, :, :, y], sy.at[h, 1], ry.at[h, 1], to_y[3]).start()
        rcopy(kv.at[h], kvb.at[h, c, :, :, y], ss.at[h, 0], rs.at[h, 0], sib).start()
        lcopy(kv.at[h], kvb.at[h, c, :, :, y], kl.at[h]).start()

    for h in range(HG):

        def per_block(j, carry, h=h):
            p, r = j // 2, pl.ds(pl.multiple_of((j % 2) * ROWS, ROWS), ROWS)
            cosine, sine = turn_of(inner, outer, block_index(c, y, j))
            raw = y0[p, r, h * 128 : (h + 1) * 128] if h < 4 else y1[p, r, 0:128]
            t = raw * cosine + swap(raw, lane) * sine
            unit = t * lax.rsqrt(half_means(t * t, lane) + EPS)
            both = unit * scale_o[0:1, h * 128 : (h + 1) * 128]
            pair = y1[p, r, 128 + (h // 2) * 128 : 256 + (h // 2) * 128]
            v = pair if h % 2 else pltpu.roll(pair, 64, 1)
            kv[h, p, j % 2] = jnp.where(lane < 64, pltpu.roll(both, 64, 1), v).astype(BF)
            rows = pl.ds(pl.multiple_of(j * ROWS, ROWS), ROWS)
            tt[h, rows, :] = t
            q[h, rows, :] = (jnp.where(lane < 64, both, 0.0).astype(BF).astype(F32) * 0.125).astype(BF)
            return carry

        lax.fori_loop(0, BLOCKS, per_block, 0, unroll=True)
        if h < 2:
            send(h)
    landed(wd.at[y, x, :, half], fl.at[2])
    for d in (1, 2, 3):
        landed(wd.at[step(y, d), x, :, half], f2r.at[1, step(y, d)])
    for d in near_first:
        rcopy(wd.at[:, x, :, half], wd.at[:, x, :, half], f3s.at[d], f3r.at[x], to_x[d]).start()
    rcopy(wd.at[:, x, :, half], wd.at[:, x, :, half], f4s.at[0], f4r.at[x], sib).start()
    lcopy(q, q_o, ol.at[2]).start()
    lcopy(tt, t_o, ol.at[3]).start()

    def near(h):
        for k, src, to in ((0, step(y, 3), to_y[1]), (1, step(y, 1), to_y[3])):
            landed(kvb.at[h, c, :, :, src], ry.at[h, k])
            rcopy(kvb.at[h, c, k, :, src], kvb.at[h, c, k, :, src], sf.at[h, k], rf.at[h, k], to).start()
            rcopy(kvb.at[h, c, :, :, src], kvb.at[h, c, :, :, src], ss.at[h, 1 + k], rs.at[h, 1 + k], sib).start()

    def far(h):
        src = step(y, 2)
        for k in range(2):
            landed(kvb.at[h, c, k, :, src], rf.at[h, k])
            rcopy(kvb.at[h, c, k, :, src], kvb.at[h, c, k, :, src], ss.at[h, 3 + k], rs.at[h, 3 + k], sib).start()

    def ready(h):
        landed(kvb.at[h, c, :, :, y], kl.at[h])
        landed(kvb.at[h, 1 - c, :, :, y], rs.at[h, 0])
        landed(kvb.at[h, 1 - c, :, :, step(y, 3)], rs.at[h, 1])
        landed(kvb.at[h, 1 - c, :, :, step(y, 1)], rs.at[h, 2])
        for k in range(2):
            landed(kvb.at[h, 1 - c, k, :, step(y, 2)], rs.at[h, 3 + k])
        lcopy(kvb.at[h], kv_o.at[h], kl.at[h]).start()

    item = work_items(c, y, length[0])

    def compute(h):
        acc[...] = jnp.zeros_like(acc)
        tot[...] = jnp.zeros_like(tot)

        def body(g, carry):
            key = lax.broadcasted_iota(jnp.int32, (TILE, ROWS), 0)
            its = [item(g * STEP + u) for u in range(STEP)]
            ks = [key_tile(kvb, h, t) for _, t, _ in its]
            ss_ = [
                nt(k, q[h, pl.ds(pl.multiple_of(j * ROWS, ROWS), ROWS), :]) for k, (j, _, _) in zip(ks, its)
            ]
            ps = [jnp.where(key <= bound, jnp.exp(s), 0.0) for s, (_, _, bound) in zip(ss_, its)]
            for k, p, (j, _, _) in zip(ks, ps, its):
                tot[j] += jnp.sum(p.reshape(TILE // 8, 8, ROWS), axis=0)
                acc[j] += tn(k, p.astype(BF))
            return carry

        lax.fori_loop(0, 18 // STEP, body, 0)
        for j in range(BLOCKS):
            total = jnp.sum(tot[j], axis=0, keepdims=True)
            lse[h, j : j + 1, :] = jnp.log(total)
            att[h, j * ROWS : (j + 1) * ROWS, :] = (acc[j, HDIM:] / total).T

    def spread_up():
        landed(uz, f1r.at[0])
        for d in near_first:
            rcopy(uz, uq.at[y], f2s.at[0, d], f2r.at[0, y], to_y[d]).start()
        lcopy(uz, uq.at[y], fl.at[1]).start()

    near(0)
    send(2)

    def per_head(i, carry):
        @pl.when(i + 1 < HG)
        def _():
            near(i + 1)

        @pl.when(i + 3 < HG)
        def _():
            send(i + 3)

        @pl.when(i == HG)
        def _():
            spread_up()

        @pl.when(i > 0)
        def _():
            ready(i - 1)
            compute(i - 1)

        @pl.when(i < HG)
        def _():
            far(i)

        return carry

    lax.fori_loop(0, HG + 1, per_head, 0)
    for h in range(HG):
        low[:, h * HDIM : (h + 1) * HDIM] = att[h].astype(BF)
    for d in near_first:
        y2 = step(y, d)
        landed(wo.at[y2, :, half], orr.at[0, y2])
        rcopy(wo.at[y2, :, half], wo.at[y2, :, half], os.at[1, d], orr.at[1, y2], sib).start()
    landed(wo.at[y, :, half], lo.at[2])
    for k in range(4):
        landed(wo.at[k, :, other], orr.at[1, k])
    lcopy(wo, wo_o, ol.at[4]).start()
    for p in range(2):
        v = jnp.dot(low[p * 256 : (p + 1) * 256, :], wo[...].reshape(GROUP, D), preferred_element_type=F32)
        part[p] = v.astype(BF).reshape(2, ROWS, D)

    for d in near_first:
        x2 = step(x, d)
        landed(wd.at[:, x2, :, half], f3r.at[x2])
        rcopy(wd.at[:, x2, :, half], wd.at[:, x2, :, half], f4s.at[d], f4r.at[x2], sib).start()
    landed(uz, fl.at[1])
    landed(uz, fl.at[0])
    for d in (1, 2, 3):
        landed(uq.at[step(y, d)], f2r.at[0, step(y, d)])
        landed(gz.at[step(z, d)], f1r.at[1 + step(z, d)])

    def sent(h, carry):
        for k in range(2):
            landed(kv.at[h], sy.at[h, k])
            landed(kv.at[h, 0], sf.at[h, k])
            landed(kv.at[h, 0], ss.at[h, 3 + k])
        for k in range(3):
            landed(kv.at[h], ss.at[h, k])
        landed(kvb.at[h], kl.at[h])
        return carry

    lax.fori_loop(0, HG, sent, 0)
    z_gather_sent(st, xs, c, z)
    for k in range(4):
        landed(wd.at[:, k, :, other], f4r.at[k])
        landed(wd.at[:, k, :, half], f4s.at[k])
    landed(wo.at[0, :, half], os.at[0, 0])
    for k in range(2):
        landed(mine, w2s.at[k])
        landed(wqkv.at[c, 0:2, y], w2s.at[2 + k])
        landed(wqkv.at[c, 0:2, y], w3s.at[3 + k])
    for k in range(3):
        landed(mine, w3s.at[k])
    for d in (1, 2, 3):
        landed(wqkv.at[c, z, y], w1s.at[d])
        landed(vec, vs.at[0, d])
        landed(vecs.at[:, y], vs.at[1, d])
        landed(wo.at[0, :, half], os.at[0, d])
        landed(wo.at[0, :, half], os.at[1, d])
        landed(uz, f1s.at[1, d])
        landed(uz, f2s.at[0, d])
        landed(uz, f2s.at[1, d])
        landed(wd.at[:, x, :, half], f3s.at[d])

    @pl.when(z == x)
    def _():
        for d in (1, 2, 3):
            landed(uz, f1s.at[0, d])

    landed(xg, ol.at[0])
    landed(wqkv, ol.at[1])
    landed(q, ol.at[2])
    landed(tt, ol.at[3])
    landed(wo, ol.at[4])


def front(length, st, w_query, w_key, w_value, vectors, w_out, w_up, w_gate, w_down, inner, outer):
    n = BLOCKS * ROWS
    V = pltpu.VMEM
    return remote_call(
        front_kernel,
        [
            ((2, 2, ROWS, D), BF, "v"),
            ((HG, n, HDIM), F32, "v"),
            ((HG, BLOCKS, 128), F32, "v"),
            ((HG, 2, 2, 2, 4, ROWS, 128), BF, "a"),
            ((HG, n, 128), BF, "a"),
            ((HG, n, 128), F32, "a"),
            ((2, 2, ROWS, D), BF, "a"),
            ((2, 4, 4, 80, 512), BF, "a"),
            ((4, 80, D), BF, "a"),
            ((8, HG * 128), F32, "v"),
            ((8, D), F32, "v"),
            ((8, D), F32, "v"),
            ((8, D), F32, "v"),
            ((8, D), F32, "v"),
            ((4, 80, 640), BF, "a"),
            ((4, 4, 80, D), BF, "a"),
            ((4, 80, 640), BF, "a"),
        ],
        "savvvvvvvvaaaavv",
        [
            V((2, 2, ROWS, D), BF), V((2, 4, 4, 80, 512), BF), V((4, 4, 8, 896), F32), V((4, 80, D), BF),
            V((2, 256, 512), F32), V((2, 256, 512), F32),
            V((HG, 2, 2, ROWS, 128), BF), V((HG, 2, 2, 2, 4, ROWS, 128), BF), V((HG, n, 128), BF), V((HG, n, 128), F32),
            V((n, GROUP), BF), V((BLOCKS, 128, ROWS), F32), V((BLOCKS, 8, ROWS), F32), V((80, 640), BF),
            V((4, 80, 512), BF), V((8, 896), F32),
            dma(4), dma(2, 2), dma(4), dma(4), dma(4), dma(4), dma(5), dma(5), dma(2, 4), dma(2, 4), dma(2, 4), dma(2, 4), dma(3),
            dma(2, 4), dma(5), dma(2, 4), dma(2, 4), dma(4), dma(4), dma(4), dma(4), dma(3),
            dma(HG, 2), dma(HG, 2), dma(HG, 2), dma(HG, 2), dma(HG, 5), dma(HG, 5), dma(HG), dma(5),
        ],
        0,
        "front",
    )(length, st, w_query, w_key, w_value, *vectors, w_out, w_up, w_gate, w_down, inner, outer)


def inv_rms(v):
    return lax.rsqrt(jnp.mean(v * v, axis=-1, keepdims=True) + EPS)


def back_rms(dy, yy, inv):
    return (dy - yy * jnp.mean(dy * yy, axis=-1, keepdims=True)) * inv


def total_of(buf):
    return (buf[0].astype(F32) + buf[1].astype(F32)) + (buf[2].astype(F32) + buf[3].astype(F32))


def mix_of(res, part, rate):
    inv_p = inv_rms(part)
    unit = part * inv_p
    diff = unit - res
    u = res + rate * diff
    inv_u = inv_rms(u)
    return u * inv_u, unit, inv_p, inv_u, diff


def mix_back(dy, res, part, rate):
    yy, unit, inv_p, inv_u, diff = mix_of(res, part, rate)
    du = back_rms(dy, yy, inv_u)
    return du * (1.0 - rate), back_rms(du * rate, unit, inv_p), jnp.sum(du * diff, axis=0, keepdims=True)


HALF = ROWS // 2


def mid_kernel(
    length, part0, st, cot, rate_a, rate_m, su, sg, uq, wd_in, gz,
    result, d_st, dm, ha, hd, vec,
    buf, low, xg, dd, wu, wg, wd, up, gate, hid, dug, part, xt, ht, mixed, first, dfirst, ga, gd, ra, rd, rdy,
    ps, pr, gs, gr, s2, r2, s3, r3, sx, rx, sy, ry, lo,
):
    x, c, z, y = here()
    sib = dev(x, 1 - c, z, y)
    half = pl.ds(pl.multiple_of(c * 640, 128), 640)
    other = pl.ds(pl.multiple_of((1 - c) * 640, 128), 640)
    to_x = [None] + [dev(step(x, d), c, z, y) for d in (1, 2, 3)]
    to_y = [None] + [dev(x, c, z, step(y, d)) for d in (1, 2, 3)]

    def cut(k):
        return pl.ds(k * HALF, HALF)

    def scatter(n, src, k):
        for p in range(2):
            oz = owner_z(c, p)
            for oc in range(2):
                mine = jnp.logical_and(c == oc, z == oz)
                piece, to = src.at[p, oc, cut(k)], buf.at[n, z, cut(k)]

                @pl.when(mine)
                def _(piece=piece, to=to):
                    lcopy(piece, to, pr.at[n, k, z]).start()

                @pl.when(jnp.logical_not(mine))
                def _(piece=piece, to=to, p=p, oc=oc, oz=oz):
                    rcopy(piece, to, ps.at[n, k, p, oc], pr.at[n, k, z], dev(x, oc, oz, y)).start()

    def scatter_take(n, k):
        for i in range(4):
            landed(buf.at[n, i, cut(k)], pr.at[n, k, i])
        return total_of(buf.at[n, :, cut(k)])

    def scatter_sent(n, src):
        for k in range(2):
            for p in range(2):
                for oc in range(2):
                    mine = jnp.logical_and(c == oc, z == owner_z(c, p))

                    @pl.when(jnp.logical_not(mine))
                    def _(k=k, p=p, oc=oc):
                        landed(src.at[p, oc, cut(k)], ps.at[n, k, p, oc])

    def gather(n, dst, k):
        w = worker(z)
        piece, to, sem = low.at[n, cut(k)], dst.at[z // 2, c, cut(k)], gr.at[n, k, z // 2, c]
        for d in (1, 3, 2):
            rcopy(piece, to, gs.at[n, k, d], sem, dev(x, w, step(z, d), y)).start()

        @pl.when(c == w)
        def _():
            lcopy(piece, to, sem).start()

        @pl.when(c != w)
        def _():
            rcopy(piece, to, gs.at[n, k, 0], sem, dev(x, w, z, y)).start()

    def gather_take(n, dst, k):
        for p in range(2):
            for i in range(2):
                landed(dst.at[p, i, cut(k)], gr.at[n, k, p, i])

    def gather_sent(n):
        for k in range(2):
            for d in (1, 2, 3):
                landed(low.at[n, cut(k)], gs.at[n, k, d])

            @pl.when(c != worker(z))
            def _(k=k):
                landed(low.at[n, cut(k)], gs.at[n, k, 0])

    greet(z_peers(x, c, z, y) + to_x[1:] + to_y[1:])
    for k in range(2):
        scatter(0, part0, k)
    for d in (1, 3, 2):
        rcopy(uq, wu.at[x, :, :, half], s2.at[0, d], r2.at[0, x], to_x[d]).start()
        rcopy(gz, wg.at[:, y, :, half], s2.at[1, d], r2.at[1, y], to_y[d]).start()
    rcopy(uq, wu.at[x, :, :, half], s3.at[0, 0], r3.at[0, x], sib).start()
    rcopy(gz, wg.at[:, y, :, half], s3.at[1, 0], r3.at[1, y], sib).start()
    lcopy(uq, wu.at[x, :, :, half], lo.at[0]).start()
    lcopy(gz, wg.at[:, y, :, half], lo.at[1]).start()
    lcopy(wd_in, wd, lo.at[2]).start()
    vec[...] = jnp.zeros_like(vec)

    for k in range(2):
        total = scatter_take(0, k)
        out = mix_of(st[cut(k)].astype(F32), total, rate_a[0:1])[0]
        low[0, cut(k)] = out.astype(BF)
        gather(0, xg, k)
        mixed[cut(k)] = total
        first[cut(k)] = out

    for d in (1, 3, 2):
        x2, y2 = step(x, d), step(y, d)
        landed(wu.at[x2, :, :, half], r2.at[0, x2])
        rcopy(wu.at[x2, :, :, half], wu.at[x2, :, :, half], s3.at[0, d], r3.at[0, x2], sib).start()
        landed(wg.at[:, y2, :, half], r2.at[1, y2])
        rcopy(wg.at[:, y2, :, half], wg.at[:, y2, :, half], s3.at[1, d], r3.at[1, y2], sib).start()
    landed(wu.at[x, :, :, half], lo.at[0])
    landed(wg.at[:, y, :, half], lo.at[1])
    landed(wd, lo.at[2])
    for k in range(4):
        landed(wu.at[k, :, :, other], r3.at[0, k])
        landed(wg.at[:, k, :, other], r3.at[1, k])

    def rows_of(ref, k):
        return ref[:, :, cut(k)].reshape(4 * HALF, D)

    def forward(k):
        gather_take(0, xg, k)

        def cols(t, carry):
            cs = pl.ds(pl.multiple_of(t * 256, 256), 256)
            xs = rows_of(xg, k)
            u = jnp.dot(xs, wu[:, :, :, cs].reshape(D, 256), preferred_element_type=F32)
            g = jnp.dot(xs, wg[:, :, :, cs].reshape(D, 256), preferred_element_type=F32)
            tt = g * sg[0:1, cs]
            up[k, :, cs] = u
            gate[k, :, cs] = g
            hid[k, :, cs] = (u * su[0:1, cs] * (tt * jax.nn.sigmoid(tt))).astype(BF)
            return carry

        lax.fori_loop(0, 5, cols, 0)

        def down(t, carry):
            cs = pl.ds(pl.multiple_of(t * 256, 256), 256)
            v = jnp.dot(hid[k], wd[:, cs], preferred_element_type=F32)
            part[0, :, :, cut(k), cs] = v.astype(BF).reshape(2, 2, HALF, 256)
            return carry

        lax.fori_loop(0, 5, down, 0)
        scatter(1, part.at[0], k)

    for k in range(2):
        forward(k)

    def turn(dst, load):
        def body(t, carry):
            cs = pl.ds(pl.multiple_of(t * 256, 256), 256)
            for k in range(2):
                dst[cs, k * 256 : (k + 1) * 256] = load(k, cs).T
            return carry

        lax.fori_loop(0, 5, body, 0)

    turn(ht, lambda k, cs: hid[k, :, cs])
    am = rate_m[0:1]
    at = (c * 16 + z * 4 + y) * ROWS
    for k in range(2):
        total = scatter_take(1, k)
        position = at + k * HALF + lax.broadcasted_iota(jnp.int32, (HALF, 1), 0)
        live = (position < length[0]).astype(F32)
        base = first[cut(k)]
        d_base, d_part, g_am = mix_back(cot[cut(k)].astype(F32) * live, base, total, am)
        low[1, cut(k)] = d_part.astype(BF)
        gather(1, dd, k)
        dfirst[cut(k)] = d_base
        vec[1:2] += g_am
        result[cut(k)] = (mix_of(base, total, am)[0] * live).astype(BF)
    turn(xt, lambda k, cs: xg[:, :, cut(k), cs].reshape(256, 256))

    def backward(k):
        gather_take(1, dd, k)

        def cols(t, carry):
            cs = pl.ds(pl.multiple_of(t * 256, 256), 256)
            dh = nt(rows_of(dd, k), wd[cs, :])
            u, g = up[k, :, cs], gate[k, :, cs]
            sc, sgc = su[0:1, cs], sg[0:1, cs]
            tt = g * sgc
            sig = jax.nn.sigmoid(tt)
            silu = tt * sig
            dsilu = sig * (1.0 + tt * (1.0 - sig))
            dhs = dh * sc
            dhu = dh * u
            both = dhu * dsilu * sc
            dug[0, k, :, cs] = (dhs * silu).astype(BF)
            dug[1, k, :, cs] = (both * sgc).astype(BF)
            vec[2:3, cs] += jnp.sum(dhu * silu, axis=0, keepdims=True)
            vec[3:4, cs] += jnp.sum(both * g, axis=0, keepdims=True)
            return carry

        lax.fori_loop(0, 5, cols, 0)
        for t in range(2):
            v = nt(dug[0, k], wu[2 * t : 2 * t + 2].reshape(640, D)) + nt(
                dug[1, k], wg[2 * t : 2 * t + 2].reshape(640, D)
            )
            part[1, :, :, cut(k), t * 640 : (t + 1) * 640] = v.astype(BF).reshape(2, 2, HALF, 640)
        scatter(2, part.at[1], k)

    for k in range(2):
        backward(k)

    def meet(k):
        dy = dfirst[cut(k)] + scatter_take(2, k)
        d_res, d_part, g_aa = mix_back(dy, st[cut(k)].astype(F32), mixed[cut(k)], rate_a[0:1])
        low[2, cut(k)] = d_part.astype(BF)
        gather(2, dm, k)
        d_st[cut(k)] = d_res
        vec[0:1] += g_aa

    def grad_down(i, carry):
        w = jnp.where(i == 0, 1 - c, c)
        cols = pl.ds(pl.multiple_of(w * 640, 128), 640)
        for k in range(4):
            rhs = jnp.concatenate([dd[:, :, cut(j), cols].reshape(256, 640) for j in range(2)], axis=0)
            v = jnp.dot(ht[k * 320 : (k + 1) * 320, :], rhs, preferred_element_type=F32)
            gd[w, k] = v.astype(BF).reshape(4, 80, 640)

        @pl.when(i == 0)
        def _():
            rcopy(gd.at[1 - c], rd, sx.at[1], rx.at[1], sib).start()

        return carry

    def grad_up(w):
        def body(k, carry):
            rows = pl.ds(pl.multiple_of(k * 320, 64), 320)
            for t in range(2):
                cs = slice(t * 640, (t + 1) * 640)
                v = jnp.dot(xt[rows, :], dug[w, :, :, cs].reshape(512, 640), preferred_element_type=F32)
                ga[w, k, :, :, cs] = v.astype(BF).reshape(4, 80, 640)
            return carry

        lax.fori_loop(0, 4, body, 0)

    lax.fori_loop(0, 2, grad_down, 0)
    meet(0)
    landed(rd, rx.at[1])

    def add_d(k, carry):
        i, j = k // 4, k % 4
        rd[i, j] = (gd[c, i, j].astype(F32) + rd[i, j].astype(F32)).astype(BF)
        return carry

    lax.fori_loop(0, 16, add_d, 0)
    for d in (1, 3, 2):
        rcopy(rd.at[step(y, d)], rdy.at[y], sy.at[d], ry.at[y], to_y[d]).start()
    grad_up(1 - c)
    rcopy(ga.at[1 - c], ra, sx.at[0], rx.at[0], sib).start()
    meet(1)
    grad_up(c)
    landed(ra, rx.at[0])

    def add_a(k, carry):
        i, j = k // 4, k % 4
        ha[i, j] = (ga[c, i, j].astype(F32) + ra[i, j].astype(F32)).astype(BF)
        return carry

    lax.fori_loop(0, 16, add_a, 0)
    for d in (1, 2, 3):
        landed(rdy.at[step(y, d)], ry.at[step(y, d)])

    def sum_d(k, carry):
        v = rd[y, k].astype(F32)
        for d in (1, 2, 3):
            v = v + rdy[step(y, d), k].astype(F32)
        hd[k] = v.astype(BF)
        return carry

    lax.fori_loop(0, 4, sum_d, 0)
    for k in range(2):
        gather_take(2, dm, k)
    for n in range(3):
        gather_sent(n)
    for n, src in ((0, part0), (1, part.at[0]), (2, part.at[1])):
        scatter_sent(n, src)
    for i in range(2):
        for k in range(4):
            landed(gz, s3.at[i, k])
        for d in (1, 2, 3):
            landed(gz, s2.at[i, d])
    landed(ra, sx.at[0])
    landed(rd, sx.at[1])
    for d in (1, 2, 3):
        landed(rdy.at[y], sy.at[d])


def middle(length, part0, st, cot, rate_a, rate_m, su, sg, uq, wd, gz):
    V = pltpu.VMEM
    return remote_call(
        mid_kernel,
        [
            ((ROWS, D), BF, "v"),
            ((ROWS, D), F32, "v"),
            ((2, 2, ROWS, D), BF, "a"),
            ((4, 4, 80, D), BF, "v"),
            ((4, 80, 640), BF, "v"),
            ((8, D), F32, "v"),
        ],
        "savvvvvvaaa",
        [
            V((3, 4, ROWS, D), BF), V((3, ROWS, D), BF), V((2, 2, ROWS, D), BF), V((2, 2, ROWS, D), BF),
            V((4, 4, 80, D), BF), V((4, 4, 80, D), BF), V((D, D), BF),
            V((2, 256, D), F32), V((2, 256, D), F32), V((2, 256, D), BF), V((2, 2, 256, D), BF),
            V((2, 2, 2, ROWS, D), BF), V((D, 512), BF), V((D, 512), BF),
            V((ROWS, D), F32), V((ROWS, D), F32), V((ROWS, D), F32),
            V((2, 4, 4, 80, D), BF), V((2, 4, 4, 80, 640), BF), V((4, 4, 80, D), BF), V((4, 4, 80, 640), BF),
            V((4, 4, 80, 640), BF),
            dma(3, 2, 2, 2), dma(3, 2, 4), dma(3, 2, 4), dma(3, 2, 2, 2),
            dma(2, 4), dma(2, 4), dma(2, 4), dma(2, 4), dma(2), dma(2), dma(4), dma(4), dma(3),
        ],
        2,
        "middle",
    )(length, part0, st, cot, rate_a, rate_m, su, sg, uq, wd, gz)


CUT = 768


def back_kernel(
    length, q, kv_in, wo, dmix, att, lse, ha, hd, tt_in, xg_in, wq_in, scale, inner, outer, vec,
    pbuf, za, zd, zq, o_out, o_vec,
    kv, tt, xg, wq,
    qdo, delta, dqt, acc, low, give, mine, got, got_y, dq, dd, sums, part, gq, go,
    oax, oay, rax, ray, fax, fay, fd, hq, rqx, rqy, fqx, fqy, ob, ox, o2, vs, vb, ws, wb,
    lo, sg, rg, sy, ry, s1, r1, s2, r2, s3, r3, sz, rz, sc, rc, q1, p1, q2, p2, q3, p3, so, ro, sv, rv, sw, rw, ps, pr, sf, rf,
):
    x, c, z, y = here()
    sib = dev(x, 1 - c, z, y)
    to_y = [None] + [dev(x, c, z, step(y, d)) for d in (1, 2, 3)]
    to_x = [None] + [dev(step(x, d), c, z, y) for d in (1, 2, 3)]
    to_z = [None] + [dev(x, c, step(z, d), y) for d in (1, 2, 3)]
    near_first = (1, 3, 2)
    lcopy(kv_in, kv, lo.at[0]).start()
    lcopy(ha.at[x, :, :, 0:CUT], oax, lo.at[1]).start()
    lcopy(ha.at[:, y, :, CUT:D], oay, lo.at[2]).start()
    lcopy(tt_in, tt, lo.at[3]).start()
    lcopy(xg_in, xg, lo.at[4]).start()
    lcopy(wq_in, wq, lo.at[5]).start()
    greet(z_peers(x, c, z, y) + to_y[1:] + to_x[1:])
    for d in near_first:
        rcopy(hd.at[step(x, d)], fd.at[x], s2.at[1, d], r2.at[1, x], to_x[d]).start()
    for d in near_first:
        rcopy(ha.at[step(x, d), :, :, 0:CUT], rax.at[x], s1.at[0, d], r1.at[0, x], to_x[d]).start()
        rcopy(ha.at[:, step(y, d), :, CUT:D], ray.at[y], s1.at[1, d], r1.at[1, y], to_y[d]).start()

    def settle(h):
        landed(got.at[h], rg.at[h])
        for i in range(2):
            for k in range(2):
                mine[h, i, k] = (mine[h, i, k].astype(F32) + got[h, i, k].astype(F32)).astype(BF)
        for d in near_first:
            rcopy(mine.at[h, :, :, step(y, d)], got_y.at[h, y], sy.at[h, d], ry.at[h, y], to_y[d]).start()

    d_att = nt(dmix[...], wo[...]).astype(BF)
    for h in range(HG):
        low[:, h * HDIM : (h + 1) * HDIM] = att[h].astype(BF)
        dh = d_att[:, h * HDIM : (h + 1) * HDIM].astype(F32)
        wide = jnp.concatenate([jnp.zeros_like(dh), dh], axis=1).astype(BF)
        prod = dh * att[h]
        for j in range(BLOCKS):
            rows = slice(j * ROWS, (j + 1) * ROWS)
            qdo[h, j, :ROWS] = q[h, rows, :]
            qdo[h, j, ROWS:] = wide[rows]
            delta[h, j : j + 1, :] = jnp.sum(prod[rows].T, axis=0, keepdims=True)
    rcopy(vec, vb.at[0], sv.at[0, 0], rv.at[0, 0], sib).start()

    def small_start():
        for k in range(2):
            g = tn(low[...], dmix[:, k * 640 : (k + 1) * 640])
            go[k] = g.astype(BF).reshape(4, 80, 640)
        rcopy(go.at[1 - c], ob, sc.at[1], rc.at[1], sib).start()

    def small_cores():
        landed(ob, rc.at[1])
        landed(vb.at[0], rv.at[0, 0])
        vs[...] = vec[...] + vb[0]
        for k in range(4):
            ob[k] = (go[c, k].astype(F32) + ob[k].astype(F32)).astype(BF)
        for d in near_first:
            rcopy(ob.at[step(y, d)], ox.at[y], so.at[0, d], ro.at[0, y], to_y[d]).start()
            rcopy(vs, vb.at[d], sv.at[1, d], rv.at[1, d], to_y[d]).start()

    def small_y():
        v, tot = ob[y].astype(F32), vs[...]
        for d in (1, 2, 3):
            landed(ox.at[step(y, d)], ro.at[0, step(y, d)])
            landed(vb.at[d], rv.at[1, d])
            landed(vs, sv.at[1, d])
            v = v + ox[step(y, d)].astype(F32)
            tot = tot + vb[d]
        ox[y] = v.astype(BF)
        vs[...] = tot
        for d in near_first:
            rcopy(ox.at[y], o2.at[d], so.at[1, d], ro.at[1, d], to_x[d]).start()
            rcopy(vs, vb.at[3 + d], sv.at[2, d], rv.at[2, d], to_x[d]).start()

    def small_x():
        v, tot = ox[y].astype(F32), vs[...]
        for d in (1, 2, 3):
            landed(o2.at[d], ro.at[1, d])
            landed(vb.at[3 + d], rv.at[2, d])
            landed(vs, sv.at[2, d])
            v = v + o2[d].astype(F32)
            tot = tot + vb[3 + d]
        o_out[c] = v.astype(BF)
        vs[...] = tot
        rcopy(o_out.at[c], o_out.at[c], sf.at[3], rf.at[3], sib).start()
        for d in near_first:
            rcopy(vs, vb.at[6 + d], sv.at[3, d], rv.at[3, d], to_z[d]).start()

    def small_z():
        tot = vs[...]
        for d in (1, 2, 3):
            landed(vb.at[6 + d], rv.at[3, d])
            landed(vs, sv.at[3, d])
            tot = tot + vb[6 + d]
        o_vec[0:2] = tot[0:2]
        o_vec[2:] = vs[2:]

    def down_x():
        v = hd[x].astype(F32)
        for d in (1, 2, 3):
            landed(fd.at[step(x, d)], r2.at[1, step(x, d)])
            v = v + fd[step(x, d)].astype(F32)
        zd[c, x] = v.astype(BF)
        for d in near_first:
            rcopy(zd.at[c, x], zd.at[c, x], s3.at[1, d], r3.at[1, x], to_x[d]).start()

    def down_done():
        for d in (1, 2, 3):
            landed(zd.at[c, step(x, d)], r3.at[1, step(x, d)])
        rcopy(zd.at[c], zd.at[c], sf.at[1], rf.at[1], sib).start()

    def up_first():
        landed(oax, lo.at[1])
        landed(oay, lo.at[2])
        for d in (1, 2, 3):
            landed(rax.at[step(x, d)], r1.at[0, step(x, d)])
            landed(ray.at[step(y, d)], r1.at[1, step(y, d)])

        def body(k, carry):
            v, w = oax[k].astype(F32), oay[k].astype(F32)
            for d in (1, 2, 3):
                v = v + rax[step(x, d), k].astype(F32)
                w = w + ray[step(y, d), k].astype(F32)
            oax[k] = v.astype(BF)
            oay[k] = w.astype(BF)
            return carry

        lax.fori_loop(0, 4, body, 0)
        for d in near_first:
            rcopy(oax.at[step(y, d)], fax.at[y], s2.at[0, d], r2.at[0, y], to_y[d]).start()
            rcopy(oay.at[step(x, d)], fay.at[x], s2.at[2, d], r2.at[2, x], to_x[d]).start()

    landed(kv, lo.at[0])
    item = work_items(c, y, length[0])

    def per_head(h, carry):
        acc[...] = jnp.zeros_like(acc)
        dqt[...] = jnp.zeros_like(dqt)
        for k, f in ((1, small_start), (2, small_cores), (3, small_y), (2, down_x), (4, small_x), (4, down_done)):
            pl.when(h == k)(f)

        def body(g, carry):
            @pl.when(jnp.logical_and(g == 1, h > 0))
            def _():
                settle(h - 1)

            pl.when(jnp.logical_and(g == 0, h == HG - 1))(up_first)
            key = lax.broadcasted_iota(jnp.int32, (TILE, ROWS), 0)
            its = [item(g * STEP + u) for u in range(STEP)]
            ks = [key_tile(kv, h, t) for _, t, _ in its]
            bs = [qdo[h, j] for j, _, _ in its]
            sds = [nt(k, b) for k, b in zip(ks, bs)]
            dss, pp = [], []
            for sd, (j, _, bound) in zip(sds, its):
                p = jnp.where(key <= bound, jnp.exp(sd[:, :ROWS] - lse[h, pl.ds(j, 1), :]), 0.0)
                dss.append((p * (sd[:, ROWS:] - delta[h, pl.ds(j, 1), :])).astype(BF))
                pp.append(p.astype(BF))
            for ds, p, b, (_, t, _) in zip(dss, pp, bs, its):
                acc[t] += jnp.dot(jnp.concatenate([ds, p], axis=1), b, preferred_element_type=F32)
            for k, ds, (j, _, _) in zip(ks, dss, its):
                dqt[j] += tn(k, ds)
            return carry

        lax.fori_loop(0, 18 // STEP, body, 0)

        def store(i, carry):
            zi, k = i // 2, i % 2
            give[h, zi, k] = acc[k * 4 + owner_z(1 - c, zi)].astype(BF).reshape(4, ROWS, 128)
            mine[h, zi, k] = acc[k * 4 + owner_z(c, zi)].astype(BF).reshape(4, ROWS, 128)
            return carry

        lax.fori_loop(0, 4, store, 0, unroll=True)
        rcopy(give.at[h], got.at[h], sg.at[h], rg.at[h], sib).start()
        for j in range(BLOCKS):
            dq[h, j * ROWS : (j + 1) * ROWS, :] = dqt[j].T * 0.125
        return carry

    lax.fori_loop(0, HG, per_head, 0)
    settle(HG - 1)
    for d in (1, 2, 3):
        landed(fax.at[step(y, d)], r2.at[0, step(y, d)])
        landed(fay.at[step(x, d)], r2.at[2, step(x, d)])
    v, w = oax[y].astype(F32), oay[x].astype(F32)
    for d in (1, 2, 3):
        v = v + fax[step(y, d)].astype(F32)
        w = w + fay[step(x, d)].astype(F32)
    za[2, x, :, 0:CUT] = v.astype(BF)
    za[2, x, :, CUT:D] = w.astype(BF)
    for d in near_first:
        rcopy(za.at[2, x], za.at[2, x], s3.at[0, d], r3.at[0, x], to_x[d]).start()
    ws[...] = jnp.zeros_like(ws)
    landed(tt, lo.at[3])
    landed(xg, lo.at[4])
    landed(wq, lo.at[5])
    sums[...] = jnp.zeros_like(sums)
    lane = lanes()

    def through(h, carry):
        for d in (1, 2, 3):
            landed(got_y.at[h, step(y, d)], ry.at[h, step(y, d)])
        cols = pl.ds(pl.multiple_of(h * 128, 128), 128)
        pair = pl.ds(pl.multiple_of(640 + (h // 2) * 128, 128), 128)
        odd = h % 2 == 1

        def per_block(j, carry):
            i, k = j // 2, j % 2
            rows = pl.ds(pl.multiple_of(j * ROWS, ROWS), ROWS)
            cosine, sine = turn_of(inner, outer, block_index(c, y, j))
            grads = mine[h, i, k, y].astype(F32)
            for d in (1, 2, 3):
                grads = grads + got_y[h, step(y, d), i, k].astype(F32)
            grads = grads.astype(BF).astype(F32)
            turned = pltpu.roll(grads, 64, 1)
            t = tt[h, rows, :]
            dy = jnp.where(lane < 64, dq[h, rows, :].astype(BF).astype(F32), turned)
            inv = lax.rsqrt(half_means(t * t, lane) + EPS)
            unit = t * inv
            sums[:, cols] += jnp.sum((dy * unit).reshape(ROWS // 8, 8, 128), axis=0)
            dyh = dy * scale[0:1, cols]
            dt = (dyh - unit * half_means(dyh * unit, lane)) * inv
            dd[rows, cols] = (dt * cosine + swap(dt * sine, lane)).astype(BF)
            before = jnp.where(odd, dd[rows, pair].astype(F32), turned)
            dd[rows, pair] = jnp.where(lane < 64, before, jnp.where(odd, grads, 0.0)).astype(BF)
            return carry

        lax.fori_loop(0, BLOCKS, per_block, 0, unroll=True)
        return carry

    lax.fori_loop(0, HG, through, 0)
    small_z()

    def inputs(p, carry):
        rows = pl.ds(pl.multiple_of(p * 256, 256), 256)
        v = nt(dd[rows, 0:512], wq[0].reshape(D, 512)) + nt(dd[rows, 512:1024], wq[1].reshape(D, 512))
        part[p] = v.astype(BF).reshape(2, ROWS, D)
        z_scatter_pair(part, pbuf, ps, pr, p, x, c, z, y)
        return carry

    def along_z():
        for d in (1, 2, 3):
            landed(za.at[2, step(x, d)], r3.at[0, step(x, d)])
        for d in near_first:
            rcopy(za.at[2, step(z, d)], za.at[c, z], sz.at[0, d], rz.at[0, z], to_z[d]).start()
        za[c, z] = za[2, z]

    def weights(i, carry):
        h = jnp.where(i == 0, 1 - c, c)
        cols = pl.ds(pl.multiple_of(h * 512, 128), 512)
        gq[h] = tn(xg[...].reshape(512, D), dd[:, cols]).astype(BF).reshape(4, 4, 80, 512)

        @pl.when(i == 0)
        def _():
            rcopy(gq.at[1 - c], hq, sc.at[0], rc.at[0], sib).start()
            along_z()
            lax.fori_loop(0, 2, inputs, 0)

        return carry

    lax.fori_loop(0, 2, weights, 0)
    for h in range(HG):
        v = jnp.sum(sums[:, h * 128 : (h + 1) * 128], axis=0, keepdims=True)
        ws[:, h * HDIM : (h + 1) * HDIM] = jnp.broadcast_to(v[:, :HDIM] + v[:, HDIM:], (8, HDIM))
    rcopy(ws, wb.at[0], sw.at[0, 0], rw.at[0, 0], sib).start()

    landed(hq, rc.at[0])

    def add_q(k, carry):
        i, j = k // 4, k % 4
        v = (gq[c, i, j].astype(F32) + hq[i, j].astype(F32)).astype(BF)
        fqx[i, j] = v[:, :256]
        fqy[j, i] = v[:, 256:]
        return carry

    lax.fori_loop(0, 16, add_q, 0)
    for d in near_first:
        rcopy(fqx.at[step(x, d)], rqx.at[x], q1.at[0, d], p1.at[0, x], to_x[d]).start()
        rcopy(fqy.at[step(y, d)], rqy.at[y], q1.at[1, d], p1.at[1, y], to_y[d]).start()
    landed(wb.at[0], rw.at[0, 0])
    landed(ws, sw.at[0, 0])
    ws[...] = ws[...] + wb[0]
    for d in near_first:
        rcopy(ws, wb.at[d], sw.at[1, d], rw.at[1, d], to_y[d]).start()
    for d in (1, 2, 3):
        landed(rqx.at[step(x, d)], p1.at[0, step(x, d)])
        landed(rqy.at[step(y, d)], p1.at[1, step(y, d)])

    def add_q1(k, carry):
        a, b = fqx[x, k].astype(F32), fqy[y, k].astype(F32)
        for d in (1, 2, 3):
            a = a + rqx[step(x, d), k].astype(F32)
            b = b + rqy[step(y, d), k].astype(F32)
        rqx[x, k] = a.astype(BF)
        rqy[y, k] = b.astype(BF)
        return carry

    lax.fori_loop(0, 4, add_q1, 0)
    for d in near_first:
        rcopy(rqx.at[x, step(y, d)], fqx.at[4, y], q2.at[0, d], p2.at[0, y], to_y[d]).start()
        rcopy(rqy.at[y, step(x, d)], fqy.at[4, x], q2.at[1, d], p2.at[1, x], to_x[d]).start()
    tot = ws[...]
    for d in (1, 2, 3):
        landed(wb.at[d], rw.at[1, d])
        landed(ws, sw.at[1, d])
        tot = tot + wb[d]
    ws[...] = tot
    for d in near_first:
        rcopy(ws, wb.at[3 + d], sw.at[2, d], rw.at[2, d], to_x[d]).start()
    for d in (1, 2, 3):
        landed(fqx.at[4, step(y, d)], p2.at[0, step(y, d)])
        landed(fqy.at[4, step(x, d)], p2.at[1, step(x, d)])
    a, b = rqx[x, y].astype(F32), rqy[y, x].astype(F32)
    for d in (1, 2, 3):
        a = a + fqx[4, step(y, d)].astype(F32)
        b = b + fqy[4, step(x, d)].astype(F32)
    zq[0, x] = jnp.concatenate([a, b], axis=1).astype(BF)
    for d in near_first:
        rcopy(zq.at[0, x], zq.at[0, x], q3.at[d], p3.at[x], to_x[d]).start()
    tot = ws[...]
    for d in (1, 2, 3):
        landed(wb.at[3 + d], rw.at[2, d])
        landed(ws, sw.at[2, d])
        tot = tot + wb[3 + d]
    o_vec[4:5, 0:384] = tot[0:1]
    for d in (1, 2, 3):
        landed(zq.at[0, step(x, d)], p3.at[step(x, d)])
    for d in near_first:
        rcopy(zq.at[0, step(z, d)], zq.at[1 + c, z], sz.at[1, d], rz.at[1, z], to_z[d]).start()
    zq[1 + c, z] = zq[0, z]
    for d in (1, 2, 3):
        landed(za.at[c, step(z, d)], rz.at[0, step(z, d)])
    rcopy(za.at[c], za.at[c], sf.at[0], rf.at[0], sib).start()
    for d in (1, 2, 3):
        landed(zq.at[1 + c, step(z, d)], rz.at[1, step(z, d)])
    rcopy(zq.at[1 + c], zq.at[1 + c], sf.at[2], rf.at[2], sib).start()
    z_scatter_take(pbuf, pr)
    landed(za.at[1 - c], rf.at[0])
    landed(zd.at[1 - c], rf.at[1])
    landed(zq.at[2 - c], rf.at[2])
    landed(o_out.at[1 - c], rf.at[3])
    def sent(h, carry):
        landed(give.at[h], sg.at[h])
        for d in (1, 2, 3):
            landed(got_y.at[h, y], sy.at[h, d])
        return carry

    lax.fori_loop(0, HG, sent, 0)
    z_scatter_sent(part, ps, c, z)
    landed(hq, sc.at[0])
    landed(ob, sc.at[1])
    landed(vec, sv.at[0, 0])
    landed(o_out.at[0], sf.at[3])
    landed(za.at[0], sf.at[0])
    landed(zd.at[0], sf.at[1])
    landed(zq.at[1], sf.at[2])
    for d in (1, 2, 3):
        landed(rax.at[x], s1.at[0, d])
        landed(ray.at[y], s1.at[1, d])
        landed(fax.at[0], s2.at[0, d])
        landed(fd.at[0], s2.at[1, d])
        landed(fay.at[0], s2.at[2, d])
        landed(za.at[0, 0], s3.at[0, d])
        landed(fd.at[0], s3.at[1, d])
        landed(za.at[0, 0], sz.at[0, d])
        landed(zq.at[0, 0], sz.at[1, d])
        landed(rqx.at[0], q1.at[0, d])
        landed(rqy.at[0], q1.at[1, d])
        landed(fqx.at[0, 0], q2.at[0, d])
        landed(fqy.at[0, 0], q2.at[1, d])
        landed(zq.at[0, 0], q3.at[d])
        landed(ox.at[0], so.at[0, d])
        landed(ox.at[0], so.at[1, d])


def back(length, q, kv, wo, dmix, att, lse, ha, hd, tt, xg, wq, scale, inner, outer, vec):
    n = BLOCKS * ROWS
    V = pltpu.VMEM
    return remote_call(
        back_kernel,
        [
            ((4, ROWS, D), BF, "v"),
            ((3, 4, 80, D), BF, "v"),
            ((2, 4, 80, 640), BF, "v"),
            ((3, 4, 80, 512), BF, "v"),
            ((2, 80, 640), BF, "v"),
            ((8, D), F32, "v"),
        ],
        "svavvvvavaaavvvv",
        [
            V((HG, 2, 2, 2, 4, ROWS, 128), BF), V((HG, n, 128), F32), V((2, 2, ROWS, D), BF), V((2, 4, 4, 80, 512), BF),
            V((HG, BLOCKS, 2 * ROWS, 128), BF), V((HG, BLOCKS, 128), F32), V((BLOCKS, 128, ROWS), F32), V((8, TILE, 128), F32),
            V((n, GROUP), BF),
            V((HG, 2, 2, 4, ROWS, 128), BF), V((HG, 2, 2, 4, ROWS, 128), BF), V((HG, 2, 2, 4, ROWS, 128), BF),
            V((HG, 4, 2, 2, ROWS, 128), BF), V((HG, n, 128), F32), V((n, 1024), BF), V((8, HG * 128), F32),
            V((2, 2, ROWS, D), BF), V((2, 4, 4, 80, 512), BF), V((2, 4, 80, 640), BF),
            V((4, 80, CUT), BF), V((4, 80, D - CUT), BF), V((4, 4, 80, CUT), BF), V((4, 4, 80, D - CUT), BF),
            V((4, 80, CUT), BF), V((4, 80, D - CUT), BF), V((4, 80, 640), BF),
            V((4, 4, 80, 512), BF), V((4, 4, 80, 256), BF), V((4, 4, 80, 256), BF), V((5, 4, 80, 256), BF), V((5, 4, 80, 256), BF),
            V((4, 80, 640), BF), V((4, 80, 640), BF), V((4, 80, 640), BF), V((8, D), F32), V((10, 8, D), F32), V((8, 384), F32), V((7, 8, 384), F32),
            dma(6), dma(HG), dma(HG), dma(HG, 4), dma(HG, 4),
            dma(2, 4), dma(2, 4), dma(3, 4), dma(3, 4), dma(2, 4), dma(2, 4), dma(2, 4), dma(2, 4), dma(2), dma(2),
            dma(2, 4), dma(2, 4), dma(2, 4), dma(2, 4), dma(4), dma(4), dma(2, 4), dma(2, 4), dma(4, 4), dma(4, 4), dma(3, 4), dma(3, 4),
            dma(2, 2), dma(4), dma(4), dma(4),
        ],
        3,
        "back",
    )(length, q, kv, wo, dmix, att, lse, ha, hd, tt, xg, wq, scale, inner, outer, vec)


def finish_kernel(
    res, d_st, pbuf, za, zd, zq, out, vec,
    result, g_in, o_q, o_k, o_v, o_out, o_up, o_gate, o_down, v_qk, v_attn, v_mlp, v_up, v_gate,
):
    _, _, z, y = here()
    step_no = pl.program_id(0)
    result[...] = res[...]
    g_in[...] = d_st[...] + total_of(pbuf)
    o_up[...] = za[0, 0].astype(F32)
    o_gate[...] = za[1, 0].astype(F32)
    for h in range(2):
        o_down[:, h * 640 : (h + 1) * 640] = zd[h, 0].astype(F32)
    a, b = zq[1, 0].astype(F32), zq[2, 0].astype(F32)
    pairs = [a[:, h * 128 : (h + 1) * 128] for h in range(4)] + [b[:, :128]]
    for k in range(4):

        @pl.when(step_no == k)
        def _(at=k * GROUP):
            o_q[:, at : at + GROUP] = jnp.concatenate([v[:, :HDIM] for v in pairs], axis=1)
            o_k[:, at : at + GROUP] = jnp.concatenate([v[:, HDIM:] for v in pairs], axis=1)
            o_v[:, at : at + GROUP] = b[:, 128:448]

    @pl.when(step_no == 0)
    def _():
        o_out[:, :640] = out[0].astype(F32)
        o_out[:, 640:] = out[1].astype(F32)
        v = vec[...]
        by_shard = pltpu.roll(v, (16 - (z * 4 + y)) % 16 * 80, 1)
        by_y = pltpu.roll(v, (4 - y) % 4 * 320, 1)
        v_attn[...] = by_shard[0:1, :80]
        v_mlp[...] = by_shard[1:2, :80]
        v_up[...] = by_y[2:3, :320]
        v_gate[...] = by_y[3:4, :320]
        v_qk[...] = pltpu.roll(v, (16 - y) % 16 * 80, 1)[4:5, :80]


def finish(res, d_st, pbuf, za, zd, zq, out, vec):
    def whole(*shape):
        return pl.BlockSpec(shape, lambda k: (0,) * len(shape))

    rows = ROWS // 4
    outs = [
        ((ROWS, D), BF, pl.BlockSpec((rows, D), lambda k: (k, 0))),
        ((ROWS, D), F32, pl.BlockSpec((rows, D), lambda k: (k, 0))),
        ((80, D), F32, whole(80, D)),
        ((80, D), F32, whole(80, D)),
        ((80, D), F32, whole(80, D)),
        ((80, D), F32, whole(80, D)),
        ((80, FF), F32, pl.BlockSpec((80, D), lambda k: (0, k))),
        ((80, FF), F32, pl.BlockSpec((80, D), lambda k: (0, k))),
        ((320, D), F32, pl.BlockSpec((80, D), lambda k: (k, 0))),
        ((1, 80), F32, whole(1, 80)),
        ((1, 80), F32, whole(1, 80)),
        ((1, 80), F32, whole(1, 80)),
        ((1, 320), F32, whole(1, 320)),
        ((1, 320), F32, whole(1, 320)),
    ]
    return pl.pallas_call(
        finish_kernel,
        grid=(4,),
        out_shape=[jax.ShapeDtypeStruct(s, d) for s, d, _ in outs],
        in_specs=[
            pl.BlockSpec((rows, D), lambda k: (k, 0)),
            pl.BlockSpec((rows, D), lambda k: (k, 0)),
            pl.BlockSpec((4, rows, D), lambda k: (0, k, 0)),
            pl.BlockSpec((2, 1, 80, D), lambda k: (0, k, 0, 0)),
            pl.BlockSpec((2, 1, 80, 640), lambda k: (0, k, 0, 0)),
            pl.BlockSpec((3, 1, 80, 512), lambda k: (0, k, 0, 0)),
            whole(2, 80, 640),
            whole(8, D),
        ],
        out_specs=[spec for _, _, spec in outs],
        compiler_params=pltpu.CompilerParams(vmem_limit_bytes=VMEM_LIMIT),
        name="finish",
    )(res, d_st, pbuf, za, zd, zq, out, vec)


def shards(
    states, w_query, w_key, w_value, w_out, w_up, w_gate, w_down,
    scale_qk, alpha_attn, alpha_mlp, scale_up, scale_gate, lengths, cotangent,
):
    x, c, z, y = here()
    st = states[0]

    vectors = [v.reshape(1, -1) for v in (scale_qk, alpha_attn, alpha_mlp, scale_up, scale_gate)]
    inner, outer = (jnp.asarray(t) for t in rope_tables())
    n = BLOCKS * ROWS
    part, att, lse, kv, q, turned, xg, wqkv, wo, scale, rate_a, rate_m, su, sg, uq, wd, gz = front(
        lengths, st, w_query, w_key, w_value, vectors, w_out, w_up, w_gate, w_down, inner, outer
    )
    result, d_st, dm, ha, hd, vec = middle(
        lengths, part, st, cotangent[0], rate_a, rate_m, su, sg, uq, wd.reshape(D, D), gz
    )
    pbuf, za, zd, zq, out, vec = back(
        lengths, q, kv, wo.reshape(GROUP, D), dm.reshape(n, D), att, lse, ha, hd, turned, xg, wqkv, scale, inner, outer, vec
    )
    outs = finish(result, d_st, pbuf, za, zd, zq, out, vec)
    return (outs[0][None], outs[1][None], *outs[2:9], *(v.reshape(-1) for v in outs[9:]))


def solution(mesh):
    row = P("grp", ("seq", "shard"), None)
    mat = P("shard", None)
    one = P("shard")
    return jax.shard_map(
        shards,
        mesh=mesh,
        in_specs=(row,) + (mat,) * 7 + (one,) * 5 + (P("grp"), row),
        out_specs=(row, row) + (mat,) * 7 + (one,) * 5,
        check_vma=False,
    )
```

```python
import functools
import math

import jax
import jax.numpy as jnp
import numpy as np
from jax import lax
from jax.experimental import pallas as pl
from jax.experimental.pallas import tpu as pltpu
from jax.sharding import PartitionSpec as P


D, HEADS, HDIM, FF = 1280, 20, 64, 5120
ROWS, BLOCKS, HG = 128, 4, 5
GROUP = HG * HDIM
EPS = 1e-6
BF, F32 = jnp.bfloat16, jnp.float32
MESH = pl.DeviceIdType.MESH
VMEM_LIMIT = 60 << 20


def here():
    s = lax.axis_index("shard")
    return lax.axis_index("grp"), lax.axis_index("seq"), s // 4, s % 4


def dev(x, c, z, y):
    return (x, c, z * 4 + y)


def worker(z):
    return ((z + 1) // 2) % 2


def owner_z(w, i):
    return i * (3 - 2 * w) + w


def step(v, d):
    return (v + d) % 4


def rcopy(src, dst, ss, rs, to):
    return pltpu.make_async_remote_copy(
        src_ref=src, dst_ref=dst, send_sem=ss, recv_sem=rs, device_id=to, device_id_type=MESH
    )


def lcopy(src, dst, sem):
    return pltpu.make_async_copy(src, dst, sem)


def landed(dst, sem):
    pltpu.make_async_copy(dst, dst, sem).wait()


def greet(peers):
    bar = pltpu.get_barrier_semaphore()
    for p in peers:
        pl.semaphore_signal(bar, inc=1, device_id=p, device_id_type=MESH)
    pl.semaphore_wait(bar, len(peers))


def z_peers(x, c, z, y):
    far = [dev(x, cc, step(z, d), y) for d in (1, 2, 3) for cc in (0, 1)]
    return [dev(x, 1 - c, z, y)] + far


def z_gather_start(src, dst, ss, rs, x, c, z, y):
    w = worker(z)
    slot = (z // 2, c)
    for d in (1, 3, 2):
        rcopy(src, dst.at[slot], ss.at[d], rs.at[slot], dev(x, w, step(z, d), y)).start()

    @pl.when(c == w)
    def _():
        lcopy(src, dst.at[slot], rs.at[slot]).start()

    @pl.when(c != w)
    def _():
        rcopy(src, dst.at[slot], ss.at[0], rs.at[slot], dev(x, w, z, y)).start()


def z_gather_take(dst, rs, p):
    for k in range(2):
        landed(dst.at[p, k], rs.at[p, k])


def z_gather_sent(src, ss, c, z):
    for d in (1, 2, 3):
        landed(src, ss.at[d])

    @pl.when(c != worker(z))
    def _():
        landed(src, ss.at[0])


def z_gather_wait(src, dst, ss, rs, c, z):
    for p in range(2):
        z_gather_take(dst, rs, p)
    z_gather_sent(src, ss, c, z)


def z_scatter_pair(part, dst, ss, rs, p, x, c, z, y):
    oz = owner_z(c, p)
    for oc in range(2):
        mine = jnp.logical_and(c == oc, z == oz)

        @pl.when(mine)
        def _(oc=oc):
            lcopy(part.at[p, oc], dst.at[z], rs.at[z]).start()

        @pl.when(jnp.logical_not(mine))
        def _(oc=oc):
            rcopy(part.at[p, oc], dst.at[z], ss.at[p, oc], rs.at[z], dev(x, oc, oz, y)).start()


def z_scatter_start(part, dst, ss, rs, x, c, z, y):
    for p in range(2):
        z_scatter_pair(part, dst, ss, rs, p, x, c, z, y)


def z_scatter_take(dst, rs):
    for k in range(4):
        landed(dst.at[k], rs.at[k])


def z_scatter_sent(part, ss, c, z):
    for p in range(2):
        for oc in range(2):
            mine = jnp.logical_and(c == oc, z == owner_z(c, p))

            @pl.when(jnp.logical_not(mine))
            def _(p=p, oc=oc):
                landed(part.at[p, oc], ss.at[p, oc])


def remote_call(kernel, outs, ins_spaces, scratch, cid, name):
    spec = {
        "a": pl.BlockSpec(memory_space=pl.ANY),
        "v": pl.BlockSpec(memory_space=pltpu.VMEM),
        "s": pl.BlockSpec(memory_space=pltpu.SMEM),
    }
    return pl.pallas_call(
        kernel,
        out_shape=[jax.ShapeDtypeStruct(s, d) for s, d, _ in outs],
        in_specs=[spec[s] for s in ins_spaces],
        out_specs=[spec[s] for _, _, s in outs],
        scratch_shapes=scratch,
        compiler_params=pltpu.CompilerParams(
            collective_id=cid, has_side_effects=True, vmem_limit_bytes=VMEM_LIMIT
        ),
        name=name,
    )


def local_call(kernel, outs, n_in, scratch, name, smem=0):
    vmem = pl.BlockSpec(memory_space=pltpu.VMEM)
    sm = pl.BlockSpec(memory_space=pltpu.SMEM)
    return pl.pallas_call(
        kernel,
        out_shape=[jax.ShapeDtypeStruct(s, d) for s, d in outs],
        in_specs=[sm] * smem + [vmem] * n_in,
        out_specs=[vmem for _ in outs],
        scratch_shapes=scratch,
        compiler_params=pltpu.CompilerParams(vmem_limit_bytes=VMEM_LIMIT),
        name=name,
    )


def dma(*shape):
    return pltpu.SemaphoreType.DMA(shape)


def rope_tables():
    freqs = np.exp(np.arange(32) * (-2.0 * math.log(10000.0) / 64))
    freqs = np.tile(freqs, 4)
    sign = np.tile(np.concatenate([-np.ones(32), np.ones(32)]), 2)
    inner = np.arange(ROWS)[:, None] * freqs
    outer = (np.arange(32) * ROWS)[:, None] * freqs
    return (
        np.stack([np.cos(inner), np.sin(inner) * sign]).astype(np.float32),
        np.stack([np.cos(outer), np.sin(outer) * sign]).astype(np.float32),
    )


def block_index(c, y, j):
    return (j % 2) * 16 + owner_z(c, j // 2) * 4 + y


def turn_of(inner, outer, b):
    oc = outer[0, pl.ds(b, 1), :]
    os = outer[1, pl.ds(b, 1), :]
    return oc * inner[0] - os * inner[1], os * inner[0] + oc * inner[1]


def lanes():
    return lax.broadcasted_iota(jnp.int32, (ROWS, 128), 1)


def swap(v, lane):
    return jnp.where(lane % 64 < 32, pltpu.roll(v, 96, 1), pltpu.roll(v, 32, 1))


def half_means(v, lane):
    low = jnp.sum(jnp.where(lane < 64, v, 0.0), axis=-1, keepdims=True)
    high = jnp.sum(jnp.where(lane < 64, 0.0, v), axis=-1, keepdims=True)
    return jnp.where(lane < 64, low, high) * (1.0 / 64)


TILE = 512
STEP = 6


def tiles_of(c, j):
    return (j % 2) * 4 + owner_z(c, j // 2) + 1


def nt(a, b):
    return lax.dot_general(a, b, (((1,), (1,)), ((), ())), preferred_element_type=F32)


def tn(a, b):
    return lax.dot_general(a, b, (((0,), (0,)), ((), ())), preferred_element_type=F32)


def key_tile(ref, h, t):
    zz = t % 4
    return ref[h, worker(zz), zz // 2, t // 4].reshape(TILE, 128)


def work_items(c, y, length):
    n = [tiles_of(c, j) for j in range(BLOCKS)]
    starts = [n[0], n[0] + n[1], n[0] + n[1] + n[2]]
    query = lax.broadcasted_iota(jnp.int32, (1, ROWS), 1)

    def item(i):
        hits = [(i >= s).astype(jnp.int32) for s in starts]
        j = hits[0] + hits[1] + hits[2]
        t = i - hits[0] * n[0] - hits[1] * n[1] - hits[2] * n[2]
        last = query + y * ROWS + (tiles_of(c, j) - 1 - t) * TILE
        return j, t, jnp.minimum(last, length - 1 - t * TILE)

    return item


def columns(ref, k, half):
    return ref.at[:, pl.ds(pl.multiple_of(k * D + half * 640, 128), 640)]


def front_kernel(
    length, st, w_query, w_key, w_value, v_qk, v_attn, v_mlp, v_up, v_gate, w_out, w_up, w_gate, w_down, inner, outer,
    part, att, lse, kv_o, q_o, t_o, xg_o, wqkv_o, wo_o, scale_o, rate_a, rate_m, su, sg, uq, wd, gz,
    xg, wqkv, vecs, wo, y0, y1, kv, kvb, q, tt, low, acc, tot, uz, wq, vec,
    xs, xr, w1s, w1r, w2s, w2r, w3s, w3r, vs, vr, os, orr, lo,
    f1s, f1r, f2s, f2r, f3s, f3r, f4s, f4r, fl, sy, ry, sf, rf, ss, rs, kl, ol,
):
    x, c, z, y = here()
    sib = dev(x, 1 - c, z, y)
    half = pl.ds(pl.multiple_of(c * 640, 128), 640)
    other = pl.ds(pl.multiple_of((1 - c) * 640, 128), 640)
    to_z = [None] + [dev(x, c, step(z, d), y) for d in (1, 2, 3)]
    to_y = [None] + [dev(x, c, z, step(y, d)) for d in (1, 2, 3)]
    to_x = [None] + [dev(step(x, d), c, z, y) for d in (1, 2, 3)]
    near_first = (1, 3, 2)

    def head(ref, k):
        return ref[:, k * HDIM : (k + 1) * HDIM]

    @pl.when(c == 0)
    def _():
        for zz in range(4):
            for h in range(4):
                k = zz * HG + h
                wq[zz, :, h * 128 : (h + 1) * 128] = jnp.concatenate([head(w_query, k), head(w_key, k)], axis=1)

    @pl.when(c == 1)
    def _():
        for zz in range(4):
            k = zz * HG
            wq[zz, :, 0:128] = jnp.concatenate([head(w_query, k + 4), head(w_key, k + 4)], axis=1)
            for h in range(2):
                wq[zz, :, 128 + h * 128 : 256 + h * 128] = w_value[:, (k + 2 * h) * HDIM : (k + 2 * h + 2) * HDIM]
            last = head(w_value, k + 4)
            wq[zz, :, 384:512] = jnp.concatenate([last, jnp.zeros_like(last)], axis=1)

    vec[...] = jnp.zeros_like(vec)
    for ref, at, n in ((v_qk, 0, 80), (v_attn, 80, 80), (v_mlp, 160, 80), (v_up, 240, 320), (v_gate, 560, 320)):
        vec[:, at : at + n] = jnp.broadcast_to(ref[...].astype(F32).reshape(1, n), (8, n))
    greet(z_peers(x, c, z, y) + to_y[1:] + to_x[1:])

    for d in near_first:
        rcopy(wq.at[step(z, d)], wqkv.at[c, z, y], w1s.at[d], w1r.at[z], to_z[d]).start()
        rcopy(vec, vecs.at[z, y], vs.at[0, d], vr.at[0, z], to_z[d]).start()
    lcopy(wq.at[z], wqkv.at[c, z, y], lo.at[0]).start()
    lcopy(vec, vecs.at[z, y], lo.at[1]).start()
    for d in near_first:
        rcopy(w_out.at[:, half], wo.at[y, :, half], os.at[0, d], orr.at[0, y], to_y[d]).start()
    rcopy(w_out.at[:, half], wo.at[y, :, half], os.at[0, 0], orr.at[1, y], sib).start()
    lcopy(w_out.at[:, half], wo.at[y, :, half], lo.at[2]).start()

    for d in (1, 2, 3):
        landed(wqkv.at[c, step(z, d), y], w1r.at[step(z, d)])
        landed(vecs.at[step(z, d), y], vr.at[0, step(z, d)])
    landed(wqkv.at[c, z, y], lo.at[0])
    landed(vecs.at[z, y], lo.at[1])
    mine = wqkv.at[c, :, y]
    rcopy(mine, mine, w2s.at[0], w2r.at[0], to_y[1]).start()
    rcopy(mine, mine, w2s.at[1], w2r.at[1], to_y[3]).start()
    rcopy(mine, mine, w3s.at[0], w3r.at[0], sib).start()
    for d in near_first:
        rcopy(vecs.at[:, y], vecs.at[:, y], vs.at[1, d], vr.at[1, y], to_y[d]).start()
    z_gather_start(st, xg, xs, xr, x, c, z, y)
    for k, src, to in ((0, step(y, 3), to_y[1]), (1, step(y, 1), to_y[3])):
        block, piece = wqkv.at[c, :, src], wqkv.at[c, 2 * k : 2 * k + 2, src]
        landed(block, w2r.at[k])
        rcopy(piece, piece, w2s.at[2 + k], w2r.at[2 + k], to).start()
        rcopy(block, block, w3s.at[1 + k], w3r.at[1 + k], sib).start()
    for k in range(2):
        piece = wqkv.at[c, 2 * k : 2 * k + 2, step(y, 2)]
        landed(piece, w2r.at[2 + k])
        rcopy(piece, piece, w3s.at[3 + k], w3r.at[3 + k], sib).start()
    down = w_down.at[pl.ds(pl.multiple_of(x * 80, 16), 80), half]
    for d in near_first:
        rcopy(down, wd.at[y, x, :, half], f2s.at[1, d], f2r.at[1, y], to_y[d]).start()
    lcopy(down, wd.at[y, x, :, half], fl.at[2]).start()
    for d in (1, 2, 3):
        landed(vecs.at[:, step(y, d)], vr.at[1, step(y, d)])
    for zz in range(4):
        for yy in range(4):
            at = (zz * 4 + yy) * 80
            rate_a[:, at : at + 80] = vecs[zz, yy, :, 80:160]
            rate_m[:, at : at + 80] = vecs[zz, yy, :, 160:240]
    for yy in range(4):
        su[:, yy * 320 : (yy + 1) * 320] = vecs[z, yy, :, 240:560]
        sg[:, yy * 320 : (yy + 1) * 320] = vecs[z, yy, :, 560:880]
    scale = jnp.concatenate([vecs[z, yy, :, :80] for yy in range(4)], axis=1)
    for h in range(HG):
        sh = scale[:, h * HDIM : (h + 1) * HDIM]
        scale_o[:, h * 128 : (h + 1) * 128] = jnp.concatenate([sh, sh], axis=1)

    for p in range(2):
        z_gather_take(xg, xr, p)
    for d in near_first:
        rcopy(columns(w_gate, step(z, d), c), gz.at[z], f1s.at[1, d], f1r.at[1 + z], to_z[d]).start()
    lcopy(columns(w_gate, z, c), gz.at[z], fl.at[0]).start()

    @pl.when(z == x)
    def _():
        for d in near_first:
            rcopy(columns(w_up, step(z, d), c), uz, f1s.at[0, d], f1r.at[0], to_z[d]).start()
        lcopy(columns(w_up, z, c), uz, f1r.at[0]).start()

    for k, src in ((0, y), (1, step(y, 3)), (2, step(y, 1))):
        landed(wqkv.at[1 - c, :, src], w3r.at[k])
    for k in range(2):
        landed(wqkv.at[1 - c, 2 * k : 2 * k + 2, step(y, 2)], w3r.at[3 + k])
    lcopy(xg, xg_o, ol.at[0]).start()
    lcopy(wqkv, wqkv_o, ol.at[1]).start()

    def project(p, carry):
        rows = xg[p].reshape(2 * ROWS, D)
        y0[p] = jnp.dot(rows, wqkv[0].reshape(D, 512), preferred_element_type=F32)
        y1[p] = jnp.dot(rows, wqkv[1].reshape(D, 512), preferred_element_type=F32)
        return carry

    lax.fori_loop(0, 2, project, 0)
    lane = lanes()

    def send(h):
        rcopy(kv.at[h], kvb.at[h, c, :, :, y], sy.at[h, 0], ry.at[h, 0], to_y[1]).start()
        rcopy(kv.at[h], kvb.at[h, c, :, :, y], sy.at[h, 1], ry.at[h, 1], to_y[3]).start()
        rcopy(kv.at[h], kvb.at[h, c, :, :, y], ss.at[h, 0], rs.at[h, 0], sib).start()
        lcopy(kv.at[h], kvb.at[h, c, :, :, y], kl.at[h]).start()

    for h in range(HG):

        def per_block(j, carry, h=h):
            p, r = j // 2, pl.ds(pl.multiple_of((j % 2) * ROWS, ROWS), ROWS)
            cosine, sine = turn_of(inner, outer, block_index(c, y, j))
            raw = y0[p, r, h * 128 : (h + 1) * 128] if h < 4 else y1[p, r, 0:128]
            t = raw * cosine + swap(raw, lane) * sine
            unit = t * lax.rsqrt(half_means(t * t, lane) + EPS)
            both = unit * scale_o[0:1, h * 128 : (h + 1) * 128]
            pair = y1[p, r, 128 + (h // 2) * 128 : 256 + (h // 2) * 128]
            v = pair if h % 2 else pltpu.roll(pair, 64, 1)
            kv[h, p, j % 2] = jnp.where(lane < 64, pltpu.roll(both, 64, 1), v).astype(BF)
            rows = pl.ds(pl.multiple_of(j * ROWS, ROWS), ROWS)
            tt[h, rows, :] = t
            q[h, rows, :] = (jnp.where(lane < 64, both, 0.0).astype(BF).astype(F32) * 0.125).astype(BF)
            return carry

        lax.fori_loop(0, BLOCKS, per_block, 0, unroll=True)
        if h < 2:
            send(h)
    landed(wd.at[y, x, :, half], fl.at[2])
    for d in (1, 2, 3):
        landed(wd.at[step(y, d), x, :, half], f2r.at[1, step(y, d)])
    for d in near_first:
        rcopy(wd.at[:, x, :, half], wd.at[:, x, :, half], f3s.at[d], f3r.at[x], to_x[d]).start()
    rcopy(wd.at[:, x, :, half], wd.at[:, x, :, half], f4s.at[0], f4r.at[x], sib).start()
    lcopy(q, q_o, ol.at[2]).start()
    lcopy(tt, t_o, ol.at[3]).start()

    def near(h):
        for k, src, to in ((0, step(y, 3), to_y[1]), (1, step(y, 1), to_y[3])):
            landed(kvb.at[h, c, :, :, src], ry.at[h, k])
            rcopy(kvb.at[h, c, k, :, src], kvb.at[h, c, k, :, src], sf.at[h, k], rf.at[h, k], to).start()
            rcopy(kvb.at[h, c, :, :, src], kvb.at[h, c, :, :, src], ss.at[h, 1 + k], rs.at[h, 1 + k], sib).start()

    def far(h):
        src = step(y, 2)
        for k in range(2):
            landed(kvb.at[h, c, k, :, src], rf.at[h, k])
            rcopy(kvb.at[h, c, k, :, src], kvb.at[h, c, k, :, src], ss.at[h, 3 + k], rs.at[h, 3 + k], sib).start()

    def ready(h):
        landed(kvb.at[h, c, :, :, y], kl.at[h])
        landed(kvb.at[h, 1 - c, :, :, y], rs.at[h, 0])
        landed(kvb.at[h, 1 - c, :, :, step(y, 3)], rs.at[h, 1])
        landed(kvb.at[h, 1 - c, :, :, step(y, 1)], rs.at[h, 2])
        for k in range(2):
            landed(kvb.at[h, 1 - c, k, :, step(y, 2)], rs.at[h, 3 + k])
        lcopy(kvb.at[h], kv_o.at[h], kl.at[h]).start()

    item = work_items(c, y, length[0])

    def compute(h):
        acc[...] = jnp.zeros_like(acc)
        tot[...] = jnp.zeros_like(tot)

        def body(g, carry):
            key = lax.broadcasted_iota(jnp.int32, (TILE, ROWS), 0)
            its = [item(g * STEP + u) for u in range(STEP)]
            ks = [key_tile(kvb, h, t) for _, t, _ in its]
            ss_ = [
                nt(k, q[h, pl.ds(pl.multiple_of(j * ROWS, ROWS), ROWS), :]) for k, (j, _, _) in zip(ks, its)
            ]
            ps = [jnp.where(key <= bound, jnp.exp(s), 0.0) for s, (_, _, bound) in zip(ss_, its)]
            for k, p, (j, _, _) in zip(ks, ps, its):
                tot[j] += jnp.sum(p.reshape(TILE // 8, 8, ROWS), axis=0)
                acc[j] += tn(k, p.astype(BF))
            return carry

        lax.fori_loop(0, 18 // STEP, body, 0)
        for j in range(BLOCKS):
            total = jnp.sum(tot[j], axis=0, keepdims=True)
            lse[h, j : j + 1, :] = jnp.log(total)
            att[h, j * ROWS : (j + 1) * ROWS, :] = (acc[j, HDIM:] / total).T

    def spread_up():
        landed(uz, f1r.at[0])
        for d in near_first:
            rcopy(uz, uq.at[y], f2s.at[0, d], f2r.at[0, y], to_y[d]).start()
        lcopy(uz, uq.at[y], fl.at[1]).start()

    near(0)
    send(2)

    def per_head(i, carry):
        @pl.when(i + 1 < HG)
        def _():
            near(i + 1)

        @pl.when(i + 3 < HG)
        def _():
            send(i + 3)

        @pl.when(i == HG)
        def _():
            spread_up()

        @pl.when(i > 0)
        def _():
            ready(i - 1)
            compute(i - 1)

        @pl.when(i < HG)
        def _():
            far(i)

        return carry

    lax.fori_loop(0, HG + 1, per_head, 0)
    for h in range(HG):
        low[:, h * HDIM : (h + 1) * HDIM] = att[h].astype(BF)
    for d in near_first:
        y2 = step(y, d)
        landed(wo.at[y2, :, half], orr.at[0, y2])
        rcopy(wo.at[y2, :, half], wo.at[y2, :, half], os.at[1, d], orr.at[1, y2], sib).start()
    landed(wo.at[y, :, half], lo.at[2])
    for k in range(4):
        landed(wo.at[k, :, other], orr.at[1, k])
    lcopy(wo, wo_o, ol.at[4]).start()
    for p in range(2):
        v = jnp.dot(low[p * 256 : (p + 1) * 256, :], wo[...].reshape(GROUP, D), preferred_element_type=F32)
        part[p] = v.astype(BF).reshape(2, ROWS, D)

    for d in near_first:
        x2 = step(x, d)
        landed(wd.at[:, x2, :, half], f3r.at[x2])
        rcopy(wd.at[:, x2, :, half], wd.at[:, x2, :, half], f4s.at[d], f4r.at[x2], sib).start()
    landed(uz, fl.at[1])
    landed(uz, fl.at[0])
    for d in (1, 2, 3):
        landed(uq.at[step(y, d)], f2r.at[0, step(y, d)])
        landed(gz.at[step(z, d)], f1r.at[1 + step(z, d)])

    def sent(h, carry):
        for k in range(2):
            landed(kv.at[h], sy.at[h, k])
            landed(kv.at[h, 0], sf.at[h, k])
            landed(kv.at[h, 0], ss.at[h, 3 + k])
        for k in range(3):
            landed(kv.at[h], ss.at[h, k])
        landed(kvb.at[h], kl.at[h])
        return carry

    lax.fori_loop(0, HG, sent, 0)
    z_gather_sent(st, xs, c, z)
    for k in range(4):
        landed(wd.at[:, k, :, other], f4r.at[k])
        landed(wd.at[:, k, :, half], f4s.at[k])
    landed(wo.at[0, :, half], os.at[0, 0])
    for k in range(2):
        landed(mine, w2s.at[k])
        landed(wqkv.at[c, 0:2, y], w2s.at[2 + k])
        landed(wqkv.at[c, 0:2, y], w3s.at[3 + k])
    for k in range(3):
        landed(mine, w3s.at[k])
    for d in (1, 2, 3):
        landed(wqkv.at[c, z, y], w1s.at[d])
        landed(vec, vs.at[0, d])
        landed(vecs.at[:, y], vs.at[1, d])
        landed(wo.at[0, :, half], os.at[0, d])
        landed(wo.at[0, :, half], os.at[1, d])
        landed(uz, f1s.at[1, d])
        landed(uz, f2s.at[0, d])
        landed(uz, f2s.at[1, d])
        landed(wd.at[:, x, :, half], f3s.at[d])

    @pl.when(z == x)
    def _():
        for d in (1, 2, 3):
            landed(uz, f1s.at[0, d])

    landed(xg, ol.at[0])
    landed(wqkv, ol.at[1])
    landed(q, ol.at[2])
    landed(tt, ol.at[3])
    landed(wo, ol.at[4])


def front(length, st, w_query, w_key, w_value, vectors, w_out, w_up, w_gate, w_down, inner, outer):
    n = BLOCKS * ROWS
    V = pltpu.VMEM
    return remote_call(
        front_kernel,
        [
            ((2, 2, ROWS, D), BF, "v"),
            ((HG, n, HDIM), F32, "v"),
            ((HG, BLOCKS, 128), F32, "v"),
            ((HG, 2, 2, 2, 4, ROWS, 128), BF, "a"),
            ((HG, n, 128), BF, "a"),
            ((HG, n, 128), F32, "a"),
            ((2, 2, ROWS, D), BF, "a"),
            ((2, 4, 4, 80, 512), BF, "a"),
            ((4, 80, D), BF, "a"),
            ((8, HG * 128), F32, "v"),
            ((8, D), F32, "v"),
            ((8, D), F32, "v"),
            ((8, D), F32, "v"),
            ((8, D), F32, "v"),
            ((4, 80, 640), BF, "a"),
            ((4, 4, 80, D), BF, "a"),
            ((4, 80, 640), BF, "a"),
        ],
        "savvvvvvvvaaaavv",
        [
            V((2, 2, ROWS, D), BF), V((2, 4, 4, 80, 512), BF), V((4, 4, 8, 896), F32), V((4, 80, D), BF),
            V((2, 256, 512), F32), V((2, 256, 512), F32),
            V((HG, 2, 2, ROWS, 128), BF), V((HG, 2, 2, 2, 4, ROWS, 128), BF), V((HG, n, 128), BF), V((HG, n, 128), F32),
            V((n, GROUP), BF), V((BLOCKS, 128, ROWS), F32), V((BLOCKS, 8, ROWS), F32), V((80, 640), BF),
            V((4, 80, 512), BF), V((8, 896), F32),
            dma(4), dma(2, 2), dma(4), dma(4), dma(4), dma(4), dma(5), dma(5), dma(2, 4), dma(2, 4), dma(2, 4), dma(2, 4), dma(3),
            dma(2, 4), dma(5), dma(2, 4), dma(2, 4), dma(4), dma(4), dma(4), dma(4), dma(3),
            dma(HG, 2), dma(HG, 2), dma(HG, 2), dma(HG, 2), dma(HG, 5), dma(HG, 5), dma(HG), dma(5),
        ],
        0,
        "front",
    )(length, st, w_query, w_key, w_value, *vectors, w_out, w_up, w_gate, w_down, inner, outer)


def inv_rms(v):
    return lax.rsqrt(jnp.mean(v * v, axis=-1, keepdims=True) + EPS)


def back_rms(dy, yy, inv):
    return (dy - yy * jnp.mean(dy * yy, axis=-1, keepdims=True)) * inv


def total_of(buf):
    return (buf[0].astype(F32) + buf[1].astype(F32)) + (buf[2].astype(F32) + buf[3].astype(F32))


def mix_of(res, part, rate):
    inv_p = inv_rms(part)
    unit = part * inv_p
    diff = unit - res
    u = res + rate * diff
    inv_u = inv_rms(u)
    return u * inv_u, unit, inv_p, inv_u, diff


def mix_back(dy, res, part, rate):
    yy, unit, inv_p, inv_u, diff = mix_of(res, part, rate)
    du = back_rms(dy, yy, inv_u)
    return du * (1.0 - rate), back_rms(du * rate, unit, inv_p), jnp.sum(du * diff, axis=0, keepdims=True)


HALF = ROWS // 2


def mid_kernel(
    length, part0, st, cot, rate_a, rate_m, su, sg, uq, wd_in, gz,
    result, d_st, dm, ha, hd, vec,
    buf, low, xg, dd, wu, wg, wd, up, gate, hid, dug, part, xt, ht, mixed, first, dfirst, ga, gd, ra, rd, rdy,
    ps, pr, gs, gr, s2, r2, s3, r3, sx, rx, sy, ry, lo,
):
    x, c, z, y = here()
    sib = dev(x, 1 - c, z, y)
    half = pl.ds(pl.multiple_of(c * 640, 128), 640)
    other = pl.ds(pl.multiple_of((1 - c) * 640, 128), 640)
    to_x = [None] + [dev(step(x, d), c, z, y) for d in (1, 2, 3)]
    to_y = [None] + [dev(x, c, z, step(y, d)) for d in (1, 2, 3)]

    def cut(k):
        return pl.ds(k * HALF, HALF)

    def scatter(n, src, k):
        for p in range(2):
            oz = owner_z(c, p)
            for oc in range(2):
                mine = jnp.logical_and(c == oc, z == oz)
                piece, to = src.at[p, oc, cut(k)], buf.at[n, z, cut(k)]

                @pl.when(mine)
                def _(piece=piece, to=to):
                    lcopy(piece, to, pr.at[n, k, z]).start()

                @pl.when(jnp.logical_not(mine))
                def _(piece=piece, to=to, p=p, oc=oc, oz=oz):
                    rcopy(piece, to, ps.at[n, k, p, oc], pr.at[n, k, z], dev(x, oc, oz, y)).start()

    def scatter_take(n, k):
        for i in range(4):
            landed(buf.at[n, i, cut(k)], pr.at[n, k, i])
        return total_of(buf.at[n, :, cut(k)])

    def scatter_sent(n, src):
        for k in range(2):
            for p in range(2):
                for oc in range(2):
                    mine = jnp.logical_and(c == oc, z == owner_z(c, p))

                    @pl.when(jnp.logical_not(mine))
                    def _(k=k, p=p, oc=oc):
                        landed(src.at[p, oc, cut(k)], ps.at[n, k, p, oc])

    def gather(n, dst, k):
        w = worker(z)
        piece, to, sem = low.at[n, cut(k)], dst.at[z // 2, c, cut(k)], gr.at[n, k, z // 2, c]
        for d in (1, 3, 2):
            rcopy(piece, to, gs.at[n, k, d], sem, dev(x, w, step(z, d), y)).start()

        @pl.when(c == w)
        def _():
            lcopy(piece, to, sem).start()

        @pl.when(c != w)
        def _():
            rcopy(piece, to, gs.at[n, k, 0], sem, dev(x, w, z, y)).start()

    def gather_take(n, dst, k):
        for p in range(2):
            for i in range(2):
                landed(dst.at[p, i, cut(k)], gr.at[n, k, p, i])

    def gather_sent(n):
        for k in range(2):
            for d in (1, 2, 3):
                landed(low.at[n, cut(k)], gs.at[n, k, d])

            @pl.when(c != worker(z))
            def _(k=k):
                landed(low.at[n, cut(k)], gs.at[n, k, 0])

    greet(z_peers(x, c, z, y) + to_x[1:] + to_y[1:])
    for k in range(2):
        scatter(0, part0, k)
    for d in (1, 3, 2):
        rcopy(uq, wu.at[x, :, :, half], s2.at[0, d], r2.at[0, x], to_x[d]).start()
        rcopy(gz, wg.at[:, y, :, half], s2.at[1, d], r2.at[1, y], to_y[d]).start()
    rcopy(uq, wu.at[x, :, :, half], s3.at[0, 0], r3.at[0, x], sib).start()
    rcopy(gz, wg.at[:, y, :, half], s3.at[1, 0], r3.at[1, y], sib).start()
    lcopy(uq, wu.at[x, :, :, half], lo.at[0]).start()
    lcopy(gz, wg.at[:, y, :, half], lo.at[1]).start()
    lcopy(wd_in, wd, lo.at[2]).start()
    vec[...] = jnp.zeros_like(vec)

    for k in range(2):
        total = scatter_take(0, k)
        out = mix_of(st[cut(k)].astype(F32), total, rate_a[0:1])[0]
        low[0, cut(k)] = out.astype(BF)
        gather(0, xg, k)
        mixed[cut(k)] = total
        first[cut(k)] = out

    for d in (1, 3, 2):
        x2, y2 = step(x, d), step(y, d)
        landed(wu.at[x2, :, :, half], r2.at[0, x2])
        rcopy(wu.at[x2, :, :, half], wu.at[x2, :, :, half], s3.at[0, d], r3.at[0, x2], sib).start()
        landed(wg.at[:, y2, :, half], r2.at[1, y2])
        rcopy(wg.at[:, y2, :, half], wg.at[:, y2, :, half], s3.at[1, d], r3.at[1, y2], sib).start()
    landed(wu.at[x, :, :, half], lo.at[0])
    landed(wg.at[:, y, :, half], lo.at[1])
    landed(wd, lo.at[2])
    for k in range(4):
        landed(wu.at[k, :, :, other], r3.at[0, k])
        landed(wg.at[:, k, :, other], r3.at[1, k])

    def rows_of(ref, k):
        return ref[:, :, cut(k)].reshape(4 * HALF, D)

    def forward(k):
        gather_take(0, xg, k)

        def cols(t, carry):
            cs = pl.ds(pl.multiple_of(t * 256, 256), 256)
            xs = rows_of(xg, k)
            u = jnp.dot(xs, wu[:, :, :, cs].reshape(D, 256), preferred_element_type=F32)
            g = jnp.dot(xs, wg[:, :, :, cs].reshape(D, 256), preferred_element_type=F32)
            tt = g * sg[0:1, cs]
            up[k, :, cs] = u
            gate[k, :, cs] = g
            hid[k, :, cs] = (u * su[0:1, cs] * (tt * jax.nn.sigmoid(tt))).astype(BF)
            return carry

        lax.fori_loop(0, 5, cols, 0)

        def down(t, carry):
            cs = pl.ds(pl.multiple_of(t * 256, 256), 256)
            v = jnp.dot(hid[k], wd[:, cs], preferred_element_type=F32)
            part[0, :, :, cut(k), cs] = v.astype(BF).reshape(2, 2, HALF, 256)
            return carry

        lax.fori_loop(0, 5, down, 0)
        scatter(1, part.at[0], k)

    for k in range(2):
        forward(k)

    def turn(dst, load):
        def body(t, carry):
            cs = pl.ds(pl.multiple_of(t * 256, 256), 256)
            for k in range(2):
                dst[cs, k * 256 : (k + 1) * 256] = load(k, cs).T
            return carry

        lax.fori_loop(0, 5, body, 0)

    turn(ht, lambda k, cs: hid[k, :, cs])
    am = rate_m[0:1]
    at = (c * 16 + z * 4 + y) * ROWS
    for k in range(2):
        total = scatter_take(1, k)
        position = at + k * HALF + lax.broadcasted_iota(jnp.int32, (HALF, 1), 0)
        live = (position < length[0]).astype(F32)
        base = first[cut(k)]
        d_base, d_part, g_am = mix_back(cot[cut(k)].astype(F32) * live, base, total, am)
        low[1, cut(k)] = d_part.astype(BF)
        gather(1, dd, k)
        dfirst[cut(k)] = d_base
        vec[1:2] += g_am
        result[cut(k)] = (mix_of(base, total, am)[0] * live).astype(BF)
    turn(xt, lambda k, cs: xg[:, :, cut(k), cs].reshape(256, 256))

    def backward(k):
        gather_take(1, dd, k)

        def cols(t, carry):
            cs = pl.ds(pl.multiple_of(t * 256, 256), 256)
            dh = nt(rows_of(dd, k), wd[cs, :])
            u, g = up[k, :, cs], gate[k, :, cs]
            sc, sgc = su[0:1, cs], sg[0:1, cs]
            tt = g * sgc
            sig = jax.nn.sigmoid(tt)
            silu = tt * sig
            dsilu = sig * (1.0 + tt * (1.0 - sig))
            dhs = dh * sc
            dhu = dh * u
            both = dhu * dsilu * sc
            dug[0, k, :, cs] = (dhs * silu).astype(BF)
            dug[1, k, :, cs] = (both * sgc).astype(BF)
            vec[2:3, cs] += jnp.sum(dhu * silu, axis=0, keepdims=True)
            vec[3:4, cs] += jnp.sum(both * g, axis=0, keepdims=True)
            return carry

        lax.fori_loop(0, 5, cols, 0)
        for t in range(2):
            v = nt(dug[0, k], wu[2 * t : 2 * t + 2].reshape(640, D)) + nt(
                dug[1, k], wg[2 * t : 2 * t + 2].reshape(640, D)
            )
            part[1, :, :, cut(k), t * 640 : (t + 1) * 640] = v.astype(BF).reshape(2, 2, HALF, 640)
        scatter(2, part.at[1], k)

    for k in range(2):
        backward(k)

    def meet(k):
        dy = dfirst[cut(k)] + scatter_take(2, k)
        d_res, d_part, g_aa = mix_back(dy, st[cut(k)].astype(F32), mixed[cut(k)], rate_a[0:1])
        low[2, cut(k)] = d_part.astype(BF)
        gather(2, dm, k)
        d_st[cut(k)] = d_res
        vec[0:1] += g_aa

    def grad_down(i, carry):
        w = jnp.where(i == 0, 1 - c, c)
        cols = pl.ds(pl.multiple_of(w * 640, 128), 640)
        for k in range(4):
            rhs = jnp.concatenate([dd[:, :, cut(j), cols].reshape(256, 640) for j in range(2)], axis=0)
            v = jnp.dot(ht[k * 320 : (k + 1) * 320, :], rhs, preferred_element_type=F32)
            gd[w, k] = v.astype(BF).reshape(4, 80, 640)

        @pl.when(i == 0)
        def _():
            rcopy(gd.at[1 - c], rd, sx.at[1], rx.at[1], sib).start()

        return carry

    def grad_up(w):
        def body(k, carry):
            rows = pl.ds(pl.multiple_of(k * 320, 64), 320)
            for t in range(2):
                cs = slice(t * 640, (t + 1) * 640)
                v = jnp.dot(xt[rows, :], dug[w, :, :, cs].reshape(512, 640), preferred_element_type=F32)
                ga[w, k, :, :, cs] = v.astype(BF).reshape(4, 80, 640)
            return carry

        lax.fori_loop(0, 4, body, 0)

    lax.fori_loop(0, 2, grad_down, 0)
    meet(0)
    landed(rd, rx.at[1])

    def add_d(k, carry):
        i, j = k // 4, k % 4
        rd[i, j] = (gd[c, i, j].astype(F32) + rd[i, j].astype(F32)).astype(BF)
        return carry

    lax.fori_loop(0, 16, add_d, 0)
    for d in (1, 3, 2):
        rcopy(rd.at[step(y, d)], rdy.at[y], sy.at[d], ry.at[y], to_y[d]).start()
    grad_up(1 - c)
    rcopy(ga.at[1 - c], ra, sx.at[0], rx.at[0], sib).start()
    meet(1)
    grad_up(c)
    landed(ra, rx.at[0])

    def add_a(k, carry):
        i, j = k // 4, k % 4
        ha[i, j] = (ga[c, i, j].astype(F32) + ra[i, j].astype(F32)).astype(BF)
        return carry

    lax.fori_loop(0, 16, add_a, 0)
    for d in (1, 2, 3):
        landed(rdy.at[step(y, d)], ry.at[step(y, d)])

    def sum_d(k, carry):
        v = rd[y, k].astype(F32)
        for d in (1, 2, 3):
            v = v + rdy[step(y, d), k].astype(F32)
        hd[k] = v.astype(BF)
        return carry

    lax.fori_loop(0, 4, sum_d, 0)
    for k in range(2):
        gather_take(2, dm, k)
    for n in range(3):
        gather_sent(n)
    for n, src in ((0, part0), (1, part.at[0]), (2, part.at[1])):
        scatter_sent(n, src)
    for i in range(2):
        for k in range(4):
            landed(gz, s3.at[i, k])
        for d in (1, 2, 3):
            landed(gz, s2.at[i, d])
    landed(ra, sx.at[0])
    landed(rd, sx.at[1])
    for d in (1, 2, 3):
        landed(rdy.at[y], sy.at[d])


def middle(length, part0, st, cot, rate_a, rate_m, su, sg, uq, wd, gz):
    V = pltpu.VMEM
    return remote_call(
        mid_kernel,
        [
            ((ROWS, D), BF, "v"),
            ((ROWS, D), F32, "v"),
            ((2, 2, ROWS, D), BF, "a"),
            ((4, 4, 80, D), BF, "v"),
            ((4, 80, 640), BF, "v"),
            ((8, D), F32, "v"),
        ],
        "savvvvvvaaa",
        [
            V((3, 4, ROWS, D), BF), V((3, ROWS, D), BF), V((2, 2, ROWS, D), BF), V((2, 2, ROWS, D), BF),
            V((4, 4, 80, D), BF), V((4, 4, 80, D), BF), V((D, D), BF),
            V((2, 256, D), F32), V((2, 256, D), F32), V((2, 256, D), BF), V((2, 2, 256, D), BF),
            V((2, 2, 2, ROWS, D), BF), V((D, 512), BF), V((D, 512), BF),
            V((ROWS, D), F32), V((ROWS, D), F32), V((ROWS, D), F32),
            V((2, 4, 4, 80, D), BF), V((2, 4, 4, 80, 640), BF), V((4, 4, 80, D), BF), V((4, 4, 80, 640), BF),
            V((4, 4, 80, 640), BF),
            dma(3, 2, 2, 2), dma(3, 2, 4), dma(3, 2, 4), dma(3, 2, 2, 2),
            dma(2, 4), dma(2, 4), dma(2, 4), dma(2, 4), dma(2), dma(2), dma(4), dma(4), dma(3),
        ],
        2,
        "middle",
    )(length, part0, st, cot, rate_a, rate_m, su, sg, uq, wd, gz)


CUT = 768


def back_kernel(
    length, q_in, kv_in, wo_in, dmix_in, att_in, lse, ha, hd, tt_in, xg_in, wq_in, scale, inner, outer, vec,
    pbuf, za, zd, zq, o_out, o_vec,
    q, wo, dmix, att, kv, tt, xg, wq,
    qdo, delta, dqt, acc, low, give, mine, got, got_y, dq, dd, sums, part, gq, go,
    oax, oay, rax, ray, fax, fay, fd, hq, rqx, rqy, fqx, fqy, ob, ox, o2, vs, vb, ws, wb,
    lo, sg, rg, sy, ry, s1, r1, s2, r2, s3, r3, sz, rz, sc, rc, q1, p1, q2, p2, q3, p3, so, ro, sv, rv, sw, rw, ps, pr, sf, rf,
):
    x, c, z, y = here()
    sib = dev(x, 1 - c, z, y)
    to_y = [None] + [dev(x, c, z, step(y, d)) for d in (1, 2, 3)]
    to_x = [None] + [dev(step(x, d), c, z, y) for d in (1, 2, 3)]
    to_z = [None] + [dev(x, c, step(z, d), y) for d in (1, 2, 3)]
    near_first = (1, 3, 2)
    for i, (a, b) in enumerate(((dmix_in, dmix), (wo_in, wo), (att_in, att), (q_in, q))):
        lcopy(a, b, lo.at[6 + i]).start()
    lcopy(kv_in, kv, lo.at[0]).start()
    lcopy(ha.at[x, :, :, 0:CUT], oax, lo.at[1]).start()
    lcopy(ha.at[:, y, :, CUT:D], oay, lo.at[2]).start()
    lcopy(tt_in, tt, lo.at[3]).start()
    lcopy(xg_in, xg, lo.at[4]).start()
    lcopy(wq_in, wq, lo.at[5]).start()
    greet(z_peers(x, c, z, y) + to_y[1:] + to_x[1:])
    for d in near_first:
        rcopy(ha.at[step(x, d), :, :, 0:CUT], rax.at[x], s1.at[0, d], r1.at[0, x], to_x[d]).start()
        rcopy(ha.at[:, step(y, d), :, CUT:D], ray.at[y], s1.at[1, d], r1.at[1, y], to_y[d]).start()

    def settle(h):
        landed(got.at[h], rg.at[h])
        for i in range(2):
            for k in range(2):
                mine[h, i, k] = (mine[h, i, k].astype(F32) + got[h, i, k].astype(F32)).astype(BF)
        for d in near_first:
            rcopy(mine.at[h, :, :, step(y, d)], got_y.at[h, y], sy.at[h, d], ry.at[h, y], to_y[d]).start()

    for i, b in enumerate((dmix, wo, att, q)):
        landed(b, lo.at[6 + i])
    d_att = nt(dmix[...], wo[...]).astype(BF)
    for h in range(HG):
        low[:, h * HDIM : (h + 1) * HDIM] = att[h].astype(BF)
        dh = d_att[:, h * HDIM : (h + 1) * HDIM].astype(F32)
        wide = jnp.concatenate([jnp.zeros_like(dh), dh], axis=1).astype(BF)
        prod = dh * att[h]
        for j in range(BLOCKS):
            rows = slice(j * ROWS, (j + 1) * ROWS)
            qdo[h, j, :ROWS] = q[h, rows, :]
            qdo[h, j, ROWS:] = wide[rows]
            delta[h, j : j + 1, :] = jnp.sum(prod[rows].T, axis=0, keepdims=True)
    rcopy(vec, vb.at[0], sv.at[0, 0], rv.at[0, 0], sib).start()

    def small_start():
        for k in range(2):
            g = tn(low[...], dmix[:, k * 640 : (k + 1) * 640])
            go[k] = g.astype(BF).reshape(4, 80, 640)
        rcopy(go.at[1 - c], ob, sc.at[1], rc.at[1], sib).start()

    def small_cores():
        landed(ob, rc.at[1])
        landed(vb.at[0], rv.at[0, 0])
        vs[...] = vec[...] + vb[0]
        for k in range(4):
            ob[k] = (go[c, k].astype(F32) + ob[k].astype(F32)).astype(BF)
        for d in near_first:
            rcopy(ob.at[step(y, d)], ox.at[y], so.at[0, d], ro.at[0, y], to_y[d]).start()
            rcopy(vs, vb.at[d], sv.at[1, d], rv.at[1, d], to_y[d]).start()

    def small_y():
        v, tot = ob[y].astype(F32), vs[...]
        for d in (1, 2, 3):
            landed(ox.at[step(y, d)], ro.at[0, step(y, d)])
            landed(vb.at[d], rv.at[1, d])
            landed(vs, sv.at[1, d])
            v = v + ox[step(y, d)].astype(F32)
            tot = tot + vb[d]
        ox[y] = v.astype(BF)
        vs[...] = tot
        for d in near_first:
            rcopy(ox.at[y], o2.at[d], so.at[1, d], ro.at[1, d], to_x[d]).start()
            rcopy(vs, vb.at[3 + d], sv.at[2, d], rv.at[2, d], to_x[d]).start()

    def small_x():
        v, tot = ox[y].astype(F32), vs[...]
        for d in (1, 2, 3):
            landed(o2.at[d], ro.at[1, d])
            landed(vb.at[3 + d], rv.at[2, d])
            landed(vs, sv.at[2, d])
            v = v + o2[d].astype(F32)
            tot = tot + vb[3 + d]
        o_out[c] = v.astype(BF)
        vs[...] = tot
        rcopy(o_out.at[c], o_out.at[c], sf.at[3], rf.at[3], sib).start()
        for d in near_first:
            rcopy(vs, vb.at[6 + d], sv.at[3, d], rv.at[3, d], to_z[d]).start()

    def small_z():
        tot = vs[...]
        for d in (1, 2, 3):
            landed(vb.at[6 + d], rv.at[3, d])
            landed(vs, sv.at[3, d])
            tot = tot + vb[6 + d]
        o_vec[0:2] = tot[0:2]
        o_vec[2:] = vs[2:]

    def down_x():
        v = hd[x].astype(F32)
        for d in (1, 2, 3):
            landed(fd.at[step(x, d)], r2.at[1, step(x, d)])
            v = v + fd[step(x, d)].astype(F32)
        zd[c, x] = v.astype(BF)
        for d in near_first:
            rcopy(zd.at[c, x], zd.at[c, x], s3.at[1, d], r3.at[1, x], to_x[d]).start()

    def down_done():
        for d in (1, 2, 3):
            landed(zd.at[c, step(x, d)], r3.at[1, step(x, d)])
        rcopy(zd.at[c], zd.at[c], sf.at[1], rf.at[1], sib).start()

    def up_first():
        landed(oax, lo.at[1])
        landed(oay, lo.at[2])
        for d in (1, 2, 3):
            landed(rax.at[step(x, d)], r1.at[0, step(x, d)])
            landed(ray.at[step(y, d)], r1.at[1, step(y, d)])

        def body(k, carry):
            v, w = oax[k].astype(F32), oay[k].astype(F32)
            for d in (1, 2, 3):
                v = v + rax[step(x, d), k].astype(F32)
                w = w + ray[step(y, d), k].astype(F32)
            oax[k] = v.astype(BF)
            oay[k] = w.astype(BF)
            return carry

        lax.fori_loop(0, 4, body, 0)
        for d in near_first:
            rcopy(oax.at[step(y, d)], fax.at[y], s2.at[0, d], r2.at[0, y], to_y[d]).start()
            rcopy(oay.at[step(x, d)], fay.at[x], s2.at[2, d], r2.at[2, x], to_x[d]).start()
        for d in near_first:
            rcopy(hd.at[step(x, d)], fd.at[x], s2.at[1, d], r2.at[1, x], to_x[d]).start()

    landed(kv, lo.at[0])
    item = work_items(c, y, length[0])

    def per_head(h, carry):
        acc[...] = jnp.zeros_like(acc)
        dqt[...] = jnp.zeros_like(dqt)
        for k, f in ((1, small_start), (3, small_cores)):
            pl.when(h == k)(f)

        def body(g, carry):
            @pl.when(jnp.logical_and(g == 1, h > 0))
            def _():
                settle(h - 1)

            pl.when(jnp.logical_and(g == 0, h == HG - 1))(up_first)
            pl.when(jnp.logical_and(g == 1, h == HG - 1))(small_y)
            key = lax.broadcasted_iota(jnp.int32, (TILE, ROWS), 0)
            its = [item(g * STEP + u) for u in range(STEP)]
            ks = [key_tile(kv, h, t) for _, t, _ in its]
            bs = [qdo[h, j] for j, _, _ in its]
            sds = [nt(k, b) for k, b in zip(ks, bs)]
            dss, pp = [], []
            for sd, (j, _, bound) in zip(sds, its):
                p = jnp.where(key <= bound, jnp.exp(sd[:, :ROWS] - lse[h, pl.ds(j, 1), :]), 0.0)
                dss.append((p * (sd[:, ROWS:] - delta[h, pl.ds(j, 1), :])).astype(BF))
                pp.append(p.astype(BF))
            for ds, p, b, (_, t, _) in zip(dss, pp, bs, its):
                acc[t] += jnp.dot(jnp.concatenate([ds, p], axis=1), b, preferred_element_type=F32)
            for k, ds, (j, _, _) in zip(ks, dss, its):
                dqt[j] += tn(k, ds)
            return carry

        lax.fori_loop(0, 18 // STEP, body, 0)

        def store(i, carry):
            zi, k = i // 2, i % 2
            give[h, zi, k] = acc[k * 4 + owner_z(1 - c, zi)].astype(BF).reshape(4, ROWS, 128)
            mine[h, zi, k] = acc[k * 4 + owner_z(c, zi)].astype(BF).reshape(4, ROWS, 128)
            return carry

        lax.fori_loop(0, 4, store, 0, unroll=True)
        rcopy(give.at[h], got.at[h], sg.at[h], rg.at[h], sib).start()
        for j in range(BLOCKS):
            dq[h, j * ROWS : (j + 1) * ROWS, :] = dqt[j].T * 0.125
        return carry

    lax.fori_loop(0, HG, per_head, 0)
    settle(HG - 1)
    for d in (1, 2, 3):
        landed(fax.at[step(y, d)], r2.at[0, step(y, d)])
        landed(fay.at[step(x, d)], r2.at[2, step(x, d)])
    v, w = oax[y].astype(F32), oay[x].astype(F32)
    for d in (1, 2, 3):
        v = v + fax[step(y, d)].astype(F32)
        w = w + fay[step(x, d)].astype(F32)
    za[2, x, :, 0:CUT] = v.astype(BF)
    za[2, x, :, CUT:D] = w.astype(BF)
    for d in near_first:
        rcopy(za.at[2, x], za.at[2, x], s3.at[0, d], r3.at[0, x], to_x[d]).start()
    ws[...] = jnp.zeros_like(ws)
    landed(tt, lo.at[3])
    landed(xg, lo.at[4])
    landed(wq, lo.at[5])
    sums[...] = jnp.zeros_like(sums)
    lane = lanes()

    def through(h, carry):
        for d in (1, 2, 3):
            landed(got_y.at[h, step(y, d)], ry.at[h, step(y, d)])
        cols = pl.ds(pl.multiple_of(h * 128, 128), 128)
        pair = pl.ds(pl.multiple_of(640 + (h // 2) * 128, 128), 128)
        odd = h % 2 == 1

        def per_block(j, carry):
            i, k = j // 2, j % 2
            rows = pl.ds(pl.multiple_of(j * ROWS, ROWS), ROWS)
            cosine, sine = turn_of(inner, outer, block_index(c, y, j))
            grads = mine[h, i, k, y].astype(F32)
            for d in (1, 2, 3):
                grads = grads + got_y[h, step(y, d), i, k].astype(F32)
            grads = grads.astype(BF).astype(F32)
            turned = pltpu.roll(grads, 64, 1)
            t = tt[h, rows, :]
            dy = jnp.where(lane < 64, dq[h, rows, :].astype(BF).astype(F32), turned)
            inv = lax.rsqrt(half_means(t * t, lane) + EPS)
            unit = t * inv
            sums[:, cols] += jnp.sum((dy * unit).reshape(ROWS // 8, 8, 128), axis=0)
            dyh = dy * scale[0:1, cols]
            dt = (dyh - unit * half_means(dyh * unit, lane)) * inv
            dd[rows, cols] = (dt * cosine + swap(dt * sine, lane)).astype(BF)
            before = jnp.where(odd, dd[rows, pair].astype(F32), turned)
            dd[rows, pair] = jnp.where(lane < 64, before, jnp.where(odd, grads, 0.0)).astype(BF)
            return carry

        lax.fori_loop(0, BLOCKS, per_block, 0, unroll=True)
        return carry

    lax.fori_loop(0, 2, through, 0)
    down_x()
    small_x()
    lax.fori_loop(2, HG, through, 0)

    def inputs(p, carry):
        rows = pl.ds(pl.multiple_of(p * 256, 256), 256)
        v = nt(dd[rows, 0:512], wq[0].reshape(D, 512)) + nt(dd[rows, 512:1024], wq[1].reshape(D, 512))
        part[p] = v.astype(BF).reshape(2, ROWS, D)
        z_scatter_pair(part, pbuf, ps, pr, p, x, c, z, y)
        return carry

    def along_z():
        for d in (1, 2, 3):
            landed(za.at[2, step(x, d)], r3.at[0, step(x, d)])
        for d in near_first:
            rcopy(za.at[2, step(z, d)], za.at[c, z], sz.at[0, d], rz.at[0, z], to_z[d]).start()
        za[c, z] = za[2, z]

    def weights(i, carry):
        h = jnp.where(i == 0, 1 - c, c)
        cols = pl.ds(pl.multiple_of(h * 512, 128), 512)
        gq[h] = tn(xg[...].reshape(512, D), dd[:, cols]).astype(BF).reshape(4, 4, 80, 512)

        @pl.when(i == 0)
        def _():
            rcopy(gq.at[1 - c], hq, sc.at[0], rc.at[0], sib).start()
            along_z()
            lax.fori_loop(0, 2, inputs, 0)

        return carry

    lax.fori_loop(0, 2, weights, 0)
    for h in range(HG):
        v = jnp.sum(sums[:, h * 128 : (h + 1) * 128], axis=0, keepdims=True)
        ws[:, h * HDIM : (h + 1) * HDIM] = jnp.broadcast_to(v[:, :HDIM] + v[:, HDIM:], (8, HDIM))
    rcopy(ws, wb.at[0], sw.at[0, 0], rw.at[0, 0], sib).start()

    small_z()
    landed(hq, rc.at[0])

    def add_q(k, carry):
        i, j = k // 4, k % 4
        v = (gq[c, i, j].astype(F32) + hq[i, j].astype(F32)).astype(BF)
        fqx[i, j] = v[:, :256]
        fqy[j, i] = v[:, 256:]
        return carry

    lax.fori_loop(0, 16, add_q, 0)
    for d in near_first:
        rcopy(fqx.at[step(x, d)], rqx.at[x], q1.at[0, d], p1.at[0, x], to_x[d]).start()
        rcopy(fqy.at[step(y, d)], rqy.at[y], q1.at[1, d], p1.at[1, y], to_y[d]).start()
    landed(wb.at[0], rw.at[0, 0])
    landed(ws, sw.at[0, 0])
    ws[...] = ws[...] + wb[0]
    for d in near_first:
        rcopy(ws, wb.at[d], sw.at[1, d], rw.at[1, d], to_y[d]).start()
    for d in (1, 2, 3):
        landed(rqx.at[step(x, d)], p1.at[0, step(x, d)])
        landed(rqy.at[step(y, d)], p1.at[1, step(y, d)])

    def add_q1(k, carry):
        a, b = fqx[x, k].astype(F32), fqy[y, k].astype(F32)
        for d in (1, 2, 3):
            a = a + rqx[step(x, d), k].astype(F32)
            b = b + rqy[step(y, d), k].astype(F32)
        rqx[x, k] = a.astype(BF)
        rqy[y, k] = b.astype(BF)
        return carry

    lax.fori_loop(0, 4, add_q1, 0)
    for d in near_first:
        rcopy(rqx.at[x, step(y, d)], fqx.at[4, y], q2.at[0, d], p2.at[0, y], to_y[d]).start()
        rcopy(rqy.at[y, step(x, d)], fqy.at[4, x], q2.at[1, d], p2.at[1, x], to_x[d]).start()
    tot = ws[...]
    for d in (1, 2, 3):
        landed(wb.at[d], rw.at[1, d])
        landed(ws, sw.at[1, d])
        tot = tot + wb[d]
    ws[...] = tot
    for d in near_first:
        rcopy(ws, wb.at[3 + d], sw.at[2, d], rw.at[2, d], to_x[d]).start()
    for d in (1, 2, 3):
        landed(fqx.at[4, step(y, d)], p2.at[0, step(y, d)])
        landed(fqy.at[4, step(x, d)], p2.at[1, step(x, d)])
    a, b = rqx[x, y].astype(F32), rqy[y, x].astype(F32)
    for d in (1, 2, 3):
        a = a + fqx[4, step(y, d)].astype(F32)
        b = b + fqy[4, step(x, d)].astype(F32)
    zq[0, x] = jnp.concatenate([a, b], axis=1).astype(BF)
    for d in near_first:
        rcopy(zq.at[0, x], zq.at[0, x], q3.at[d], p3.at[x], to_x[d]).start()
    down_done()
    tot = ws[...]
    for d in (1, 2, 3):
        landed(wb.at[3 + d], rw.at[2, d])
        landed(ws, sw.at[2, d])
        tot = tot + wb[3 + d]
    o_vec[4:5, 0:384] = tot[0:1]
    for d in (1, 2, 3):
        landed(zq.at[0, step(x, d)], p3.at[step(x, d)])
    for d in near_first:
        rcopy(zq.at[0, step(z, d)], zq.at[1 + c, z], sz.at[1, d], rz.at[1, z], to_z[d]).start()
    zq[1 + c, z] = zq[0, z]
    for d in (1, 2, 3):
        landed(za.at[c, step(z, d)], rz.at[0, step(z, d)])
    rcopy(za.at[c], za.at[c], sf.at[0], rf.at[0], sib).start()
    for d in (1, 2, 3):
        landed(zq.at[1 + c, step(z, d)], rz.at[1, step(z, d)])
    rcopy(zq.at[1 + c], zq.at[1 + c], sf.at[2], rf.at[2], sib).start()
    z_scatter_take(pbuf, pr)
    landed(za.at[1 - c], rf.at[0])
    landed(zd.at[1 - c], rf.at[1])
    landed(zq.at[2 - c], rf.at[2])
    landed(o_out.at[1 - c], rf.at[3])
    def sent(h, carry):
        landed(give.at[h], sg.at[h])
        for d in (1, 2, 3):
            landed(got_y.at[h, y], sy.at[h, d])
        return carry

    lax.fori_loop(0, HG, sent, 0)
    z_scatter_sent(part, ps, c, z)
    landed(hq, sc.at[0])
    landed(ob, sc.at[1])
    landed(vec, sv.at[0, 0])
    landed(o_out.at[0], sf.at[3])
    landed(za.at[0], sf.at[0])
    landed(zd.at[0], sf.at[1])
    landed(zq.at[1], sf.at[2])
    for d in (1, 2, 3):
        landed(rax.at[x], s1.at[0, d])
        landed(ray.at[y], s1.at[1, d])
        landed(fax.at[0], s2.at[0, d])
        landed(fd.at[0], s2.at[1, d])
        landed(fay.at[0], s2.at[2, d])
        landed(za.at[0, 0], s3.at[0, d])
        landed(fd.at[0], s3.at[1, d])
        landed(za.at[0, 0], sz.at[0, d])
        landed(zq.at[0, 0], sz.at[1, d])
        landed(rqx.at[0], q1.at[0, d])
        landed(rqy.at[0], q1.at[1, d])
        landed(fqx.at[0, 0], q2.at[0, d])
        landed(fqy.at[0, 0], q2.at[1, d])
        landed(zq.at[0, 0], q3.at[d])
        landed(ox.at[0], so.at[0, d])
        landed(ox.at[0], so.at[1, d])


def back(length, q, kv, wo, dmix, att, lse, ha, hd, tt, xg, wq, scale, inner, outer, vec):
    n = BLOCKS * ROWS
    V = pltpu.VMEM
    return remote_call(
        back_kernel,
        [
            ((4, ROWS, D), BF, "v"),
            ((3, 4, 80, D), BF, "v"),
            ((2, 4, 80, 640), BF, "v"),
            ((3, 4, 80, 512), BF, "v"),
            ((2, 80, 640), BF, "v"),
            ((8, D), F32, "v"),
        ],
        "saaaaavavaaavvvv",
        [
            V((HG, n, 128), BF), V((GROUP, D), BF), V((n, D), BF), V((HG, n, HDIM), F32),
            V((HG, 2, 2, 2, 4, ROWS, 128), BF), V((HG, n, 128), F32), V((2, 2, ROWS, D), BF), V((2, 4, 4, 80, 512), BF),
            V((HG, BLOCKS, 2 * ROWS, 128), BF), V((HG, BLOCKS, 128), F32), V((BLOCKS, 128, ROWS), F32), V((8, TILE, 128), F32),
            V((n, GROUP), BF),
            V((HG, 2, 2, 4, ROWS, 128), BF), V((HG, 2, 2, 4, ROWS, 128), BF), V((HG, 2, 2, 4, ROWS, 128), BF),
            V((HG, 4, 2, 2, ROWS, 128), BF), V((HG, n, 128), F32), V((n, 1024), BF), V((8, HG * 128), F32),
            V((2, 2, ROWS, D), BF), V((2, 4, 4, 80, 512), BF), V((2, 4, 80, 640), BF),
            V((4, 80, CUT), BF), V((4, 80, D - CUT), BF), V((4, 4, 80, CUT), BF), V((4, 4, 80, D - CUT), BF),
            V((4, 80, CUT), BF), V((4, 80, D - CUT), BF), V((4, 80, 640), BF),
            V((4, 4, 80, 512), BF), V((4, 4, 80, 256), BF), V((4, 4, 80, 256), BF), V((5, 4, 80, 256), BF), V((5, 4, 80, 256), BF),
            V((4, 80, 640), BF), V((4, 80, 640), BF), V((4, 80, 640), BF), V((8, D), F32), V((10, 8, D), F32), V((8, 384), F32), V((7, 8, 384), F32),
            dma(10), dma(HG), dma(HG), dma(HG, 4), dma(HG, 4),
            dma(2, 4), dma(2, 4), dma(3, 4), dma(3, 4), dma(2, 4), dma(2, 4), dma(2, 4), dma(2, 4), dma(2), dma(2),
            dma(2, 4), dma(2, 4), dma(2, 4), dma(2, 4), dma(4), dma(4), dma(2, 4), dma(2, 4), dma(4, 4), dma(4, 4), dma(3, 4), dma(3, 4),
            dma(2, 2), dma(4), dma(4), dma(4),
        ],
        3,
        "back",
    )(length, q, kv, wo, dmix, att, lse, ha, hd, tt, xg, wq, scale, inner, outer, vec)


def finish_kernel(
    res, d_st, pbuf, za, zd, zq, out, vec,
    result, g_in, o_q, o_k, o_v, o_out, o_up, o_gate, o_down, v_qk, v_attn, v_mlp, v_up, v_gate,
):
    _, _, z, y = here()
    step_no = pl.program_id(0)
    result[...] = res[...]
    g_in[...] = d_st[...] + total_of(pbuf)
    o_up[...] = za[0, 0].astype(F32)
    o_gate[...] = za[1, 0].astype(F32)
    for h in range(2):
        o_down[:, h * 640 : (h + 1) * 640] = zd[h, 0].astype(F32)
    a, b = zq[1, 0].astype(F32), zq[2, 0].astype(F32)
    pairs = [a[:, h * 128 : (h + 1) * 128] for h in range(4)] + [b[:, :128]]
    for k in range(4):

        @pl.when(step_no == k)
        def _(at=k * GROUP):
            o_q[:, at : at + GROUP] = jnp.concatenate([v[:, :HDIM] for v in pairs], axis=1)
            o_k[:, at : at + GROUP] = jnp.concatenate([v[:, HDIM:] for v in pairs], axis=1)
            o_v[:, at : at + GROUP] = b[:, 128:448]

    @pl.when(step_no == 0)
    def _():
        o_out[:, :640] = out[0].astype(F32)
        o_out[:, 640:] = out[1].astype(F32)
        v = vec[...]
        by_shard = pltpu.roll(v, (16 - (z * 4 + y)) % 16 * 80, 1)
        by_y = pltpu.roll(v, (4 - y) % 4 * 320, 1)
        v_attn[...] = by_shard[0:1, :80].reshape(80)
        v_mlp[...] = by_shard[1:2, :80].reshape(80)
        v_up[...] = by_y[2:3, :320].reshape(320)
        v_gate[...] = by_y[3:4, :320].reshape(320)
        v_qk[...] = pltpu.roll(v, (16 - y) % 16 * 80, 1)[4:5, :80].reshape(80)


def finish(res, d_st, pbuf, za, zd, zq, out, vec):
    def whole(*shape):
        return pl.BlockSpec(shape, lambda k: (0,) * len(shape))

    rows = ROWS // 4
    outs = [
        ((ROWS, D), BF, pl.BlockSpec((rows, D), lambda k: (k, 0))),
        ((ROWS, D), F32, pl.BlockSpec((rows, D), lambda k: (k, 0))),
        ((80, D), F32, whole(80, D)),
        ((80, D), F32, whole(80, D)),
        ((80, D), F32, whole(80, D)),
        ((80, D), F32, whole(80, D)),
        ((80, FF), F32, pl.BlockSpec((80, D), lambda k: (0, k))),
        ((80, FF), F32, pl.BlockSpec((80, D), lambda k: (0, k))),
        ((320, D), F32, pl.BlockSpec((80, D), lambda k: (k, 0))),
        ((80,), F32, whole(80)),
        ((80,), F32, whole(80)),
        ((80,), F32, whole(80)),
        ((320,), F32, whole(320)),
        ((320,), F32, whole(320)),
    ]
    return pl.pallas_call(
        finish_kernel,
        grid=(4,),
        out_shape=[jax.ShapeDtypeStruct(s, d) for s, d, _ in outs],
        in_specs=[
            pl.BlockSpec((rows, D), lambda k: (k, 0)),
            pl.BlockSpec((rows, D), lambda k: (k, 0)),
            pl.BlockSpec((4, rows, D), lambda k: (0, k, 0)),
            pl.BlockSpec((2, 1, 80, D), lambda k: (0, k, 0, 0)),
            pl.BlockSpec((2, 1, 80, 640), lambda k: (0, k, 0, 0)),
            pl.BlockSpec((3, 1, 80, 512), lambda k: (0, k, 0, 0)),
            whole(2, 80, 640),
            whole(8, D),
        ],
        out_specs=[spec for _, _, spec in outs],
        compiler_params=pltpu.CompilerParams(vmem_limit_bytes=VMEM_LIMIT),
        name="finish",
    )(res, d_st, pbuf, za, zd, zq, out, vec)


def shards(
    states, w_query, w_key, w_value, w_out, w_up, w_gate, w_down,
    scale_qk, alpha_attn, alpha_mlp, scale_up, scale_gate, lengths, cotangent,
):
    x, c, z, y = here()
    st = states[0]

    vectors = (scale_qk, alpha_attn, alpha_mlp, scale_up, scale_gate)
    inner, outer = (jnp.asarray(t) for t in rope_tables())
    n = BLOCKS * ROWS
    part, att, lse, kv, q, turned, xg, wqkv, wo, scale, rate_a, rate_m, su, sg, uq, wd, gz = front(
        lengths, st, w_query, w_key, w_value, vectors, w_out, w_up, w_gate, w_down, inner, outer
    )
    result, d_st, dm, ha, hd, vec = middle(
        lengths, part, st, cotangent[0], rate_a, rate_m, su, sg, uq, wd.reshape(D, D), gz
    )
    pbuf, za, zd, zq, out, vec = back(
        lengths, q, kv, wo.reshape(GROUP, D), dm.reshape(n, D), att, lse, ha, hd, turned, xg, wqkv, scale, inner, outer, vec
    )
    outs = finish(result, d_st, pbuf, za, zd, zq, out, vec)
    return (outs[0][None], outs[1][None], *outs[2:])


def solution(mesh):
    row = P("grp", ("seq", "shard"), None)
    mat = P("shard", None)
    one = P("shard")
    return jax.shard_map(
        shards,
        mesh=mesh,
        in_specs=(row,) + (mat,) * 7 + (one,) * 5 + (P("grp"), row),
        out_specs=(row, row) + (mat,) * 7 + (one,) * 5,
        check_vma=False,
    )
```

```python
import functools
import math

import jax
import jax.numpy as jnp
import numpy as np
from jax import lax
from jax.experimental import pallas as pl
from jax.experimental.pallas import tpu as pltpu
from jax.sharding import PartitionSpec as P


D, HEADS, HDIM, FF = 1280, 20, 64, 5120
ROWS, BLOCKS, HG = 128, 4, 5
GROUP = HG * HDIM
EPS = 1e-6
BF, F32 = jnp.bfloat16, jnp.float32
MESH = pl.DeviceIdType.MESH
VMEM_LIMIT = 60 << 20


def here():
    s = lax.axis_index("shard")
    return lax.axis_index("grp"), lax.axis_index("seq"), s // 4, s % 4


def dev(x, c, z, y):
    return (x, c, z * 4 + y)


def worker(z):
    return ((z + 1) // 2) % 2


def owner_z(w, i):
    return i * (3 - 2 * w) + w


def step(v, d):
    return (v + d) % 4


def rcopy(src, dst, ss, rs, to):
    return pltpu.make_async_remote_copy(
        src_ref=src, dst_ref=dst, send_sem=ss, recv_sem=rs, device_id=to, device_id_type=MESH
    )


def lcopy(src, dst, sem):
    return pltpu.make_async_copy(src, dst, sem)


def landed(dst, sem):
    pltpu.make_async_copy(dst, dst, sem).wait()


def greet(peers):
    bar = pltpu.get_barrier_semaphore()
    for p in peers:
        pl.semaphore_signal(bar, inc=1, device_id=p, device_id_type=MESH)
    pl.semaphore_wait(bar, len(peers))


def z_peers(x, c, z, y):
    far = [dev(x, cc, step(z, d), y) for d in (1, 2, 3) for cc in (0, 1)]
    return [dev(x, 1 - c, z, y)] + far


def z_gather_start(src, dst, ss, rs, x, c, z, y):
    w = worker(z)
    slot = (z // 2, c)
    for d in (1, 3, 2):
        rcopy(src, dst.at[slot], ss.at[d], rs.at[slot], dev(x, w, step(z, d), y)).start()

    @pl.when(c == w)
    def _():
        lcopy(src, dst.at[slot], rs.at[slot]).start()

    @pl.when(c != w)
    def _():
        rcopy(src, dst.at[slot], ss.at[0], rs.at[slot], dev(x, w, z, y)).start()


def z_gather_take(dst, rs, p):
    for k in range(2):
        landed(dst.at[p, k], rs.at[p, k])


def z_gather_sent(src, ss, c, z):
    for d in (1, 2, 3):
        landed(src, ss.at[d])

    @pl.when(c != worker(z))
    def _():
        landed(src, ss.at[0])


def z_gather_wait(src, dst, ss, rs, c, z):
    for p in range(2):
        z_gather_take(dst, rs, p)
    z_gather_sent(src, ss, c, z)


def z_scatter_pair(part, dst, ss, rs, p, x, c, z, y):
    oz = owner_z(c, p)
    for oc in range(2):
        mine = jnp.logical_and(c == oc, z == oz)

        @pl.when(mine)
        def _(oc=oc):
            lcopy(part.at[p, oc], dst.at[z], rs.at[z]).start()

        @pl.when(jnp.logical_not(mine))
        def _(oc=oc):
            rcopy(part.at[p, oc], dst.at[z], ss.at[p, oc], rs.at[z], dev(x, oc, oz, y)).start()


def z_scatter_start(part, dst, ss, rs, x, c, z, y):
    for p in range(2):
        z_scatter_pair(part, dst, ss, rs, p, x, c, z, y)


def z_scatter_take(dst, rs):
    for k in range(4):
        landed(dst.at[k], rs.at[k])


def z_scatter_sent(part, ss, c, z):
    for p in range(2):
        for oc in range(2):
            mine = jnp.logical_and(c == oc, z == owner_z(c, p))

            @pl.when(jnp.logical_not(mine))
            def _(p=p, oc=oc):
                landed(part.at[p, oc], ss.at[p, oc])


def remote_call(kernel, outs, ins_spaces, scratch, cid, name):
    spec = {
        "a": pl.BlockSpec(memory_space=pl.ANY),
        "v": pl.BlockSpec(memory_space=pltpu.VMEM),
        "s": pl.BlockSpec(memory_space=pltpu.SMEM),
    }
    return pl.pallas_call(
        kernel,
        out_shape=[jax.ShapeDtypeStruct(s, d) for s, d, _ in outs],
        in_specs=[spec[s] for s in ins_spaces],
        out_specs=[spec[s] for _, _, s in outs],
        scratch_shapes=scratch,
        compiler_params=pltpu.CompilerParams(
            collective_id=cid, has_side_effects=True, vmem_limit_bytes=VMEM_LIMIT
        ),
        name=name,
    )


def local_call(kernel, outs, n_in, scratch, name, smem=0):
    vmem = pl.BlockSpec(memory_space=pltpu.VMEM)
    sm = pl.BlockSpec(memory_space=pltpu.SMEM)
    return pl.pallas_call(
        kernel,
        out_shape=[jax.ShapeDtypeStruct(s, d) for s, d in outs],
        in_specs=[sm] * smem + [vmem] * n_in,
        out_specs=[vmem for _ in outs],
        scratch_shapes=scratch,
        compiler_params=pltpu.CompilerParams(vmem_limit_bytes=VMEM_LIMIT),
        name=name,
    )


def dma(*shape):
    return pltpu.SemaphoreType.DMA(shape)


def rope_tables():
    freqs = np.exp(np.arange(32) * (-2.0 * math.log(10000.0) / 64))
    freqs = np.tile(freqs, 4)
    sign = np.tile(np.concatenate([-np.ones(32), np.ones(32)]), 2)
    inner = np.arange(ROWS)[:, None] * freqs
    outer = (np.arange(32) * ROWS)[:, None] * freqs
    return (
        np.stack([np.cos(inner), np.sin(inner) * sign]).astype(np.float32),
        np.stack([np.cos(outer), np.sin(outer) * sign]).astype(np.float32),
    )


def block_index(c, y, j):
    return (j % 2) * 16 + owner_z(c, j // 2) * 4 + y


def turn_of(inner, outer, b):
    oc = outer[0, pl.ds(b, 1), :]
    os = outer[1, pl.ds(b, 1), :]
    return oc * inner[0] - os * inner[1], os * inner[0] + oc * inner[1]


def lanes():
    return lax.broadcasted_iota(jnp.int32, (ROWS, 128), 1)


def swap(v, lane):
    return jnp.where(lane % 64 < 32, pltpu.roll(v, 96, 1), pltpu.roll(v, 32, 1))


def half_means(v, lane):
    low = jnp.sum(jnp.where(lane < 64, v, 0.0), axis=-1, keepdims=True)
    high = jnp.sum(jnp.where(lane < 64, 0.0, v), axis=-1, keepdims=True)
    return jnp.where(lane < 64, low, high) * (1.0 / 64)


TILE = 512
STEP = 6


def tiles_of(c, j):
    return (j % 2) * 4 + owner_z(c, j // 2) + 1


def nt(a, b):
    return lax.dot_general(a, b, (((1,), (1,)), ((), ())), preferred_element_type=F32)


def tn(a, b):
    return lax.dot_general(a, b, (((0,), (0,)), ((), ())), preferred_element_type=F32)


def key_tile(ref, h, t):
    zz = t % 4
    return ref[h, worker(zz), zz // 2, t // 4].reshape(TILE, 128)


def work_items(c, y, length):
    n = [tiles_of(c, j) for j in range(BLOCKS)]
    starts = [n[0], n[0] + n[1], n[0] + n[1] + n[2]]
    query = lax.broadcasted_iota(jnp.int32, (1, ROWS), 1)

    def item(i):
        hits = [(i >= s).astype(jnp.int32) for s in starts]
        j = hits[0] + hits[1] + hits[2]
        t = i - hits[0] * n[0] - hits[1] * n[1] - hits[2] * n[2]
        last = query + y * ROWS + (tiles_of(c, j) - 1 - t) * TILE
        return j, t, jnp.minimum(last, length - 1 - t * TILE)

    return item


def columns(ref, k, half):
    return ref.at[:, pl.ds(pl.multiple_of(k * D + half * 640, 128), 640)]


def front_kernel(
    length, st, w_query, w_key, w_value, v_qk, v_attn, v_mlp, v_up, v_gate, w_out, w_up, w_gate, w_down, inner, outer,
    part, att, lse, kv_o, q_o, t_o, xg_o, wqkv_o, wo_o, scale_o, rate_a, rate_m, su, sg, uq, wd, gz,
    xg, wqkv, vecs, wo, y0, y1, kv, kvb, q, tt, low, acc, tot, uz, wq, vec,
    xs, xr, w1s, w1r, w2s, w2r, w3s, w3r, vs, vr, os, orr, lo,
    f1s, f1r, f2s, f2r, f3s, f3r, f4s, f4r, fl, sy, ry, sf, rf, ss, rs, kl, ol,
):
    x, c, z, y = here()
    sib = dev(x, 1 - c, z, y)
    half = pl.ds(pl.multiple_of(c * 640, 128), 640)
    other = pl.ds(pl.multiple_of((1 - c) * 640, 128), 640)
    to_z = [None] + [dev(x, c, step(z, d), y) for d in (1, 2, 3)]
    to_y = [None] + [dev(x, c, z, step(y, d)) for d in (1, 2, 3)]
    to_x = [None] + [dev(step(x, d), c, z, y) for d in (1, 2, 3)]
    near_first = (1, 3, 2)

    def head(ref, k):
        return ref[:, k * HDIM : (k + 1) * HDIM]

    @pl.when(c == 0)
    def _():
        for zz in range(4):
            for h in range(4):
                k = zz * HG + h
                wq[zz, :, h * 128 : (h + 1) * 128] = jnp.concatenate([head(w_query, k), head(w_key, k)], axis=1)

    @pl.when(c == 1)
    def _():
        for zz in range(4):
            k = zz * HG
            wq[zz, :, 0:128] = jnp.concatenate([head(w_query, k + 4), head(w_key, k + 4)], axis=1)
            for h in range(2):
                wq[zz, :, 128 + h * 128 : 256 + h * 128] = w_value[:, (k + 2 * h) * HDIM : (k + 2 * h + 2) * HDIM]
            last = head(w_value, k + 4)
            wq[zz, :, 384:512] = jnp.concatenate([last, jnp.zeros_like(last)], axis=1)

    vec[...] = jnp.zeros_like(vec)
    for ref, at, n in ((v_qk, 0, 80), (v_attn, 80, 80), (v_mlp, 160, 80), (v_up, 240, 320), (v_gate, 560, 320)):
        vec[:, at : at + n] = jnp.broadcast_to(ref[...].astype(F32).reshape(1, n), (8, n))
    greet(z_peers(x, c, z, y) + to_y[1:] + to_x[1:])

    for d in near_first:
        rcopy(wq.at[step(z, d)], wqkv.at[c, z, y], w1s.at[d], w1r.at[z], to_z[d]).start()
        rcopy(vec, vecs.at[z, y], vs.at[0, d], vr.at[0, z], to_z[d]).start()
    lcopy(wq.at[z], wqkv.at[c, z, y], lo.at[0]).start()
    lcopy(vec, vecs.at[z, y], lo.at[1]).start()
    for d in near_first:
        rcopy(w_out.at[:, half], wo.at[y, :, half], os.at[0, d], orr.at[0, y], to_y[d]).start()
    rcopy(w_out.at[:, half], wo.at[y, :, half], os.at[0, 0], orr.at[1, y], sib).start()
    lcopy(w_out.at[:, half], wo.at[y, :, half], lo.at[2]).start()

    for d in (1, 2, 3):
        landed(wqkv.at[c, step(z, d), y], w1r.at[step(z, d)])
        landed(vecs.at[step(z, d), y], vr.at[0, step(z, d)])
    landed(wqkv.at[c, z, y], lo.at[0])
    landed(vecs.at[z, y], lo.at[1])
    mine = wqkv.at[c, :, y]
    rcopy(mine, mine, w2s.at[0], w2r.at[0], to_y[1]).start()
    rcopy(mine, mine, w2s.at[1], w2r.at[1], to_y[3]).start()
    rcopy(mine, mine, w3s.at[0], w3r.at[0], sib).start()
    for d in near_first:
        rcopy(vecs.at[:, y], vecs.at[:, y], vs.at[1, d], vr.at[1, y], to_y[d]).start()
    z_gather_start(st, xg, xs, xr, x, c, z, y)
    for k, src, to in ((0, step(y, 3), to_y[1]), (1, step(y, 1), to_y[3])):
        block, piece = wqkv.at[c, :, src], wqkv.at[c, 2 * k : 2 * k + 2, src]
        landed(block, w2r.at[k])
        rcopy(piece, piece, w2s.at[2 + k], w2r.at[2 + k], to).start()
        rcopy(block, block, w3s.at[1 + k], w3r.at[1 + k], sib).start()
    for k in range(2):
        piece = wqkv.at[c, 2 * k : 2 * k + 2, step(y, 2)]
        landed(piece, w2r.at[2 + k])
        rcopy(piece, piece, w3s.at[3 + k], w3r.at[3 + k], sib).start()
    down = w_down.at[pl.ds(pl.multiple_of(x * 80, 16), 80), half]
    for d in near_first:
        rcopy(down, wd.at[y, x, :, half], f2s.at[1, d], f2r.at[1, y], to_y[d]).start()
    lcopy(down, wd.at[y, x, :, half], fl.at[2]).start()
    for d in (1, 2, 3):
        landed(vecs.at[:, step(y, d)], vr.at[1, step(y, d)])
    for zz in range(4):
        for yy in range(4):
            at = (zz * 4 + yy) * 80
            rate_a[:, at : at + 80] = vecs[zz, yy, :, 80:160]
            rate_m[:, at : at + 80] = vecs[zz, yy, :, 160:240]
    for yy in range(4):
        su[:, yy * 320 : (yy + 1) * 320] = vecs[z, yy, :, 240:560]
        sg[:, yy * 320 : (yy + 1) * 320] = vecs[z, yy, :, 560:880]
    scale = jnp.concatenate([vecs[z, yy, :, :80] for yy in range(4)], axis=1)
    for h in range(HG):
        sh = scale[:, h * HDIM : (h + 1) * HDIM]
        scale_o[:, h * 128 : (h + 1) * 128] = jnp.concatenate([sh, sh], axis=1)

    for p in range(2):
        z_gather_take(xg, xr, p)
    for d in near_first:
        rcopy(columns(w_gate, step(z, d), c), gz.at[z], f1s.at[1, d], f1r.at[1 + z], to_z[d]).start()
    lcopy(columns(w_gate, z, c), gz.at[z], fl.at[0]).start()

    @pl.when(z == x)
    def _():
        for d in near_first:
            rcopy(columns(w_up, step(z, d), c), uz, f1s.at[0, d], f1r.at[0], to_z[d]).start()
        lcopy(columns(w_up, z, c), uz, f1r.at[0]).start()

    for k, src in ((0, y), (1, step(y, 3)), (2, step(y, 1))):
        landed(wqkv.at[1 - c, :, src], w3r.at[k])
    for k in range(2):
        landed(wqkv.at[1 - c, 2 * k : 2 * k + 2, step(y, 2)], w3r.at[3 + k])
    lcopy(xg, xg_o, ol.at[0]).start()
    lcopy(wqkv, wqkv_o, ol.at[1]).start()

    def project(p, carry):
        rows = xg[p].reshape(2 * ROWS, D)
        y0[p] = jnp.dot(rows, wqkv[0].reshape(D, 512), preferred_element_type=F32)
        y1[p] = jnp.dot(rows, wqkv[1].reshape(D, 512), preferred_element_type=F32)
        return carry

    lax.fori_loop(0, 2, project, 0)
    lane = lanes()

    def send(h):
        rcopy(kv.at[h], kvb.at[h, c, :, :, y], sy.at[h, 0], ry.at[h, 0], to_y[1]).start()
        rcopy(kv.at[h], kvb.at[h, c, :, :, y], sy.at[h, 1], ry.at[h, 1], to_y[3]).start()
        rcopy(kv.at[h], kvb.at[h, c, :, :, y], ss.at[h, 0], rs.at[h, 0], sib).start()
        lcopy(kv.at[h], kvb.at[h, c, :, :, y], kl.at[h]).start()

    for h in range(HG):

        def per_block(j, carry, h=h):
            p, r = j // 2, pl.ds(pl.multiple_of((j % 2) * ROWS, ROWS), ROWS)
            cosine, sine = turn_of(inner, outer, block_index(c, y, j))
            raw = y0[p, r, h * 128 : (h + 1) * 128] if h < 4 else y1[p, r, 0:128]
            t = raw * cosine + swap(raw, lane) * sine
            unit = t * lax.rsqrt(half_means(t * t, lane) + EPS)
            both = unit * scale_o[0:1, h * 128 : (h + 1) * 128]
            pair = y1[p, r, 128 + (h // 2) * 128 : 256 + (h // 2) * 128]
            v = pair if h % 2 else pltpu.roll(pair, 64, 1)
            kv[h, p, j % 2] = jnp.where(lane < 64, pltpu.roll(both, 64, 1), v).astype(BF)
            rows = pl.ds(pl.multiple_of(j * ROWS, ROWS), ROWS)
            tt[h, rows, :] = t
            q[h, rows, :] = (jnp.where(lane < 64, both, 0.0).astype(BF).astype(F32) * 0.125).astype(BF)
            return carry

        lax.fori_loop(0, BLOCKS, per_block, 0, unroll=True)
        if h < 2:
            send(h)
    landed(wd.at[y, x, :, half], fl.at[2])
    for d in (1, 2, 3):
        landed(wd.at[step(y, d), x, :, half], f2r.at[1, step(y, d)])
    for d in near_first:
        rcopy(wd.at[:, x, :, half], wd.at[:, x, :, half], f3s.at[d], f3r.at[x], to_x[d]).start()
    rcopy(wd.at[:, x, :, half], wd.at[:, x, :, half], f4s.at[0], f4r.at[x], sib).start()
    lcopy(q, q_o, ol.at[2]).start()
    lcopy(tt, t_o, ol.at[3]).start()

    def near(h):
        for k, src, to in ((0, step(y, 3), to_y[1]), (1, step(y, 1), to_y[3])):
            landed(kvb.at[h, c, :, :, src], ry.at[h, k])
            rcopy(kvb.at[h, c, k, :, src], kvb.at[h, c, k, :, src], sf.at[h, k], rf.at[h, k], to).start()
            rcopy(kvb.at[h, c, :, :, src], kvb.at[h, c, :, :, src], ss.at[h, 1 + k], rs.at[h, 1 + k], sib).start()

    def far(h):
        src = step(y, 2)
        for k in range(2):
            landed(kvb.at[h, c, k, :, src], rf.at[h, k])
            rcopy(kvb.at[h, c, k, :, src], kvb.at[h, c, k, :, src], ss.at[h, 3 + k], rs.at[h, 3 + k], sib).start()

    def ready(h):
        landed(kvb.at[h, c, :, :, y], kl.at[h])
        landed(kvb.at[h, 1 - c, :, :, y], rs.at[h, 0])
        landed(kvb.at[h, 1 - c, :, :, step(y, 3)], rs.at[h, 1])
        landed(kvb.at[h, 1 - c, :, :, step(y, 1)], rs.at[h, 2])
        for k in range(2):
            landed(kvb.at[h, 1 - c, k, :, step(y, 2)], rs.at[h, 3 + k])
        lcopy(kvb.at[h], kv_o.at[h], kl.at[h]).start()

    item = work_items(c, y, length[0])

    def compute(h):
        acc[...] = jnp.zeros_like(acc)
        tot[...] = jnp.zeros_like(tot)

        def body(g, carry):
            key = lax.broadcasted_iota(jnp.int32, (TILE, ROWS), 0)
            its = [item(g * STEP + u) for u in range(STEP)]
            ks = [key_tile(kvb, h, t) for _, t, _ in its]
            ss_ = [
                nt(k, q[h, pl.ds(pl.multiple_of(j * ROWS, ROWS), ROWS), :]) for k, (j, _, _) in zip(ks, its)
            ]
            ps = [jnp.where(key <= bound, jnp.exp(s), 0.0) for s, (_, _, bound) in zip(ss_, its)]
            for k, p, (j, _, _) in zip(ks, ps, its):
                tot[j] += jnp.sum(p.reshape(TILE // 8, 8, ROWS), axis=0)
                acc[j] += tn(k, p.astype(BF))
            return carry

        lax.fori_loop(0, 18 // STEP, body, 0)
        for j in range(BLOCKS):
            total = jnp.sum(tot[j], axis=0, keepdims=True)
            lse[h, j : j + 1, :] = jnp.log(total)
            att[h, j * ROWS : (j + 1) * ROWS, :] = (acc[j, HDIM:] / total).T

    def spread_up():
        landed(uz, f1r.at[0])
        for d in near_first:
            rcopy(uz, uq.at[y], f2s.at[0, d], f2r.at[0, y], to_y[d]).start()
        lcopy(uz, uq.at[y], fl.at[1]).start()

    near(0)
    send(2)

    def per_head(i, carry):
        @pl.when(i + 1 < HG)
        def _():
            near(i + 1)

        @pl.when(i + 3 < HG)
        def _():
            send(i + 3)

        @pl.when(i == HG)
        def _():
            spread_up()

        @pl.when(i > 0)
        def _():
            ready(i - 1)
            compute(i - 1)

        @pl.when(i < HG)
        def _():
            far(i)

        return carry

    lax.fori_loop(0, HG + 1, per_head, 0)
    for h in range(HG):
        low[:, h * HDIM : (h + 1) * HDIM] = att[h].astype(BF)
    for d in near_first:
        y2 = step(y, d)
        landed(wo.at[y2, :, half], orr.at[0, y2])
        rcopy(wo.at[y2, :, half], wo.at[y2, :, half], os.at[1, d], orr.at[1, y2], sib).start()
    landed(wo.at[y, :, half], lo.at[2])
    for k in range(4):
        landed(wo.at[k, :, other], orr.at[1, k])
    lcopy(wo, wo_o, ol.at[4]).start()
    for p in range(2):
        v = jnp.dot(low[p * 256 : (p + 1) * 256, :], wo[...].reshape(GROUP, D), preferred_element_type=F32)
        part[p] = v.astype(BF).reshape(2, ROWS, D)

    for d in near_first:
        x2 = step(x, d)
        landed(wd.at[:, x2, :, half], f3r.at[x2])
        rcopy(wd.at[:, x2, :, half], wd.at[:, x2, :, half], f4s.at[d], f4r.at[x2], sib).start()
    landed(uz, fl.at[1])
    landed(uz, fl.at[0])
    for d in (1, 2, 3):
        landed(uq.at[step(y, d)], f2r.at[0, step(y, d)])
        landed(gz.at[step(z, d)], f1r.at[1 + step(z, d)])

    def sent(h, carry):
        for k in range(2):
            landed(kv.at[h], sy.at[h, k])
            landed(kv.at[h, 0], sf.at[h, k])
            landed(kv.at[h, 0], ss.at[h, 3 + k])
        for k in range(3):
            landed(kv.at[h], ss.at[h, k])
        landed(kvb.at[h], kl.at[h])
        return carry

    lax.fori_loop(0, HG, sent, 0)
    z_gather_sent(st, xs, c, z)
    for k in range(4):
        landed(wd.at[:, k, :, other], f4r.at[k])
        landed(wd.at[:, k, :, half], f4s.at[k])
    landed(wo.at[0, :, half], os.at[0, 0])
    for k in range(2):
        landed(mine, w2s.at[k])
        landed(wqkv.at[c, 0:2, y], w2s.at[2 + k])
        landed(wqkv.at[c, 0:2, y], w3s.at[3 + k])
    for k in range(3):
        landed(mine, w3s.at[k])
    for d in (1, 2, 3):
        landed(wqkv.at[c, z, y], w1s.at[d])
        landed(vec, vs.at[0, d])
        landed(vecs.at[:, y], vs.at[1, d])
        landed(wo.at[0, :, half], os.at[0, d])
        landed(wo.at[0, :, half], os.at[1, d])
        landed(uz, f1s.at[1, d])
        landed(uz, f2s.at[0, d])
        landed(uz, f2s.at[1, d])
        landed(wd.at[:, x, :, half], f3s.at[d])

    @pl.when(z == x)
    def _():
        for d in (1, 2, 3):
            landed(uz, f1s.at[0, d])

    landed(xg, ol.at[0])
    landed(wqkv, ol.at[1])
    landed(q, ol.at[2])
    landed(tt, ol.at[3])
    landed(wo, ol.at[4])


def front(length, st, w_query, w_key, w_value, vectors, w_out, w_up, w_gate, w_down, inner, outer):
    n = BLOCKS * ROWS
    V = pltpu.VMEM
    return remote_call(
        front_kernel,
        [
            ((2, 2, ROWS, D), BF, "v"),
            ((HG, n, HDIM), F32, "v"),
            ((HG, BLOCKS, 128), F32, "v"),
            ((HG, 2, 2, 2, 4, ROWS, 128), BF, "a"),
            ((HG, n, 128), BF, "a"),
            ((HG, n, 128), F32, "a"),
            ((2, 2, ROWS, D), BF, "a"),
            ((2, 4, 4, 80, 512), BF, "a"),
            ((4, 80, D), BF, "a"),
            ((8, HG * 128), F32, "v"),
            ((8, D), F32, "v"),
            ((8, D), F32, "v"),
            ((8, D), F32, "v"),
            ((8, D), F32, "v"),
            ((4, 80, 640), BF, "a"),
            ((4, 4, 80, D), BF, "a"),
            ((4, 80, 640), BF, "a"),
        ],
        "savvvvvvvvaaaavv",
        [
            V((2, 2, ROWS, D), BF), V((2, 4, 4, 80, 512), BF), V((4, 4, 8, 896), F32), V((4, 80, D), BF),
            V((2, 256, 512), F32), V((2, 256, 512), F32),
            V((HG, 2, 2, ROWS, 128), BF), V((HG, 2, 2, 2, 4, ROWS, 128), BF), V((HG, n, 128), BF), V((HG, n, 128), F32),
            V((n, GROUP), BF), V((BLOCKS, 128, ROWS), F32), V((BLOCKS, 8, ROWS), F32), V((80, 640), BF),
            V((4, 80, 512), BF), V((8, 896), F32),
            dma(4), dma(2, 2), dma(4), dma(4), dma(4), dma(4), dma(5), dma(5), dma(2, 4), dma(2, 4), dma(2, 4), dma(2, 4), dma(3),
            dma(2, 4), dma(5), dma(2, 4), dma(2, 4), dma(4), dma(4), dma(4), dma(4), dma(3),
            dma(HG, 2), dma(HG, 2), dma(HG, 2), dma(HG, 2), dma(HG, 5), dma(HG, 5), dma(HG), dma(5),
        ],
        0,
        "front",
    )(length, st, w_query, w_key, w_value, *vectors, w_out, w_up, w_gate, w_down, inner, outer)


def inv_rms(v):
    return lax.rsqrt(jnp.mean(v * v, axis=-1, keepdims=True) + EPS)


def back_rms(dy, yy, inv):
    return (dy - yy * jnp.mean(dy * yy, axis=-1, keepdims=True)) * inv


def total_of(buf):
    return (buf[0].astype(F32) + buf[1].astype(F32)) + (buf[2].astype(F32) + buf[3].astype(F32))


def mix_of(res, part, rate):
    inv_p = inv_rms(part)
    unit = part * inv_p
    diff = unit - res
    u = res + rate * diff
    inv_u = inv_rms(u)
    return u * inv_u, unit, inv_p, inv_u, diff


def mix_back(dy, res, part, rate):
    yy, unit, inv_p, inv_u, diff = mix_of(res, part, rate)
    du = back_rms(dy, yy, inv_u)
    return du * (1.0 - rate), back_rms(du * rate, unit, inv_p), jnp.sum(du * diff, axis=0, keepdims=True)


HALF = ROWS // 2


def mid_kernel(
    length, part0, st, cot, rate_a, rate_m, su, sg, uq, wd_in, gz,
    result, d_st, dm, ha_out, hd, vec,
    ha, buf, low, xg, dd, wu, wg, wd, up, gate, hid, dug, part, xt, ht, mixed, first, dfirst, ga, gd, ra, rd, rdy,
    ps, pr, gs, gr, s2, r2, s3, r3, sx, rx, sy, ry, lo,
):
    x, c, z, y = here()
    sib = dev(x, 1 - c, z, y)
    half = pl.ds(pl.multiple_of(c * 640, 128), 640)
    other = pl.ds(pl.multiple_of((1 - c) * 640, 128), 640)
    to_x = [None] + [dev(step(x, d), c, z, y) for d in (1, 2, 3)]
    to_y = [None] + [dev(x, c, z, step(y, d)) for d in (1, 2, 3)]

    def cut(k):
        return pl.ds(k * HALF, HALF)

    def scatter(n, src, k):
        for p in range(2):
            oz = owner_z(c, p)
            for oc in range(2):
                mine = jnp.logical_and(c == oc, z == oz)
                piece, to = src.at[p, oc, cut(k)], buf.at[n, z, cut(k)]

                @pl.when(mine)
                def _(piece=piece, to=to):
                    lcopy(piece, to, pr.at[n, k, z]).start()

                @pl.when(jnp.logical_not(mine))
                def _(piece=piece, to=to, p=p, oc=oc, oz=oz):
                    rcopy(piece, to, ps.at[n, k, p, oc], pr.at[n, k, z], dev(x, oc, oz, y)).start()

    def scatter_take(n, k):
        for i in range(4):
            landed(buf.at[n, i, cut(k)], pr.at[n, k, i])
        return total_of(buf.at[n, :, cut(k)])

    def scatter_sent(n, src):
        for k in range(2):
            for p in range(2):
                for oc in range(2):
                    mine = jnp.logical_and(c == oc, z == owner_z(c, p))

                    @pl.when(jnp.logical_not(mine))
                    def _(k=k, p=p, oc=oc):
                        landed(src.at[p, oc, cut(k)], ps.at[n, k, p, oc])

    def gather(n, dst, k):
        w = worker(z)
        piece, to, sem = low.at[n, cut(k)], dst.at[z // 2, c, cut(k)], gr.at[n, k, z // 2, c]
        for d in (1, 3, 2):
            rcopy(piece, to, gs.at[n, k, d], sem, dev(x, w, step(z, d), y)).start()

        @pl.when(c == w)
        def _():
            lcopy(piece, to, sem).start()

        @pl.when(c != w)
        def _():
            rcopy(piece, to, gs.at[n, k, 0], sem, dev(x, w, z, y)).start()

    def gather_take(n, dst, k):
        for p in range(2):
            for i in range(2):
                landed(dst.at[p, i, cut(k)], gr.at[n, k, p, i])

    def gather_sent(n):
        for k in range(2):
            for d in (1, 2, 3):
                landed(low.at[n, cut(k)], gs.at[n, k, d])

            @pl.when(c != worker(z))
            def _(k=k):
                landed(low.at[n, cut(k)], gs.at[n, k, 0])

    greet(z_peers(x, c, z, y) + to_x[1:] + to_y[1:])
    for k in range(2):
        scatter(0, part0, k)
    for d in (1, 3, 2):
        rcopy(uq, wu.at[x, :, :, half], s2.at[0, d], r2.at[0, x], to_x[d]).start()
        rcopy(gz, wg.at[:, y, :, half], s2.at[1, d], r2.at[1, y], to_y[d]).start()
    rcopy(uq, wu.at[x, :, :, half], s3.at[0, 0], r3.at[0, x], sib).start()
    rcopy(gz, wg.at[:, y, :, half], s3.at[1, 0], r3.at[1, y], sib).start()
    lcopy(uq, wu.at[x, :, :, half], lo.at[0]).start()
    lcopy(gz, wg.at[:, y, :, half], lo.at[1]).start()
    lcopy(wd_in, wd, lo.at[2]).start()
    vec[...] = jnp.zeros_like(vec)

    for k in range(2):
        total = scatter_take(0, k)
        out = mix_of(st[cut(k)].astype(F32), total, rate_a[0:1])[0]
        low[0, cut(k)] = out.astype(BF)
        gather(0, xg, k)
        mixed[cut(k)] = total
        first[cut(k)] = out

    for d in (1, 3, 2):
        x2, y2 = step(x, d), step(y, d)
        landed(wu.at[x2, :, :, half], r2.at[0, x2])
        rcopy(wu.at[x2, :, :, half], wu.at[x2, :, :, half], s3.at[0, d], r3.at[0, x2], sib).start()
        landed(wg.at[:, y2, :, half], r2.at[1, y2])
        rcopy(wg.at[:, y2, :, half], wg.at[:, y2, :, half], s3.at[1, d], r3.at[1, y2], sib).start()
    landed(wu.at[x, :, :, half], lo.at[0])
    landed(wg.at[:, y, :, half], lo.at[1])
    landed(wd, lo.at[2])
    for k in range(4):
        landed(wu.at[k, :, :, other], r3.at[0, k])
        landed(wg.at[:, k, :, other], r3.at[1, k])

    def rows_of(ref, k):
        return ref[:, :, cut(k)].reshape(4 * HALF, D)

    def forward(k):
        gather_take(0, xg, k)

        def cols(t, carry):
            cs = pl.ds(pl.multiple_of(t * 256, 256), 256)
            xs = rows_of(xg, k)
            u = jnp.dot(xs, wu[:, :, :, cs].reshape(D, 256), preferred_element_type=F32)
            g = jnp.dot(xs, wg[:, :, :, cs].reshape(D, 256), preferred_element_type=F32)
            tt = g * sg[0:1, cs]
            up[k, :, cs] = u
            gate[k, :, cs] = g
            hid[k, :, cs] = (u * su[0:1, cs] * (tt * jax.nn.sigmoid(tt))).astype(BF)
            return carry

        lax.fori_loop(0, 5, cols, 0)

        def down(t, carry):
            cs = pl.ds(pl.multiple_of(t * 256, 256), 256)
            v = jnp.dot(hid[k], wd[:, cs], preferred_element_type=F32)
            part[0, :, :, cut(k), cs] = v.astype(BF).reshape(2, 2, HALF, 256)
            return carry

        lax.fori_loop(0, 5, down, 0)
        scatter(1, part.at[0], k)

    for k in range(2):
        forward(k)

    def turn(dst, load):
        def body(t, carry):
            cs = pl.ds(pl.multiple_of(t * 256, 256), 256)
            for k in range(2):
                dst[cs, k * 256 : (k + 1) * 256] = load(k, cs).T
            return carry

        lax.fori_loop(0, 5, body, 0)

    turn(ht, lambda k, cs: hid[k, :, cs])
    am = rate_m[0:1]
    at = (c * 16 + z * 4 + y) * ROWS
    for k in range(2):
        total = scatter_take(1, k)
        position = at + k * HALF + lax.broadcasted_iota(jnp.int32, (HALF, 1), 0)
        live = (position < length[0]).astype(F32)
        base = first[cut(k)]
        d_base, d_part, g_am = mix_back(cot[cut(k)].astype(F32) * live, base, total, am)
        low[1, cut(k)] = d_part.astype(BF)
        gather(1, dd, k)
        dfirst[cut(k)] = d_base
        vec[1:2] += g_am
        result[cut(k)] = (mix_of(base, total, am)[0] * live).astype(BF)
    turn(xt, lambda k, cs: xg[:, :, cut(k), cs].reshape(256, 256))

    def backward(k):
        gather_take(1, dd, k)

        def cols(t, carry):
            cs = pl.ds(pl.multiple_of(t * 256, 256), 256)
            dh = nt(rows_of(dd, k), wd[cs, :])
            u, g = up[k, :, cs], gate[k, :, cs]
            sc, sgc = su[0:1, cs], sg[0:1, cs]
            tt = g * sgc
            sig = jax.nn.sigmoid(tt)
            silu = tt * sig
            dsilu = sig * (1.0 + tt * (1.0 - sig))
            dhs = dh * sc
            dhu = dh * u
            both = dhu * dsilu * sc
            dug[0, k, :, cs] = (dhs * silu).astype(BF)
            dug[1, k, :, cs] = (both * sgc).astype(BF)
            vec[2:3, cs] += jnp.sum(dhu * silu, axis=0, keepdims=True)
            vec[3:4, cs] += jnp.sum(both * g, axis=0, keepdims=True)
            return carry

        lax.fori_loop(0, 5, cols, 0)
        for t in range(2):
            v = nt(dug[0, k], wu[2 * t : 2 * t + 2].reshape(640, D)) + nt(
                dug[1, k], wg[2 * t : 2 * t + 2].reshape(640, D)
            )
            part[1, :, :, cut(k), t * 640 : (t + 1) * 640] = v.astype(BF).reshape(2, 2, HALF, 640)
        scatter(2, part.at[1], k)

    for k in range(2):
        backward(k)

    def meet(k):
        dy = dfirst[cut(k)] + scatter_take(2, k)
        d_res, d_part, g_aa = mix_back(dy, st[cut(k)].astype(F32), mixed[cut(k)], rate_a[0:1])
        low[2, cut(k)] = d_part.astype(BF)
        gather(2, dm, k)
        d_st[cut(k)] = d_res
        vec[0:1] += g_aa

    def grad_down(i, carry):
        w = jnp.where(i == 0, 1 - c, c)
        cols = pl.ds(pl.multiple_of(w * 640, 128), 640)
        for k in range(4):
            rhs = jnp.concatenate([dd[:, :, cut(j), cols].reshape(256, 640) for j in range(2)], axis=0)
            v = jnp.dot(ht[k * 320 : (k + 1) * 320, :], rhs, preferred_element_type=F32)
            gd[w, k] = v.astype(BF).reshape(4, 80, 640)

        @pl.when(i == 0)
        def _():
            rcopy(gd.at[1 - c], rd, sx.at[1], rx.at[1], sib).start()

        return carry

    def grad_up(w):
        def body(k, carry):
            rows = pl.ds(pl.multiple_of(k * 320, 64), 320)
            for t in range(2):
                cs = slice(t * 640, (t + 1) * 640)
                v = jnp.dot(xt[rows, :], dug[w, :, :, cs].reshape(512, 640), preferred_element_type=F32)
                ga[w, k, :, :, cs] = v.astype(BF).reshape(4, 80, 640)
            return carry

        lax.fori_loop(0, 4, body, 0)

    lax.fori_loop(0, 2, grad_down, 0)
    meet(0)
    landed(rd, rx.at[1])

    def add_d(k, carry):
        i, j = k // 4, k % 4
        rd[i, j] = (gd[c, i, j].astype(F32) + rd[i, j].astype(F32)).astype(BF)
        return carry

    lax.fori_loop(0, 16, add_d, 0)
    for d in (1, 3, 2):
        rcopy(rd.at[step(y, d)], rdy.at[y], sy.at[d], ry.at[y], to_y[d]).start()
    grad_up(1 - c)
    rcopy(ga.at[1 - c], ra, sx.at[0], rx.at[0], sib).start()
    meet(1)
    grad_up(c)
    landed(ra, rx.at[0])

    def add_a(k, carry):
        i, j = k // 4, k % 4
        ha[i, j] = (ga[c, i, j].astype(F32) + ra[i, j].astype(F32)).astype(BF)
        return carry

    lax.fori_loop(0, 16, add_a, 0)
    lcopy(ha, ha_out, lo.at[3]).start()
    for d in (1, 2, 3):
        landed(rdy.at[step(y, d)], ry.at[step(y, d)])

    def sum_d(k, carry):
        v = rd[y, k].astype(F32)
        for d in (1, 2, 3):
            v = v + rdy[step(y, d), k].astype(F32)
        hd[k] = v.astype(BF)
        return carry

    lax.fori_loop(0, 4, sum_d, 0)
    for k in range(2):
        gather_take(2, dm, k)
    for n in range(3):
        gather_sent(n)
    for n, src in ((0, part0), (1, part.at[0]), (2, part.at[1])):
        scatter_sent(n, src)
    for i in range(2):
        for k in range(4):
            landed(gz, s3.at[i, k])
        for d in (1, 2, 3):
            landed(gz, s2.at[i, d])
    landed(ra, sx.at[0])
    landed(rd, sx.at[1])
    landed(ha, lo.at[3])
    for d in (1, 2, 3):
        landed(rdy.at[y], sy.at[d])


def middle(length, part0, st, cot, rate_a, rate_m, su, sg, uq, wd, gz):
    V = pltpu.VMEM
    return remote_call(
        mid_kernel,
        [
            ((ROWS, D), BF, "v"),
            ((ROWS, D), F32, "v"),
            ((2, 2, ROWS, D), BF, "a"),
            ((4, 4, 80, D), BF, "a"),
            ((4, 80, 640), BF, "v"),
            ((8, D), F32, "v"),
        ],
        "savvvvvvaaa",
        [
            V((4, 4, 80, D), BF),
            V((3, 4, ROWS, D), BF), V((3, ROWS, D), BF), V((2, 2, ROWS, D), BF), V((2, 2, ROWS, D), BF),
            V((4, 4, 80, D), BF), V((4, 4, 80, D), BF), V((D, D), BF),
            V((2, 256, D), F32), V((2, 256, D), F32), V((2, 256, D), BF), V((2, 2, 256, D), BF),
            V((2, 2, 2, ROWS, D), BF), V((D, 512), BF), V((D, 512), BF),
            V((ROWS, D), F32), V((ROWS, D), F32), V((ROWS, D), F32),
            V((2, 4, 4, 80, D), BF), V((2, 4, 4, 80, 640), BF), V((4, 4, 80, D), BF), V((4, 4, 80, 640), BF),
            V((4, 4, 80, 640), BF),
            dma(3, 2, 2, 2), dma(3, 2, 4), dma(3, 2, 4), dma(3, 2, 2, 2),
            dma(2, 4), dma(2, 4), dma(2, 4), dma(2, 4), dma(2), dma(2), dma(4), dma(4), dma(4),
        ],
        2,
        "middle",
    )(length, part0, st, cot, rate_a, rate_m, su, sg, uq, wd, gz)


CUT = 896


def back_kernel(
    length, q_in, kv_in, wo_in, dmix_in, att_in, lse, ha, hd, tt_in, xg_in, wq_in, scale, inner, outer, vec,
    pbuf, za, zd, zq, o_out, o_vec,
    q, wo, dmix, att, kv, tt, xg, wq,
    qdo, delta, dqt, acc, low, give, mine, got, got_y, dq, dd, sums, part, gq, go,
    oax, oay, rax, ray, fax, fay, fd, hq, rqx, rqy, fqx, fqy, ob, ox, o2, vs, vb, ws, wb,
    lo, sg, rg, sy, ry, s1, r1, s2, r2, s3, r3, sz, rz, sc, rc, q1, p1, q2, p2, q3, p3, so, ro, sv, rv, sw, rw, ps, pr, sf, rf,
):
    x, c, z, y = here()
    sib = dev(x, 1 - c, z, y)
    to_y = [None] + [dev(x, c, z, step(y, d)) for d in (1, 2, 3)]
    to_x = [None] + [dev(step(x, d), c, z, y) for d in (1, 2, 3)]
    to_z = [None] + [dev(x, c, step(z, d), y) for d in (1, 2, 3)]
    near_first = (1, 3, 2)
    for i, (a, b) in enumerate(((dmix_in, dmix), (wo_in, wo), (att_in, att), (q_in, q))):
        lcopy(a, b, lo.at[6 + i]).start()
    lcopy(kv_in, kv, lo.at[0]).start()
    lcopy(ha.at[x, :, :, 0:CUT], oax, lo.at[1]).start()
    lcopy(ha.at[:, y, :, CUT:D], oay, lo.at[2]).start()
    lcopy(tt_in, tt, lo.at[3]).start()
    lcopy(xg_in, xg, lo.at[4]).start()
    lcopy(wq_in, wq, lo.at[5]).start()
    greet(z_peers(x, c, z, y) + to_y[1:] + to_x[1:])
    for d in near_first:
        rcopy(ha.at[step(x, d), :, :, 0:CUT], rax.at[x], s1.at[0, d], r1.at[0, x], to_x[d]).start()
        rcopy(ha.at[:, step(y, d), :, CUT:D], ray.at[y], s1.at[1, d], r1.at[1, y], to_y[d]).start()

    def settle(h):
        landed(got.at[h], rg.at[h])
        for i in range(2):
            for k in range(2):
                mine[h, i, k] = (mine[h, i, k].astype(F32) + got[h, i, k].astype(F32)).astype(BF)
        for d in near_first:
            rcopy(mine.at[h, :, :, step(y, d)], got_y.at[h, y], sy.at[h, d], ry.at[h, y], to_y[d]).start()

    for i, b in enumerate((dmix, wo, att, q)):
        landed(b, lo.at[6 + i])
    d_att = nt(dmix[...], wo[...]).astype(BF)
    for h in range(HG):
        low[:, h * HDIM : (h + 1) * HDIM] = att[h].astype(BF)
        dh = d_att[:, h * HDIM : (h + 1) * HDIM].astype(F32)
        wide = jnp.concatenate([jnp.zeros_like(dh), dh], axis=1).astype(BF)
        prod = dh * att[h]
        for j in range(BLOCKS):
            rows = slice(j * ROWS, (j + 1) * ROWS)
            qdo[h, j, :ROWS] = q[h, rows, :]
            qdo[h, j, ROWS:] = wide[rows]
            delta[h, j : j + 1, :] = jnp.sum(prod[rows].T, axis=0, keepdims=True)
    rcopy(vec, vb.at[0], sv.at[0, 0], rv.at[0, 0], sib).start()

    def small_start():
        for k in range(2):
            g = tn(low[...], dmix[:, k * 640 : (k + 1) * 640])
            go[k] = g.astype(BF).reshape(4, 80, 640)
        rcopy(go.at[1 - c], ob, sc.at[1], rc.at[1], sib).start()

    def small_cores():
        landed(ob, rc.at[1])
        landed(vb.at[0], rv.at[0, 0])
        vs[...] = vec[...] + vb[0]
        for k in range(4):
            ob[k] = (go[c, k].astype(F32) + ob[k].astype(F32)).astype(BF)
        for d in near_first:
            rcopy(ob.at[step(y, d)], ox.at[y], so.at[0, d], ro.at[0, y], to_y[d]).start()
            rcopy(vs, vb.at[d], sv.at[1, d], rv.at[1, d], to_y[d]).start()

    def small_y():
        v, tot = ob[y].astype(F32), vs[...]
        for d in (1, 2, 3):
            landed(ox.at[step(y, d)], ro.at[0, step(y, d)])
            landed(vb.at[d], rv.at[1, d])
            landed(vs, sv.at[1, d])
            v = v + ox[step(y, d)].astype(F32)
            tot = tot + vb[d]
        ox[y] = v.astype(BF)
        vs[...] = tot
        for d in near_first:
            rcopy(ox.at[y], o2.at[d], so.at[1, d], ro.at[1, d], to_x[d]).start()
            rcopy(vs, vb.at[3 + d], sv.at[2, d], rv.at[2, d], to_x[d]).start()

    def small_x():
        v, tot = ox[y].astype(F32), vs[...]
        for d in (1, 2, 3):
            landed(o2.at[d], ro.at[1, d])
            landed(vb.at[3 + d], rv.at[2, d])
            landed(vs, sv.at[2, d])
            v = v + o2[d].astype(F32)
            tot = tot + vb[3 + d]
        o_out[c] = v.astype(BF)
        vs[...] = tot
        rcopy(o_out.at[c], o_out.at[c], sf.at[3], rf.at[3], sib).start()
        for d in near_first:
            rcopy(vs, vb.at[6 + d], sv.at[3, d], rv.at[3, d], to_z[d]).start()

    def small_z():
        tot = vs[...]
        for d in (1, 2, 3):
            landed(vb.at[6 + d], rv.at[3, d])
            landed(vs, sv.at[3, d])
            tot = tot + vb[6 + d]
        o_vec[0:2] = tot[0:2]
        o_vec[2:] = vs[2:]

    def down_x():
        v = hd[x].astype(F32)
        for d in (1, 2, 3):
            landed(fd.at[step(x, d)], r2.at[1, step(x, d)])
            v = v + fd[step(x, d)].astype(F32)
        zd[c, x] = v.astype(BF)
        for d in near_first:
            rcopy(zd.at[c, x], zd.at[c, x], s3.at[1, d], r3.at[1, x], to_x[d]).start()

    def down_done():
        for d in (1, 2, 3):
            landed(zd.at[c, step(x, d)], r3.at[1, step(x, d)])
        rcopy(zd.at[c], zd.at[c], sf.at[1], rf.at[1], sib).start()

    def up_first():
        landed(oax, lo.at[1])
        landed(oay, lo.at[2])
        for d in (1, 2, 3):
            landed(rax.at[step(x, d)], r1.at[0, step(x, d)])
            landed(ray.at[step(y, d)], r1.at[1, step(y, d)])

        def body(k, carry):
            v, w = oax[k].astype(F32), oay[k].astype(F32)
            for d in (1, 2, 3):
                v = v + rax[step(x, d), k].astype(F32)
                w = w + ray[step(y, d), k].astype(F32)
            oax[k] = v.astype(BF)
            oay[k] = w.astype(BF)
            return carry

        lax.fori_loop(0, 4, body, 0)
        for d in near_first:
            rcopy(oax.at[step(y, d)], fax.at[y], s2.at[0, d], r2.at[0, y], to_y[d]).start()
            rcopy(oay.at[step(x, d)], fay.at[x], s2.at[2, d], r2.at[2, x], to_x[d]).start()
        for d in near_first:
            rcopy(hd.at[step(x, d)], fd.at[x], s2.at[1, d], r2.at[1, x], to_x[d]).start()

    landed(kv, lo.at[0])
    item = work_items(c, y, length[0])

    def per_head(h, carry):
        acc[...] = jnp.zeros_like(acc)
        dqt[...] = jnp.zeros_like(dqt)
        for k, f in ((1, small_start), (3, small_cores)):
            pl.when(h == k)(f)

        def body(g, carry):
            @pl.when(jnp.logical_and(g == 1, h > 0))
            def _():
                settle(h - 1)

            pl.when(jnp.logical_and(g == 0, h == HG - 1))(up_first)
            pl.when(jnp.logical_and(g == 1, h == HG - 1))(small_y)
            key = lax.broadcasted_iota(jnp.int32, (TILE, ROWS), 0)
            its = [item(g * STEP + u) for u in range(STEP)]
            ks = [key_tile(kv, h, t) for _, t, _ in its]
            bs = [qdo[h, j] for j, _, _ in its]
            sds = [nt(k, b) for k, b in zip(ks, bs)]
            dss, pp = [], []
            for sd, (j, _, bound) in zip(sds, its):
                p = jnp.where(key <= bound, jnp.exp(sd[:, :ROWS] - lse[h, pl.ds(j, 1), :]), 0.0)
                dss.append((p * (sd[:, ROWS:] - delta[h, pl.ds(j, 1), :])).astype(BF))
                pp.append(p.astype(BF))
            for ds, p, b, (_, t, _) in zip(dss, pp, bs, its):
                acc[t] += jnp.dot(jnp.concatenate([ds, p], axis=1), b, preferred_element_type=F32)
            for k, ds, (j, _, _) in zip(ks, dss, its):
                dqt[j] += tn(k, ds)
            return carry

        lax.fori_loop(0, 18 // STEP, body, 0)

        def store(i, carry):
            zi, k = i // 2, i % 2
            give[h, zi, k] = acc[k * 4 + owner_z(1 - c, zi)].astype(BF).reshape(4, ROWS, 128)
            mine[h, zi, k] = acc[k * 4 + owner_z(c, zi)].astype(BF).reshape(4, ROWS, 128)
            return carry

        lax.fori_loop(0, 4, store, 0, unroll=True)
        rcopy(give.at[h], got.at[h], sg.at[h], rg.at[h], sib).start()
        for j in range(BLOCKS):
            dq[h, j * ROWS : (j + 1) * ROWS, :] = dqt[j].T * 0.125
        return carry

    lax.fori_loop(0, HG, per_head, 0)
    settle(HG - 1)
    for d in (1, 2, 3):
        landed(fax.at[step(y, d)], r2.at[0, step(y, d)])
        landed(fay.at[step(x, d)], r2.at[2, step(x, d)])
    v, w = oax[y].astype(F32), oay[x].astype(F32)
    for d in (1, 2, 3):
        v = v + fax[step(y, d)].astype(F32)
        w = w + fay[step(x, d)].astype(F32)
    za[2, x, :, 0:CUT] = v.astype(BF)
    za[2, x, :, CUT:D] = w.astype(BF)
    for d in near_first:
        rcopy(za.at[2, x], za.at[2, x], s3.at[0, d], r3.at[0, x], to_x[d]).start()
    ws[...] = jnp.zeros_like(ws)
    landed(tt, lo.at[3])
    landed(xg, lo.at[4])
    landed(wq, lo.at[5])
    sums[...] = jnp.zeros_like(sums)
    lane = lanes()

    def through(h, carry):
        for d in (1, 2, 3):
            landed(got_y.at[h, step(y, d)], ry.at[h, step(y, d)])
        cols = pl.ds(pl.multiple_of(h * 128, 128), 128)
        pair = pl.ds(pl.multiple_of(640 + (h // 2) * 128, 128), 128)
        odd = h % 2 == 1

        def per_block(j, carry):
            i, k = j // 2, j % 2
            rows = pl.ds(pl.multiple_of(j * ROWS, ROWS), ROWS)
            cosine, sine = turn_of(inner, outer, block_index(c, y, j))
            grads = mine[h, i, k, y].astype(F32)
            for d in (1, 2, 3):
                grads = grads + got_y[h, step(y, d), i, k].astype(F32)
            grads = grads.astype(BF).astype(F32)
            turned = pltpu.roll(grads, 64, 1)
            t = tt[h, rows, :]
            dy = jnp.where(lane < 64, dq[h, rows, :].astype(BF).astype(F32), turned)
            inv = lax.rsqrt(half_means(t * t, lane) + EPS)
            unit = t * inv
            sums[:, cols] += jnp.sum((dy * unit).reshape(ROWS // 8, 8, 128), axis=0)
            dyh = dy * scale[0:1, cols]
            dt = (dyh - unit * half_means(dyh * unit, lane)) * inv
            dd[rows, cols] = (dt * cosine + swap(dt * sine, lane)).astype(BF)
            before = jnp.where(odd, dd[rows, pair].astype(F32), turned)
            dd[rows, pair] = jnp.where(lane < 64, before, jnp.where(odd, grads, 0.0)).astype(BF)
            return carry

        lax.fori_loop(0, BLOCKS, per_block, 0, unroll=True)
        return carry

    lax.fori_loop(0, 2, through, 0)
    down_x()
    small_x()
    lax.fori_loop(2, HG, through, 0)

    def inputs(p, carry):
        rows = pl.ds(pl.multiple_of(p * 256, 256), 256)
        v = nt(dd[rows, 0:512], wq[0].reshape(D, 512)) + nt(dd[rows, 512:1024], wq[1].reshape(D, 512))
        part[p] = v.astype(BF).reshape(2, ROWS, D)
        z_scatter_pair(part, pbuf, ps, pr, p, x, c, z, y)
        return carry

    def along_z():
        for d in (1, 2, 3):
            landed(za.at[2, step(x, d)], r3.at[0, step(x, d)])
        for d in near_first:
            rcopy(za.at[2, step(z, d)], za.at[c, z], sz.at[0, d], rz.at[0, z], to_z[d]).start()
        za[c, z] = za[2, z]

    def weights(i, carry):
        h = jnp.where(i == 0, 1 - c, c)
        cols = pl.ds(pl.multiple_of(h * 512, 128), 512)
        gq[h] = tn(xg[...].reshape(512, D), dd[:, cols]).astype(BF).reshape(4, 4, 80, 512)

        @pl.when(i == 0)
        def _():
            rcopy(gq.at[1 - c], hq, sc.at[0], rc.at[0], sib).start()
            along_z()
            lax.fori_loop(0, 2, inputs, 0)

        return carry

    lax.fori_loop(0, 2, weights, 0)
    for h in range(HG):
        v = jnp.sum(sums[:, h * 128 : (h + 1) * 128], axis=0, keepdims=True)
        ws[:, h * HDIM : (h + 1) * HDIM] = jnp.broadcast_to(v[:, :HDIM] + v[:, HDIM:], (8, HDIM))
    rcopy(ws, wb.at[0], sw.at[0, 0], rw.at[0, 0], sib).start()

    small_z()
    landed(hq, rc.at[0])

    def add_q(k, carry):
        i, j = k // 4, k % 4
        v = (gq[c, i, j].astype(F32) + hq[i, j].astype(F32)).astype(BF)
        fqx[i, j] = v[:, :256]
        fqy[j, i] = v[:, 256:]
        return carry

    lax.fori_loop(0, 16, add_q, 0)
    for d in near_first:
        rcopy(fqx.at[step(x, d)], rqx.at[x], q1.at[0, d], p1.at[0, x], to_x[d]).start()
        rcopy(fqy.at[step(y, d)], rqy.at[y], q1.at[1, d], p1.at[1, y], to_y[d]).start()
    landed(wb.at[0], rw.at[0, 0])
    landed(ws, sw.at[0, 0])
    ws[...] = ws[...] + wb[0]
    for d in near_first:
        rcopy(ws, wb.at[d], sw.at[1, d], rw.at[1, d], to_y[d]).start()
    for d in (1, 2, 3):
        landed(rqx.at[step(x, d)], p1.at[0, step(x, d)])
        landed(rqy.at[step(y, d)], p1.at[1, step(y, d)])

    def add_q1(k, carry):
        a, b = fqx[x, k].astype(F32), fqy[y, k].astype(F32)
        for d in (1, 2, 3):
            a = a + rqx[step(x, d), k].astype(F32)
            b = b + rqy[step(y, d), k].astype(F32)
        rqx[x, k] = a.astype(BF)
        rqy[y, k] = b.astype(BF)
        return carry

    lax.fori_loop(0, 4, add_q1, 0)
    for d in near_first:
        rcopy(rqx.at[x, step(y, d)], fqx.at[4, y], q2.at[0, d], p2.at[0, y], to_y[d]).start()
        rcopy(rqy.at[y, step(x, d)], fqy.at[4, x], q2.at[1, d], p2.at[1, x], to_x[d]).start()
    tot = ws[...]
    for d in (1, 2, 3):
        landed(wb.at[d], rw.at[1, d])
        landed(ws, sw.at[1, d])
        tot = tot + wb[d]
    ws[...] = tot
    for d in near_first:
        rcopy(ws, wb.at[3 + d], sw.at[2, d], rw.at[2, d], to_x[d]).start()
    for d in (1, 2, 3):
        landed(fqx.at[4, step(y, d)], p2.at[0, step(y, d)])
        landed(fqy.at[4, step(x, d)], p2.at[1, step(x, d)])
    a, b = rqx[x, y].astype(F32), rqy[y, x].astype(F32)
    for d in (1, 2, 3):
        a = a + fqx[4, step(y, d)].astype(F32)
        b = b + fqy[4, step(x, d)].astype(F32)
    zq[0, x] = jnp.concatenate([a, b], axis=1).astype(BF)
    for d in near_first:
        rcopy(zq.at[0, x], zq.at[0, x], q3.at[d], p3.at[x], to_x[d]).start()
    down_done()
    tot = ws[...]
    for d in (1, 2, 3):
        landed(wb.at[3 + d], rw.at[2, d])
        landed(ws, sw.at[2, d])
        tot = tot + wb[3 + d]
    o_vec[4:5, 0:384] = tot[0:1]
    for d in (1, 2, 3):
        landed(zq.at[0, step(x, d)], p3.at[step(x, d)])
    for d in near_first:
        rcopy(zq.at[0, step(z, d)], zq.at[1 + c, z], sz.at[1, d], rz.at[1, z], to_z[d]).start()
    zq[1 + c, z] = zq[0, z]
    for d in (1, 2, 3):
        landed(za.at[c, step(z, d)], rz.at[0, step(z, d)])
    rcopy(za.at[c], za.at[c], sf.at[0], rf.at[0], sib).start()
    for d in (1, 2, 3):
        landed(zq.at[1 + c, step(z, d)], rz.at[1, step(z, d)])
    rcopy(zq.at[1 + c], zq.at[1 + c], sf.at[2], rf.at[2], sib).start()
    z_scatter_take(pbuf, pr)
    landed(za.at[1 - c], rf.at[0])
    landed(zd.at[1 - c], rf.at[1])
    landed(zq.at[2 - c], rf.at[2])
    landed(o_out.at[1 - c], rf.at[3])
    def sent(h, carry):
        landed(give.at[h], sg.at[h])
        for d in (1, 2, 3):
            landed(got_y.at[h, y], sy.at[h, d])
        return carry

    lax.fori_loop(0, HG, sent, 0)
    z_scatter_sent(part, ps, c, z)
    landed(hq, sc.at[0])
    landed(ob, sc.at[1])
    landed(vec, sv.at[0, 0])
    landed(o_out.at[0], sf.at[3])
    landed(za.at[0], sf.at[0])
    landed(zd.at[0], sf.at[1])
    landed(zq.at[1], sf.at[2])
    for d in (1, 2, 3):
        landed(rax.at[x], s1.at[0, d])
        landed(ray.at[y], s1.at[1, d])
        landed(fax.at[0], s2.at[0, d])
        landed(fd.at[0], s2.at[1, d])
        landed(fay.at[0], s2.at[2, d])
        landed(za.at[0, 0], s3.at[0, d])
        landed(fd.at[0], s3.at[1, d])
        landed(za.at[0, 0], sz.at[0, d])
        landed(zq.at[0, 0], sz.at[1, d])
        landed(rqx.at[0], q1.at[0, d])
        landed(rqy.at[0], q1.at[1, d])
        landed(fqx.at[0, 0], q2.at[0, d])
        landed(fqy.at[0, 0], q2.at[1, d])
        landed(zq.at[0, 0], q3.at[d])
        landed(ox.at[0], so.at[0, d])
        landed(ox.at[0], so.at[1, d])


def back(length, q, kv, wo, dmix, att, lse, ha, hd, tt, xg, wq, scale, inner, outer, vec):
    n = BLOCKS * ROWS
    V = pltpu.VMEM
    return remote_call(
        back_kernel,
        [
            ((4, ROWS, D), BF, "v"),
            ((3, 4, 80, D), BF, "v"),
            ((2, 4, 80, 640), BF, "v"),
            ((3, 4, 80, 512), BF, "v"),
            ((2, 80, 640), BF, "v"),
            ((8, D), F32, "v"),
        ],
        "saaaaavavaaavvvv",
        [
            V((HG, n, 128), BF), V((GROUP, D), BF), V((n, D), BF), V((HG, n, HDIM), F32),
            V((HG, 2, 2, 2, 4, ROWS, 128), BF), V((HG, n, 128), F32), V((2, 2, ROWS, D), BF), V((2, 4, 4, 80, 512), BF),
            V((HG, BLOCKS, 2 * ROWS, 128), BF), V((HG, BLOCKS, 128), F32), V((BLOCKS, 128, ROWS), F32), V((8, TILE, 128), F32),
            V((n, GROUP), BF),
            V((HG, 2, 2, 4, ROWS, 128), BF), V((HG, 2, 2, 4, ROWS, 128), BF), V((HG, 2, 2, 4, ROWS, 128), BF),
            V((HG, 4, 2, 2, ROWS, 128), BF), V((HG, n, 128), F32), V((n, 1024), BF), V((8, HG * 128), F32),
            V((2, 2, ROWS, D), BF), V((2, 4, 4, 80, 512), BF), V((2, 4, 80, 640), BF),
            V((4, 80, CUT), BF), V((4, 80, D - CUT), BF), V((4, 4, 80, CUT), BF), V((4, 4, 80, D - CUT), BF),
            V((4, 80, CUT), BF), V((4, 80, D - CUT), BF), V((4, 80, 640), BF),
            V((4, 4, 80, 512), BF), V((4, 4, 80, 256), BF), V((4, 4, 80, 256), BF), V((5, 4, 80, 256), BF), V((5, 4, 80, 256), BF),
            V((4, 80, 640), BF), V((4, 80, 640), BF), V((4, 80, 640), BF), V((8, D), F32), V((10, 8, D), F32), V((8, 384), F32), V((7, 8, 384), F32),
            dma(10), dma(HG), dma(HG), dma(HG, 4), dma(HG, 4),
            dma(2, 4), dma(2, 4), dma(3, 4), dma(3, 4), dma(2, 4), dma(2, 4), dma(2, 4), dma(2, 4), dma(2), dma(2),
            dma(2, 4), dma(2, 4), dma(2, 4), dma(2, 4), dma(4), dma(4), dma(2, 4), dma(2, 4), dma(4, 4), dma(4, 4), dma(3, 4), dma(3, 4),
            dma(2, 2), dma(4), dma(4), dma(4),
        ],
        3,
        "back",
    )(length, q, kv, wo, dmix, att, lse, ha, hd, tt, xg, wq, scale, inner, outer, vec)


def finish_kernel(
    res, d_st, pbuf, za, zd, zq, out, vec,
    result, g_in, o_q, o_k, o_v, o_out, o_up, o_gate, o_down, v_qk, v_attn, v_mlp, v_up, v_gate,
):
    _, _, z, y = here()
    step_no = pl.program_id(0)
    result[...] = res[...]
    g_in[...] = d_st[...] + total_of(pbuf)
    o_up[...] = za[0, 0].astype(F32)
    o_gate[...] = za[1, 0].astype(F32)
    for h in range(2):
        o_down[:, h * 640 : (h + 1) * 640] = zd[h, 0].astype(F32)
    a, b = zq[1, 0].astype(F32), zq[2, 0].astype(F32)
    pairs = [a[:, h * 128 : (h + 1) * 128] for h in range(4)] + [b[:, :128]]
    for k in range(4):

        @pl.when(step_no == k)
        def _(at=k * GROUP):
            o_q[:, at : at + GROUP] = jnp.concatenate([v[:, :HDIM] for v in pairs], axis=1)
            o_k[:, at : at + GROUP] = jnp.concatenate([v[:, HDIM:] for v in pairs], axis=1)
            o_v[:, at : at + GROUP] = b[:, 128:448]

    @pl.when(step_no == 0)
    def _():
        o_out[:, :640] = out[0].astype(F32)
        o_out[:, 640:] = out[1].astype(F32)
        v = vec[...]
        by_shard = pltpu.roll(v, (16 - (z * 4 + y)) % 16 * 80, 1)
        by_y = pltpu.roll(v, (4 - y) % 4 * 320, 1)
        v_attn[...] = by_shard[0:1, :80].reshape(80)
        v_mlp[...] = by_shard[1:2, :80].reshape(80)
        v_up[...] = by_y[2:3, :320].reshape(320)
        v_gate[...] = by_y[3:4, :320].reshape(320)
        v_qk[...] = pltpu.roll(v, (16 - y) % 16 * 80, 1)[4:5, :80].reshape(80)


def finish(res, d_st, pbuf, za, zd, zq, out, vec):
    def whole(*shape):
        return pl.BlockSpec(shape, lambda k: (0,) * len(shape))

    rows = ROWS // 4
    outs = [
        ((ROWS, D), BF, pl.BlockSpec((rows, D), lambda k: (k, 0))),
        ((ROWS, D), F32, pl.BlockSpec((rows, D), lambda k: (k, 0))),
        ((80, D), F32, whole(80, D)),
        ((80, D), F32, whole(80, D)),
        ((80, D), F32, whole(80, D)),
        ((80, D), F32, whole(80, D)),
        ((80, FF), F32, pl.BlockSpec((80, D), lambda k: (0, k))),
        ((80, FF), F32, pl.BlockSpec((80, D), lambda k: (0, k))),
        ((320, D), F32, pl.BlockSpec((80, D), lambda k: (k, 0))),
        ((80,), F32, whole(80)),
        ((80,), F32, whole(80)),
        ((80,), F32, whole(80)),
        ((320,), F32, whole(320)),
        ((320,), F32, whole(320)),
    ]
    return pl.pallas_call(
        finish_kernel,
        grid=(4,),
        out_shape=[jax.ShapeDtypeStruct(s, d) for s, d, _ in outs],
        in_specs=[
            pl.BlockSpec((rows, D), lambda k: (k, 0)),
            pl.BlockSpec((rows, D), lambda k: (k, 0)),
            pl.BlockSpec((4, rows, D), lambda k: (0, k, 0)),
            pl.BlockSpec((2, 1, 80, D), lambda k: (0, k, 0, 0)),
            pl.BlockSpec((2, 1, 80, 640), lambda k: (0, k, 0, 0)),
            pl.BlockSpec((3, 1, 80, 512), lambda k: (0, k, 0, 0)),
            whole(2, 80, 640),
            whole(8, D),
        ],
        out_specs=[spec for _, _, spec in outs],
        compiler_params=pltpu.CompilerParams(vmem_limit_bytes=VMEM_LIMIT),
        name="finish",
    )(res, d_st, pbuf, za, zd, zq, out, vec)


def shards(
    states, w_query, w_key, w_value, w_out, w_up, w_gate, w_down,
    scale_qk, alpha_attn, alpha_mlp, scale_up, scale_gate, lengths, cotangent,
):
    x, c, z, y = here()
    st = states[0]

    vectors = (scale_qk, alpha_attn, alpha_mlp, scale_up, scale_gate)
    inner, outer = (jnp.asarray(t) for t in rope_tables())
    n = BLOCKS * ROWS
    part, att, lse, kv, q, turned, xg, wqkv, wo, scale, rate_a, rate_m, su, sg, uq, wd, gz = front(
        lengths, st, w_query, w_key, w_value, vectors, w_out, w_up, w_gate, w_down, inner, outer
    )
    result, d_st, dm, ha, hd, vec = middle(
        lengths, part, st, cotangent[0], rate_a, rate_m, su, sg, uq, wd.reshape(D, D), gz
    )
    pbuf, za, zd, zq, out, vec = back(
        lengths, q, kv, wo.reshape(GROUP, D), dm.reshape(n, D), att, lse, ha, hd, turned, xg, wqkv, scale, inner, outer, vec
    )
    outs = finish(result, d_st, pbuf, za, zd, zq, out, vec)
    return (outs[0][None], outs[1][None], *outs[2:])


def solution(mesh):
    row = P("grp", ("seq", "shard"), None)
    mat = P("shard", None)
    one = P("shard")
    return jax.shard_map(
        shards,
        mesh=mesh,
        in_specs=(row,) + (mat,) * 7 + (one,) * 5 + (P("grp"), row),
        out_specs=(row, row) + (mat,) * 7 + (one,) * 5,
        check_vma=False,
    )
```
